32 devices in a mesh: dom: 8 (over z, core), four: 4 (over y, x).
Axes of the slice: x: 2, y: 2, z: 4, core: 2. Of those that a mesh axis runs over, the one named last changes fastest.
Arguments:
- velocity: float32 [3, 128, 18432], P(None, 'four', 'dom'), may hold values from -16 to 16
- partner: int32 [8, 4], P('dom'), may hold values from -1 to 7, as said below
- partner_side: int32 [8, 4], P('dom'), may hold values from -1 to 3, as said below
- flipped: int32 [8, 4], P('dom'), may hold values from 0 to 1, as said below
Outputs:
- new_velocity: float32 [3, 128, 18432], P(None, 'four', 'dom')
- residual: float32 [3, 128, 18432], P(None, 'four', 'dom')
The draws below stay inside these ranges and needn't reach their ends.
Inputs may be any that keep to these rules, and one draw needn't show every extreme that they name: `partner`: sides are numbered 0 bottom, 1 right, 2 top, 3 left. Gluing is symmetric: if side s of partition p is glued to side s2 of partition q, then side s2 of q is glued to side s of p with the same flipped value. No side is glued to itself, and exactly 4 sides are walls (-1). `partner_side`: -1 exactly where partner is -1. `flipped`: 0 on wall sides.
All inputs are finite; a program needn't handle non-finite values.
Results may differ from the reference program's by a relative error of at most 0.0003.
Values sent between devices are 32-bit elements; how exact they have to be, the bound alone decides.
No kernel may reach another device: no remote copies, remote signals or barrier semaphores. Data moves between devices by JAX's collectives and lax.ppermute only.
A program may use at most 128 MiB of HBM per device.

```python
import math
import jax
import jax.numpy as jnp
import numpy as np
from jax import lax

EB = 8
PLANES = 128
ITERS = 4
PARTS_SIZE = 8


def draw_velocity(key, part):
    noise_key, scale_key = jax.random.split(key, 2)
    full_shape = (3, PLANES, PARTS_SIZE, EB, 6, EB, 6)
    log_scale = jax.random.uniform(scale_key, (1, 1, PARTS_SIZE, EB, 1, EB, 1), jnp.float32, math.log(0.2), math.log(2.0))
    element_scale = jnp.exp(log_scale)
    position = jnp.arange(PARTS_SIZE, dtype=jnp.float32).reshape(1, 1, PARTS_SIZE, 1, 1, 1, 1) / (PARTS_SIZE - 1)
    noise_values = jnp.clip(jax.random.normal(noise_key, full_shape, jnp.float32), -4.0, 4.0)
    field = noise_values * element_scale * (1.0 + position)
    return field.reshape(3, PLANES, PARTS_SIZE * EB * EB * 36)


def matching_tables(key):
    mixed_key = jax.random.fold_in(key, 4242)
    order_key, flip_key = jax.random.split(mixed_key)
    side_total = 4 * PARTS_SIZE
    glued_pairs = (side_total - PARTS_SIZE // 2) // 2
    shuffled = jax.random.permutation(order_key, side_total).astype(jnp.int32)
    first_half = shuffled[0:2 * glued_pairs:2]
    second_half = shuffled[1:2 * glued_pairs:2]
    flip_bits = jax.random.randint(flip_key, (glued_pairs,), 0, 2).astype(jnp.int32)
    partner_table = jnp.full((side_total,), -1, jnp.int32)
    partner_table = partner_table.at[first_half].set(second_half // 4).at[second_half].set(first_half // 4)
    side_table = jnp.full((side_total,), -1, jnp.int32)
    side_table = side_table.at[first_half].set(second_half % 4).at[second_half].set(first_half % 4)
    flip_table = jnp.zeros((side_total,), jnp.int32)
    flip_table = flip_table.at[first_half].set(flip_bits).at[second_half].set(flip_bits)
    return (partner_table.reshape(PARTS_SIZE, 4), side_table.reshape(PARTS_SIZE, 4), flip_table.reshape(PARTS_SIZE, 4))


def draw_partner(key, part):
    return matching_tables(key)[0]


def draw_partner_side(key, part):
    return matching_tables(key)[1]


def draw_flipped(key, part):
    return matching_tables(key)[2]


def setup_inputs(seed: int = 0) -> dict:
    keys = jax.random.split(jax.random.key(seed), 5)
    velocity = draw_velocity(jax.random.fold_in(keys[4], 71), 0)
    partner = draw_partner(jax.random.fold_in(keys[4], 71), 0)
    partner_side = draw_partner_side(jax.random.fold_in(keys[4], 71), 0)
    flipped = draw_flipped(jax.random.fold_in(keys[4], 71), 0)
    return {"velocity": velocity, "partner": partner, "partner_side": partner_side, "flipped": flipped}


REACTION = 2.0
WAVE_STEP = 0.0625
HIGHEST = lax.Precision.HIGHEST

def gll_tables():
    inner_near = math.sqrt(1.0 / 3.0 - 2.0 * math.sqrt(7.0) / 21.0)
    inner_far = math.sqrt(1.0 / 3.0 + 2.0 * math.sqrt(7.0) / 21.0)
    points = np.array([-1.0, -inner_far, -inner_near, inner_near, inner_far, 1.0])
    values = (63.0 * points ** 5 - 70.0 * points ** 3 + 15.0 * points) / 8.0
    weights = 2.0 / (30.0 * values * values)
    spacing = points[:, None] - points[None, :]
    same_point = spacing == 0.0
    derivative = np.where(same_point, 0.0, values[:, None] / (values[None, :] * np.where(same_point, 1.0, spacing)))
    end_fix = np.array([-7.5, 0.0, 0.0, 0.0, 0.0, 7.5])
    derivative = derivative + np.eye(6) * end_fix[None, :]
    stiffness = derivative.T @ (weights[:, None] * derivative)
    return (weights, derivative, stiffness)

def block_tables(blocks):
    weights, derivative, stiffness = gll_tables()
    identity = np.eye(blocks)
    weights_line = jnp.asarray(np.tile(weights, blocks), dtype=jnp.float32)
    deriv_block = jnp.asarray(np.kron(identity, derivative), dtype=jnp.float32)
    stiff_block = jnp.asarray(np.kron(identity, stiffness), dtype=jnp.float32)
    return (weights_line, deriv_block, stiff_block)

def fourier_tables(planes):
    plane_ids = jnp.arange(planes, dtype=jnp.int32)
    mode_ids = jnp.arange(planes, dtype=jnp.int32)
    waves = jnp.where(mode_ids < 2, 0, mode_ids // 2)
    phase_index = plane_ids[:, None] * waves[None, :] % planes
    angle = phase_index.astype(jnp.float32) * (2.0 * math.pi / planes)
    is_sine = (mode_ids % 2 == 1) & (mode_ids >= 2)
    basis = jnp.where(is_sine[None, :], jnp.sin(angle), jnp.cos(angle))
    alternating = jnp.where(plane_ids % 2 == 0, 1.0, -1.0).astype(jnp.float32)
    basis = jnp.where(mode_ids[None, :] == 1, alternating[:, None], basis)
    row_scale = jnp.where(mode_ids < 2, 1.0, 2.0).astype(jnp.float32) / planes
    forward = basis.T * row_scale[:, None]
    return (basis, forward)

def helmholtz_rates(mode_ids, planes):
    waves = jnp.where(mode_ids == 0, 0, jnp.where(mode_ids == 1, planes // 2, mode_ids // 2))
    scaled = waves.astype(jnp.float32) * WAVE_STEP
    return REACTION + scaled * scaled

def z_derivative(fields, mode_ids):
    waves = (mode_ids[0::2] // 2).astype(jnp.float32) * WAVE_STEP
    paired = fields.reshape(fields.shape[:1] + (-1, 2) + fields.shape[2:])
    cosine = paired[:, :, 0]
    sine = paired[:, :, 1]
    pair_waves = waves[None, :, None, None]
    result = jnp.stack([pair_waves * sine, -pair_waves * cosine], axis=2)
    return result.reshape(fields.shape)

def nonlinear_term(grids, mode_ids, deriv_block):
    along_x = jnp.matmul(grids[0:3], deriv_block.T, precision=HIGHEST)
    along_y = jnp.matmul(deriv_block, jnp.stack([grids[1], grids[3], grids[4]]), precision=HIGHEST)
    along_z = z_derivative(jnp.stack([grids[2], grids[4], grids[5]]), mode_ids)
    return -(along_x + along_y + along_z)

def pair_products(physical):
    return jnp.stack([physical[0] * physical[0], physical[0] * physical[1], physical[0] * physical[2], physical[1] * physical[1], physical[1] * physical[2], physical[2] * physical[2]])

def junction_flags(side_nodes):
    positions = jnp.arange(side_nodes)
    at_end = (positions % 6 == 5) & (positions < side_nodes - 1)
    at_start = (positions % 6 == 0) & (positions > 0)
    return (at_end, at_start)

def dss_local(field):
    side_nodes = field.shape[-1]
    at_end, at_start = junction_flags(side_nodes)
    zero_col = jnp.zeros(field.shape[:-1] + (1,), field.dtype)
    from_right = jnp.concatenate([field[..., 1:], zero_col], axis=-1)
    from_left = jnp.concatenate([zero_col, field[..., :-1]], axis=-1)
    field = field + jnp.where(at_end, from_right, 0.0) + jnp.where(at_start, from_left, 0.0)
    zero_row = jnp.zeros(field.shape[:-2] + (1, side_nodes), field.dtype)
    from_below = jnp.concatenate([field[..., 1:, :], zero_row], axis=-2)
    from_above = jnp.concatenate([zero_row, field[..., :-1, :]], axis=-2)
    field = field + jnp.where(at_end[:, None], from_below, 0.0) + jnp.where(at_start[:, None], from_above, 0.0)
    return field

def side_values(grid):
    return jnp.stack([grid[..., 0, :], grid[..., :, -1], grid[..., -1, :], grid[..., :, 0]], axis=-2)

def add_sides(grid, incoming):
    grid = grid.at[..., 0, :].add(incoming[..., 0, :])
    grid = grid.at[..., :, -1].add(incoming[..., 1, :])
    grid = grid.at[..., -1, :].add(incoming[..., 2, :])
    grid = grid.at[..., :, 0].add(incoming[..., 3, :])
    return grid

def edge_tables(partner_rows, side_nodes):
    positions = jnp.arange(side_nodes)
    rows_at = jnp.broadcast_to(positions[:, None], (side_nodes, side_nodes))
    cols_at = jnp.broadcast_to(positions[None, :], (side_nodes, side_nodes))
    on_side = jnp.stack([rows_at == 0, cols_at == side_nodes - 1, rows_at == side_nodes - 1, cols_at == 0])
    is_glued = (partner_rows >= 0)[..., :, None, None]
    wall_node = jnp.any(on_side & jnp.logical_not(is_glued), axis=-3)
    glued_node = jnp.any(on_side & is_glued, axis=-3)
    corner = ((rows_at == 0) | (rows_at == side_nodes - 1)) & ((cols_at == 0) | (cols_at == side_nodes - 1))
    kept_node = jnp.logical_not(wall_node | corner)
    dirichlet_mask = kept_node.astype(jnp.float32)
    at_end, at_start = junction_flags(side_nodes)
    copies = jnp.where(at_end | at_start, 2.0, 1.0).astype(jnp.float32)
    weight = dirichlet_mask / (copies[:, None] * copies[None, :] * jnp.where(glued_node, 2.0, 1.0))
    return (dirichlet_mask, weight)

def apply_element(field, rates, weights_line, stiff_block):
    rows_part = jnp.matmul(stiff_block, field, precision=HIGHEST) * weights_line[None, :]
    cols_part = jnp.matmul(field, stiff_block, precision=HIGHEST) * weights_line[:, None]
    return rows_part + cols_part + rates * (weights_line[:, None] * weights_line[None, :]) * field

def assemble_all(field, partner, partner_side, flipped):
    joined = dss_local(field)
    edges = side_values(joined)
    picked = edges[:, jnp.maximum(partner, 0), jnp.maximum(partner_side, 0), :]
    picked = jnp.where(flipped[None, :, :, None] == 1, picked[..., ::-1], picked)
    incoming = jnp.where(partner[None, :, :, None] >= 0, picked, 0.0)
    return add_sides(joined, incoming)

def reference(velocity, partner, partner_side, flipped):
    side_nodes = 6 * EB
    weights_line, deriv_block, stiff_block = block_tables(EB)
    basis, forward = fourier_tables(PLANES)
    mode_ids = jnp.arange(PLANES, dtype=jnp.int32)
    mass_grid = weights_line[:, None] * weights_line[None, :]
    fields = velocity.reshape(3, PLANES, PARTS_SIZE, side_nodes * side_nodes)
    by_part = jnp.moveaxis(fields, 2, 0)

    def local_rhs(block):
        physical = jnp.einsum('jm,cmn->cjn', basis, block, precision=HIGHEST)
        modal = jnp.einsum('mj,cjn->cmn', forward, pair_products(physical), precision=HIGHEST)
        grids = modal.reshape(6, PLANES, side_nodes, side_nodes)
        nonlinear = nonlinear_term(grids, mode_ids, deriv_block)
        current = block.reshape(3, PLANES, side_nodes, side_nodes)
        return mass_grid * (REACTION * current + nonlinear)
    rhs_local = jnp.moveaxis(lax.map(local_rhs, by_part), 0, 2)
    dirichlet_mask, weight = edge_tables(partner, side_nodes)
    rates = helmholtz_rates(mode_ids, PLANES)[:, None, None, None]

    def operate(field):
        return dirichlet_mask * assemble_all(apply_element(field, rates, weights_line, stiff_block), partner, partner_side, flipped)

    def inner(first_field, second_field):
        return lax.optimization_barrier(jnp.sum(weight * first_field * second_field, axis=(1, 2, 3)))[:, None, None, None]

    def solve_component(local_part):
        rhs = dirichlet_mask * assemble_all(local_part, partner, partner_side, flipped)
        solution = jnp.zeros_like(rhs)
        residual = rhs
        direction = rhs
        norm_now = inner(residual, residual)
        for iteration in range(ITERS):
            image = operate(direction)
            alpha = norm_now / inner(direction, image)
            solution = solution + alpha * direction
            residual = residual - alpha * image
            norm_next = inner(residual, residual)
            direction = residual + norm_next / norm_now * direction
            norm_now = norm_next
        return jnp.stack([solution, residual])
    outcome = lax.map(solve_component, rhs_local)
    new_velocity = outcome[:, 0].reshape(3, PLANES, PARTS_SIZE * side_nodes * side_nodes)
    residual = outcome[:, 1].reshape(3, PLANES, PARTS_SIZE * side_nodes * side_nodes)
    return (new_velocity, residual)
```

```python
import functools
import math

import jax
import jax.numpy as jnp
import numpy as np
from jax import lax
from jax.experimental import pallas as pl
from jax.experimental.pallas import tpu as pltpu
from jax.sharding import PartitionSpec as P

ITERS = 4
REACTION = 2.0
WAVE_STEP = 0.0625
LANES = 128
POINTS = 36
BLOCKS = 8
SIDE = 48
NODES = 2304
CENTRE = 9.0
SPREAD = 9.0
TWICE = 2.0 / SPREAD
SUM_ROWS = 16
VMEM_LIMIT = 56 * 1024 * 1024
F32 = jnp.float32
BF16 = jnp.bfloat16


def gll_tables():
    inner_near = math.sqrt(1.0 / 3.0 - 2.0 * math.sqrt(7.0) / 21.0)
    inner_far = math.sqrt(1.0 / 3.0 + 2.0 * math.sqrt(7.0) / 21.0)
    points = np.array([-1.0, -inner_far, -inner_near, inner_near, inner_far, 1.0])
    values = (63.0 * points**5 - 70.0 * points**3 + 15.0 * points) / 8.0
    weights = 2.0 / (30.0 * values * values)
    spacing = points[:, None] - points[None, :]
    same_point = spacing == 0.0
    derivative = np.where(
        same_point, 0.0, values[:, None] / (values[None, :] * np.where(same_point, 1.0, spacing))
    )
    end_fix = np.array([-7.5, 0.0, 0.0, 0.0, 0.0, 7.5])
    derivative = derivative + np.eye(6) * end_fix[None, :]
    stiffness = derivative.T @ (weights[:, None] * derivative)
    return (weights, derivative, stiffness)


WEIGHTS, DERIV, STIFF = gll_tables()
STIFF_HAT = STIFF / WEIGHTS[:, None]


def fourier_tables(planes):
    plane_ids = np.arange(planes)
    mode_ids = np.arange(planes)
    waves = np.where(mode_ids < 2, 0, mode_ids // 2)
    angle = (plane_ids[:, None] * waves[None, :] % planes) * (2.0 * math.pi / planes)
    is_sine = (mode_ids % 2 == 1) & (mode_ids >= 2)
    basis = np.where(is_sine[None, :], np.sin(angle), np.cos(angle))
    alternating = np.where(plane_ids % 2 == 0, 1.0, -1.0)
    basis = np.where(mode_ids[None, :] == 1, alternating[:, None], basis)
    row_scale = np.where(mode_ids < 2, 1.0, 2.0) / planes
    forward = basis.T * row_scale[:, None]
    rates = (np.arange(planes // 2) * WAVE_STEP)[:, None]
    forward_z = np.zeros_like(forward)
    forward_z[0::2] = rates * forward[1::2]
    forward_z[1::2] = -rates * forward[0::2]
    forward_z[0:2] = 0.0
    return (basis, forward, forward_z)


def split_table(table):
    high = np.asarray(table, np.float32).astype(jnp.bfloat16)
    low = (np.asarray(table, np.float64) - high.astype(np.float64)).astype(np.float32)
    return high, low.astype(jnp.bfloat16)


def transform_tables(count):
    planes = LANES
    modes = planes // count
    basis, forward, forward_z = fourier_tables(planes)
    inverse = np.zeros((count * LANES, 3 * planes))
    back = np.zeros((3 * 2 * planes, count * LANES))
    for block in range(count):
        ids = slice(block * modes, (block + 1) * modes)
        for comp in range(3):
            at = block * LANES + comp * modes
            inverse[at : at + modes, comp * planes : (comp + 1) * planes] = basis[:, ids].T
            row = comp * 2 * planes
            back[row : row + planes, at : at + modes] = -forward[ids].T
            back[row + planes : row + 2 * planes, at : at + modes] = -forward_z[ids].T
    return split_table(inverse), split_table(back)


def order_tables(count):
    group = BLOCKS * BLOCKS // count
    width = 0
    starts = []
    for index in range(count):
        first = group * index // BLOCKS * 6 * SIDE
        last = ((group * index + group - 1) // BLOCKS + 1) * 6 * SIDE
        start = first // LANES * LANES
        starts.append(start)
        width = max(width, -(-(last - start) // LANES) * LANES)
    starts = [min(start, NODES - width) for start in starts]
    tables = []
    which = []
    for index in range(count):
        table = np.zeros((POINTS * group, width), np.float32)
        for point in range(POINTS):
            for member in range(group):
                element = index * group + member
                row = 6 * (element // BLOCKS) + point // 6
                col = 6 * (element % BLOCKS) + point % 6
                table[point * group + member, row * SIDE + col - starts[index]] = 1.0
        for place, known in enumerate(tables):
            if np.array_equal(known, table):
                which.append(place)
                break
        else:
            which.append(len(tables))
            tables.append(table)
    return np.stack(tables).astype(jnp.bfloat16), which, starts


def halves(value):
    high = value.astype(BF16)
    low = (value - high.astype(F32)).astype(BF16)
    return high, low


def dot(left, right, dims):
    return lax.dot_general(left, right, (dims, ((), ())), preferred_element_type=F32)


def dot3(left, right_high, right_low):
    high, low = halves(left)
    dims = ((1,), (0,))
    return dot(high, right_high, dims) + (dot(low, right_high, dims) + dot(high, right_low, dims))


def start_of(point, ey):
    return pl.multiple_of(point * 64 + ey * 8, 8)


def get(ref, point, ey):
    return ref[pl.ds(start_of(point, ey), 8), :]


def put(ref, point, ey, value):
    ref[pl.ds(start_of(point, ey), 8), :] = value


def ex_ids():
    return lax.broadcasted_iota(jnp.int32, (8, LANES), 0)


def helmholtz_rates(four, modes):
    lane = lax.broadcasted_iota(jnp.int32, (8, LANES), 1)
    mode = four * modes + lax.rem(lane, jnp.int32(modes))
    wave = jnp.where(mode == 0, 0, jnp.where(mode == 1, LANES // 2, lax.div(mode, jnp.int32(2))))
    scaled = wave.astype(F32) * WAVE_STEP
    return REACTION + scaled * scaled


def glued_flags(partner_ref):
    return [jnp.where(partner_ref[0, side] >= 0, 1.0, 0.0).astype(F32) for side in range(4)]


def col_masks(flags):
    ex = ex_ids()
    return jnp.where(ex == 0, flags[3], 1.0), jnp.where(ex == 7, flags[1], 1.0)


def join_cols(first, last, masks):
    ex = ex_ids()
    from_right = jnp.where(ex < 7, pltpu.roll(first, 7, 0), 0.0)
    from_left = jnp.where(ex > 0, pltpu.roll(last, 1, 0), 0.0)
    return (first + from_left) * masks[0], (last + from_right) * masks[1]


def join_rows(ref, flags):
    ex = ex_ids()
    not_first = jnp.where(ex == 0, 0.0, 1.0)
    not_last = jnp.where(ex == 7, 0.0, 1.0)
    for ix in range(6):
        for ey in range(7):
            total = get(ref, 30 + ix, ey) + get(ref, ix, ey + 1)
            put(ref, 30 + ix, ey, total)
            put(ref, ix, ey + 1, total)
        low = get(ref, ix, 0) * flags[0]
        high = get(ref, 30 + ix, 7) * flags[2]
        if ix == 0:
            low, high = low * not_first, high * not_first
        if ix == 5:
            low, high = low * not_last, high * not_last
        put(ref, ix, 0, low)
        put(ref, 30 + ix, 7, high)


def line_product(line, table):
    sums = [line[j] + line[5 - j] for j in range(3)]
    gaps = [line[j] - line[5 - j] for j in range(3)]
    out = [None] * 6
    for i in range(3):
        even = None
        odd = None
        for j in range(3):
            even_term = sums[j] * float(0.5 * (table[i, j] + table[i, 5 - j]))
            odd_term = gaps[j] * float(0.5 * (table[i, j] - table[i, 5 - j]))
            even = even_term if even is None else even + even_term
            odd = odd_term if odd is None else odd + odd_term
        out[i] = even + odd
        out[5 - i] = even - odd
    return out


def apply_local(src, dst, rates, flags, energy=False):
    masks = col_masks(flags)

    def body(ey, total):
        for ix in range(6):
            line = [get(src, 6 * iy + ix, ey) for iy in range(6)]
            out = line_product(line, STIFF_HAT)
            for iy in range(6):
                put(dst, 6 * iy + ix, ey, out[iy] + rates * line[iy])
        for iy in range(6):
            line = [get(src, 6 * iy + ix, ey) for ix in range(6)]
            out = line_product(line, STIFF_HAT)
            full = [
                (get(dst, 6 * iy + ix, ey) + out[ix]) * float(WEIGHTS[iy] * WEIGHTS[ix])
                for ix in range(6)
            ]
            if energy:
                for ix in range(6):
                    total = total + full[ix] * line[ix]
            full[0], full[5] = join_cols(full[0], full[5], masks)
            for ix in range(6):
                put(dst, 6 * iy + ix, ey, full[ix])
        return total

    total = lax.fori_loop(0, BLOCKS, body, jnp.zeros((8, LANES), F32))
    join_rows(dst, flags)
    return total


def side_slice(side, i):
    if side == 0:
        return pl.ds(i * 64, 8)
    if side == 2:
        return pl.ds((30 + i) * 64 + 56, 8)
    if side == 1:
        return pl.ds((6 * i + 5) * 64 + 7, 8, stride=8)
    return pl.ds(6 * i * 64, 8, stride=8)


def read_line(ref, side):
    return [ref[side_slice(side, i), :] for i in range(6)]


def write_lines(ref, lines_ref, base):
    for side in range(4):
        line = read_line(ref, side)
        for i in range(6):
            lines_ref[pl.ds(base + side * SIDE + i * 8, 8), :] = line[i]


def add_lines(ref, lines):
    for side in range(4):
        for i in range(6):
            where = side_slice(side, i)
            ref[where, :] = ref[where, :] + lines[side][i]


def reverse_rows(value):
    ex = ex_ids()
    value = pltpu.roll(value, 4, 0)
    value = jnp.where((ex & 2) == 0, pltpu.roll(value, 6, 0), pltpu.roll(value, 2, 0))
    return jnp.where((ex & 1) == 0, pltpu.roll(value, 7, 0), pltpu.roll(value, 1, 0))


def incoming_lines(gath_ref, base, partner_ref, side_ref, flip_ref):
    lines = []
    for side in range(4):
        part = partner_ref[0, side]
        glued = part >= 0
        part = jnp.maximum(part, 0)
        start = base + jnp.maximum(side_ref[0, side], 0) * SIDE
        turned = flip_ref[0, side] == 1
        line = []
        for i in range(6):
            at = pl.multiple_of(start + jnp.where(turned, 5 - i, i) * 8, 8)
            value = gath_ref[part, pl.ds(at, 8), :]
            value = jnp.where(turned, reverse_rows(value), value)
            line.append(jnp.where(glued, value, 0.0))
        lines.append(line)
    return lines


def own_reaction(lines_ref, rates, flags, scale):
    ex = ex_ids()
    edge = float(WEIGHTS[0])
    corner = float(STIFF[0, 0])
    lines = []
    for side in range(4):
        line = [lines_ref[pl.ds(side * SIDE + i * 8, 8), :] for i in range(6)]
        along = line_product(line, STIFF_HAT)
        out = [
            (along[i] * edge + line[i] * (corner + rates * edge)) * float(WEIGHTS[i])
            for i in range(6)
        ]
        first = out[0] + pltpu.roll(out[5], 1, 0)
        last = out[5] + pltpu.roll(out[0], 7, 0)
        out[0] = jnp.where(ex > 0, first, 0.0)
        out[5] = jnp.where(ex < 7, last, 0.0)
        lines.append([value * (flags[side] * scale) for value in out])
    return lines


def combine(dst, terms):
    def body(ey, carry):
        for point in range(POINTS):
            total = None
            for factor, ref in terms:
                value = get(ref, point, ey)
                value = value if factor == 1.0 else value * factor
                total = value if total is None else total + value
            put(dst, point, ey, total)
        return carry

    lax.fori_loop(0, BLOCKS, body, 0)


def pack_kernel(which, starts, velocity_ref, order_ref, send_ref):
    modes = velocity_ref.shape[1]
    width = order_ref.shape[2]
    for index in range(len(starts)):
        window = pl.ds(starts[index], width)
        rows = [velocity_ref[comp, :, window] for comp in range(3)]
        pad = jnp.zeros((LANES - 3 * modes, width), F32)
        high, low = halves(jnp.concatenate(rows + [pad], axis=0))
        both = jnp.concatenate([high, low], axis=0)
        out = dot(order_ref[which[index]], both, ((1,), (1,)))
        send_ref[index] = out[:, :LANES] + out[:, LANES:]


def product_kernel(recv_ref, inv_high, inv_low, back_high, back_low, send_ref, phys, prod, out):
    count = recv_ref.shape[0]
    rows = recv_ref.shape[1]
    group = rows // POINTS
    total = None
    for index in range(count):
        where = pl.ds(index * LANES, LANES)
        part = dot3(recv_ref[index], inv_high[where, :], inv_low[where, :])
        total = part if total is None else total + part
    phys[...] = total
    step = min(group, 8)
    width = 2 * LANES

    def fields(point, base):
        return [
            phys[pl.ds(point * group + base, step), comp * LANES : (comp + 1) * LANES]
            for comp in range(3)
        ]

    for base in range(0, group, step):
        for comp in range(3):
            for iy in range(6):
                line = []
                for ix in range(6):
                    point = 6 * iy + ix
                    at = pl.ds(point * group + base, step)
                    value = fields(point, base)
                    line.append(value[comp] * value[0])
                    prod[at, comp * width + LANES : (comp + 1) * width] = value[comp] * value[2]
                for ix in range(6):
                    total = None
                    for j in range(6):
                        if DERIV[ix, j] != 0.0:
                            term = line[j] * float(DERIV[ix, j])
                            total = term if total is None else total + term
                    at = pl.ds((6 * iy + ix) * group + base, step)
                    prod[at, comp * width : comp * width + LANES] = total
            for ix in range(6):
                line = []
                for iy in range(6):
                    value = fields(6 * iy + ix, base)
                    line.append(value[comp] * value[1])
                for iy in range(6):
                    at = pl.ds((6 * iy + ix) * group + base, step)
                    total = prod[at, comp * width : comp * width + LANES]
                    for j in range(6):
                        if DERIV[iy, j] != 0.0:
                            total = total + line[j] * float(DERIV[iy, j])
                    prod[at, comp * width : comp * width + LANES] = total
    out[...] = dot3(prod[...], back_high[...], back_low[...])
    for index in range(count):
        for point in range(POINTS):
            at = pl.ds(point * group, group)
            mass = float(WEIGHTS[point // 6] * WEIGHTS[point % 6])
            nonlinear = out[at, index * LANES : (index + 1) * LANES]
            send_ref[index, at, :] = mass * (REACTION * recv_ref[index, at, :] + nonlinear)


def first_kernel(modes, four_ref, partner_ref, recv_ref, base_ref, lines_ref, work):
    count = recv_ref.shape[0]
    group = recv_ref.shape[1] // POINTS
    rates = helmholtz_rates(four_ref[0], modes)
    flags = glued_flags(partner_ref)
    for index in range(count):
        for point in range(POINTS):
            base_ref[pl.ds(point * 64 + index * group, group), :] = recv_ref[
                index, pl.ds(point * group, group), :
            ]
    masks = col_masks(flags)
    for ey in range(BLOCKS):
        for iy in range(6):
            first, last = join_cols(get(base_ref, 6 * iy, ey), get(base_ref, 6 * iy + 5, ey), masks)
            put(base_ref, 6 * iy, ey, first)
            put(base_ref, 6 * iy + 5, ey, last)
    join_rows(base_ref, flags)
    apply_local(base_ref, work, rates, flags)
    write_lines(base_ref, lines_ref, 0)
    write_lines(work, lines_ref, 4 * SIDE)


def second_kernel(
    modes, four_ref, partner_ref, side_ref, flip_ref, gath_ref, lines_ref, base_ref,
    k0_ref, k1_ref, k2_ref, next_ref, work,
):
    rates = helmholtz_rates(four_ref[0], modes)
    flags = glued_flags(partner_ref)
    tables = (partner_ref, side_ref, flip_ref)
    back = own_reaction(lines_ref, rates, flags, 1.0)
    k0_ref[...] = base_ref[...]
    add_lines(k0_ref, incoming_lines(gath_ref, 0, *tables))
    apply_local(k0_ref, work, rates, flags)
    add_lines(work, incoming_lines(gath_ref, 4 * SIDE, *tables))
    add_lines(work, back)
    combine(k1_ref, [(1.0 / SPREAD, work), (-CENTRE / SPREAD, k0_ref)])
    apply_local(k1_ref, work, rates, flags)
    write_lines(work, next_ref, 0)
    combine(k2_ref, [(TWICE, work), (-CENTRE * TWICE, k1_ref), (-1.0, k0_ref)])
    apply_local(k2_ref, work, rates, flags)
    write_lines(work, next_ref, 4 * SIDE)


def third_kernel(
    modes, four_ref, partner_ref, side_ref, flip_ref, gath_ref, lines_ref, k0_ref, k1_ref, base_ref,
    k2_ref, k3_ref, a3_ref, next_ref, work,
):
    rates = helmholtz_rates(four_ref[0], modes)
    flags = glued_flags(partner_ref)
    tables = (partner_ref, side_ref, flip_ref)
    back = own_reaction(lines_ref, rates, flags, TWICE)
    k2_ref[...] = base_ref[...]
    incoming = incoming_lines(gath_ref, 0, *tables)
    add_lines(k2_ref, [[value * TWICE for value in line] for line in incoming])
    apply_local(k2_ref, work, rates, flags)
    add_lines(work, incoming_lines(gath_ref, 4 * SIDE, *tables))
    add_lines(work, back)
    combine(k3_ref, [(TWICE, work), (-CENTRE * TWICE, k2_ref), (-1.0, k1_ref)])
    energy = apply_local(k3_ref, a3_ref, rates, flags, energy=True)
    write_lines(a3_ref, next_ref, 0)
    refs = (k0_ref, k1_ref, k2_ref, k3_ref)

    def body(ey, sums):
        sums = list(sums)
        for point in range(POINTS):
            ends = (point // 6 in (0, 5)) + (point % 6 in (0, 5))
            values = [get(ref, point, ey) for ref in refs]
            place = 0
            for i in range(4):
                scaled = values[i] * (0.5**ends) if ends else values[i]
                for j in range(i, 4):
                    sums[place] = sums[place] + scaled * values[j]
                    place += 1
        return tuple(sums)

    zero = jnp.zeros((8, LANES), F32)
    sums = lax.fori_loop(0, BLOCKS, body, (zero,) * 10)
    rows = [jnp.sum(value, axis=0, keepdims=True) for value in sums]
    rows.append(jnp.sum(energy, axis=0, keepdims=True))
    rows.append(jnp.zeros((SUM_ROWS - len(rows), LANES), F32))
    next_ref[pl.ds(4 * SIDE, SUM_ROWS), :] = jnp.concatenate(rows, axis=0)


def conjugate_coefficients(gram, energy):
    zero = jnp.zeros_like(energy)

    def image(vec):
        out = [zero] * 5
        for j in range(4):
            if vec[j] is None:
                continue
            out[j] = out[j] + CENTRE * vec[j]
            out[j + 1] = out[j + 1] + (SPREAD if j == 0 else 0.5 * SPREAD) * vec[j]
            if j > 0:
                out[j - 1] = out[j - 1] + 0.5 * SPREAD * vec[j]
        return out

    def inner(left, right):
        total = zero
        for i in range(4):
            for j in range(4):
                if left[i] is not None and right[j] is not None:
                    total = total + left[i] * right[j] * gram[i][j]
        return total

    moments = [[None] * 4 for _ in range(4)]
    for j in range(3):
        column = image([jnp.ones_like(energy) if i == j else None for i in range(4)])
        for i in range(4):
            total = zero
            for m in range(max(j - 1, 0), j + 2):
                total = total + column[m] * gram[i][m]
            moments[i][j] = total
    for i in range(3):
        moments[i][3] = moments[3][i]
    moments[3][3] = energy

    def pad(vec, size):
        return [vec[i] if i < size else None for i in range(4)]

    residual = [jnp.ones_like(energy), zero, zero, zero, zero]
    direction = list(residual)
    solution = [zero] * 4
    norm_now = gram[0][0]
    for step in range(ITERS):
        trimmed = pad(direction, step + 1)
        bend = zero
        for i in range(step + 1):
            for j in range(step + 1):
                bend = bend + direction[i] * direction[j] * moments[i][j]
        alpha = norm_now / bend
        moved = image(trimmed)
        for i in range(step + 1):
            solution[i] = solution[i] + alpha * direction[i]
        for i in range(step + 2):
            residual[i] = residual[i] - alpha * moved[i]
        if step < ITERS - 1:
            kept = pad(residual, step + 2)
            norm_next = inner(kept, kept)
            ratio = norm_next / norm_now
            direction = [residual[i] + ratio * direction[i] for i in range(5)]
            norm_now = norm_next
    return solution, residual


def last_kernel(
    which, starts, partner_ref, side_ref, flip_ref, gath_ref, k0_ref, k1_ref, k2_ref, k3_ref, base_ref,
    order_ref, sol_ref, res_ref, work, sol_rows, res_rows, flat,
):
    parts = gath_ref.shape[0]
    count, rows, _ = sol_rows.shape
    group = rows // POINTS
    modes = sol_ref.shape[1]
    width = order_ref.shape[2]
    sums = gath_ref[0, pl.ds(4 * SIDE, SUM_ROWS), :]
    for part in range(1, parts):
        sums = sums + gath_ref[part, pl.ds(4 * SIDE, SUM_ROWS), :]

    def row(place):
        return jnp.broadcast_to(sums[place : place + 1, :], (8, LANES))

    gram = [[None] * 4 for _ in range(4)]
    place = 0
    for i in range(4):
        for j in range(i, 4):
            gram[i][j] = row(place)
            gram[j][i] = gram[i][j]
            place += 1
    solution, residual = conjugate_coefficients(gram, row(place))
    work[...] = base_ref[...]
    add_lines(work, incoming_lines(gath_ref, 0, partner_ref, side_ref, flip_ref))
    on_a3 = residual[4] * TWICE
    on_k3 = residual[3] - on_a3 * CENTRE
    on_k2 = residual[2] - residual[4]

    def body(ey, carry):
        for point in range(POINTS):
            k0, k1, k2, k3, a3 = [
                get(ref, point, ey) for ref in (k0_ref, k1_ref, k2_ref, k3_ref, work)
            ]
            sol = (solution[0] * k0 + solution[1] * k1) + (solution[2] * k2 + solution[3] * k3)
            res = (residual[0] * k0 + residual[1] * k1) + (on_k2 * k2 + on_k3 * k3) + on_a3 * a3
            for ref, value in ((sol_rows, sol), (res_rows, res)):
                if group >= 8:
                    index = lax.div(ey * 8, jnp.int32(group))
                    at = pl.multiple_of(point * group + lax.rem(ey * 8, jnp.int32(group)), 8)
                    ref[index, pl.ds(at, 8), :] = value
                else:
                    for piece in range(8 // group):
                        ref[ey * (8 // group) + piece, pl.ds(point * group, group), :] = value[
                            piece * group : (piece + 1) * group, :
                        ]
        return carry

    lax.fori_loop(0, BLOCKS, body, 0)
    for ref, out_ref in ((sol_rows, sol_ref), (res_rows, res_ref)):
        flat[...] = jnp.zeros(flat.shape, F32)
        for index in range(count):
            high, low = halves(jnp.transpose(ref[index]))
            both = jnp.concatenate([high, low], axis=0)
            out = dot(both, order_ref[which[index]], ((1,), (0,)))
            window = pl.ds(starts[index], width)
            flat[:, window] = flat[:, window] + (out[:LANES] + out[LANES:])
        for comp in range(3):
            out_ref[comp] = flat[comp * modes : (comp + 1) * modes, :]


def call(kernel, name, out_shapes, args, scratch, scalars=0):
    smem = pl.BlockSpec(memory_space=pltpu.SMEM)
    vmem = pl.BlockSpec(memory_space=pltpu.VMEM)
    return pl.pallas_call(
        kernel,
        name=name,
        out_shape=[jax.ShapeDtypeStruct(shape, F32) for shape in out_shapes],
        in_specs=[smem] * scalars + [vmem] * (len(args) - scalars),
        out_specs=[vmem] * len(out_shapes),
        scratch_shapes=[pltpu.VMEM(shape, F32) for shape in scratch],
        compiler_params=pltpu.CompilerParams(vmem_limit_bytes=VMEM_LIMIT),
    )(*args)


def shards(velocity, partner, partner_side, flipped):
    modes = velocity.shape[1]
    count = lax.axis_size("four")
    rows = NODES // count
    (inv_high, inv_low), (back_high, back_low) = transform_tables(count)
    order, which, starts = order_tables(count)
    four = lax.axis_index("four").astype(jnp.int32).reshape(1)
    field = (NODES, LANES)
    swapped = (count, rows, LANES)

    (sent,) = call(
        functools.partial(pack_kernel, which, starts), "pack", [swapped], (velocity, order), []
    )
    spread = lax.all_to_all(sent, "four", split_axis=0, concat_axis=0, tiled=True)
    (sent,) = call(
        product_kernel,
        "products",
        [swapped],
        (spread, inv_high, inv_low, back_high, back_low),
        [(rows, 3 * LANES), (rows, 6 * LANES), (rows, count * LANES)],
    )
    local = lax.all_to_all(sent, "four", split_axis=0, concat_axis=0, tiled=True)

    base, lines = call(
        functools.partial(first_kernel, modes),
        "first",
        [field, (8 * SIDE, LANES)],
        (four, partner, local),
        [field],
        scalars=2,
    )
    tables = (partner, partner_side, flipped)
    gathered = lax.all_gather(lines, "dom", axis=0, tiled=False)
    k0, k1, base, lines = call(
        functools.partial(second_kernel, modes),
        "second",
        [field, field, field, (8 * SIDE, LANES)],
        (four, *tables, gathered, lines, base),
        [field],
        scalars=4,
    )
    gathered = lax.all_gather(lines, "dom", axis=0, tiled=False)
    k2, k3, a3, lines = call(
        functools.partial(third_kernel, modes),
        "third",
        [field, field, field, (4 * SIDE + SUM_ROWS, LANES)],
        (four, *tables, gathered, lines, k0, k1, base),
        [field],
        scalars=4,
    )
    gathered = lax.all_gather(lines, "dom", axis=0, tiled=False)
    outs = call(
        functools.partial(last_kernel, which, starts),
        "last",
        [velocity.shape, velocity.shape],
        (*tables, gathered, k0, k1, k2, k3, a3, order),
        [field, swapped, swapped, (LANES, NODES)],
        scalars=3,
    )
    return tuple(outs)


def solution(mesh):
    return jax.shard_map(
        shards,
        mesh=mesh,
        in_specs=(P(None, "four", "dom"), P("dom", None), P("dom", None), P("dom", None)),
        out_specs=(P(None, "four", "dom"), P(None, "four", "dom")),
        check_vma=False,
    )
```

```python
import functools
import math

import jax
import jax.numpy as jnp
import numpy as np
from jax import lax
from jax.experimental import pallas as pl
from jax.experimental.pallas import tpu as pltpu
from jax.sharding import PartitionSpec as P

ITERS = 4
REACTION = 2.0
WAVE_STEP = 0.0625
LANES = 128
POINTS = 36
BLOCKS = 8
SIDE = 48
NODES = 2304
CENTRE = 9.0
SPREAD = 9.0
TWICE = 2.0 / SPREAD
SUM_ROWS = 16
VMEM_LIMIT = 56 * 1024 * 1024
F32 = jnp.float32
BF16 = jnp.bfloat16


def gll_tables():
    inner_near = math.sqrt(1.0 / 3.0 - 2.0 * math.sqrt(7.0) / 21.0)
    inner_far = math.sqrt(1.0 / 3.0 + 2.0 * math.sqrt(7.0) / 21.0)
    points = np.array([-1.0, -inner_far, -inner_near, inner_near, inner_far, 1.0])
    values = (63.0 * points**5 - 70.0 * points**3 + 15.0 * points) / 8.0
    weights = 2.0 / (30.0 * values * values)
    spacing = points[:, None] - points[None, :]
    same_point = spacing == 0.0
    derivative = np.where(
        same_point, 0.0, values[:, None] / (values[None, :] * np.where(same_point, 1.0, spacing))
    )
    end_fix = np.array([-7.5, 0.0, 0.0, 0.0, 0.0, 7.5])
    derivative = derivative + np.eye(6) * end_fix[None, :]
    stiffness = derivative.T @ (weights[:, None] * derivative)
    return (weights, derivative, stiffness)


WEIGHTS, DERIV, STIFF = gll_tables()
STIFF_HAT = STIFF / WEIGHTS[:, None]


def fourier_tables(planes):
    plane_ids = np.arange(planes)
    mode_ids = np.arange(planes)
    waves = np.where(mode_ids < 2, 0, mode_ids // 2)
    angle = (plane_ids[:, None] * waves[None, :] % planes) * (2.0 * math.pi / planes)
    is_sine = (mode_ids % 2 == 1) & (mode_ids >= 2)
    basis = np.where(is_sine[None, :], np.sin(angle), np.cos(angle))
    alternating = np.where(plane_ids % 2 == 0, 1.0, -1.0)
    basis = np.where(mode_ids[None, :] == 1, alternating[:, None], basis)
    row_scale = np.where(mode_ids < 2, 1.0, 2.0) / planes
    forward = basis.T * row_scale[:, None]
    rates = (np.arange(planes // 2) * WAVE_STEP)[:, None]
    forward_z = np.zeros_like(forward)
    forward_z[0::2] = rates * forward[1::2]
    forward_z[1::2] = -rates * forward[0::2]
    forward_z[0:2] = 0.0
    return (basis, forward, forward_z)


def split_table(table):
    high = np.asarray(table, np.float32).astype(jnp.bfloat16)
    low = (np.asarray(table, np.float64) - high.astype(np.float64)).astype(np.float32)
    return high, low.astype(jnp.bfloat16)


def transform_tables(count):
    planes = LANES
    modes = planes // count
    basis, forward, forward_z = fourier_tables(planes)
    inverse = np.zeros((count, LANES, 3 * planes))
    for block in range(count):
        ids = slice(block * modes, (block + 1) * modes)
        for comp in range(3):
            at = comp * modes
            inverse[block, at : at + modes, comp * planes : (comp + 1) * planes] = basis[:, ids].T
    back = -np.concatenate([forward.T, forward_z.T], axis=0)
    return split_table(inverse), split_table(back)


def chunk_sizes(count):
    group = BLOCKS * BLOCKS // count
    step = min(group, BLOCKS)
    return step, group // step


def order_tables(count):
    step, _ = chunk_sizes(count)
    units = BLOCKS * BLOCKS // step
    width = 3 * LANES
    starts = []
    tables = []
    which = []
    for index in range(units):
        start = step * index // BLOCKS * 6 * SIDE // LANES * LANES
        starts.append(start)
        table = np.zeros((POINTS * step, width), np.float32)
        for point in range(POINTS):
            for member in range(step):
                element = index * step + member
                row = 6 * (element // BLOCKS) + point // 6
                col = 6 * (element % BLOCKS) + point % 6
                table[point * step + member, row * SIDE + col - start] = 1.0
        for place, known in enumerate(tables):
            if np.array_equal(known, table):
                which.append(place)
                break
        else:
            which.append(len(tables))
            tables.append(table)
    return np.stack(tables).astype(jnp.bfloat16), which, starts


def halves(value):
    high = value.astype(BF16)
    low = (value - high.astype(F32)).astype(BF16)
    return high, low


def dot(left, right, dims):
    return lax.dot_general(left, right, (dims, ((), ())), preferred_element_type=F32)


def dot3(left, right_high, right_low):
    high, low = halves(left)
    dims = ((1,), (0,))
    return dot(high, right_high, dims) + (dot(low, right_high, dims) + dot(high, right_low, dims))


def start_of(point, ey):
    return pl.multiple_of(point * 64 + ey * 8, 8)


def get(ref, point, ey):
    return ref[pl.ds(start_of(point, ey), 8), :]


def put(ref, point, ey, value):
    ref[pl.ds(start_of(point, ey), 8), :] = value


def ex_ids():
    return lax.broadcasted_iota(jnp.int32, (8, LANES), 0)


def helmholtz_rates(four, modes):
    lane = lax.broadcasted_iota(jnp.int32, (8, LANES), 1)
    mode = four * modes + lax.rem(lane, jnp.int32(modes))
    wave = jnp.where(mode == 0, 0, jnp.where(mode == 1, LANES // 2, lax.div(mode, jnp.int32(2))))
    scaled = wave.astype(F32) * WAVE_STEP
    return REACTION + scaled * scaled


def glued_flags(partner_ref):
    return [jnp.where(partner_ref[0, side] >= 0, 1.0, 0.0).astype(F32) for side in range(4)]


def col_masks(flags):
    ex = ex_ids()
    return jnp.where(ex == 0, flags[3], 1.0), jnp.where(ex == 7, flags[1], 1.0)


def join_cols(first, last, masks):
    ex = ex_ids()
    from_right = jnp.where(ex < 7, pltpu.roll(first, 7, 0), 0.0)
    from_left = jnp.where(ex > 0, pltpu.roll(last, 1, 0), 0.0)
    return (first + from_left) * masks[0], (last + from_right) * masks[1]


def join_rows(ref, flags):
    ex = ex_ids()
    not_first = jnp.where(ex == 0, 0.0, 1.0)
    not_last = jnp.where(ex == 7, 0.0, 1.0)
    for ix in range(6):
        for ey in range(7):
            total = get(ref, 30 + ix, ey) + get(ref, ix, ey + 1)
            put(ref, 30 + ix, ey, total)
            put(ref, ix, ey + 1, total)
        low = get(ref, ix, 0) * flags[0]
        high = get(ref, 30 + ix, 7) * flags[2]
        if ix == 0:
            low, high = low * not_first, high * not_first
        if ix == 5:
            low, high = low * not_last, high * not_last
        put(ref, ix, 0, low)
        put(ref, 30 + ix, 7, high)


def line_product(line, table, mirrored=1.0):
    sums = [line[j] + line[5 - j] for j in range(3)]
    gaps = [line[j] - line[5 - j] for j in range(3)]
    out = [None] * 6
    for i in range(3):
        even = None
        odd = None
        for j in range(3):
            even_term = sums[j] * float(0.5 * (table[i, j] + table[i, 5 - j]))
            odd_term = gaps[j] * float(0.5 * (table[i, j] - table[i, 5 - j]))
            even = even_term if even is None else even + even_term
            odd = odd_term if odd is None else odd + odd_term
        out[i] = even + odd
        out[5 - i] = even - odd if mirrored > 0 else odd - even
    return out


def apply_local(src, dst, rates, flags, energy=False):
    masks = col_masks(flags)

    def body(ey, total):
        for ix in range(6):
            line = [get(src, 6 * iy + ix, ey) for iy in range(6)]
            out = line_product(line, STIFF_HAT)
            for iy in range(6):
                put(dst, 6 * iy + ix, ey, out[iy] + rates * line[iy])
        for iy in range(6):
            line = [get(src, 6 * iy + ix, ey) for ix in range(6)]
            out = line_product(line, STIFF_HAT)
            full = [
                (get(dst, 6 * iy + ix, ey) + out[ix]) * float(WEIGHTS[iy] * WEIGHTS[ix])
                for ix in range(6)
            ]
            if energy:
                for ix in range(6):
                    total = total + full[ix] * line[ix]
            full[0], full[5] = join_cols(full[0], full[5], masks)
            for ix in range(6):
                put(dst, 6 * iy + ix, ey, full[ix])
        return total

    total = lax.fori_loop(0, BLOCKS, body, jnp.zeros((8, LANES), F32))
    join_rows(dst, flags)
    return total


def side_slice(side, i):
    if side == 0:
        return pl.ds(i * 64, 8)
    if side == 2:
        return pl.ds((30 + i) * 64 + 56, 8)
    if side == 1:
        return pl.ds((6 * i + 5) * 64 + 7, 8, stride=8)
    return pl.ds(6 * i * 64, 8, stride=8)


def read_line(ref, side):
    return [ref[side_slice(side, i), :] for i in range(6)]


def lane_ids():
    return lax.broadcasted_iota(jnp.int32, (8, LANES), 1)


def is_packed(modes):
    return 3 * modes + modes == LANES


def pack_lanes(values, modes):
    if not is_packed(modes):
        return values
    third = len(values) // 4
    inside = lane_ids() < 3 * modes
    return [
        jnp.where(
            inside,
            values[comp * third + at],
            pltpu.roll(values[3 * third + at], (3 - comp) * modes, 1),
        )
        for comp in range(3)
        for at in range(third)
    ]


def unpack_last(pieces, modes):
    block = lax.div(lane_ids(), jnp.int32(modes))
    turned = [pltpu.roll(pieces[comp], (comp + 1) * modes, 1) for comp in range(3)]
    return jnp.where(block == 0, turned[0], jnp.where(block == 1, turned[1], turned[2]))


def unpack_lanes(values, modes):
    if not is_packed(modes):
        return values
    third = len(values) // 3
    return values + [
        unpack_last([values[comp * third + at] for comp in range(3)], modes) for at in range(third)
    ]


def line_rows(modes):
    return 3 * SIDE if is_packed(modes) else 4 * SIDE


def write_lines(ref, lines_ref, base, modes):
    values = []
    for side in range(4):
        values += read_line(ref, side)
    for at, value in enumerate(pack_lanes(values, modes)):
        lines_ref[pl.ds(base + at * 8, 8), :] = value


def load_lines(lines_ref, modes):
    count = line_rows(modes) // 8
    values = unpack_lanes([lines_ref[pl.ds(at * 8, 8), :] for at in range(count)], modes)
    return [values[side * 6 : side * 6 + 6] for side in range(4)]


def add_lines(ref, lines):
    for side in range(4):
        for i in range(6):
            where = side_slice(side, i)
            ref[where, :] = ref[where, :] + lines[side][i]


def reverse_rows(value):
    ex = ex_ids()
    value = pltpu.roll(value, 4, 0)
    value = jnp.where((ex & 2) == 0, pltpu.roll(value, 6, 0), pltpu.roll(value, 2, 0))
    return jnp.where((ex & 1) == 0, pltpu.roll(value, 7, 0), pltpu.roll(value, 1, 0))


def collect_sides(gath_refs, own, partner_ref, side_ref, sides, modes):
    sets = sides.shape[1] // SIDE
    step = line_rows(modes)

    def copy_side(side, load):
        there = jnp.maximum(side_ref[0, side], 0)

        def plain():
            for place in range(sets):
                for i in range(6):
                    at = pl.multiple_of(place * step + there * SIDE + i * 8, 8)
                    sides[side, pl.ds(place * SIDE + i * 8, 8), :] = load(at)

        if not is_packed(modes):
            plain()
            return
        pl.when(there < 3)(plain)

        @pl.when(there == 3)
        def _():
            for place in range(sets):
                for i in range(6):
                    pieces = [load(place * step + comp * SIDE + i * 8) for comp in range(3)]
                    sides[side, pl.ds(place * SIDE + i * 8, 8), :] = unpack_last(pieces, modes)

    def body(side, carry):
        part = partner_ref[0, side]
        if len(gath_refs) == 1:
            source = jnp.maximum(part, 0)
            copy_side(side, lambda at: gath_refs[0][source, pl.ds(at, 8), :])
            return carry
        for slot, ref in enumerate(gath_refs):
            here = jnp.logical_and(part >= 0, jnp.bitwise_xor(part, own) == slot)

            @pl.when(here)
            def _(ref=ref):
                copy_side(side, lambda at: ref[pl.ds(at, 8), :])

        return carry

    lax.fori_loop(0, 4, body, 0)


def incoming_lines(sides, place, partner_ref, flip_ref):
    lines = []
    for side in range(4):
        glued = partner_ref[0, side] >= 0
        turned = flip_ref[0, side] == 1
        line = []
        for i in range(6):
            at = pl.multiple_of(place * SIDE + jnp.where(turned, 5 - i, i) * 8, 8)
            value = sides[side, pl.ds(at, 8), :]
            value = jnp.where(turned, reverse_rows(value), value)
            line.append(jnp.where(glued, value, 0.0))
        lines.append(line)
    return lines


def own_reaction(own_lines, rates, flags, scale):
    ex = ex_ids()
    edge = float(WEIGHTS[0])
    corner = float(STIFF[0, 0])
    lines = []
    for side in range(4):
        line = own_lines[side]
        along = line_product(line, STIFF_HAT)
        out = [
            (along[i] * edge + line[i] * (corner + rates * edge)) * float(WEIGHTS[i])
            for i in range(6)
        ]
        first = out[0] + pltpu.roll(out[5], 1, 0)
        last = out[5] + pltpu.roll(out[0], 7, 0)
        out[0] = jnp.where(ex > 0, first, 0.0)
        out[5] = jnp.where(ex < 7, last, 0.0)
        lines.append([value * (flags[side] * scale) for value in out])
    return lines


def combine(dst, terms):
    def body(ey, carry):
        for point in range(POINTS):
            total = None
            for factor, ref in terms:
                value = get(ref, point, ey)
                value = value if factor == 1.0 else value * factor
                total = value if total is None else total + value
            put(dst, point, ey, total)
        return carry

    lax.fori_loop(0, BLOCKS, body, 0)


def block_of(place, four):
    return place if isinstance(four, int) else jnp.bitwise_xor(four, place)


def pack_kernel(step, count, dynamic, ids_ref, which_ref, starts_ref, velocity_ref, order_ref, *send_refs):
    modes = velocity_ref.shape[1]
    width = order_ref.shape[2]
    four = ids_ref[1] if dynamic else 0
    for place in range(count):
        index = block_of(place, four)
        window = pl.ds(pl.multiple_of(starts_ref[index], LANES), width)
        rows = [velocity_ref[comp, :, window] for comp in range(3)]
        pad = jnp.zeros((LANES - 3 * modes, width), F32)
        high, low = halves(jnp.concatenate(rows + [pad], axis=0))
        both = jnp.concatenate([high, low], axis=0)
        out = dot(order_ref[which_ref[index]], both, ((1,), (1,)))
        out = out[:, :LANES] + out[:, LANES:]
        if not is_packed(modes):
            send_refs[place][...] = out
            continue
        values = [out[point * step : (point + 1) * step] for point in range(POINTS)]
        for at, value in enumerate(pack_lanes(values, modes)):
            send_refs[place][pl.ds(at * step, step), :] = value


def product_kernel(modes, step, count, dynamic, ids_ref, *refs):
    recv_refs = refs[:count]
    inv_high, inv_low, back_high, back_low = refs[count : count + 4]
    send_refs = refs[count + 4 : 2 * count + 4]
    full, phys, prod, spec = refs[2 * count + 4 :]
    four = ids_ref[1] if dynamic else 0
    packed = is_packed(modes)
    total = None
    for place in range(count):
        index = block_of(place, four)
        if packed:
            ready = 3 * POINTS // 4
            values = [recv_refs[place][pl.ds(at * step, step), :] for at in range(ready)]
            for at, value in enumerate(unpack_lanes(values, modes)):
                full[place, pl.ds(at * step, step), :] = value
        else:
            full[place] = recv_refs[place][...]
        part = dot3(full[place], inv_high[index], inv_low[index])
        total = part if total is None else total + part
    phys[...] = total
    width = 2 * LANES

    def field(point, comp):
        return phys[pl.ds(point * step, step), comp * LANES : (comp + 1) * LANES]

    for comp in range(3):
        wide = pl.ds(comp * width, LANES)
        for iy in range(6):
            line = []
            for ix in range(6):
                point = 6 * iy + ix
                value = field(point, comp)
                line.append(value * field(point, 0))
                prod[pl.ds(point * step, step), pl.ds(comp * width + LANES, LANES)] = (
                    value * field(point, 2)
                )
            out = line_product(line, DERIV, -1.0)
            for ix in range(6):
                prod[pl.ds((6 * iy + ix) * step, step), wide] = out[ix]
        for ix in range(6):
            line = [field(6 * iy + ix, comp) * field(6 * iy + ix, 1) for iy in range(6)]
            out = line_product(line, DERIV, -1.0)
            for iy in range(6):
                at = pl.ds((6 * iy + ix) * step, step)
                prod[at, wide] = prod[at, wide] + out[iy]
        spec[comp] = dot3(prod[:, comp * width : (comp + 1) * width], back_high[...], back_low[...])

    lane_block = lax.div(lax.broadcasted_iota(jnp.int32, (step, LANES), 1), jnp.int32(modes))
    masks = []
    shifts = []
    for place in range(count):
        index = block_of(place, four)
        masks.append([lane_block == lax.rem(index + comp, count) for comp in range(2)])
        shifts.append(lax.rem(LANES - index * modes, LANES))
    kept = []
    for point in range(POINTS):
        at = pl.ds(point * step, step)
        mass = float(WEIGHTS[point // 6] * WEIGHTS[point % 6])
        turned = [spec[0, at, :]]
        turned += [pltpu.roll(spec[comp, at, :], comp * modes, 1) for comp in (1, 2)]
        for place in range(count):
            mask = masks[place]
            mixed = jnp.where(mask[0], turned[0], jnp.where(mask[1], turned[1], turned[2]))
            nonlinear = pltpu.roll(mixed, shifts[place], 1)
            full[place, at, :] = mass * (REACTION * full[place, at, :] + nonlinear)
    for place in range(count):
        values = [full[place, pl.ds(point * step, step), :] for point in range(POINTS)]
        for at, value in enumerate(pack_lanes(values, modes)):
            send_refs[place][pl.ds(at * step, step), :] = value


def first_kernel(modes, step, count, chunks, dynamic, ids_ref, partner_ref, *refs):
    recv_refs = refs[: count * chunks]
    base_ref, lines_ref, work = refs[count * chunks :]
    four = ids_ref[1] if dynamic else 0
    rates = helmholtz_rates(ids_ref[1], modes)
    flags = glued_flags(partner_ref)
    for chunk in range(chunks):
        for place in range(count):
            ref = recv_refs[chunk * count + place]
            ready = ref.shape[0] // step
            first = (block_of(place, four) * chunks + chunk) * step
            values = unpack_lanes([ref[pl.ds(at * step, step), :] for at in range(ready)], modes)
            for point in range(POINTS):
                at = point * 64 + first
                at = at if isinstance(at, int) else pl.multiple_of(at, step)
                base_ref[pl.ds(at, step), :] = values[point]
    masks = col_masks(flags)
    for ey in range(BLOCKS):
        for iy in range(6):
            first, last = join_cols(get(base_ref, 6 * iy, ey), get(base_ref, 6 * iy + 5, ey), masks)
            put(base_ref, 6 * iy, ey, first)
            put(base_ref, 6 * iy + 5, ey, last)
    join_rows(base_ref, flags)
    apply_local(base_ref, work, rates, flags)
    write_lines(base_ref, lines_ref, 0, modes)
    write_lines(work, lines_ref, line_rows(modes), modes)


def second_kernel(modes, slots, ids_ref, partner_ref, side_ref, flip_ref, *refs):
    gath_refs = refs[:slots]
    lines_ref, base_ref, k0_ref, k1_ref, k2_ref, next_ref, work, sides = refs[slots:]
    rates = helmholtz_rates(ids_ref[1], modes)
    flags = glued_flags(partner_ref)
    collect_sides(gath_refs, ids_ref[0], partner_ref, side_ref, sides, modes)
    back = own_reaction(load_lines(lines_ref, modes), rates, flags, 1.0)
    k0_ref[...] = base_ref[...]
    add_lines(k0_ref, incoming_lines(sides, 0, partner_ref, flip_ref))
    apply_local(k0_ref, work, rates, flags)
    add_lines(work, incoming_lines(sides, 1, partner_ref, flip_ref))
    add_lines(work, back)
    combine(k1_ref, [(1.0 / SPREAD, work), (-CENTRE / SPREAD, k0_ref)])
    apply_local(k1_ref, work, rates, flags)
    write_lines(work, next_ref, 0, modes)
    combine(k2_ref, [(TWICE, work), (-CENTRE * TWICE, k1_ref), (-1.0, k0_ref)])
    apply_local(k2_ref, work, rates, flags)
    write_lines(work, next_ref, line_rows(modes), modes)


def third_kernel(modes, slots, ids_ref, partner_ref, side_ref, flip_ref, *refs):
    gath_refs = refs[:slots]
    lines_ref, k0_ref, k1_ref, base_ref = refs[slots : slots + 4]
    k2_ref, k3_ref, a3_ref, next_ref, work, sides = refs[slots + 4 :]
    rates = helmholtz_rates(ids_ref[1], modes)
    flags = glued_flags(partner_ref)
    collect_sides(gath_refs, ids_ref[0], partner_ref, side_ref, sides, modes)
    back = own_reaction(load_lines(lines_ref, modes), rates, flags, TWICE)
    k2_ref[...] = base_ref[...]
    incoming = incoming_lines(sides, 0, partner_ref, flip_ref)
    add_lines(k2_ref, [[value * TWICE for value in line] for line in incoming])
    apply_local(k2_ref, work, rates, flags)
    add_lines(work, incoming_lines(sides, 1, partner_ref, flip_ref))
    add_lines(work, back)
    combine(k3_ref, [(TWICE, work), (-CENTRE * TWICE, k2_ref), (-1.0, k1_ref)])
    energy = apply_local(k3_ref, a3_ref, rates, flags, energy=True)
    write_lines(a3_ref, next_ref, 0, modes)
    refs = (k0_ref, k1_ref, k2_ref, k3_ref)

    def body(ey, sums):
        sums = list(sums)
        for point in range(POINTS):
            ends = (point // 6 in (0, 5)) + (point % 6 in (0, 5))
            values = [get(ref, point, ey) for ref in refs]
            place = 0
            for i in range(4):
                scaled = values[i] * (0.5**ends) if ends else values[i]
                for j in range(i, 4):
                    sums[place] = sums[place] + scaled * values[j]
                    place += 1
        return tuple(sums)

    zero = jnp.zeros((8, LANES), F32)
    sums = lax.fori_loop(0, BLOCKS, body, (zero,) * 10)
    rows = [jnp.sum(value, axis=0, keepdims=True) for value in sums]
    rows.append(jnp.sum(energy, axis=0, keepdims=True))
    rows.append(jnp.zeros((SUM_ROWS - len(rows), LANES), F32))
    next_ref[pl.ds(line_rows(modes), SUM_ROWS), :] = jnp.concatenate(rows, axis=0)


def conjugate_coefficients(gram, energy):
    zero = jnp.zeros_like(energy)

    def image(vec):
        out = [zero] * 5
        for j in range(4):
            if vec[j] is None:
                continue
            out[j] = out[j] + CENTRE * vec[j]
            out[j + 1] = out[j + 1] + (SPREAD if j == 0 else 0.5 * SPREAD) * vec[j]
            if j > 0:
                out[j - 1] = out[j - 1] + 0.5 * SPREAD * vec[j]
        return out

    def inner(left, right):
        total = zero
        for i in range(4):
            for j in range(4):
                if left[i] is not None and right[j] is not None:
                    total = total + left[i] * right[j] * gram[i][j]
        return total

    moments = [[None] * 4 for _ in range(4)]
    for j in range(3):
        column = image([jnp.ones_like(energy) if i == j else None for i in range(4)])
        for i in range(4):
            total = zero
            for m in range(max(j - 1, 0), j + 2):
                total = total + column[m] * gram[i][m]
            moments[i][j] = total
    for i in range(3):
        moments[i][3] = moments[3][i]
    moments[3][3] = energy

    def pad(vec, size):
        return [vec[i] if i < size else None for i in range(4)]

    residual = [jnp.ones_like(energy), zero, zero, zero, zero]
    direction = list(residual)
    solution = [zero] * 4
    norm_now = gram[0][0]
    for step in range(ITERS):
        trimmed = pad(direction, step + 1)
        bend = zero
        for i in range(step + 1):
            for j in range(step + 1):
                bend = bend + direction[i] * direction[j] * moments[i][j]
        alpha = norm_now / bend
        moved = image(trimmed)
        for i in range(step + 1):
            solution[i] = solution[i] + alpha * direction[i]
        for i in range(step + 2):
            residual[i] = residual[i] - alpha * moved[i]
        if step < ITERS - 1:
            kept = pad(residual, step + 2)
            norm_next = inner(kept, kept)
            ratio = norm_next / norm_now
            direction = [residual[i] + ratio * direction[i] for i in range(5)]
            norm_now = norm_next
    return solution, residual


def last_kernel(which, starts, slots, ids_ref, partner_ref, side_ref, flip_ref, *refs):
    gath_refs = refs[:slots]
    k0_ref, k1_ref, k2_ref, k3_ref, base_ref, order_ref, sol_ref, res_ref = refs[slots : slots + 8]
    work, sol_rows, res_rows, flat, sides = refs[slots + 8 :]
    count, rows, _ = sol_rows.shape
    group = rows // POINTS
    modes = sol_ref.shape[1]
    width = order_ref.shape[2]
    where = pl.ds(line_rows(modes), SUM_ROWS)
    if slots == 1:
        parts = [gath_refs[0][part, where, :] for part in range(gath_refs[0].shape[0])]
    else:
        parts = [ref[where, :] for ref in gath_refs]
    sums = functools.reduce(lambda left, right: left + right, parts)
    collect_sides(gath_refs, ids_ref[0], partner_ref, side_ref, sides, modes)

    def row(place):
        return jnp.broadcast_to(sums[place : place + 1, :], (8, LANES))

    gram = [[None] * 4 for _ in range(4)]
    place = 0
    for i in range(4):
        for j in range(i, 4):
            gram[i][j] = row(place)
            gram[j][i] = gram[i][j]
            place += 1
    solution, residual = conjugate_coefficients(gram, row(place))
    work[...] = base_ref[...]
    add_lines(work, incoming_lines(sides, 0, partner_ref, flip_ref))
    on_a3 = residual[4] * TWICE
    on_k3 = residual[3] - on_a3 * CENTRE
    on_k2 = residual[2] - residual[4]

    def body(ey, carry):
        for point in range(POINTS):
            k0, k1, k2, k3, a3 = [
                get(ref, point, ey) for ref in (k0_ref, k1_ref, k2_ref, k3_ref, work)
            ]
            sol = (solution[0] * k0 + solution[1] * k1) + (solution[2] * k2 + solution[3] * k3)
            res = (residual[0] * k0 + residual[1] * k1) + (on_k2 * k2 + on_k3 * k3) + on_a3 * a3
            for ref, value in ((sol_rows, sol), (res_rows, res)):
                if group >= 8:
                    index = lax.div(ey * 8, jnp.int32(group))
                    at = pl.multiple_of(point * group + lax.rem(ey * 8, jnp.int32(group)), 8)
                    ref[index, pl.ds(at, 8), :] = value
                else:
                    for piece in range(8 // group):
                        ref[ey * (8 // group) + piece, pl.ds(point * group, group), :] = value[
                            piece * group : (piece + 1) * group, :
                        ]
        return carry

    lax.fori_loop(0, BLOCKS, body, 0)
    for ref, out_ref in ((sol_rows, sol_ref), (res_rows, res_ref)):
        flat[...] = jnp.zeros(flat.shape, F32)
        for index in range(count):
            high, low = halves(jnp.transpose(ref[index]))
            both = jnp.concatenate([high, low], axis=0)
            out = dot(both, order_ref[which[index]], ((1,), (0,)))
            window = pl.ds(starts[index], width)
            flat[:, window] = flat[:, window] + (out[:LANES] + out[LANES:])
        for comp in range(3):
            out_ref[comp] = flat[comp * modes : (comp + 1) * modes, :]


def call(kernel, name, out_shapes, args, scratch, scalars=0):
    smem = pl.BlockSpec(memory_space=pltpu.SMEM)
    vmem = pl.BlockSpec(memory_space=pltpu.VMEM)
    return pl.pallas_call(
        kernel,
        name=name,
        out_shape=[jax.ShapeDtypeStruct(shape, F32) for shape in out_shapes],
        in_specs=[smem] * scalars + [vmem] * (len(args) - scalars),
        out_specs=[vmem] * len(out_shapes),
        scratch_shapes=[pltpu.VMEM(shape, F32) for shape in scratch],
        compiler_params=pltpu.CompilerParams(vmem_limit_bytes=VMEM_LIMIT),
    )(*args)


def swap_blocks(blocks, dynamic):
    if not dynamic:
        stacked = lax.all_to_all(jnp.stack(blocks), "four", split_axis=0, concat_axis=0, tiled=True)
        return [stacked[place] for place in range(len(blocks))]
    size = len(blocks)
    return [blocks[0]] + [
        lax.ppermute(blocks[place], "four", [(i, i ^ place) for i in range(size)])
        for place in range(1, size)
    ]


def share_lines(lines):
    parts = lax.axis_size("dom")
    if parts != 8:
        return [lax.all_gather(lines, "dom", axis=0, tiled=False)]
    slots = [lines] + [None] * (parts - 1)
    for slot in range(2, parts, 2):
        slots[slot] = lax.ppermute(lines, "dom", [(i, i ^ slot) for i in range(parts)])
    for slot in range(0, parts, 2):
        slots[slot + 1] = lax.ppermute(slots[slot], "dom", [(i, i ^ 1) for i in range(parts)])
    return slots


def shards(velocity, partner, partner_side, flipped):
    modes = velocity.shape[1]
    count = lax.axis_size("four")
    step, chunks = chunk_sizes(count)
    rows = POINTS * step
    sent_rows = 3 * rows // 4 if is_packed(modes) else rows
    dynamic = step == BLOCKS
    (inv_high, inv_low), (back_high, back_low) = transform_tables(count)
    order, which, starts = order_tables(count)
    ids = jnp.stack([lax.axis_index("dom"), lax.axis_index("four")]).astype(jnp.int32)
    field = (NODES, LANES)
    blocks = [(sent_rows, LANES)] * count
    lined = line_rows(modes)

    spread = []
    for chunk in range(chunks):
        mine = which[chunk::chunks]
        used = sorted(set(mine))
        sent = call(
            functools.partial(pack_kernel, step, count, dynamic),
            "pack",
            blocks,
            (
                ids,
                np.array([used.index(one) for one in mine], np.int32),
                np.array(starts[chunk::chunks], np.int32),
                velocity,
                order[np.array(used)],
            ),
            [],
            scalars=3,
        )
        spread.append(swap_blocks(sent, dynamic))
    local = []
    for chunk in range(chunks):
        sent = call(
            functools.partial(product_kernel, modes, step, count, dynamic),
            "products",
            blocks,
            (ids, *spread[chunk], inv_high, inv_low, back_high, back_low),
            [(count, rows, LANES), (rows, 3 * LANES), (rows, 6 * LANES), (3, rows, LANES)],
            scalars=1,
        )
        local += swap_blocks(sent, dynamic)

    base, lines = call(
        functools.partial(first_kernel, modes, step, count, chunks, dynamic),
        "first",
        [field, (2 * lined, LANES)],
        (ids, partner, *local),
        [field],
        scalars=2,
    )
    tables = (ids, partner, partner_side, flipped)
    gathered = share_lines(lines)
    slots = len(gathered)
    k0, k1, base, lines = call(
        functools.partial(second_kernel, modes, slots),
        "second",
        [field, field, field, (2 * lined, LANES)],
        (*tables, *gathered, lines, base),
        [field, (4, 2 * SIDE, LANES)],
        scalars=4,
    )
    gathered = share_lines(lines)
    k2, k3, a3, lines = call(
        functools.partial(third_kernel, modes, slots),
        "third",
        [field, field, field, (lined + SUM_ROWS, LANES)],
        (*tables, *gathered, lines, k0, k1, base),
        [field, (4, 2 * SIDE, LANES)],
        scalars=4,
    )
    gathered = share_lines(lines)
    units = count * chunks
    outs = call(
        functools.partial(last_kernel, which, starts, slots),
        "last",
        [velocity.shape, velocity.shape],
        (*tables, *gathered, k0, k1, k2, k3, a3, order),
        [field, (units, rows, LANES), (units, rows, LANES), (LANES, NODES), (4, SIDE, LANES)],
        scalars=4,
    )
    return tuple(outs)


def solution(mesh):
    return jax.shard_map(
        shards,
        mesh=mesh,
        in_specs=(P(None, "four", "dom"), P("dom", None), P("dom", None), P("dom", None)),
        out_specs=(P(None, "four", "dom"), P(None, "four", "dom")),
        check_vma=False,
    )
```

```python
import functools
import math

import jax
import jax.numpy as jnp
import numpy as np
from jax import lax
from jax.experimental import pallas as pl
from jax.experimental.pallas import tpu as pltpu
from jax.sharding import PartitionSpec as P

ITERS = 4
REACTION = 2.0
WAVE_STEP = 0.0625
LANES = 128
POINTS = 36
BLOCKS = 8
SIDE = 48
NODES = 2304
CENTRE = 9.0
SPREAD = 9.0
TWICE = 2.0 / SPREAD
SUM_ROWS = 16
VMEM_LIMIT = 32 * 1024 * 1024
F32 = jnp.float32
BF16 = jnp.bfloat16


def gll_tables():
    inner_near = math.sqrt(1.0 / 3.0 - 2.0 * math.sqrt(7.0) / 21.0)
    inner_far = math.sqrt(1.0 / 3.0 + 2.0 * math.sqrt(7.0) / 21.0)
    points = np.array([-1.0, -inner_far, -inner_near, inner_near, inner_far, 1.0])
    values = (63.0 * points**5 - 70.0 * points**3 + 15.0 * points) / 8.0
    weights = 2.0 / (30.0 * values * values)
    spacing = points[:, None] - points[None, :]
    same_point = spacing == 0.0
    derivative = np.where(
        same_point, 0.0, values[:, None] / (values[None, :] * np.where(same_point, 1.0, spacing))
    )
    end_fix = np.array([-7.5, 0.0, 0.0, 0.0, 0.0, 7.5])
    derivative = derivative + np.eye(6) * end_fix[None, :]
    stiffness = derivative.T @ (weights[:, None] * derivative)
    return (weights, derivative, stiffness)


WEIGHTS, DERIV, STIFF = gll_tables()
STIFF_HAT = STIFF / WEIGHTS[:, None]


def fourier_tables(planes):
    plane_ids = np.arange(planes)
    mode_ids = np.arange(planes)
    waves = np.where(mode_ids < 2, 0, mode_ids // 2)
    angle = (plane_ids[:, None] * waves[None, :] % planes) * (2.0 * math.pi / planes)
    is_sine = (mode_ids % 2 == 1) & (mode_ids >= 2)
    basis = np.where(is_sine[None, :], np.sin(angle), np.cos(angle))
    alternating = np.where(plane_ids % 2 == 0, 1.0, -1.0)
    basis = np.where(mode_ids[None, :] == 1, alternating[:, None], basis)
    row_scale = np.where(mode_ids < 2, 1.0, 2.0) / planes
    forward = basis.T * row_scale[:, None]
    rates = (np.arange(planes // 2) * WAVE_STEP)[:, None]
    forward_z = np.zeros_like(forward)
    forward_z[0::2] = rates * forward[1::2]
    forward_z[1::2] = -rates * forward[0::2]
    forward_z[0:2] = 0.0
    return (basis, forward, forward_z)


def split_table(table):
    high = np.asarray(table, np.float32).astype(jnp.bfloat16)
    low = (np.asarray(table, np.float64) - high.astype(np.float64)).astype(np.float32)
    return high, low.astype(jnp.bfloat16)


def transform_tables(count):
    planes = LANES
    modes = planes // count
    basis, forward, forward_z = fourier_tables(planes)
    inverse = np.zeros((count, LANES, 3 * planes))
    for block in range(count):
        ids = slice(block * modes, (block + 1) * modes)
        for comp in range(3):
            at = comp * modes
            inverse[block, at : at + modes, comp * planes : (comp + 1) * planes] = basis[:, ids].T
    back = -np.concatenate([forward.T, forward_z.T], axis=0)
    return split_table(inverse), split_table(back)


def chunk_sizes(count):
    group = BLOCKS * BLOCKS // count
    step = min(group, BLOCKS)
    return step, group // step


def order_tables(count):
    step, _ = chunk_sizes(count)
    units = BLOCKS * BLOCKS // step
    width = 3 * LANES
    starts = []
    tables = []
    which = []
    for index in range(units):
        start = step * index // BLOCKS * 6 * SIDE // LANES * LANES
        starts.append(start)
        table = np.zeros((POINTS * step, width), np.float32)
        for point in range(POINTS):
            for member in range(step):
                element = index * step + member
                row = 6 * (element // BLOCKS) + point // 6
                col = 6 * (element % BLOCKS) + point % 6
                table[point * step + member, row * SIDE + col - start] = 1.0
        for place, known in enumerate(tables):
            if np.array_equal(known, table):
                which.append(place)
                break
        else:
            which.append(len(tables))
            tables.append(table)
    return np.stack(tables).astype(jnp.bfloat16), which, starts


def halves(value):
    high = value.astype(BF16)
    low = (value - high.astype(F32)).astype(BF16)
    return high, low


def dot(left, right, dims):
    return lax.dot_general(left, right, (dims, ((), ())), preferred_element_type=F32)


def dot3(left, right_high, right_low):
    high, low = halves(left)
    dims = ((1,), (0,))
    return dot(high, right_high, dims) + (dot(low, right_high, dims) + dot(high, right_low, dims))


def start_of(point, ey):
    return pl.multiple_of(point * 64 + ey * 8, 8)


def get(ref, point, ey):
    return ref[pl.ds(start_of(point, ey), 8), :]


def put(ref, point, ey, value):
    ref[pl.ds(start_of(point, ey), 8), :] = value


def ex_ids():
    return lax.broadcasted_iota(jnp.int32, (8, LANES), 0)


def helmholtz_rates(four, modes):
    lane = lax.broadcasted_iota(jnp.int32, (8, LANES), 1)
    mode = four * modes + lax.rem(lane, jnp.int32(modes))
    wave = jnp.where(mode == 0, 0, jnp.where(mode == 1, LANES // 2, lax.div(mode, jnp.int32(2))))
    scaled = wave.astype(F32) * WAVE_STEP
    return REACTION + scaled * scaled


def glued_flags(partner_ref):
    return [jnp.where(partner_ref[0, side] >= 0, 1.0, 0.0).astype(F32) for side in range(4)]


def col_masks(flags):
    ex = ex_ids()
    return jnp.where(ex == 0, flags[3], 1.0), jnp.where(ex == 7, flags[1], 1.0)


def join_cols(first, last, masks):
    ex = ex_ids()
    from_right = jnp.where(ex < 7, pltpu.roll(first, 7, 0), 0.0)
    from_left = jnp.where(ex > 0, pltpu.roll(last, 1, 0), 0.0)
    return (first + from_left) * masks[0], (last + from_right) * masks[1]


def join_rows(ref, flags):
    ex = ex_ids()
    not_first = jnp.where(ex == 0, 0.0, 1.0)
    not_last = jnp.where(ex == 7, 0.0, 1.0)
    for ix in range(6):
        for ey in range(7):
            total = get(ref, 30 + ix, ey) + get(ref, ix, ey + 1)
            put(ref, 30 + ix, ey, total)
            put(ref, ix, ey + 1, total)
        low = get(ref, ix, 0) * flags[0]
        high = get(ref, 30 + ix, 7) * flags[2]
        if ix == 0:
            low, high = low * not_first, high * not_first
        if ix == 5:
            low, high = low * not_last, high * not_last
        put(ref, ix, 0, low)
        put(ref, 30 + ix, 7, high)


def line_product(line, table, mirrored=1.0):
    sums = [line[j] + line[5 - j] for j in range(3)]
    gaps = [line[j] - line[5 - j] for j in range(3)]
    out = [None] * 6
    for i in range(3):
        even = None
        odd = None
        for j in range(3):
            even_term = sums[j] * float(0.5 * (table[i, j] + table[i, 5 - j]))
            odd_term = gaps[j] * float(0.5 * (table[i, j] - table[i, 5 - j]))
            even = even_term if even is None else even + even_term
            odd = odd_term if odd is None else odd + odd_term
        out[i] = even + odd
        out[5 - i] = even - odd if mirrored > 0 else odd - even
    return out


def apply_local(src, dst, rates, flags, energy=False):
    masks = col_masks(flags)

    def body(ey, total):
        for ix in range(6):
            line = [get(src, 6 * iy + ix, ey) for iy in range(6)]
            out = line_product(line, STIFF_HAT)
            for iy in range(6):
                put(dst, 6 * iy + ix, ey, out[iy] + rates * line[iy])
        for iy in range(6):
            line = [get(src, 6 * iy + ix, ey) for ix in range(6)]
            out = line_product(line, STIFF_HAT)
            full = [
                (get(dst, 6 * iy + ix, ey) + out[ix]) * float(WEIGHTS[iy] * WEIGHTS[ix])
                for ix in range(6)
            ]
            if energy:
                for ix in range(6):
                    total = total + full[ix] * line[ix]
            full[0], full[5] = join_cols(full[0], full[5], masks)
            for ix in range(6):
                put(dst, 6 * iy + ix, ey, full[ix])
        return total

    total = lax.fori_loop(0, BLOCKS, body, jnp.zeros((8, LANES), F32))
    join_rows(dst, flags)
    return total


def side_slice(side, i):
    if side == 0:
        return pl.ds(i * 64, 8)
    if side == 2:
        return pl.ds((30 + i) * 64 + 56, 8)
    if side == 1:
        return pl.ds((6 * i + 5) * 64 + 7, 8, stride=8)
    return pl.ds(6 * i * 64, 8, stride=8)


def read_line(ref, side):
    return [ref[side_slice(side, i), :] for i in range(6)]


def lane_ids():
    return lax.broadcasted_iota(jnp.int32, (8, LANES), 1)


def is_packed(modes):
    return 3 * modes + modes == LANES


def pack_lanes(values, modes):
    if not is_packed(modes):
        return values
    third = len(values) // 4
    inside = lane_ids() < 3 * modes
    return [
        jnp.where(
            inside,
            values[comp * third + at],
            pltpu.roll(values[3 * third + at], (3 - comp) * modes, 1),
        )
        for comp in range(3)
        for at in range(third)
    ]


def unpack_last(pieces, modes):
    block = lax.div(lane_ids(), jnp.int32(modes))
    turned = [pltpu.roll(pieces[comp], (comp + 1) * modes, 1) for comp in range(3)]
    return jnp.where(block == 0, turned[0], jnp.where(block == 1, turned[1], turned[2]))


def unpack_lanes(values, modes):
    if not is_packed(modes):
        return values
    third = len(values) // 3
    return values + [
        unpack_last([values[comp * third + at] for comp in range(3)], modes) for at in range(third)
    ]


def line_rows(modes):
    return 3 * SIDE if is_packed(modes) else 4 * SIDE


def write_lines(ref, lines_ref, base, modes):
    values = []
    for side in range(4):
        values += read_line(ref, side)
    for at, value in enumerate(pack_lanes(values, modes)):
        lines_ref[pl.ds(base + at * 8, 8), :] = value


def load_lines(lines_ref, modes):
    count = line_rows(modes) // 8
    values = unpack_lanes([lines_ref[pl.ds(at * 8, 8), :] for at in range(count)], modes)
    return [values[side * 6 : side * 6 + 6] for side in range(4)]


def add_lines(ref, lines):
    for side in range(4):
        for i in range(6):
            where = side_slice(side, i)
            ref[where, :] = ref[where, :] + lines[side][i]


def reverse_rows(value):
    ex = ex_ids()
    value = pltpu.roll(value, 4, 0)
    value = jnp.where((ex & 2) == 0, pltpu.roll(value, 6, 0), pltpu.roll(value, 2, 0))
    return jnp.where((ex & 1) == 0, pltpu.roll(value, 7, 0), pltpu.roll(value, 1, 0))


def collect_sides(gath_refs, own, partner_ref, side_ref, sides, modes):
    sets = sides.shape[1] // SIDE
    step = line_rows(modes)

    def copy_side(side, load):
        there = jnp.maximum(side_ref[0, side], 0)

        def plain():
            for place in range(sets):
                for i in range(6):
                    at = pl.multiple_of(place * step + there * SIDE + i * 8, 8)
                    sides[side, pl.ds(place * SIDE + i * 8, 8), :] = load(at)

        if not is_packed(modes):
            plain()
            return
        pl.when(there < 3)(plain)

        @pl.when(there == 3)
        def _():
            for place in range(sets):
                for i in range(6):
                    pieces = [load(place * step + comp * SIDE + i * 8) for comp in range(3)]
                    sides[side, pl.ds(place * SIDE + i * 8, 8), :] = unpack_last(pieces, modes)

    def body(side, carry):
        part = partner_ref[0, side]
        if len(gath_refs) == 1:
            source = jnp.maximum(part, 0)
            copy_side(side, lambda at: gath_refs[0][source, pl.ds(at, 8), :])
            return carry
        for slot, ref in enumerate(gath_refs):
            here = jnp.logical_and(part >= 0, jnp.bitwise_xor(part, own) == slot)

            @pl.when(here)
            def _(ref=ref):
                copy_side(side, lambda at: ref[pl.ds(at, 8), :])

        return carry

    lax.fori_loop(0, 4, body, 0)


def incoming_lines(sides, place, partner_ref, flip_ref):
    lines = []
    for side in range(4):
        glued = partner_ref[0, side] >= 0
        turned = flip_ref[0, side] == 1
        line = []
        for i in range(6):
            at = pl.multiple_of(place * SIDE + jnp.where(turned, 5 - i, i) * 8, 8)
            value = sides[side, pl.ds(at, 8), :]
            value = jnp.where(turned, reverse_rows(value), value)
            line.append(jnp.where(glued, value, 0.0))
        lines.append(line)
    return lines


def own_reaction(own_lines, rates, flags, scale):
    ex = ex_ids()
    edge = float(WEIGHTS[0])
    corner = float(STIFF[0, 0])
    lines = []
    for side in range(4):
        line = own_lines[side]
        along = line_product(line, STIFF_HAT)
        out = [
            (along[i] * edge + line[i] * (corner + rates * edge)) * float(WEIGHTS[i])
            for i in range(6)
        ]
        first = out[0] + pltpu.roll(out[5], 1, 0)
        last = out[5] + pltpu.roll(out[0], 7, 0)
        out[0] = jnp.where(ex > 0, first, 0.0)
        out[5] = jnp.where(ex < 7, last, 0.0)
        lines.append([value * (flags[side] * scale) for value in out])
    return lines


def combine(dst, terms):
    def body(ey, carry):
        for point in range(POINTS):
            total = None
            for factor, ref in terms:
                value = get(ref, point, ey)
                value = value if factor == 1.0 else value * factor
                total = value if total is None else total + value
            put(dst, point, ey, total)
        return carry

    lax.fori_loop(0, BLOCKS, body, 0)


def block_of(place, four):
    return place if isinstance(four, int) else jnp.bitwise_xor(four, place)


def pack_kernel(step, count, dynamic, ids_ref, which_ref, starts_ref, velocity_ref, order_ref, *send_refs):
    modes = velocity_ref.shape[1]
    width = order_ref.shape[2]
    four = ids_ref[1] if dynamic else 0
    for place in range(count):
        index = block_of(place, four)
        window = pl.ds(pl.multiple_of(starts_ref[index], LANES), width)
        rows = [velocity_ref[comp, :, window] for comp in range(3)]
        pad = jnp.zeros((LANES - 3 * modes, width), F32)
        high, low = halves(jnp.concatenate(rows + [pad], axis=0))
        both = jnp.concatenate([high, low], axis=0)
        out = dot(order_ref[which_ref[index]], both, ((1,), (1,)))
        out = out[:, :LANES] + out[:, LANES:]
        if not is_packed(modes):
            send_refs[place][...] = out
            continue
        values = [out[point * step : (point + 1) * step] for point in range(POINTS)]
        for at, value in enumerate(pack_lanes(values, modes)):
            send_refs[place][pl.ds(at * step, step), :] = value


def product_kernel(modes, step, count, dynamic, ids_ref, *refs):
    recv_refs = refs[:count]
    inv_high, inv_low, back_high, back_low = refs[count : count + 4]
    send_refs = refs[count + 4 : 2 * count + 4]
    full, phys, prod, spec = refs[2 * count + 4 :]
    four = ids_ref[1] if dynamic else 0
    packed = is_packed(modes)
    total = None
    for place in range(count):
        index = block_of(place, four)
        if packed:
            ready = 3 * POINTS // 4
            values = [recv_refs[place][pl.ds(at * step, step), :] for at in range(ready)]
            for at, value in enumerate(unpack_lanes(values, modes)):
                full[place, pl.ds(at * step, step), :] = value
        else:
            full[place] = recv_refs[place][...]
        part = dot3(full[place], inv_high[index], inv_low[index])
        total = part if total is None else total + part
    phys[...] = total
    width = 2 * LANES

    def field(point, comp):
        return phys[pl.ds(point * step, step), comp * LANES : (comp + 1) * LANES]

    for comp in range(3):
        wide = pl.ds(comp * width, LANES)
        for iy in range(6):
            line = []
            for ix in range(6):
                point = 6 * iy + ix
                value = field(point, comp)
                line.append(value * field(point, 0))
                prod[pl.ds(point * step, step), pl.ds(comp * width + LANES, LANES)] = (
                    value * field(point, 2)
                )
            out = line_product(line, DERIV, -1.0)
            for ix in range(6):
                prod[pl.ds((6 * iy + ix) * step, step), wide] = out[ix]
        for ix in range(6):
            line = [field(6 * iy + ix, comp) * field(6 * iy + ix, 1) for iy in range(6)]
            out = line_product(line, DERIV, -1.0)
            for iy in range(6):
                at = pl.ds((6 * iy + ix) * step, step)
                prod[at, wide] = prod[at, wide] + out[iy]
        spec[comp] = dot3(prod[:, comp * width : (comp + 1) * width], back_high[...], back_low[...])

    lane_block = lax.div(lax.broadcasted_iota(jnp.int32, (step, LANES), 1), jnp.int32(modes))
    masks = []
    shifts = []
    for place in range(count):
        index = block_of(place, four)
        masks.append([lane_block == lax.rem(index + comp, count) for comp in range(2)])
        shifts.append(lax.rem(LANES - index * modes, LANES))
    kept = []
    for point in range(POINTS):
        at = pl.ds(point * step, step)
        mass = float(WEIGHTS[point // 6] * WEIGHTS[point % 6])
        turned = [spec[0, at, :]]
        turned += [pltpu.roll(spec[comp, at, :], comp * modes, 1) for comp in (1, 2)]
        for place in range(count):
            mask = masks[place]
            mixed = jnp.where(mask[0], turned[0], jnp.where(mask[1], turned[1], turned[2]))
            nonlinear = pltpu.roll(mixed, shifts[place], 1)
            full[place, at, :] = mass * (REACTION * full[place, at, :] + nonlinear)
    for place in range(count):
        values = [full[place, pl.ds(point * step, step), :] for point in range(POINTS)]
        for at, value in enumerate(pack_lanes(values, modes)):
            send_refs[place][pl.ds(at * step, step), :] = value


def first_kernel(modes, step, count, chunks, dynamic, ids_ref, partner_ref, *refs):
    recv_refs = refs[: count * chunks]
    base_ref, lines_ref, work = refs[count * chunks :]
    four = ids_ref[1] if dynamic else 0
    rates = helmholtz_rates(ids_ref[1], modes)
    flags = glued_flags(partner_ref)
    for chunk in range(chunks):
        for place in range(count):
            ref = recv_refs[chunk * count + place]
            ready = ref.shape[0] // step
            first = (block_of(place, four) * chunks + chunk) * step
            values = unpack_lanes([ref[pl.ds(at * step, step), :] for at in range(ready)], modes)
            for point in range(POINTS):
                at = point * 64 + first
                at = at if isinstance(at, int) else pl.multiple_of(at, step)
                base_ref[pl.ds(at, step), :] = values[point]
    masks = col_masks(flags)
    for ey in range(BLOCKS):
        for iy in range(6):
            first, last = join_cols(get(base_ref, 6 * iy, ey), get(base_ref, 6 * iy + 5, ey), masks)
            put(base_ref, 6 * iy, ey, first)
            put(base_ref, 6 * iy + 5, ey, last)
    join_rows(base_ref, flags)
    apply_local(base_ref, work, rates, flags)
    write_lines(base_ref, lines_ref, 0, modes)
    write_lines(work, lines_ref, line_rows(modes), modes)


def second_kernel(modes, slots, ids_ref, partner_ref, side_ref, flip_ref, *refs):
    gath_refs = refs[:slots]
    lines_ref, base_ref, k0_ref, k1_ref, k2_ref, next_ref, work, sides = refs[slots:]
    rates = helmholtz_rates(ids_ref[1], modes)
    flags = glued_flags(partner_ref)
    collect_sides(gath_refs, ids_ref[0], partner_ref, side_ref, sides, modes)
    back = own_reaction(load_lines(lines_ref, modes), rates, flags, 1.0)
    k0_ref[...] = base_ref[...]
    add_lines(k0_ref, incoming_lines(sides, 0, partner_ref, flip_ref))
    apply_local(k0_ref, work, rates, flags)
    add_lines(work, incoming_lines(sides, 1, partner_ref, flip_ref))
    add_lines(work, back)
    combine(k1_ref, [(1.0 / SPREAD, work), (-CENTRE / SPREAD, k0_ref)])
    apply_local(k1_ref, work, rates, flags)
    write_lines(work, next_ref, 0, modes)
    combine(k2_ref, [(TWICE, work), (-CENTRE * TWICE, k1_ref), (-1.0, k0_ref)])
    apply_local(k2_ref, work, rates, flags)
    write_lines(work, next_ref, line_rows(modes), modes)


def third_kernel(modes, slots, ids_ref, partner_ref, side_ref, flip_ref, *refs):
    gath_refs = refs[:slots]
    lines_ref, k0_ref, k1_ref, base_ref = refs[slots : slots + 4]
    k2_ref, k3_ref, a3_ref, next_ref, work, sides = refs[slots + 4 :]
    rates = helmholtz_rates(ids_ref[1], modes)
    flags = glued_flags(partner_ref)
    collect_sides(gath_refs, ids_ref[0], partner_ref, side_ref, sides, modes)
    back = own_reaction(load_lines(lines_ref, modes), rates, flags, TWICE)
    k2_ref[...] = base_ref[...]
    incoming = incoming_lines(sides, 0, partner_ref, flip_ref)
    add_lines(k2_ref, [[value * TWICE for value in line] for line in incoming])
    apply_local(k2_ref, work, rates, flags)
    add_lines(work, incoming_lines(sides, 1, partner_ref, flip_ref))
    add_lines(work, back)
    combine(k3_ref, [(TWICE, work), (-CENTRE * TWICE, k2_ref), (-1.0, k1_ref)])
    energy = apply_local(k3_ref, a3_ref, rates, flags, energy=True)
    write_lines(a3_ref, next_ref, 0, modes)
    refs = (k0_ref, k1_ref, k2_ref, k3_ref)

    def body(ey, sums):
        sums = list(sums)
        for point in range(POINTS):
            ends = (point // 6 in (0, 5)) + (point % 6 in (0, 5))
            values = [get(ref, point, ey) for ref in refs]
            place = 0
            for i in range(4):
                scaled = values[i] * (0.5**ends) if ends else values[i]
                for j in range(i, 4):
                    sums[place] = sums[place] + scaled * values[j]
                    place += 1
        return tuple(sums)

    zero = jnp.zeros((8, LANES), F32)
    sums = lax.fori_loop(0, BLOCKS, body, (zero,) * 10)
    rows = [jnp.sum(value, axis=0, keepdims=True) for value in sums]
    rows.append(jnp.sum(energy, axis=0, keepdims=True))
    rows.append(jnp.zeros((SUM_ROWS - len(rows), LANES), F32))
    next_ref[pl.ds(line_rows(modes), SUM_ROWS), :] = jnp.concatenate(rows, axis=0)


def conjugate_coefficients(gram, energy):
    zero = jnp.zeros_like(energy)

    def image(vec):
        out = [zero] * 5
        for j in range(4):
            if vec[j] is None:
                continue
            out[j] = out[j] + CENTRE * vec[j]
            out[j + 1] = out[j + 1] + (SPREAD if j == 0 else 0.5 * SPREAD) * vec[j]
            if j > 0:
                out[j - 1] = out[j - 1] + 0.5 * SPREAD * vec[j]
        return out

    def inner(left, right):
        total = zero
        for i in range(4):
            for j in range(4):
                if left[i] is not None and right[j] is not None:
                    total = total + left[i] * right[j] * gram[i][j]
        return total

    moments = [[None] * 4 for _ in range(4)]
    for j in range(3):
        column = image([jnp.ones_like(energy) if i == j else None for i in range(4)])
        for i in range(4):
            total = zero
            for m in range(max(j - 1, 0), j + 2):
                total = total + column[m] * gram[i][m]
            moments[i][j] = total
    for i in range(3):
        moments[i][3] = moments[3][i]
    moments[3][3] = energy

    def pad(vec, size):
        return [vec[i] if i < size else None for i in range(4)]

    residual = [jnp.ones_like(energy), zero, zero, zero, zero]
    direction = list(residual)
    solution = [zero] * 4
    norm_now = gram[0][0]
    for step in range(ITERS):
        trimmed = pad(direction, step + 1)
        bend = zero
        for i in range(step + 1):
            for j in range(step + 1):
                bend = bend + direction[i] * direction[j] * moments[i][j]
        alpha = norm_now / bend
        moved = image(trimmed)
        for i in range(step + 1):
            solution[i] = solution[i] + alpha * direction[i]
        for i in range(step + 2):
            residual[i] = residual[i] - alpha * moved[i]
        if step < ITERS - 1:
            kept = pad(residual, step + 2)
            norm_next = inner(kept, kept)
            ratio = norm_next / norm_now
            direction = [residual[i] + ratio * direction[i] for i in range(5)]
            norm_now = norm_next
    return solution, residual


def last_kernel(which, starts, slots, ids_ref, partner_ref, side_ref, flip_ref, *refs):
    gath_refs = refs[:slots]
    k0_ref, k1_ref, k2_ref, k3_ref, base_ref, order_ref, sol_ref, res_ref = refs[slots : slots + 8]
    work, sol_rows, res_rows, flat, sides = refs[slots + 8 :]
    count, rows, _ = sol_rows.shape
    group = rows // POINTS
    modes = sol_ref.shape[1]
    width = order_ref.shape[2]
    where = pl.ds(line_rows(modes), SUM_ROWS)
    if slots == 1:
        parts = [gath_refs[0][part, where, :] for part in range(gath_refs[0].shape[0])]
    else:
        parts = [ref[where, :] for ref in gath_refs]
    sums = functools.reduce(lambda left, right: left + right, parts)
    collect_sides(gath_refs, ids_ref[0], partner_ref, side_ref, sides, modes)

    def row(place):
        return jnp.broadcast_to(sums[place : place + 1, :], (8, LANES))

    gram = [[None] * 4 for _ in range(4)]
    place = 0
    for i in range(4):
        for j in range(i, 4):
            gram[i][j] = row(place)
            gram[j][i] = gram[i][j]
            place += 1
    solution, residual = conjugate_coefficients(gram, row(place))
    work[...] = base_ref[...]
    add_lines(work, incoming_lines(sides, 0, partner_ref, flip_ref))
    on_a3 = residual[4] * TWICE
    on_k3 = residual[3] - on_a3 * CENTRE
    on_k2 = residual[2] - residual[4]

    def body(ey, carry):
        for point in range(POINTS):
            k0, k1, k2, k3, a3 = [
                get(ref, point, ey) for ref in (k0_ref, k1_ref, k2_ref, k3_ref, work)
            ]
            sol = (solution[0] * k0 + solution[1] * k1) + (solution[2] * k2 + solution[3] * k3)
            res = (residual[0] * k0 + residual[1] * k1) + (on_k2 * k2 + on_k3 * k3) + on_a3 * a3
            for ref, value in ((sol_rows, sol), (res_rows, res)):
                if group >= 8:
                    index = lax.div(ey * 8, jnp.int32(group))
                    at = pl.multiple_of(point * group + lax.rem(ey * 8, jnp.int32(group)), 8)
                    ref[index, pl.ds(at, 8), :] = value
                else:
                    for piece in range(8 // group):
                        ref[ey * (8 // group) + piece, pl.ds(point * group, group), :] = value[
                            piece * group : (piece + 1) * group, :
                        ]
        return carry

    lax.fori_loop(0, BLOCKS, body, 0)
    for ref, out_ref in ((sol_rows, sol_ref), (res_rows, res_ref)):
        flat[...] = jnp.zeros(flat.shape, F32)
        for index in range(count):
            high, low = halves(jnp.transpose(ref[index]))
            both = jnp.concatenate([high, low], axis=0)
            out = dot(both, order_ref[which[index]], ((1,), (0,)))
            window = pl.ds(starts[index], width)
            flat[:, window] = flat[:, window] + (out[:LANES] + out[LANES:])
        for comp in range(3):
            out_ref[comp] = flat[comp * modes : (comp + 1) * modes, :]


def call(kernel, name, out_shapes, args, scratch, scalars=0, keep=True):
    smem = pl.BlockSpec(memory_space=pltpu.SMEM)
    vmem = pl.BlockSpec(memory_space=pltpu.VMEM)
    return pl.pallas_call(
        kernel,
        name=name,
        out_shape=[pltpu.VMEM(shape, F32) if keep else jax.ShapeDtypeStruct(shape, F32) for shape in out_shapes],
        in_specs=[smem] * scalars + [vmem] * (len(args) - scalars),
        out_specs=[vmem] * len(out_shapes),
        scratch_shapes=[pltpu.VMEM(shape, F32) for shape in scratch],
        compiler_params=pltpu.CompilerParams(vmem_limit_bytes=VMEM_LIMIT),
    )(*args[:scalars], *[held(arg) for arg in args[scalars:]])


def held(arg):
    return arg if isinstance(arg, np.ndarray) else pltpu.with_memory_space_constraint(arg, pltpu.VMEM)


def swap_blocks(blocks, dynamic):
    if not dynamic:
        stacked = lax.all_to_all(jnp.stack(blocks), "four", split_axis=0, concat_axis=0, tiled=True)
        return [stacked[place] for place in range(len(blocks))]
    size = len(blocks)
    return [blocks[0]] + [
        lax.ppermute(blocks[place], "four", [(i, i ^ place) for i in range(size)])
        for place in range(1, size)
    ]


def share_lines(lines):
    parts = lax.axis_size("dom")
    if parts != 8:
        return [lax.all_gather(lines, "dom", axis=0, tiled=False)]
    slots = [lines] + [None] * (parts - 1)
    for slot in range(2, parts, 2):
        slots[slot] = lax.ppermute(lines, "dom", [(i, i ^ slot) for i in range(parts)])
    for slot in range(0, parts, 2):
        slots[slot + 1] = lax.ppermute(slots[slot], "dom", [(i, i ^ 1) for i in range(parts)])
    return slots


def shards(velocity, partner, partner_side, flipped):
    modes = velocity.shape[1]
    count = lax.axis_size("four")
    step, chunks = chunk_sizes(count)
    rows = POINTS * step
    sent_rows = 3 * rows // 4 if is_packed(modes) else rows
    dynamic = step == BLOCKS
    (inv_high, inv_low), (back_high, back_low) = transform_tables(count)
    order, which, starts = order_tables(count)
    ids = jnp.stack([lax.axis_index("dom"), lax.axis_index("four")]).astype(jnp.int32)
    field = (NODES, LANES)
    blocks = [(sent_rows, LANES)] * count
    lined = line_rows(modes)

    spread = []
    for chunk in range(chunks):
        mine = which[chunk::chunks]
        used = sorted(set(mine))
        sent = call(
            functools.partial(pack_kernel, step, count, dynamic),
            "pack",
            blocks,
            (
                ids,
                np.array([used.index(one) for one in mine], np.int32),
                np.array(starts[chunk::chunks], np.int32),
                velocity,
                order[np.array(used)],
            ),
            [],
            scalars=3,
        )
        spread.append(swap_blocks(sent, dynamic))
    local = []
    for chunk in range(chunks):
        sent = call(
            functools.partial(product_kernel, modes, step, count, dynamic),
            "products",
            blocks,
            (ids, *spread[chunk], inv_high, inv_low, back_high, back_low),
            [(count, rows, LANES), (rows, 3 * LANES), (rows, 6 * LANES), (3, rows, LANES)],
            scalars=1,
        )
        local += swap_blocks(sent, dynamic)

    base, lines = call(
        functools.partial(first_kernel, modes, step, count, chunks, dynamic),
        "first",
        [field, (2 * lined, LANES)],
        (ids, partner, *local),
        [field],
        scalars=2,
    )
    tables = (ids, partner, partner_side, flipped)
    gathered = share_lines(lines)
    slots = len(gathered)
    k0, k1, base, lines = call(
        functools.partial(second_kernel, modes, slots),
        "second",
        [field, field, field, (2 * lined, LANES)],
        (*tables, *gathered, lines, base),
        [field, (4, 2 * SIDE, LANES)],
        scalars=4,
    )
    gathered = share_lines(lines)
    k2, k3, a3, lines = call(
        functools.partial(third_kernel, modes, slots),
        "third",
        [field, field, field, (lined + SUM_ROWS, LANES)],
        (*tables, *gathered, lines, k0, k1, base),
        [field, (4, 2 * SIDE, LANES)],
        scalars=4,
    )
    gathered = share_lines(lines)
    units = count * chunks
    outs = call(
        functools.partial(last_kernel, which, starts, slots),
        "last",
        [velocity.shape, velocity.shape],
        (*tables, *gathered, k0, k1, k2, k3, a3, order),
        [field, (units, rows, LANES), (units, rows, LANES), (LANES, NODES), (4, SIDE, LANES)],
        scalars=4,
        keep=False,
    )
    return tuple(outs)


def solution(mesh):
    return jax.shard_map(
        shards,
        mesh=mesh,
        in_specs=(P(None, "four", "dom"), P("dom", None), P("dom", None), P("dom", None)),
        out_specs=(P(None, "four", "dom"), P(None, "four", "dom")),
        check_vma=False,
    )
```

```python
import functools
import math

import jax
import jax.numpy as jnp
import numpy as np
from jax import lax
from jax.experimental import pallas as pl
from jax.experimental.pallas import tpu as pltpu
from jax.sharding import PartitionSpec as P

ITERS = 4
REACTION = 2.0
WAVE_STEP = 0.0625
LANES = 128
POINTS = 36
BLOCKS = 8
SIDE = 48
NODES = 2304
CENTRE = 9.0
SPREAD = 9.0
TWICE = 2.0 / SPREAD
SUM_ROWS = 8
VMEM_LIMIT = 32 * 1024 * 1024
F32 = jnp.float32
BF16 = jnp.bfloat16


def gll_tables():
    inner_near = math.sqrt(1.0 / 3.0 - 2.0 * math.sqrt(7.0) / 21.0)
    inner_far = math.sqrt(1.0 / 3.0 + 2.0 * math.sqrt(7.0) / 21.0)
    points = np.array([-1.0, -inner_far, -inner_near, inner_near, inner_far, 1.0])
    values = (63.0 * points**5 - 70.0 * points**3 + 15.0 * points) / 8.0
    weights = 2.0 / (30.0 * values * values)
    spacing = points[:, None] - points[None, :]
    same_point = spacing == 0.0
    derivative = np.where(
        same_point, 0.0, values[:, None] / (values[None, :] * np.where(same_point, 1.0, spacing))
    )
    end_fix = np.array([-7.5, 0.0, 0.0, 0.0, 0.0, 7.5])
    derivative = derivative + np.eye(6) * end_fix[None, :]
    stiffness = derivative.T @ (weights[:, None] * derivative)
    return (weights, derivative, stiffness)


WEIGHTS, DERIV, STIFF = gll_tables()
STIFF_HAT = STIFF / WEIGHTS[:, None]


def fourier_tables(planes):
    plane_ids = np.arange(planes)
    mode_ids = np.arange(planes)
    waves = np.where(mode_ids < 2, 0, mode_ids // 2)
    angle = (plane_ids[:, None] * waves[None, :] % planes) * (2.0 * math.pi / planes)
    is_sine = (mode_ids % 2 == 1) & (mode_ids >= 2)
    basis = np.where(is_sine[None, :], np.sin(angle), np.cos(angle))
    alternating = np.where(plane_ids % 2 == 0, 1.0, -1.0)
    basis = np.where(mode_ids[None, :] == 1, alternating[:, None], basis)
    row_scale = np.where(mode_ids < 2, 1.0, 2.0) / planes
    forward = basis.T * row_scale[:, None]
    rates = (np.arange(planes // 2) * WAVE_STEP)[:, None]
    forward_z = np.zeros_like(forward)
    forward_z[0::2] = rates * forward[1::2]
    forward_z[1::2] = -rates * forward[0::2]
    forward_z[0:2] = 0.0
    return (basis, forward, forward_z)


def split_table(table):
    high = np.asarray(table, np.float32).astype(jnp.bfloat16)
    low = (np.asarray(table, np.float64) - high.astype(np.float64)).astype(np.float32)
    return high, low.astype(jnp.bfloat16)


def transform_tables(count):
    planes = LANES
    modes = planes // count
    basis, forward, forward_z = fourier_tables(planes)
    inverse = np.zeros((count, LANES, 3 * planes))
    for block in range(count):
        ids = slice(block * modes, (block + 1) * modes)
        for comp in range(3):
            at = comp * modes
            inverse[block, at : at + modes, comp * planes : (comp + 1) * planes] = basis[:, ids].T
    back = -np.concatenate([forward.T, forward_z.T], axis=0)
    return split_table(inverse), split_table(back)


def chunk_sizes(count):
    group = BLOCKS * BLOCKS // count
    step = min(group, BLOCKS)
    return step, group // step


def order_tables(count):
    step, _ = chunk_sizes(count)
    units = BLOCKS * BLOCKS // step
    width = 3 * LANES
    starts = []
    tables = []
    which = []
    for index in range(units):
        start = step * index // BLOCKS * 6 * SIDE // LANES * LANES
        starts.append(start)
        table = np.zeros((POINTS * step, width), np.float32)
        for point in range(POINTS):
            for member in range(step):
                element = index * step + member
                row = 6 * (element // BLOCKS) + point // 6
                col = 6 * (element % BLOCKS) + point % 6
                table[point * step + member, row * SIDE + col - start] = 1.0
        for place, known in enumerate(tables):
            if np.array_equal(known, table):
                which.append(place)
                break
        else:
            which.append(len(tables))
            tables.append(table)
    return np.stack(tables).astype(jnp.bfloat16), which, starts


def halves(value):
    high = value.astype(BF16)
    low = (value - high.astype(F32)).astype(BF16)
    return high, low


def dot(left, right, dims):
    return lax.dot_general(left, right, (dims, ((), ())), preferred_element_type=F32)


def dot3(left, right_high, right_low):
    high, low = halves(left)
    dims = ((1,), (0,))
    return dot(high, right_high, dims) + (dot(low, right_high, dims) + dot(high, right_low, dims))


def start_of(point, ey):
    return pl.multiple_of(point * 64 + ey * 8, 8)


def get(ref, point, ey):
    return ref[pl.ds(start_of(point, ey), 8), :]


def put(ref, point, ey, value):
    ref[pl.ds(start_of(point, ey), 8), :] = value


def ex_ids():
    return lax.broadcasted_iota(jnp.int32, (8, LANES), 0)


def helmholtz_rates(four, modes):
    lane = lax.broadcasted_iota(jnp.int32, (8, LANES), 1)
    mode = four * modes + lax.rem(lane, jnp.int32(modes))
    wave = jnp.where(mode == 0, 0, jnp.where(mode == 1, LANES // 2, lax.div(mode, jnp.int32(2))))
    scaled = wave.astype(F32) * WAVE_STEP
    return REACTION + scaled * scaled


def glued_flags(partner_ref):
    return [jnp.where(partner_ref[0, side] >= 0, 1.0, 0.0).astype(F32) for side in range(4)]


def col_masks(flags):
    ex = ex_ids()
    return jnp.where(ex == 0, flags[3], 1.0), jnp.where(ex == 7, flags[1], 1.0)


def join_cols(first, last, masks):
    ex = ex_ids()
    from_right = jnp.where(ex < 7, pltpu.roll(first, 7, 0), 0.0)
    from_left = jnp.where(ex > 0, pltpu.roll(last, 1, 0), 0.0)
    return (first + from_left) * masks[0], (last + from_right) * masks[1]


def join_rows(ref, flags):
    ex = ex_ids()
    not_first = jnp.where(ex == 0, 0.0, 1.0)
    not_last = jnp.where(ex == 7, 0.0, 1.0)
    for ix in range(6):
        for ey in range(7):
            total = get(ref, 30 + ix, ey) + get(ref, ix, ey + 1)
            put(ref, 30 + ix, ey, total)
            put(ref, ix, ey + 1, total)
        low = get(ref, ix, 0) * flags[0]
        high = get(ref, 30 + ix, 7) * flags[2]
        if ix == 0:
            low, high = low * not_first, high * not_first
        if ix == 5:
            low, high = low * not_last, high * not_last
        put(ref, ix, 0, low)
        put(ref, 30 + ix, 7, high)


def line_product(line, table, mirrored=1.0):
    sums = [line[j] + line[5 - j] for j in range(3)]
    gaps = [line[j] - line[5 - j] for j in range(3)]
    out = [None] * 6
    for i in range(3):
        even = None
        odd = None
        for j in range(3):
            even_term = sums[j] * float(0.5 * (table[i, j] + table[i, 5 - j]))
            odd_term = gaps[j] * float(0.5 * (table[i, j] - table[i, 5 - j]))
            even = even_term if even is None else even + even_term
            odd = odd_term if odd is None else odd + odd_term
        out[i] = even + odd
        out[5 - i] = even - odd if mirrored > 0 else odd - even
    return out


def apply_local(src, dst, rates, flags, terms=(), products=(), energy=False):
    masks = col_masks(flags)

    def body(ey, sums):
        sums = list(sums)
        for ix in range(6):
            line = []
            for iy in range(6):
                point = 6 * iy + ix
                if not terms:
                    line.append(get(src, point, ey))
                    continue
                values = [get(ref, point, ey) for _, ref in terms]
                value = None
                for (factor, _), part in zip(terms, values):
                    part = -part if factor == -1.0 else part * factor
                    value = part if value is None else value + part
                put(src, point, ey, value)
                line.append(value)
                values.append(value)
                ends = (iy in (0, 5)) + (ix in (0, 5))
                for place, (left, right) in enumerate(products):
                    both = values[left] * values[right]
                    sums[place] = sums[place] + (both * (0.5**ends) if ends else both)
            out = line_product(line, STIFF_HAT)
            for iy in range(6):
                put(dst, 6 * iy + ix, ey, out[iy] + rates * line[iy])
        for iy in range(6):
            line = [get(src, 6 * iy + ix, ey) for ix in range(6)]
            out = line_product(line, STIFF_HAT)
            full = [
                (get(dst, 6 * iy + ix, ey) + out[ix]) * float(WEIGHTS[iy] * WEIGHTS[ix])
                for ix in range(6)
            ]
            if energy:
                for ix in range(6):
                    sums[-1] = sums[-1] + full[ix] * line[ix]
            full[0], full[5] = join_cols(full[0], full[5], masks)
            for ix in range(6):
                put(dst, 6 * iy + ix, ey, full[ix])
        return tuple(sums)

    zero = jnp.zeros((8, LANES), F32)
    sums = lax.fori_loop(0, BLOCKS, body, (zero,) * (len(products) + int(energy)))
    join_rows(dst, flags)
    return sums


def side_slice(side, i):
    if side == 0:
        return pl.ds(i * 64, 8)
    if side == 2:
        return pl.ds((30 + i) * 64 + 56, 8)
    if side == 1:
        return pl.ds((6 * i + 5) * 64 + 7, 8, stride=8)
    return pl.ds(6 * i * 64, 8, stride=8)


def read_line(ref, side):
    return [ref[side_slice(side, i), :] for i in range(6)]


def lane_ids():
    return lax.broadcasted_iota(jnp.int32, (8, LANES), 1)


def is_packed(modes):
    return 3 * modes + modes == LANES


def pack_lanes(values, modes):
    if not is_packed(modes):
        return values
    third = len(values) // 4
    inside = lane_ids() < 3 * modes
    return [
        jnp.where(
            inside,
            values[comp * third + at],
            pltpu.roll(values[3 * third + at], (3 - comp) * modes, 1),
        )
        for comp in range(3)
        for at in range(third)
    ]


def unpack_last(pieces, modes):
    block = lax.div(lane_ids(), jnp.int32(modes))
    turned = [pltpu.roll(pieces[comp], (comp + 1) * modes, 1) for comp in range(3)]
    return jnp.where(block == 0, turned[0], jnp.where(block == 1, turned[1], turned[2]))


def unpack_lanes(values, modes):
    if not is_packed(modes):
        return values
    third = len(values) // 3
    return values + [
        unpack_last([values[comp * third + at] for comp in range(3)], modes) for at in range(third)
    ]


def line_rows(modes):
    return 3 * SIDE if is_packed(modes) else 4 * SIDE


def write_lines(ref, lines_ref, base, modes):
    values = []
    for side in range(4):
        values += read_line(ref, side)
    for at, value in enumerate(pack_lanes(values, modes)):
        lines_ref[pl.ds(base + at * 8, 8), :] = value


def load_lines(lines_ref, modes):
    count = line_rows(modes) // 8
    values = unpack_lanes([lines_ref[pl.ds(at * 8, 8), :] for at in range(count)], modes)
    return [values[side * 6 : side * 6 + 6] for side in range(4)]


def add_lines(ref, lines):
    for side in range(4):
        for i in range(6):
            where = side_slice(side, i)
            ref[where, :] = ref[where, :] + lines[side][i]


def reverse_rows(value):
    ex = ex_ids()
    value = pltpu.roll(value, 4, 0)
    value = jnp.where((ex & 2) == 0, pltpu.roll(value, 6, 0), pltpu.roll(value, 2, 0))
    return jnp.where((ex & 1) == 0, pltpu.roll(value, 7, 0), pltpu.roll(value, 1, 0))


def collect_sides(gath_refs, own, partner_ref, side_ref, sides, modes):
    sets = sides.shape[1] // SIDE
    step = line_rows(modes)

    def copy_side(side, load):
        there = jnp.maximum(side_ref[0, side], 0)

        def plain():
            for place in range(sets):
                for i in range(6):
                    at = pl.multiple_of(place * step + there * SIDE + i * 8, 8)
                    sides[side, pl.ds(place * SIDE + i * 8, 8), :] = load(at)

        if not is_packed(modes):
            plain()
            return
        pl.when(there < 3)(plain)

        @pl.when(there == 3)
        def _():
            for place in range(sets):
                for i in range(6):
                    pieces = [load(place * step + comp * SIDE + i * 8) for comp in range(3)]
                    sides[side, pl.ds(place * SIDE + i * 8, 8), :] = unpack_last(pieces, modes)

    def body(side, carry):
        part = partner_ref[0, side]
        if len(gath_refs) == 1:
            source = jnp.maximum(part, 0)
            copy_side(side, lambda at: gath_refs[0][source, pl.ds(at, 8), :])
            return carry
        for slot, ref in enumerate(gath_refs):
            here = jnp.logical_and(part >= 0, jnp.bitwise_xor(part, own) == slot)

            @pl.when(here)
            def _(ref=ref):
                copy_side(side, lambda at: ref[pl.ds(at, 8), :])

        return carry

    lax.fori_loop(0, 4, body, 0)


def incoming_lines(sides, place, partner_ref, flip_ref):
    lines = []
    for side in range(4):
        glued = partner_ref[0, side] >= 0
        turned = flip_ref[0, side] == 1
        line = []
        for i in range(6):
            at = pl.multiple_of(place * SIDE + jnp.where(turned, 5 - i, i) * 8, 8)
            value = sides[side, pl.ds(at, 8), :]
            value = jnp.where(turned, reverse_rows(value), value)
            line.append(jnp.where(glued, value, 0.0))
        lines.append(line)
    return lines


def own_reaction(own_lines, rates, flags, scale):
    ex = ex_ids()
    edge = float(WEIGHTS[0])
    corner = float(STIFF[0, 0])
    lines = []
    for side in range(4):
        line = own_lines[side]
        along = line_product(line, STIFF_HAT)
        out = [
            (along[i] * edge + line[i] * (corner + rates * edge)) * float(WEIGHTS[i])
            for i in range(6)
        ]
        first = out[0] + pltpu.roll(out[5], 1, 0)
        last = out[5] + pltpu.roll(out[0], 7, 0)
        out[0] = jnp.where(ex > 0, first, 0.0)
        out[5] = jnp.where(ex < 7, last, 0.0)
        lines.append([value * (flags[side] * scale) for value in out])
    return lines


def pick(index, values):
    if isinstance(index, int):
        return values[index]
    chosen = jnp.int32(values[0])
    for place in range(1, len(values)):
        chosen = jnp.where(index == place, jnp.int32(values[place]), chosen)
    return chosen


def block_of(place, four):
    return place if isinstance(four, int) else jnp.bitwise_xor(four, place)


def pack_kernel(step, count, dynamic, which, starts, ids_ref, velocity_ref, order_ref, *send_refs):
    modes = velocity_ref.shape[1]
    width = order_ref.shape[2]
    four = ids_ref[1] if dynamic else 0
    for place in range(count):
        index = block_of(place, four)
        start = pick(index, starts)
        start = start if isinstance(start, int) else pl.multiple_of(start, LANES)
        window = pl.ds(start, width)
        rows = [velocity_ref[comp, :, window] for comp in range(3)]
        pad = jnp.zeros((LANES - 3 * modes, width), F32)
        high, low = halves(jnp.concatenate(rows + [pad], axis=0))
        both = jnp.concatenate([high, low], axis=0)
        out = dot(order_ref[pick(index, which)], both, ((1,), (1,)))
        out = out[:, :LANES] + out[:, LANES:]
        if not is_packed(modes):
            send_refs[place][...] = out
            continue
        values = [out[point * step : (point + 1) * step] for point in range(POINTS)]
        for at, value in enumerate(pack_lanes(values, modes)):
            send_refs[place][pl.ds(at * step, step), :] = value


def product_kernel(modes, step, count, dynamic, ids_ref, *refs):
    recv_refs = refs[:count]
    inv_high, inv_low, back_high, back_low = refs[count : count + 4]
    send_refs = refs[count + 4 : 2 * count + 4]
    full, phys, prod, spec = refs[2 * count + 4 :]
    four = ids_ref[1] if dynamic else 0
    packed = is_packed(modes)
    total = None
    for place in range(count):
        index = block_of(place, four)
        if packed:
            ready = 3 * POINTS // 4
            values = [recv_refs[place][pl.ds(at * step, step), :] for at in range(ready)]
            for at, value in enumerate(unpack_lanes(values, modes)):
                full[place, pl.ds(at * step, step), :] = value
        else:
            full[place] = recv_refs[place][...]
        part = dot3(full[place], inv_high[index], inv_low[index])
        total = part if total is None else total + part
    phys[...] = total
    width = 2 * LANES

    def field(point, comp):
        return phys[pl.ds(point * step, step), comp * LANES : (comp + 1) * LANES]

    for comp in range(3):
        wide = pl.ds(comp * width, LANES)
        for iy in range(6):
            line = []
            for ix in range(6):
                point = 6 * iy + ix
                value = field(point, comp)
                line.append(value * field(point, 0))
                prod[pl.ds(point * step, step), pl.ds(comp * width + LANES, LANES)] = (
                    value * field(point, 2)
                )
            out = line_product(line, DERIV, -1.0)
            for ix in range(6):
                prod[pl.ds((6 * iy + ix) * step, step), wide] = out[ix]
        for ix in range(6):
            line = [field(6 * iy + ix, comp) * field(6 * iy + ix, 1) for iy in range(6)]
            out = line_product(line, DERIV, -1.0)
            for iy in range(6):
                at = pl.ds((6 * iy + ix) * step, step)
                prod[at, wide] = prod[at, wide] + out[iy]
        spec[comp] = dot3(prod[:, comp * width : (comp + 1) * width], back_high[...], back_low[...])

    lane_block = lax.div(lax.broadcasted_iota(jnp.int32, (step, LANES), 1), jnp.int32(modes))
    masks = []
    shifts = []
    for place in range(count):
        index = block_of(place, four)
        masks.append([lane_block == lax.rem(index + comp, count) for comp in range(2)])
        shifts.append(lax.rem(LANES - index * modes, LANES))
    kept = []
    for point in range(POINTS):
        at = pl.ds(point * step, step)
        mass = float(WEIGHTS[point // 6] * WEIGHTS[point % 6])
        turned = [spec[0, at, :]]
        turned += [pltpu.roll(spec[comp, at, :], comp * modes, 1) for comp in (1, 2)]
        for place in range(count):
            mask = masks[place]
            mixed = jnp.where(mask[0], turned[0], jnp.where(mask[1], turned[1], turned[2]))
            nonlinear = pltpu.roll(mixed, shifts[place], 1)
            full[place, at, :] = mass * (REACTION * full[place, at, :] + nonlinear)
    for place in range(count):
        values = [full[place, pl.ds(point * step, step), :] for point in range(POINTS)]
        for at, value in enumerate(pack_lanes(values, modes)):
            send_refs[place][pl.ds(at * step, step), :] = value


def first_kernel(modes, step, count, chunks, dynamic, ids_ref, partner_ref, *refs):
    recv_refs = refs[: count * chunks]
    base_ref, lines_ref, work = refs[count * chunks :]
    four = ids_ref[1] if dynamic else 0
    rates = helmholtz_rates(ids_ref[1], modes)
    flags = glued_flags(partner_ref)
    for chunk in range(chunks):
        for place in range(count):
            ref = recv_refs[chunk * count + place]
            ready = ref.shape[0] // step
            first = (block_of(place, four) * chunks + chunk) * step
            values = unpack_lanes([ref[pl.ds(at * step, step), :] for at in range(ready)], modes)
            for point in range(POINTS):
                at = point * 64 + first
                at = at if isinstance(at, int) else pl.multiple_of(at, step)
                base_ref[pl.ds(at, step), :] = values[point]
    masks = col_masks(flags)
    for ey in range(BLOCKS):
        for iy in range(6):
            first, last = join_cols(get(base_ref, 6 * iy, ey), get(base_ref, 6 * iy + 5, ey), masks)
            put(base_ref, 6 * iy, ey, first)
            put(base_ref, 6 * iy + 5, ey, last)
    join_rows(base_ref, flags)
    apply_local(base_ref, work, rates, flags)
    write_lines(base_ref, lines_ref, 0, modes)
    write_lines(work, lines_ref, line_rows(modes), modes)


def sum_rows(sums):
    return [jnp.sum(value, axis=0, keepdims=True) for value in sums]


def second_kernel(modes, slots, ids_ref, partner_ref, side_ref, flip_ref, *refs):
    gath_refs = refs[:slots]
    lines_ref, _, k0_ref, k1_ref, k2_ref, next_ref, sums_ref, work, sides = refs[slots:]
    rates = helmholtz_rates(ids_ref[1], modes)
    flags = glued_flags(partner_ref)
    collect_sides(gath_refs, ids_ref[0], partner_ref, side_ref, sides, modes)
    back = own_reaction(load_lines(lines_ref, modes), rates, flags, 1.0)
    add_lines(k0_ref, incoming_lines(sides, 0, partner_ref, flip_ref))
    apply_local(k0_ref, work, rates, flags)
    add_lines(work, incoming_lines(sides, 1, partner_ref, flip_ref))
    add_lines(work, back)
    sums = apply_local(
        k1_ref, work, rates, flags,
        terms=[(1.0 / SPREAD, work), (-CENTRE / SPREAD, k0_ref)],
        products=[(1, 1), (1, -1), (-1, -1)],
    )
    write_lines(work, next_ref, 0, modes)
    apply_local(
        k2_ref, work, rates, flags,
        terms=[(TWICE, work), (-CENTRE * TWICE, k1_ref), (-1.0, k0_ref)],
    )
    write_lines(work, next_ref, line_rows(modes), modes)
    sums_ref[...] = jnp.concatenate(sum_rows(sums) + [jnp.zeros((5, LANES), F32)], axis=0)


def third_kernel(modes, slots, ids_ref, partner_ref, side_ref, flip_ref, *refs):
    gath_refs = refs[:slots]
    lines_ref, k1_ref, sums_ref, _ = refs[slots : slots + 4]
    k2_ref, k3_ref, a3_ref, next_ref, work, sides = refs[slots + 4 :]
    rates = helmholtz_rates(ids_ref[1], modes)
    flags = glued_flags(partner_ref)
    collect_sides(gath_refs, ids_ref[0], partner_ref, side_ref, sides, modes)
    back = own_reaction(load_lines(lines_ref, modes), rates, flags, TWICE)
    incoming = incoming_lines(sides, 0, partner_ref, flip_ref)
    add_lines(k2_ref, [[value * TWICE for value in line] for line in incoming])
    apply_local(k2_ref, work, rates, flags)
    add_lines(work, incoming_lines(sides, 1, partner_ref, flip_ref))
    add_lines(work, back)
    sums = apply_local(
        k3_ref, a3_ref, rates, flags,
        terms=[(TWICE, work), (-CENTRE * TWICE, k2_ref), (-1.0, k1_ref)],
        products=[(2, 1), (1, 1), (1, -1), (-1, -1)],
        energy=True,
    )
    write_lines(a3_ref, next_ref, 0, modes)
    next_ref[pl.ds(line_rows(modes), SUM_ROWS), :] = jnp.concatenate(
        [sums_ref[:3, :]] + sum_rows(sums), axis=0
    )


def turn_kernel(which, starts, fields, has_scatter, *refs):
    field_refs = refs[:fields]
    order_ref = refs[fields]
    out_refs = refs[fields + 1 : 2 * fields + 1]
    rows = refs[-1]
    step = rows.shape[0] // POINTS
    used = out_refs[0].shape[0]
    width = order_ref.shape[2]
    for field_ref, out_ref in zip(field_refs, out_refs):
        out_ref[...] = jnp.zeros(out_ref.shape, F32)
        for unit in range(len(starts)):
            for point in range(POINTS):
                rows[pl.ds(point * step, step), :] = field_ref[pl.ds(point * 64 + unit * step, step), :]
            high, low = halves(jnp.transpose(rows[...])[:used])
            both = jnp.concatenate([high, low], axis=0)
            out = dot(both, order_ref[which[unit]], ((1,), (0,)))
            window = pl.ds(starts[unit], width)
            out_ref[:, window] = out_ref[:, window] + (out[:used] + out[used:])
    if has_scatter:
        scatter_ref = refs[2 * fields + 1]
        place = lax.broadcasted_iota(jnp.int32, (SIDE, NODES), 0)
        at = 6 * jnp.bitwise_and(place, 7) + lax.shift_right_logical(place, 3)
        node = lax.broadcasted_iota(jnp.int32, (SIDE, NODES), 1)
        targets = (at, at * SIDE + SIDE - 1, at + (SIDE - 1) * SIDE, at * SIDE)
        for side, target in enumerate(targets):
            scatter_ref[side * SIDE : (side + 1) * SIDE, :] = jnp.where(
                node == target, 1.0, 0.0
            ).astype(BF16)


def conjugate_coefficients(gram, energy):
    zero = jnp.zeros_like(energy)

    def image(vec):
        out = [zero] * 5
        for j in range(4):
            if vec[j] is None:
                continue
            out[j] = out[j] + CENTRE * vec[j]
            out[j + 1] = out[j + 1] + (SPREAD if j == 0 else 0.5 * SPREAD) * vec[j]
            if j > 0:
                out[j - 1] = out[j - 1] + 0.5 * SPREAD * vec[j]
        return out

    def inner(left, right):
        total = zero
        for i in range(4):
            for j in range(4):
                if left[i] is not None and right[j] is not None:
                    total = total + left[i] * right[j] * gram[i][j]
        return total

    moments = [[None] * 4 for _ in range(4)]
    for j in range(3):
        column = image([jnp.ones_like(energy) if i == j else None for i in range(4)])
        for i in range(4):
            total = zero
            for m in range(max(j - 1, 0), j + 2):
                total = total + column[m] * gram[i][m]
            moments[i][j] = total
    for i in range(3):
        moments[i][3] = moments[3][i]
    moments[3][3] = energy

    def pad(vec, size):
        return [vec[i] if i < size else None for i in range(4)]

    residual = [jnp.ones_like(energy), zero, zero, zero, zero]
    direction = list(residual)
    solution = [zero] * 4
    norm_now = gram[0][0]
    for step in range(ITERS):
        trimmed = pad(direction, step + 1)
        bend = zero
        for i in range(step + 1):
            for j in range(step + 1):
                bend = bend + direction[i] * direction[j] * moments[i][j]
        alpha = norm_now / bend
        moved = image(trimmed)
        for i in range(step + 1):
            solution[i] = solution[i] + alpha * direction[i]
        for i in range(step + 2):
            residual[i] = residual[i] - alpha * moved[i]
        if step < ITERS - 1:
            kept = pad(residual, step + 2)
            norm_next = inner(kept, kept)
            ratio = norm_next / norm_now
            direction = [residual[i] + ratio * direction[i] for i in range(5)]
            norm_now = norm_next
    return solution, residual


def last_kernel(slots, ids_ref, partner_ref, side_ref, flip_ref, *refs):
    gath_refs = refs[:slots]
    turned = refs[slots : slots + 5]
    scatter_ref, sol_ref, res_ref, lines, sides = refs[slots + 5 :]
    modes = sol_ref.shape[1]
    used = 3 * modes
    where = pl.ds(line_rows(modes), SUM_ROWS)
    if slots == 1:
        parts = [gath_refs[0][part, where, :] for part in range(gath_refs[0].shape[0])]
    else:
        parts = [ref[where, :] for ref in gath_refs]
    sums = functools.reduce(lambda left, right: left + right, parts)
    collect_sides(gath_refs, ids_ref[0], partner_ref, side_ref, sides, modes)
    g00, g01, g11, g12, g22, g23, g33, energy = [
        jnp.broadcast_to(sums[place : place + 1, :], (8, LANES)) for place in range(8)
    ]
    g02 = 2.0 * g11 - g00
    g03 = 2.0 * g12 - g01
    g13 = (g22 - g00) + g11
    gram = [
        [g00, g01, g02, g03],
        [g01, g11, g12, g13],
        [g02, g12, g22, g23],
        [g03, g13, g23, g33],
    ]
    solution, residual = conjugate_coefficients(gram, energy)
    on_a3 = residual[4] * TWICE
    on_k3 = residual[3] - on_a3 * CENTRE
    on_k2 = residual[2] - residual[4]
    factors = list(solution) + [residual[0], residual[1], on_k2, on_k3, on_a3]
    columns = jnp.transpose(
        jnp.concatenate([value[:1] for value in factors] + [jnp.zeros((LANES - 9, LANES), F32)], axis=0)
    )
    incoming = incoming_lines(sides, 0, partner_ref, flip_ref)
    for side in range(4):
        for i in range(6):
            lines[pl.ds(side * SIDE + i * 8, 8), :] = incoming[side][i] * on_a3
    high, low = halves(jnp.transpose(lines[...])[:used])
    added = dot(jnp.concatenate([high, low], axis=0), scatter_ref[...], ((1,), (0,)))
    for comp in range(3):
        for first in range(0, modes, 8):
            at = comp * modes + first
            rows = [ref[at : at + 8, :] for ref in turned]
            scale = [columns[at : at + 8, place : place + 1] for place in range(9)]
            sol_ref[comp, first : first + 8, :] = (scale[0] * rows[0] + scale[1] * rows[1]) + (
                scale[2] * rows[2] + scale[3] * rows[3]
            )
            res_ref[comp, first : first + 8, :] = (
                (scale[4] * rows[0] + scale[5] * rows[1])
                + (scale[6] * rows[2] + scale[7] * rows[3])
                + (scale[8] * rows[4] + (added[at : at + 8] + added[used + at : used + at + 8]))
            )


def call(kernel, name, out_shapes, args, scratch, scalars=0, keep=True, aliases=None):
    smem = pl.BlockSpec(memory_space=pltpu.SMEM)
    vmem = pl.BlockSpec(memory_space=pltpu.VMEM)
    shapes = [shape if isinstance(shape, jax.ShapeDtypeStruct) else jax.ShapeDtypeStruct(shape, F32) for shape in out_shapes]
    return pl.pallas_call(
        kernel,
        name=name,
        out_shape=[pltpu.VMEM(one.shape, one.dtype) if keep else one for one in shapes],
        in_specs=[smem] * scalars + [vmem] * (len(args) - scalars),
        out_specs=[vmem] * len(out_shapes),
        scratch_shapes=[pltpu.VMEM(shape, F32) for shape in scratch],
        input_output_aliases=aliases or {},
        compiler_params=pltpu.CompilerParams(vmem_limit_bytes=VMEM_LIMIT),
    )(*args[:scalars], *[held(arg) for arg in args[scalars:]])


def held(arg):
    return arg if isinstance(arg, np.ndarray) else pltpu.with_memory_space_constraint(arg, pltpu.VMEM)


def swap_blocks(blocks, dynamic):
    if not dynamic:
        stacked = lax.all_to_all(jnp.stack(blocks), "four", split_axis=0, concat_axis=0, tiled=True)
        return [stacked[place] for place in range(len(blocks))]
    size = len(blocks)
    return [blocks[0]] + [
        lax.ppermute(blocks[place], "four", [(i, i ^ place) for i in range(size)])
        for place in range(1, size)
    ]


def share_lines(lines, beside=()):
    parts = lax.axis_size("dom")
    if parts != 8:
        return [lax.all_gather(lines, "dom", axis=0, tiled=False)], list(beside)
    slots = [lines] + [None] * (parts - 1)
    for slot in range(2, parts, 2):
        slots[slot] = lax.ppermute(lines, "dom", [(i, i ^ slot) for i in range(parts)])
        if beside and slot == 2:
            slots[slot], *beside = lax.optimization_barrier((slots[slot], *beside))
    for slot in range(0, parts, 2):
        slots[slot + 1] = lax.ppermute(slots[slot], "dom", [(i, i ^ 1) for i in range(parts)])
    return slots, list(beside)


def shards(velocity, partner, partner_side, flipped):
    modes = velocity.shape[1]
    count = lax.axis_size("four")
    step, chunks = chunk_sizes(count)
    rows = POINTS * step
    sent_rows = 3 * rows // 4 if is_packed(modes) else rows
    dynamic = step == BLOCKS
    (inv_high, inv_low), (back_high, back_low) = transform_tables(count)
    order, which, starts = order_tables(count)
    ids = jnp.stack([lax.axis_index("dom"), lax.axis_index("four")]).astype(jnp.int32)
    field = (NODES, LANES)
    blocks = [(sent_rows, LANES)] * count
    lined = line_rows(modes)

    spread = []
    for chunk in range(chunks):
        sent = call(
            functools.partial(
                pack_kernel, step, count, dynamic, which[chunk::chunks], starts[chunk::chunks]
            ),
            "pack",
            blocks,
            (ids, velocity, order),
            [],
            scalars=1,
        )
        spread.append(swap_blocks(sent, dynamic))
    local = []
    for chunk in range(chunks):
        sent = call(
            functools.partial(product_kernel, modes, step, count, dynamic),
            "products",
            blocks,
            (ids, *spread[chunk], inv_high, inv_low, back_high, back_low),
            [(count, rows, LANES), (rows, 3 * LANES), (rows, 6 * LANES), (3, rows, LANES)],
            scalars=1,
        )
        local += swap_blocks(sent, dynamic)

    base, lines = call(
        functools.partial(first_kernel, modes, step, count, chunks, dynamic),
        "first",
        [field, (2 * lined, LANES)],
        (ids, partner, *local),
        [field],
        scalars=2,
    )
    tables = (ids, partner, partner_side, flipped)
    gathered, _ = share_lines(lines)
    slots = len(gathered)
    k0, k1, base, lines, sums = call(
        functools.partial(second_kernel, modes, slots),
        "second",
        [field, field, field, (2 * lined, LANES), (8, LANES)],
        (*tables, *gathered, lines, base),
        [field, (4, 2 * SIDE, LANES)],
        scalars=4,
        aliases={4 + slots + 1: 0},
    )
    flat = (3 * modes, NODES)
    turned = call(
        functools.partial(turn_kernel, which, starts, 2, True),
        "turn",
        [flat, flat, jax.ShapeDtypeStruct((4 * SIDE, NODES), BF16)],
        (k0, k1, order),
        [(rows, LANES)],
    )
    gathered, (t0, t1, scatter) = share_lines(lines, turned)
    k2, k3, a3, lines = call(
        functools.partial(third_kernel, modes, slots),
        "third",
        [field, field, field, (lined + SUM_ROWS, LANES)],
        (*tables, *gathered, lines, k1, sums, base),
        [field, (4, 2 * SIDE, LANES)],
        scalars=4,
        aliases={4 + slots + 3: 0},
    )
    turned = call(
        functools.partial(turn_kernel, which, starts, 3, False),
        "turn",
        [flat, flat, flat],
        (k2, k3, a3, order),
        [(rows, LANES)],
    )
    gathered, (t2, t3, ta) = share_lines(lines, turned)
    outs = call(
        functools.partial(last_kernel, slots),
        "last",
        [velocity.shape, velocity.shape],
        (*tables, *gathered, t0, t1, t2, t3, ta, scatter),
        [(4 * SIDE, LANES), (4, SIDE, LANES)],
        scalars=4,
        keep=False,
    )
    return tuple(outs)


def solution(mesh):
    return jax.shard_map(
        shards,
        mesh=mesh,
        in_specs=(P(None, "four", "dom"), P("dom", None), P("dom", None), P("dom", None)),
        out_specs=(P(None, "four", "dom"), P(None, "four", "dom")),
        check_vma=False,
    )
```

```python
import functools
import math

import jax
import jax.numpy as jnp
import numpy as np
from jax import lax
from jax.experimental import pallas as pl
from jax.experimental.pallas import tpu as pltpu
from jax.sharding import PartitionSpec as P

ITERS = 4
REACTION = 2.0
WAVE_STEP = 0.0625
LANES = 128
POINTS = 36
BLOCKS = 8
SIDE = 48
NODES = 2304
CENTRE = 9.0
SPREAD = 9.0
TWICE = 2.0 / SPREAD
SUM_ROWS = 8
VMEM_LIMIT = 32 * 1024 * 1024
F32 = jnp.float32
BF16 = jnp.bfloat16


def gll_tables():
    inner_near = math.sqrt(1.0 / 3.0 - 2.0 * math.sqrt(7.0) / 21.0)
    inner_far = math.sqrt(1.0 / 3.0 + 2.0 * math.sqrt(7.0) / 21.0)
    points = np.array([-1.0, -inner_far, -inner_near, inner_near, inner_far, 1.0])
    values = (63.0 * points**5 - 70.0 * points**3 + 15.0 * points) / 8.0
    weights = 2.0 / (30.0 * values * values)
    spacing = points[:, None] - points[None, :]
    same_point = spacing == 0.0
    derivative = np.where(
        same_point, 0.0, values[:, None] / (values[None, :] * np.where(same_point, 1.0, spacing))
    )
    end_fix = np.array([-7.5, 0.0, 0.0, 0.0, 0.0, 7.5])
    derivative = derivative + np.eye(6) * end_fix[None, :]
    stiffness = derivative.T @ (weights[:, None] * derivative)
    return (weights, derivative, stiffness)


WEIGHTS, DERIV, STIFF = gll_tables()
STIFF_HAT = STIFF / WEIGHTS[:, None]


def fourier_tables(planes):
    plane_ids = np.arange(planes)
    mode_ids = np.arange(planes)
    waves = np.where(mode_ids < 2, 0, mode_ids // 2)
    angle = (plane_ids[:, None] * waves[None, :] % planes) * (2.0 * math.pi / planes)
    is_sine = (mode_ids % 2 == 1) & (mode_ids >= 2)
    basis = np.where(is_sine[None, :], np.sin(angle), np.cos(angle))
    alternating = np.where(plane_ids % 2 == 0, 1.0, -1.0)
    basis = np.where(mode_ids[None, :] == 1, alternating[:, None], basis)
    row_scale = np.where(mode_ids < 2, 1.0, 2.0) / planes
    forward = basis.T * row_scale[:, None]
    rates = (np.arange(planes // 2) * WAVE_STEP)[:, None]
    forward_z = np.zeros_like(forward)
    forward_z[0::2] = rates * forward[1::2]
    forward_z[1::2] = -rates * forward[0::2]
    forward_z[0:2] = 0.0
    return (basis, forward, forward_z)


def split_table(table):
    high = np.asarray(table, np.float32).astype(jnp.bfloat16)
    low = (np.asarray(table, np.float64) - high.astype(np.float64)).astype(np.float32)
    return high, low.astype(jnp.bfloat16)


def transform_tables(count):
    planes = LANES
    modes = planes // count
    basis, forward, forward_z = fourier_tables(planes)
    inverse = np.zeros((count * LANES, 3 * planes))
    for block in range(count):
        ids = slice(block * modes, (block + 1) * modes)
        for comp in range(3):
            at = block * LANES + comp * modes
            inverse[at : at + modes, comp * planes : (comp + 1) * planes] = basis[:, ids].T
    back = -np.concatenate([forward.T, forward_z.T], axis=0)
    return split_table(inverse), split_table(back)


def chunk_sizes(count):
    group = BLOCKS * BLOCKS // count
    step = min(group, BLOCKS)
    return step, group // step


def unit_windows(count):
    step, _ = chunk_sizes(count)
    starts = []
    offsets = []
    for index in range(BLOCKS * BLOCKS // step):
        element = index * step
        first = element // BLOCKS * 6 * SIDE
        starts.append(first // LANES * LANES)
        offsets.append(first % LANES + 6 * (element % BLOCKS))
    return starts, offsets


def order_table(step, offset, scratch):
    width = scratch.shape[1]
    lane = lax.broadcasted_iota(jnp.int32, (step, width), 1)
    gap = lane - 6 * lax.broadcasted_iota(jnp.int32, (step, width), 0) - offset
    for point in range(POINTS):
        hit = gap == point // 6 * SIDE + point % 6
        scratch[pl.ds(point * step, step), :] = jnp.where(hit, 1.0, 0.0)
    return scratch[...].astype(BF16)


def halves(value):
    high = value.astype(BF16)
    low = (value - high.astype(F32)).astype(BF16)
    return high, low


def dot(left, right, dims):
    return lax.dot_general(left, right, (dims, ((), ())), preferred_element_type=F32)


def dot3(left, right_high, right_low):
    high, low = halves(left)
    dims = ((1,), (0,))
    return dot(high, right_high, dims) + (dot(low, right_high, dims) + dot(high, right_low, dims))


def start_of(point, ey):
    return pl.multiple_of(point * 64 + ey * 8, 8)


def get(ref, point, ey):
    return ref[pl.ds(start_of(point, ey), 8), :]


def put(ref, point, ey, value):
    ref[pl.ds(start_of(point, ey), 8), :] = value


def ex_ids():
    return lax.broadcasted_iota(jnp.int32, (8, LANES), 0)


def helmholtz_rates(four, modes):
    lane = lax.broadcasted_iota(jnp.int32, (8, LANES), 1)
    mode = four * modes + lax.rem(lane, jnp.int32(modes))
    wave = jnp.where(mode == 0, 0, jnp.where(mode == 1, LANES // 2, lax.div(mode, jnp.int32(2))))
    scaled = wave.astype(F32) * WAVE_STEP
    return REACTION + scaled * scaled


def glued_flags(partner_ref):
    return [jnp.where(partner_ref[0, side] >= 0, 1.0, 0.0).astype(F32) for side in range(4)]


def col_masks(flags):
    ex = ex_ids()
    return jnp.where(ex == 0, flags[3], 1.0), jnp.where(ex == 7, flags[1], 1.0)


def join_cols(first, last, masks):
    ex = ex_ids()
    from_right = jnp.where(ex < 7, pltpu.roll(first, 7, 0), 0.0)
    from_left = jnp.where(ex > 0, pltpu.roll(last, 1, 0), 0.0)
    return (first + from_left) * masks[0], (last + from_right) * masks[1]


def join_rows(ref, flags):
    ex = ex_ids()
    not_first = jnp.where(ex == 0, 0.0, 1.0)
    not_last = jnp.where(ex == 7, 0.0, 1.0)
    for ix in range(6):
        for ey in range(7):
            total = get(ref, 30 + ix, ey) + get(ref, ix, ey + 1)
            put(ref, 30 + ix, ey, total)
            put(ref, ix, ey + 1, total)
        low = get(ref, ix, 0) * flags[0]
        high = get(ref, 30 + ix, 7) * flags[2]
        if ix == 0:
            low, high = low * not_first, high * not_first
        if ix == 5:
            low, high = low * not_last, high * not_last
        put(ref, ix, 0, low)
        put(ref, 30 + ix, 7, high)


def line_product(line, table, mirrored=1.0):
    sums = [line[j] + line[5 - j] for j in range(3)]
    gaps = [line[j] - line[5 - j] for j in range(3)]
    out = [None] * 6
    for i in range(3):
        even = None
        odd = None
        for j in range(3):
            even_term = sums[j] * float(0.5 * (table[i, j] + table[i, 5 - j]))
            odd_term = gaps[j] * float(0.5 * (table[i, j] - table[i, 5 - j]))
            even = even_term if even is None else even + even_term
            odd = odd_term if odd is None else odd + odd_term
        out[i] = even + odd
        out[5 - i] = even - odd if mirrored > 0 else odd - even
    return out


def apply_local(src, dst, rates, flags, terms=(), products=(), energy=False):
    masks = col_masks(flags)

    def body(ey, sums):
        sums = list(sums)
        for ix in range(6):
            line = []
            for iy in range(6):
                point = 6 * iy + ix
                if not terms:
                    line.append(get(src, point, ey))
                    continue
                values = [get(ref, point, ey) for _, ref in terms]
                value = None
                for (factor, _), part in zip(terms, values):
                    part = -part if factor == -1.0 else part * factor
                    value = part if value is None else value + part
                put(src, point, ey, value)
                line.append(value)
                values.append(value)
                ends = (iy in (0, 5)) + (ix in (0, 5))
                for place, (left, right) in enumerate(products):
                    both = values[left] * values[right]
                    sums[place] = sums[place] + (both * (0.5**ends) if ends else both)
            out = line_product(line, STIFF_HAT)
            for iy in range(6):
                put(dst, 6 * iy + ix, ey, out[iy] + rates * line[iy])
        for iy in range(6):
            line = [get(src, 6 * iy + ix, ey) for ix in range(6)]
            out = line_product(line, STIFF_HAT)
            full = [
                (get(dst, 6 * iy + ix, ey) + out[ix]) * float(WEIGHTS[iy] * WEIGHTS[ix])
                for ix in range(6)
            ]
            if energy:
                for ix in range(6):
                    sums[-1] = sums[-1] + full[ix] * line[ix]
            full[0], full[5] = join_cols(full[0], full[5], masks)
            for ix in range(6):
                put(dst, 6 * iy + ix, ey, full[ix])
        return tuple(sums)

    zero = jnp.zeros((8, LANES), F32)
    sums = lax.fori_loop(0, BLOCKS, body, (zero,) * (len(products) + int(energy)))
    join_rows(dst, flags)
    return sums


def side_slice(side, i):
    if side == 0:
        return pl.ds(i * 64, 8)
    if side == 2:
        return pl.ds((30 + i) * 64 + 56, 8)
    if side == 1:
        return pl.ds((6 * i + 5) * 64 + 7, 8, stride=8)
    return pl.ds(6 * i * 64, 8, stride=8)


def read_line(ref, side):
    return [ref[side_slice(side, i), :] for i in range(6)]


def lane_ids():
    return lax.broadcasted_iota(jnp.int32, (8, LANES), 1)


def is_packed(modes):
    return 3 * modes + modes == LANES


def pack_lanes(values, modes):
    if not is_packed(modes):
        return values
    third = len(values) // 4
    inside = lane_ids() < 3 * modes
    return [
        jnp.where(
            inside,
            values[comp * third + at],
            pltpu.roll(values[3 * third + at], (3 - comp) * modes, 1),
        )
        for comp in range(3)
        for at in range(third)
    ]


def unpack_last(pieces, modes):
    block = lax.div(lane_ids(), jnp.int32(modes))
    turned = [pltpu.roll(pieces[comp], (comp + 1) * modes, 1) for comp in range(3)]
    return jnp.where(block == 0, turned[0], jnp.where(block == 1, turned[1], turned[2]))


def unpack_lanes(values, modes):
    if not is_packed(modes):
        return values
    third = len(values) // 3
    return values + [
        unpack_last([values[comp * third + at] for comp in range(3)], modes) for at in range(third)
    ]


def line_rows(modes):
    return 3 * SIDE if is_packed(modes) else 4 * SIDE


def write_lines(ref, lines_ref, base, modes):
    values = []
    for side in range(4):
        values += read_line(ref, side)
    for at, value in enumerate(pack_lanes(values, modes)):
        lines_ref[pl.ds(base + at * 8, 8), :] = value


def load_lines(lines_ref, modes):
    count = line_rows(modes) // 8
    values = unpack_lanes([lines_ref[pl.ds(at * 8, 8), :] for at in range(count)], modes)
    return [values[side * 6 : side * 6 + 6] for side in range(4)]


def add_lines(ref, lines):
    for side in range(4):
        for i in range(6):
            where = side_slice(side, i)
            ref[where, :] = ref[where, :] + lines[side][i]


def reverse_rows(value):
    ex = ex_ids()
    value = pltpu.roll(value, 4, 0)
    value = jnp.where((ex & 2) == 0, pltpu.roll(value, 6, 0), pltpu.roll(value, 2, 0))
    return jnp.where((ex & 1) == 0, pltpu.roll(value, 7, 0), pltpu.roll(value, 1, 0))


def collect_sides(gath_refs, own, partner_ref, side_ref, sides, modes):
    sets = sides.shape[1] // SIDE
    step = line_rows(modes)

    def copy_side(side, load):
        there = jnp.maximum(side_ref[0, side], 0)

        def plain():
            for place in range(sets):
                for i in range(6):
                    at = pl.multiple_of(place * step + there * SIDE + i * 8, 8)
                    sides[side, pl.ds(place * SIDE + i * 8, 8), :] = load(at)

        if not is_packed(modes):
            plain()
            return
        pl.when(there < 3)(plain)

        @pl.when(there == 3)
        def _():
            for place in range(sets):
                for i in range(6):
                    pieces = [load(place * step + comp * SIDE + i * 8) for comp in range(3)]
                    sides[side, pl.ds(place * SIDE + i * 8, 8), :] = unpack_last(pieces, modes)

    def body(side, carry):
        part = partner_ref[0, side]
        if len(gath_refs) == 1:
            source = jnp.maximum(part, 0)
            copy_side(side, lambda at: gath_refs[0][source, pl.ds(at, 8), :])
            return carry
        for slot, ref in enumerate(gath_refs):
            here = jnp.logical_and(part >= 0, jnp.bitwise_xor(part, own) == slot)

            @pl.when(here)
            def _(ref=ref):
                copy_side(side, lambda at: ref[pl.ds(at, 8), :])

        return carry

    lax.fori_loop(0, 4, body, 0)


def incoming_lines(sides, place, partner_ref, flip_ref):
    lines = []
    for side in range(4):
        glued = partner_ref[0, side] >= 0
        turned = flip_ref[0, side] == 1
        line = []
        for i in range(6):
            at = pl.multiple_of(place * SIDE + jnp.where(turned, 5 - i, i) * 8, 8)
            value = sides[side, pl.ds(at, 8), :]
            value = jnp.where(turned, reverse_rows(value), value)
            line.append(jnp.where(glued, value, 0.0))
        lines.append(line)
    return lines


def own_reaction(own_lines, rates, flags, scale):
    ex = ex_ids()
    edge = float(WEIGHTS[0])
    corner = float(STIFF[0, 0])
    lines = []
    for side in range(4):
        line = own_lines[side]
        along = line_product(line, STIFF_HAT)
        out = [
            (along[i] * edge + line[i] * (corner + rates * edge)) * float(WEIGHTS[i])
            for i in range(6)
        ]
        first = out[0] + pltpu.roll(out[5], 1, 0)
        last = out[5] + pltpu.roll(out[0], 7, 0)
        out[0] = jnp.where(ex > 0, first, 0.0)
        out[5] = jnp.where(ex < 7, last, 0.0)
        lines.append([value * (flags[side] * scale) for value in out])
    return lines


def pick(index, values):
    if isinstance(index, int):
        return values[index]
    chosen = jnp.int32(values[0])
    for place in range(1, len(values)):
        chosen = jnp.where(index == place, jnp.int32(values[place]), chosen)
    return chosen


def offset_of(place, size):
    return (0, 3, 1, 2)[place] if size == 4 else place


def block_of(place, four, size):
    return place if isinstance(four, int) else jnp.bitwise_xor(four, offset_of(place, size))


def pack_kernel(step, count, dynamic, load, starts, offsets, ids_ref, velocity_ref, *refs):
    send_refs = refs[:count]
    scratch = refs[-2] if load else refs[-1]
    width = scratch.shape[1]
    modes = velocity_ref.shape[1]
    four = ids_ref[1] if dynamic else 0
    copies = []
    if load:
        copies = [
            pltpu.make_async_copy(velocity_ref.at[comp], refs[count].at[comp], refs[-1].at[comp])
            for comp in range(3)
        ]
        velocity_ref = refs[count]
    for copy in copies:
        copy.start()
    for place in range(count):
        index = block_of(place, four, count)
        table = order_table(step, pick(index, offsets), scratch)
        if place == 0:
            for copy in copies:
                copy.wait()
        start = pick(index, starts)
        start = start if isinstance(start, int) else pl.multiple_of(start, LANES)
        window = pl.ds(start, width)
        rows = [velocity_ref[comp, :, window] for comp in range(3)]
        pad = jnp.zeros((LANES - 3 * modes, width), F32)
        high, low = halves(jnp.concatenate(rows + [pad], axis=0))
        both = jnp.concatenate([high, low], axis=0)
        out = dot(table, both, ((1,), (1,)))
        out = out[:, :LANES] + out[:, LANES:]
        if not is_packed(modes):
            send_refs[place][...] = out
            continue
        values = [out[point * step : (point + 1) * step] for point in range(POINTS)]
        for at, value in enumerate(pack_lanes(values, modes)):
            send_refs[place][pl.ds(at * step, step), :] = value


def product_kernel(modes, step, count, dynamic, ids_ref, *refs):
    recv_refs = refs[:count]
    inv_high, inv_low, back_high, back_low = refs[count : count + 4]
    send_refs = refs[count + 4 : 2 * count + 4]
    full, lined, phys, prod, spec = refs[2 * count + 4 :]
    four = ids_ref[1] if dynamic else 0
    packed = is_packed(modes)
    for place in range(count):
        index = block_of(place, four, count)
        if packed:
            ready = 3 * POINTS // 4
            values = [recv_refs[place][pl.ds(at * step, step), :] for at in range(ready)]
            for at, value in enumerate(unpack_lanes(values, modes)):
                full[place, pl.ds(at * step, step), :] = value
        else:
            full[place] = recv_refs[place][...]
        first = index * LANES
        first = first if isinstance(first, int) else pl.multiple_of(first, LANES)
        lined[:, pl.ds(first, LANES)] = full[place]
    phys[...] = dot3(lined[...], inv_high[...], inv_low[...])
    width = 2 * LANES

    def field(point, comp):
        return phys[pl.ds(point * step, step), comp * LANES : (comp + 1) * LANES]

    for comp in range(3):
        wide = pl.ds(comp * width, LANES)
        for iy in range(6):
            line = []
            for ix in range(6):
                point = 6 * iy + ix
                value = field(point, comp)
                line.append(value * field(point, 0))
                prod[pl.ds(point * step, step), pl.ds(comp * width + LANES, LANES)] = (
                    value * field(point, 2)
                )
            out = line_product(line, DERIV, -1.0)
            for ix in range(6):
                prod[pl.ds((6 * iy + ix) * step, step), wide] = out[ix]
        for ix in range(6):
            line = [field(6 * iy + ix, comp) * field(6 * iy + ix, 1) for iy in range(6)]
            out = line_product(line, DERIV, -1.0)
            for iy in range(6):
                at = pl.ds((6 * iy + ix) * step, step)
                prod[at, wide] = prod[at, wide] + out[iy]
        spec[comp] = dot3(prod[:, comp * width : (comp + 1) * width], back_high[...], back_low[...])

    lane_block = lax.div(lax.broadcasted_iota(jnp.int32, (step, LANES), 1), jnp.int32(modes))
    masks = []
    shifts = []
    for place in range(count):
        index = block_of(place, four, count)
        masks.append([lane_block == lax.rem(index + comp, count) for comp in range(2)])
        shifts.append(lax.rem(LANES - index * modes, LANES))
    kept = []
    for point in range(POINTS):
        at = pl.ds(point * step, step)
        mass = float(WEIGHTS[point // 6] * WEIGHTS[point % 6])
        turned = [spec[0, at, :]]
        turned += [pltpu.roll(spec[comp, at, :], comp * modes, 1) for comp in (1, 2)]
        for place in range(count):
            mask = masks[place]
            mixed = jnp.where(mask[0], turned[0], jnp.where(mask[1], turned[1], turned[2]))
            nonlinear = pltpu.roll(mixed, shifts[place], 1)
            full[place, at, :] = mass * (REACTION * full[place, at, :] + nonlinear)
    for place in range(count):
        values = [full[place, pl.ds(point * step, step), :] for point in range(POINTS)]
        for at, value in enumerate(pack_lanes(values, modes)):
            send_refs[place][pl.ds(at * step, step), :] = value


def first_kernel(modes, step, count, chunks, dynamic, ids_ref, partner_ref, *refs):
    recv_refs = refs[: count * chunks]
    base_ref, lines_ref, work = refs[count * chunks :]
    four = ids_ref[1] if dynamic else 0
    rates = helmholtz_rates(ids_ref[1], modes)
    flags = glued_flags(partner_ref)
    for chunk in range(chunks):
        for place in range(count):
            ref = recv_refs[chunk * count + place]
            ready = ref.shape[0] // step
            first = (block_of(place, four, count) * chunks + chunk) * step
            values = unpack_lanes([ref[pl.ds(at * step, step), :] for at in range(ready)], modes)
            for point in range(POINTS):
                at = point * 64 + first
                at = at if isinstance(at, int) else pl.multiple_of(at, step)
                base_ref[pl.ds(at, step), :] = values[point]
    masks = col_masks(flags)
    for ey in range(BLOCKS):
        for iy in range(6):
            first, last = join_cols(get(base_ref, 6 * iy, ey), get(base_ref, 6 * iy + 5, ey), masks)
            put(base_ref, 6 * iy, ey, first)
            put(base_ref, 6 * iy + 5, ey, last)
    join_rows(base_ref, flags)
    apply_local(base_ref, work, rates, flags)
    write_lines(base_ref, lines_ref, 0, modes)
    write_lines(work, lines_ref, line_rows(modes), modes)


def sum_rows(sums):
    return [jnp.sum(value, axis=0, keepdims=True) for value in sums]


def second_kernel(modes, slots, ids_ref, partner_ref, side_ref, flip_ref, *refs):
    gath_refs = refs[:slots]
    lines_ref, _, k0_ref, k1_ref, k2_ref, next_ref, sums_ref, work, sides = refs[slots:]
    rates = helmholtz_rates(ids_ref[1], modes)
    flags = glued_flags(partner_ref)
    collect_sides(gath_refs, ids_ref[0], partner_ref, side_ref, sides, modes)
    back = own_reaction(load_lines(lines_ref, modes), rates, flags, 1.0)
    add_lines(k0_ref, incoming_lines(sides, 0, partner_ref, flip_ref))
    apply_local(k0_ref, work, rates, flags)
    add_lines(work, incoming_lines(sides, 1, partner_ref, flip_ref))
    add_lines(work, back)
    sums = apply_local(
        k1_ref, work, rates, flags,
        terms=[(1.0 / SPREAD, work), (-CENTRE / SPREAD, k0_ref)],
        products=[(1, 1), (1, -1), (-1, -1)],
    )
    write_lines(work, next_ref, 0, modes)
    apply_local(
        k2_ref, work, rates, flags,
        terms=[(TWICE, work), (-CENTRE * TWICE, k1_ref), (-1.0, k0_ref)],
    )
    write_lines(work, next_ref, line_rows(modes), modes)
    sums_ref[...] = jnp.concatenate(sum_rows(sums) + [jnp.zeros((5, LANES), F32)], axis=0)


def third_kernel(modes, slots, ids_ref, partner_ref, side_ref, flip_ref, *refs):
    gath_refs = refs[:slots]
    lines_ref, k1_ref, sums_ref, _ = refs[slots : slots + 4]
    k2_ref, k3_ref, a3_ref, next_ref, work, sides = refs[slots + 4 :]
    rates = helmholtz_rates(ids_ref[1], modes)
    flags = glued_flags(partner_ref)
    collect_sides(gath_refs, ids_ref[0], partner_ref, side_ref, sides, modes)
    back = own_reaction(load_lines(lines_ref, modes), rates, flags, TWICE)
    incoming = incoming_lines(sides, 0, partner_ref, flip_ref)
    add_lines(k2_ref, [[value * TWICE for value in line] for line in incoming])
    apply_local(k2_ref, work, rates, flags)
    add_lines(work, incoming_lines(sides, 1, partner_ref, flip_ref))
    add_lines(work, back)
    sums = apply_local(
        k3_ref, a3_ref, rates, flags,
        terms=[(TWICE, work), (-CENTRE * TWICE, k2_ref), (-1.0, k1_ref)],
        products=[(2, 1), (1, 1), (1, -1), (-1, -1)],
        energy=True,
    )
    write_lines(a3_ref, next_ref, 0, modes)
    next_ref[pl.ds(line_rows(modes), SUM_ROWS), :] = jnp.concatenate(
        [sums_ref[:3, :]] + sum_rows(sums), axis=0
    )


def turn_kernel(starts, offsets, fields, has_scatter, *refs):
    field_refs = refs[:fields]
    out_refs = refs[fields : 2 * fields]
    scratch, rows = refs[-2:]
    step = rows.shape[0] // POINTS
    used = out_refs[0].shape[0]
    width = scratch.shape[1]
    for out_ref in out_refs:
        out_ref[...] = jnp.zeros(out_ref.shape, F32)
    for unit in range(len(starts)):
        table = order_table(step, offsets[unit], scratch)
        for field_ref, out_ref in zip(field_refs, out_refs):
            for point in range(POINTS):
                rows[pl.ds(point * step, step), :] = field_ref[pl.ds(point * 64 + unit * step, step), :]
            high, low = halves(jnp.transpose(rows[...])[:used])
            both = jnp.concatenate([high, low], axis=0)
            out = dot(both, table, ((1,), (0,)))
            window = pl.ds(starts[unit], width)
            out_ref[:, window] = out_ref[:, window] + (out[:used] + out[used:])
    if has_scatter:
        scatter_ref = refs[2 * fields]
        place = lax.broadcasted_iota(jnp.int32, (SIDE, NODES), 0)
        at = 6 * jnp.bitwise_and(place, 7) + lax.shift_right_logical(place, 3)
        node = lax.broadcasted_iota(jnp.int32, (SIDE, NODES), 1)
        targets = (at, at * SIDE + SIDE - 1, at + (SIDE - 1) * SIDE, at * SIDE)
        for side, target in enumerate(targets):
            scatter_ref[side * SIDE : (side + 1) * SIDE, :] = jnp.where(
                node == target, 1.0, 0.0
            ).astype(BF16)


def conjugate_coefficients(gram, energy):
    zero = jnp.zeros_like(energy)

    def image(vec):
        out = [zero] * 5
        for j in range(4):
            if vec[j] is None:
                continue
            out[j] = out[j] + CENTRE * vec[j]
            out[j + 1] = out[j + 1] + (SPREAD if j == 0 else 0.5 * SPREAD) * vec[j]
            if j > 0:
                out[j - 1] = out[j - 1] + 0.5 * SPREAD * vec[j]
        return out

    def inner(left, right):
        total = zero
        for i in range(4):
            for j in range(4):
                if left[i] is not None and right[j] is not None:
                    total = total + left[i] * right[j] * gram[i][j]
        return total

    moments = [[None] * 4 for _ in range(4)]
    for j in range(3):
        column = image([jnp.ones_like(energy) if i == j else None for i in range(4)])
        for i in range(4):
            total = zero
            for m in range(max(j - 1, 0), j + 2):
                total = total + column[m] * gram[i][m]
            moments[i][j] = total
    for i in range(3):
        moments[i][3] = moments[3][i]
    moments[3][3] = energy

    def pad(vec, size):
        return [vec[i] if i < size else None for i in range(4)]

    residual = [jnp.ones_like(energy), zero, zero, zero, zero]
    direction = list(residual)
    solution = [zero] * 4
    norm_now = gram[0][0]
    for step in range(ITERS):
        trimmed = pad(direction, step + 1)
        bend = zero
        for i in range(step + 1):
            for j in range(step + 1):
                bend = bend + direction[i] * direction[j] * moments[i][j]
        alpha = norm_now / bend
        moved = image(trimmed)
        for i in range(step + 1):
            solution[i] = solution[i] + alpha * direction[i]
        for i in range(step + 2):
            residual[i] = residual[i] - alpha * moved[i]
        if step < ITERS - 1:
            kept = pad(residual, step + 2)
            norm_next = inner(kept, kept)
            ratio = norm_next / norm_now
            direction = [residual[i] + ratio * direction[i] for i in range(5)]
            norm_now = norm_next
    return solution, residual


def last_kernel(slots, ids_ref, partner_ref, side_ref, flip_ref, *refs):
    gath_refs = refs[:slots]
    turned = refs[slots : slots + 5]
    scatter_ref, sol_ref, res_ref, lines, sides = refs[slots + 5 :]
    modes = sol_ref.shape[1]
    used = 3 * modes
    where = pl.ds(line_rows(modes), SUM_ROWS)
    if slots == 1:
        parts = [gath_refs[0][part, where, :] for part in range(gath_refs[0].shape[0])]
    else:
        parts = [ref[where, :] for ref in gath_refs]
    sums = functools.reduce(lambda left, right: left + right, parts)
    collect_sides(gath_refs, ids_ref[0], partner_ref, side_ref, sides, modes)
    g00, g01, g11, g12, g22, g23, g33, energy = [
        jnp.broadcast_to(sums[place : place + 1, :], (8, LANES)) for place in range(8)
    ]
    g02 = 2.0 * g11 - g00
    g03 = 2.0 * g12 - g01
    g13 = (g22 - g00) + g11
    gram = [
        [g00, g01, g02, g03],
        [g01, g11, g12, g13],
        [g02, g12, g22, g23],
        [g03, g13, g23, g33],
    ]
    solution, residual = conjugate_coefficients(gram, energy)
    on_a3 = residual[4] * TWICE
    on_k3 = residual[3] - on_a3 * CENTRE
    on_k2 = residual[2] - residual[4]
    factors = list(solution) + [residual[0], residual[1], on_k2, on_k3, on_a3]
    columns = jnp.transpose(
        jnp.concatenate([value[:1] for value in factors] + [jnp.zeros((LANES - 9, LANES), F32)], axis=0)
    )
    incoming = incoming_lines(sides, 0, partner_ref, flip_ref)
    for side in range(4):
        for i in range(6):
            lines[pl.ds(side * SIDE + i * 8, 8), :] = incoming[side][i] * on_a3
    high, low = halves(jnp.transpose(lines[...])[:used])
    added = dot(jnp.concatenate([high, low], axis=0), scatter_ref[...], ((1,), (0,)))
    for comp in range(3):
        for first in range(0, modes, 8):
            at = comp * modes + first
            rows = [ref[at : at + 8, :] for ref in turned]
            scale = [columns[at : at + 8, place : place + 1] for place in range(9)]
            sol_ref[comp, first : first + 8, :] = (scale[0] * rows[0] + scale[1] * rows[1]) + (
                scale[2] * rows[2] + scale[3] * rows[3]
            )
            res_ref[comp, first : first + 8, :] = (
                (scale[4] * rows[0] + scale[5] * rows[1])
                + (scale[6] * rows[2] + scale[7] * rows[3])
                + (scale[8] * rows[4] + (added[at : at + 8] + added[used + at : used + at + 8]))
            )


def call(kernel, name, out_shapes, args, scratch, scalars=0, keep=True, aliases=None, outside=False):
    smem = pl.BlockSpec(memory_space=pltpu.SMEM)
    vmem = pl.BlockSpec(memory_space=pltpu.VMEM)
    shapes = [shape if isinstance(shape, jax.ShapeDtypeStruct) else jax.ShapeDtypeStruct(shape, F32) for shape in out_shapes]
    return pl.pallas_call(
        kernel,
        name=name,
        out_shape=[pltpu.VMEM(one.shape, one.dtype) if keep else one for one in shapes],
        in_specs=[smem] * scalars + [pl.BlockSpec(memory_space=pltpu.HBM) if outside else vmem] * (len(args) - scalars),
        out_specs=[vmem] * len(out_shapes),
        scratch_shapes=[pltpu.VMEM(one, F32) if isinstance(one, tuple) else one for one in scratch],
        input_output_aliases=aliases or {},
        compiler_params=pltpu.CompilerParams(vmem_limit_bytes=VMEM_LIMIT),
    )(*args[:scalars], *[held(arg, pltpu.HBM if outside else pltpu.VMEM) for arg in args[scalars:]])


def held(arg, space):
    return arg if isinstance(arg, np.ndarray) else pltpu.with_memory_space_constraint(arg, space)


def swap_blocks(blocks, dynamic):
    if not dynamic:
        stacked = lax.all_to_all(jnp.stack(blocks), "four", split_axis=0, concat_axis=0, tiled=True)
        return [stacked[place] for place in range(len(blocks))]
    size = len(blocks)
    swapped = list(blocks)
    for place in range(size - 1, 0, -1):
        swapped[place] = lax.ppermute(blocks[place], "four", [(i, i ^ offset_of(place, size)) for i in range(size)])
    return swapped


def share_lines(lines, beside=()):
    parts = lax.axis_size("dom")
    if parts != 8:
        return [lax.all_gather(lines, "dom", axis=0, tiled=False)], list(beside)
    slots = [lines] + [None] * (parts - 1)
    for slot in range(2, parts, 2):
        slots[slot] = lax.ppermute(lines, "dom", [(i, i ^ slot) for i in range(parts)])
        if beside and slot == parts - 2:
            slots[slot], *beside = lax.optimization_barrier((slots[slot], *beside))
    for slot in range(0, parts, 2):
        slots[slot + 1] = lax.ppermute(slots[slot], "dom", [(i, i ^ 1) for i in range(parts)])
    return slots, list(beside)


def shards(velocity, partner, partner_side, flipped):
    modes = velocity.shape[1]
    count = lax.axis_size("four")
    step, chunks = chunk_sizes(count)
    rows = POINTS * step
    sent_rows = 3 * rows // 4 if is_packed(modes) else rows
    dynamic = step == BLOCKS
    (inv_high, inv_low), (back_high, back_low) = transform_tables(count)
    starts, offsets = unit_windows(count)
    table = (rows, 3 * LANES)
    ids = jnp.stack([lax.axis_index("dom"), lax.axis_index("four")]).astype(jnp.int32)
    field = (NODES, LANES)
    blocks = [(sent_rows, LANES)] * count
    lined = line_rows(modes)

    spread = []
    held_velocity = velocity
    for chunk in range(chunks):
        load = chunk == 0
        sent = call(
            functools.partial(
                pack_kernel, step, count, dynamic, load, starts[chunk::chunks], offsets[chunk::chunks]
            ),
            "pack",
            blocks + [velocity.shape] * load,
            (ids, held_velocity),
            [table] + [pltpu.SemaphoreType.DMA((3,))] * load,
            scalars=1,
            outside=load,
        )
        if load:
            *sent, held_velocity = sent
        spread.append(swap_blocks(sent, dynamic))
    local = []
    for chunk in range(chunks):
        sent = call(
            functools.partial(product_kernel, modes, step, count, dynamic),
            "products",
            blocks,
            (ids, *spread[chunk], inv_high, inv_low, back_high, back_low),
            [(count, rows, LANES), (rows, count * LANES), (rows, 3 * LANES), (rows, 6 * LANES), (3, rows, LANES)],
            scalars=1,
        )
        local += swap_blocks(sent, dynamic)

    base, lines = call(
        functools.partial(first_kernel, modes, step, count, chunks, dynamic),
        "first",
        [field, (2 * lined, LANES)],
        (ids, partner, *local),
        [field],
        scalars=2,
    )
    tables = (ids, partner, partner_side, flipped)
    gathered, _ = share_lines(lines)
    slots = len(gathered)
    k0, k1, base, lines, sums = call(
        functools.partial(second_kernel, modes, slots),
        "second",
        [field, field, field, (2 * lined, LANES), (8, LANES)],
        (*tables, *gathered, lines, base),
        [field, (4, 2 * SIDE, LANES)],
        scalars=4,
        aliases={4 + slots + 1: 0},
    )
    flat = (3 * modes, NODES)
    turned = call(
        functools.partial(turn_kernel, starts, offsets, 2, True),
        "turn",
        [flat, flat, jax.ShapeDtypeStruct((4 * SIDE, NODES), BF16)],
        (k0, k1),
        [table, (rows, LANES)],
    )
    gathered, (t0, t1, scatter) = share_lines(lines, turned)
    k2, k3, a3, lines = call(
        functools.partial(third_kernel, modes, slots),
        "third",
        [field, field, field, (lined + SUM_ROWS, LANES)],
        (*tables, *gathered, lines, k1, sums, base),
        [field, (4, 2 * SIDE, LANES)],
        scalars=4,
        aliases={4 + slots + 3: 0},
    )
    turned = call(
        functools.partial(turn_kernel, starts, offsets, 3, False),
        "turn",
        [flat, flat, flat],
        (k2, k3, a3),
        [table, (rows, LANES)],
    )
    gathered, (t2, t3, ta) = share_lines(lines, turned)
    outs = call(
        functools.partial(last_kernel, slots),
        "last",
        [velocity.shape, velocity.shape],
        (*tables, *gathered, t0, t1, t2, t3, ta, scatter),
        [(4 * SIDE, LANES), (4, SIDE, LANES)],
        scalars=4,
        keep=False,
    )
    return tuple(outs)


def solution(mesh):
    return jax.shard_map(
        shards,
        mesh=mesh,
        in_specs=(P(None, "four", "dom"), P("dom", None), P("dom", None), P("dom", None)),
        out_specs=(P(None, "four", "dom"), P(None, "four", "dom")),
        check_vma=False,
    )
```

```python
import functools
import math

import jax
import jax.numpy as jnp
import numpy as np
from jax import lax
from jax.experimental import pallas as pl
from jax.experimental.pallas import tpu as pltpu
from jax.sharding import PartitionSpec as P

ITERS = 4
REACTION = 2.0
WAVE_STEP = 0.0625
LANES = 128
POINTS = 36
BLOCKS = 8
SIDE = 48
SENT = 40
NODES = 2304
CENTRE = 9.0
SPREAD = 9.0
TWICE = 2.0 / SPREAD
SUM_ROWS = 8
VMEM_LIMIT = 32 * 1024 * 1024
F32 = jnp.float32
BF16 = jnp.bfloat16


def gll_tables():
    inner_near = math.sqrt(1.0 / 3.0 - 2.0 * math.sqrt(7.0) / 21.0)
    inner_far = math.sqrt(1.0 / 3.0 + 2.0 * math.sqrt(7.0) / 21.0)
    points = np.array([-1.0, -inner_far, -inner_near, inner_near, inner_far, 1.0])
    values = (63.0 * points**5 - 70.0 * points**3 + 15.0 * points) / 8.0
    weights = 2.0 / (30.0 * values * values)
    spacing = points[:, None] - points[None, :]
    same_point = spacing == 0.0
    derivative = np.where(
        same_point, 0.0, values[:, None] / (values[None, :] * np.where(same_point, 1.0, spacing))
    )
    end_fix = np.array([-7.5, 0.0, 0.0, 0.0, 0.0, 7.5])
    derivative = derivative + np.eye(6) * end_fix[None, :]
    stiffness = derivative.T @ (weights[:, None] * derivative)
    return (weights, derivative, stiffness)


WEIGHTS, DERIV, STIFF = gll_tables()
STIFF_HAT = STIFF / WEIGHTS[:, None]


def fourier_tables(planes):
    plane_ids = np.arange(planes)
    mode_ids = np.arange(planes)
    waves = np.where(mode_ids < 2, 0, mode_ids // 2)
    angle = (plane_ids[:, None] * waves[None, :] % planes) * (2.0 * math.pi / planes)
    is_sine = (mode_ids % 2 == 1) & (mode_ids >= 2)
    basis = np.where(is_sine[None, :], np.sin(angle), np.cos(angle))
    alternating = np.where(plane_ids % 2 == 0, 1.0, -1.0)
    basis = np.where(mode_ids[None, :] == 1, alternating[:, None], basis)
    row_scale = np.where(mode_ids < 2, 1.0, 2.0) / planes
    forward = basis.T * row_scale[:, None]
    rates = (np.arange(planes // 2) * WAVE_STEP)[:, None]
    forward_z = np.zeros_like(forward)
    forward_z[0::2] = rates * forward[1::2]
    forward_z[1::2] = -rates * forward[0::2]
    forward_z[0:2] = 0.0
    return (basis, forward, forward_z)


def split_table(table):
    high = np.asarray(table, np.float32).astype(jnp.bfloat16)
    low = (np.asarray(table, np.float64) - high.astype(np.float64)).astype(np.float32)
    return high, low.astype(jnp.bfloat16)


def transform_tables(count):
    planes = LANES
    modes = planes // count
    basis, forward, forward_z = fourier_tables(planes)
    inverse = np.zeros((count * LANES, 3 * planes))
    for block in range(count):
        ids = slice(block * modes, (block + 1) * modes)
        for comp in range(3):
            at = block * LANES + comp * modes
            inverse[at : at + modes, comp * planes : (comp + 1) * planes] = basis[:, ids].T
    back = -np.concatenate([forward.T, forward_z.T], axis=0)
    return split_table(inverse), split_table(back)


def chunk_sizes(count):
    group = BLOCKS * BLOCKS // count
    step = min(group, BLOCKS)
    return step, group // step


def unit_windows(count):
    step, _ = chunk_sizes(count)
    starts = []
    offsets = []
    for index in range(BLOCKS * BLOCKS // step):
        element = index * step
        first = element // BLOCKS * 6 * SIDE
        starts.append(first // LANES * LANES)
        offsets.append(first % LANES + 6 * (element % BLOCKS))
    return starts, offsets


def order_table(step, offset, scratch):
    width = scratch.shape[1]
    lane = lax.broadcasted_iota(jnp.int32, (step, width), 1)
    gap = lane - 6 * lax.broadcasted_iota(jnp.int32, (step, width), 0) - offset
    for point in range(POINTS):
        hit = gap == point // 6 * SIDE + point % 6
        scratch[pl.ds(point * step, step), :] = jnp.where(hit, 1.0, 0.0)
    return scratch[...].astype(BF16)


def halves(value):
    high = value.astype(BF16)
    low = (value - high.astype(F32)).astype(BF16)
    return high, low


def dot(left, right, dims):
    return lax.dot_general(left, right, (dims, ((), ())), preferred_element_type=F32)


def dot3(left, right_high, right_low):
    high, low = halves(left)
    dims = ((1,), (0,))
    return dot(high, right_high, dims) + (dot(low, right_high, dims) + dot(high, right_low, dims))


def start_of(point, ey):
    return pl.multiple_of(point * 64 + ey * 8, 8)


def get(ref, point, ey):
    return ref[pl.ds(start_of(point, ey), 8), :]


def put(ref, point, ey, value):
    ref[pl.ds(start_of(point, ey), 8), :] = value


def ex_ids():
    return lax.broadcasted_iota(jnp.int32, (8, LANES), 0)


def helmholtz_rates(four, modes):
    lane = lax.broadcasted_iota(jnp.int32, (8, LANES), 1)
    mode = four * modes + lax.rem(lane, jnp.int32(modes))
    wave = jnp.where(mode == 0, 0, jnp.where(mode == 1, LANES // 2, lax.div(mode, jnp.int32(2))))
    scaled = wave.astype(F32) * WAVE_STEP
    return REACTION + scaled * scaled


def glued_flags(partner_ref):
    return [jnp.where(partner_ref[0, side] >= 0, 1.0, 0.0).astype(F32) for side in range(4)]


def col_masks(flags):
    ex = ex_ids()
    return jnp.where(ex == 0, flags[3], 1.0), jnp.where(ex == 7, flags[1], 1.0)


def join_cols(first, last, masks):
    ex = ex_ids()
    from_right = jnp.where(ex < 7, pltpu.roll(first, 7, 0), 0.0)
    from_left = jnp.where(ex > 0, pltpu.roll(last, 1, 0), 0.0)
    return (first + from_left) * masks[0], (last + from_right) * masks[1]


def join_rows(ref, flags):
    ex = ex_ids()
    not_first = jnp.where(ex == 0, 0.0, 1.0)
    not_last = jnp.where(ex == 7, 0.0, 1.0)
    for ix in range(6):
        for ey in range(7):
            total = get(ref, 30 + ix, ey) + get(ref, ix, ey + 1)
            put(ref, 30 + ix, ey, total)
            put(ref, ix, ey + 1, total)
        low = get(ref, ix, 0) * flags[0]
        high = get(ref, 30 + ix, 7) * flags[2]
        if ix == 0:
            low, high = low * not_first, high * not_first
        if ix == 5:
            low, high = low * not_last, high * not_last
        put(ref, ix, 0, low)
        put(ref, 30 + ix, 7, high)


def line_product(line, table, mirrored=1.0):
    sums = [line[j] + line[5 - j] for j in range(3)]
    gaps = [line[j] - line[5 - j] for j in range(3)]
    out = [None] * 6
    for i in range(3):
        even = None
        odd = None
        for j in range(3):
            even_term = sums[j] * float(0.5 * (table[i, j] + table[i, 5 - j]))
            odd_term = gaps[j] * float(0.5 * (table[i, j] - table[i, 5 - j]))
            even = even_term if even is None else even + even_term
            odd = odd_term if odd is None else odd + odd_term
        out[i] = even + odd
        out[5 - i] = even - odd if mirrored > 0 else odd - even
    return out


def apply_local(src, dst, rates, flags, terms=(), products=(), energy=False):
    masks = col_masks(flags)

    def body(ey, sums):
        sums = list(sums)
        for ix in range(6):
            line = []
            for iy in range(6):
                point = 6 * iy + ix
                if not terms:
                    line.append(get(src, point, ey))
                    continue
                values = [get(ref, point, ey) for _, ref in terms]
                value = None
                for (factor, _), part in zip(terms, values):
                    part = -part if factor == -1.0 else part * factor
                    value = part if value is None else value + part
                put(src, point, ey, value)
                line.append(value)
                values.append(value)
                ends = (iy in (0, 5)) + (ix in (0, 5))
                for place, (left, right) in enumerate(products):
                    both = values[left] * values[right]
                    sums[place] = sums[place] + (both * (0.5**ends) if ends else both)
            out = line_product(line, STIFF_HAT)
            for iy in range(6):
                put(dst, 6 * iy + ix, ey, out[iy] + rates * line[iy])
        for iy in range(6):
            line = [get(src, 6 * iy + ix, ey) for ix in range(6)]
            out = line_product(line, STIFF_HAT)
            full = [
                (get(dst, 6 * iy + ix, ey) + out[ix]) * float(WEIGHTS[iy] * WEIGHTS[ix])
                for ix in range(6)
            ]
            if energy:
                for ix in range(6):
                    sums[-1] = sums[-1] + full[ix] * line[ix]
            full[0], full[5] = join_cols(full[0], full[5], masks)
            for ix in range(6):
                put(dst, 6 * iy + ix, ey, full[ix])
        return tuple(sums)

    zero = jnp.zeros((8, LANES), F32)
    sums = lax.fori_loop(0, BLOCKS, body, (zero,) * (len(products) + int(energy)))
    join_rows(dst, flags)
    return sums


def side_slice(side, i):
    if side == 0:
        return pl.ds(i * 64, 8)
    if side == 2:
        return pl.ds((30 + i) * 64 + 56, 8)
    if side == 1:
        return pl.ds((6 * i + 5) * 64 + 7, 8, stride=8)
    return pl.ds(6 * i * 64, 8, stride=8)


def read_line(ref, side):
    return [ref[side_slice(side, i), :] for i in range(6)]


def lane_ids():
    return lax.broadcasted_iota(jnp.int32, (8, LANES), 1)


def is_packed(modes):
    return 3 * modes + modes == LANES


def pack_lanes(values, modes):
    if not is_packed(modes):
        return values
    third = len(values) // 4
    inside = lane_ids() < 3 * modes
    return [
        jnp.where(
            inside,
            values[comp * third + at],
            pltpu.roll(values[3 * third + at], (3 - comp) * modes, 1),
        )
        for comp in range(3)
        for at in range(third)
    ]


def unpack_last(pieces, modes):
    block = lax.div(lane_ids(), jnp.int32(modes))
    turned = [pltpu.roll(pieces[comp], (comp + 1) * modes, 1) for comp in range(3)]
    return jnp.where(block == 0, turned[0], jnp.where(block == 1, turned[1], turned[2]))


def unpack_lanes(values, modes):
    if not is_packed(modes):
        return values
    third = len(values) // 3
    return values + [
        unpack_last([values[comp * third + at] for comp in range(3)], modes) for at in range(third)
    ]


def line_rows(modes):
    return 3 * SENT if is_packed(modes) else 4 * SENT


def first_points(last_points):
    return jnp.where(ex_ids() > 0, pltpu.roll(last_points, 1, 0), 0.0)


def write_lines(ref, lines_ref, base, modes):
    values = []
    for side in range(4):
        values += read_line(ref, side)[1:]
    for at, value in enumerate(pack_lanes(values, modes)):
        lines_ref[pl.ds(base + at * 8, 8), :] = value


def load_lines(lines_ref, modes):
    count = line_rows(modes) // 8
    values = unpack_lanes([lines_ref[pl.ds(at * 8, 8), :] for at in range(count)], modes)
    sides = [values[side * 5 : side * 5 + 5] for side in range(4)]
    return [[first_points(side[4])] + side for side in sides]


def add_lines(ref, lines):
    for side in range(4):
        for i in range(6):
            where = side_slice(side, i)
            ref[where, :] = ref[where, :] + lines[side][i]


def reverse_rows(value):
    ex = ex_ids()
    value = pltpu.roll(value, 4, 0)
    value = jnp.where((ex & 2) == 0, pltpu.roll(value, 6, 0), pltpu.roll(value, 2, 0))
    return jnp.where((ex & 1) == 0, pltpu.roll(value, 7, 0), pltpu.roll(value, 1, 0))


def collect_sides(gath_refs, own, partner_ref, side_ref, sides, modes):
    sets = sides.shape[1] // SIDE
    step = line_rows(modes)

    def copy_side(side, load):
        there = jnp.maximum(side_ref[0, side], 0)

        def fill(place, values):
            for i, value in enumerate([first_points(values[4])] + values):
                sides[side, pl.ds(place * SIDE + i * 8, 8), :] = value

        def plain():
            for place in range(sets):
                first = place * step + there * SENT
                fill(place, [load(pl.multiple_of(first + i * 8, 8)) for i in range(5)])

        if not is_packed(modes):
            plain()
            return
        pl.when(there < 3)(plain)

        @pl.when(there == 3)
        def _():
            for place in range(sets):
                first = place * step
                values = []
                for i in range(5):
                    pieces = [load(first + comp * SENT + i * 8) for comp in range(3)]
                    values.append(unpack_last(pieces, modes))
                fill(place, values)

    def body(side, carry):
        part = partner_ref[0, side]
        if len(gath_refs) == 1:
            source = jnp.maximum(part, 0)
            copy_side(side, lambda at: gath_refs[0][source, pl.ds(at, 8), :])
            return carry
        for slot, ref in enumerate(gath_refs):
            here = jnp.logical_and(part >= 0, jnp.bitwise_xor(part, own) == slot)

            @pl.when(here)
            def _(ref=ref):
                copy_side(side, lambda at: ref[pl.ds(at, 8), :])

        return carry

    lax.fori_loop(0, 4, body, 0)


def incoming_lines(sides, place, partner_ref, flip_ref):
    lines = []
    for side in range(4):
        glued = partner_ref[0, side] >= 0
        turned = flip_ref[0, side] == 1
        line = []
        for i in range(6):
            at = pl.multiple_of(place * SIDE + jnp.where(turned, 5 - i, i) * 8, 8)
            value = sides[side, pl.ds(at, 8), :]
            value = jnp.where(turned, reverse_rows(value), value)
            line.append(jnp.where(glued, value, 0.0))
        lines.append(line)
    return lines


def own_reaction(own_lines, rates, flags, scale):
    ex = ex_ids()
    edge = float(WEIGHTS[0])
    corner = float(STIFF[0, 0])
    lines = []
    for side in range(4):
        line = own_lines[side]
        along = line_product(line, STIFF_HAT)
        out = [
            (along[i] * edge + line[i] * (corner + rates * edge)) * float(WEIGHTS[i])
            for i in range(6)
        ]
        first = out[0] + pltpu.roll(out[5], 1, 0)
        last = out[5] + pltpu.roll(out[0], 7, 0)
        out[0] = jnp.where(ex > 0, first, 0.0)
        out[5] = jnp.where(ex < 7, last, 0.0)
        lines.append([value * (flags[side] * scale) for value in out])
    return lines


def pick(index, values):
    if isinstance(index, int):
        return values[index]
    chosen = jnp.int32(values[0])
    for place in range(1, len(values)):
        chosen = jnp.where(index == place, jnp.int32(values[place]), chosen)
    return chosen


def offset_of(place, size):
    return (0, 3, 1, 2)[place] if size == 4 else place


def block_of(place, four, size):
    return place if isinstance(four, int) else jnp.bitwise_xor(four, offset_of(place, size))


def pack_kernel(step, count, dynamic, load, starts, offsets, ids_ref, velocity_ref, *refs):
    send_refs = refs[:count]
    scratch = refs[-2] if load else refs[-1]
    width = scratch.shape[1]
    modes = velocity_ref.shape[1]
    four = ids_ref[1] if dynamic else 0
    copies = []
    if load:
        copies = [
            pltpu.make_async_copy(velocity_ref.at[comp], refs[count].at[comp], refs[-1].at[comp])
            for comp in range(3)
        ]
        velocity_ref = refs[count]
    for copy in copies:
        copy.start()
    for place in range(count):
        index = block_of(place, four, count)
        table = order_table(step, pick(index, offsets), scratch)
        if place == 0:
            for copy in copies:
                copy.wait()
        start = pick(index, starts)
        start = start if isinstance(start, int) else pl.multiple_of(start, LANES)
        window = pl.ds(start, width)
        rows = [velocity_ref[comp, :, window] for comp in range(3)]
        pad = jnp.zeros((LANES - 3 * modes, width), F32)
        high, low = halves(jnp.concatenate(rows + [pad], axis=0))
        both = jnp.concatenate([high, low], axis=0)
        out = dot(table, both, ((1,), (1,)))
        out = out[:, :LANES] + out[:, LANES:]
        if not is_packed(modes):
            send_refs[place][...] = out
            continue
        values = [out[point * step : (point + 1) * step] for point in range(POINTS)]
        for at, value in enumerate(pack_lanes(values, modes)):
            send_refs[place][pl.ds(at * step, step), :] = value


def product_kernel(modes, step, count, dynamic, ids_ref, *refs):
    recv_refs = refs[:count]
    inv_high, inv_low, back_high, back_low = refs[count : count + 4]
    send_refs = refs[count + 4 : 2 * count + 4]
    full, lined, phys, prod, spec = refs[2 * count + 4 :]
    four = ids_ref[1] if dynamic else 0
    packed = is_packed(modes)
    for place in range(count):
        index = block_of(place, four, count)
        if packed:
            ready = 3 * POINTS // 4
            values = [recv_refs[place][pl.ds(at * step, step), :] for at in range(ready)]
            for at, value in enumerate(unpack_lanes(values, modes)):
                full[place, pl.ds(at * step, step), :] = value
        else:
            full[place] = recv_refs[place][...]
        first = index * LANES
        first = first if isinstance(first, int) else pl.multiple_of(first, LANES)
        lined[:, pl.ds(first, LANES)] = full[place]
    phys[...] = dot3(lined[...], inv_high[...], inv_low[...])
    width = 2 * LANES

    def field(point, comp):
        return phys[pl.ds(point * step, step), comp * LANES : (comp + 1) * LANES]

    for comp in range(3):
        wide = pl.ds(comp * width, LANES)
        for iy in range(6):
            line = []
            for ix in range(6):
                point = 6 * iy + ix
                value = field(point, comp)
                line.append(value * field(point, 0))
                prod[pl.ds(point * step, step), pl.ds(comp * width + LANES, LANES)] = (
                    value * field(point, 2)
                )
            out = line_product(line, DERIV, -1.0)
            for ix in range(6):
                prod[pl.ds((6 * iy + ix) * step, step), wide] = out[ix]
        for ix in range(6):
            line = [field(6 * iy + ix, comp) * field(6 * iy + ix, 1) for iy in range(6)]
            out = line_product(line, DERIV, -1.0)
            for iy in range(6):
                at = pl.ds((6 * iy + ix) * step, step)
                prod[at, wide] = prod[at, wide] + out[iy]
        spec[comp] = dot3(prod[:, comp * width : (comp + 1) * width], back_high[...], back_low[...])

    lane_block = lax.div(lax.broadcasted_iota(jnp.int32, (step, LANES), 1), jnp.int32(modes))
    masks = []
    shifts = []
    for place in range(count):
        index = block_of(place, four, count)
        masks.append([lane_block == lax.rem(index + comp, count) for comp in range(2)])
        shifts.append(lax.rem(LANES - index * modes, LANES))
    kept = []
    for point in range(POINTS):
        at = pl.ds(point * step, step)
        mass = float(WEIGHTS[point // 6] * WEIGHTS[point % 6])
        turned = [spec[0, at, :]]
        turned += [pltpu.roll(spec[comp, at, :], comp * modes, 1) for comp in (1, 2)]
        for place in range(count):
            mask = masks[place]
            mixed = jnp.where(mask[0], turned[0], jnp.where(mask[1], turned[1], turned[2]))
            nonlinear = pltpu.roll(mixed, shifts[place], 1)
            full[place, at, :] = mass * (REACTION * full[place, at, :] + nonlinear)
    for place in range(count):
        values = [full[place, pl.ds(point * step, step), :] for point in range(POINTS)]
        for at, value in enumerate(pack_lanes(values, modes)):
            send_refs[place][pl.ds(at * step, step), :] = value


def first_kernel(modes, step, count, chunks, dynamic, ids_ref, partner_ref, *refs):
    recv_refs = refs[: count * chunks]
    base_ref, lines_ref, work = refs[count * chunks :]
    four = ids_ref[1] if dynamic else 0
    rates = helmholtz_rates(ids_ref[1], modes)
    flags = glued_flags(partner_ref)
    for chunk in range(chunks):
        for place in range(count):
            ref = recv_refs[chunk * count + place]
            ready = ref.shape[0] // step
            first = (block_of(place, four, count) * chunks + chunk) * step
            values = unpack_lanes([ref[pl.ds(at * step, step), :] for at in range(ready)], modes)
            for point in range(POINTS):
                at = point * 64 + first
                at = at if isinstance(at, int) else pl.multiple_of(at, step)
                base_ref[pl.ds(at, step), :] = values[point]
    masks = col_masks(flags)
    for ey in range(BLOCKS):
        for iy in range(6):
            first, last = join_cols(get(base_ref, 6 * iy, ey), get(base_ref, 6 * iy + 5, ey), masks)
            put(base_ref, 6 * iy, ey, first)
            put(base_ref, 6 * iy + 5, ey, last)
    join_rows(base_ref, flags)
    apply_local(base_ref, work, rates, flags)
    write_lines(base_ref, lines_ref, 0, modes)
    write_lines(work, lines_ref, line_rows(modes), modes)


def sum_rows(sums):
    return [jnp.sum(value, axis=0, keepdims=True) for value in sums]


def second_kernel(modes, slots, ids_ref, partner_ref, side_ref, flip_ref, *refs):
    gath_refs = refs[:slots]
    lines_ref, _, k0_ref, k1_ref, k2_ref, next_ref, sums_ref, work, sides = refs[slots:]
    rates = helmholtz_rates(ids_ref[1], modes)
    flags = glued_flags(partner_ref)
    collect_sides(gath_refs, ids_ref[0], partner_ref, side_ref, sides, modes)
    back = own_reaction(load_lines(lines_ref, modes), rates, flags, 1.0)
    add_lines(k0_ref, incoming_lines(sides, 0, partner_ref, flip_ref))
    apply_local(k0_ref, work, rates, flags)
    add_lines(work, incoming_lines(sides, 1, partner_ref, flip_ref))
    add_lines(work, back)
    sums = apply_local(
        k1_ref, work, rates, flags,
        terms=[(1.0 / SPREAD, work), (-CENTRE / SPREAD, k0_ref)],
        products=[(1, 1), (1, -1), (-1, -1)],
    )
    write_lines(work, next_ref, 0, modes)
    apply_local(
        k2_ref, work, rates, flags,
        terms=[(TWICE, work), (-CENTRE * TWICE, k1_ref), (-1.0, k0_ref)],
    )
    write_lines(work, next_ref, line_rows(modes), modes)
    sums_ref[...] = jnp.concatenate(sum_rows(sums) + [jnp.zeros((5, LANES), F32)], axis=0)


def third_kernel(modes, slots, ids_ref, partner_ref, side_ref, flip_ref, *refs):
    gath_refs = refs[:slots]
    lines_ref, k1_ref, sums_ref, _ = refs[slots : slots + 4]
    k2_ref, k3_ref, a3_ref, next_ref, work, sides = refs[slots + 4 :]
    rates = helmholtz_rates(ids_ref[1], modes)
    flags = glued_flags(partner_ref)
    collect_sides(gath_refs, ids_ref[0], partner_ref, side_ref, sides, modes)
    back = own_reaction(load_lines(lines_ref, modes), rates, flags, TWICE)
    incoming = incoming_lines(sides, 0, partner_ref, flip_ref)
    add_lines(k2_ref, [[value * TWICE for value in line] for line in incoming])
    apply_local(k2_ref, work, rates, flags)
    add_lines(work, incoming_lines(sides, 1, partner_ref, flip_ref))
    add_lines(work, back)
    sums = apply_local(
        k3_ref, a3_ref, rates, flags,
        terms=[(TWICE, work), (-CENTRE * TWICE, k2_ref), (-1.0, k1_ref)],
        products=[(2, 1), (1, 1), (1, -1), (-1, -1)],
        energy=True,
    )
    write_lines(a3_ref, next_ref, 0, modes)
    next_ref[pl.ds(line_rows(modes), SUM_ROWS), :] = jnp.concatenate(
        [sums_ref[:3, :]] + sum_rows(sums), axis=0
    )


def turn_kernel(starts, offsets, fields, has_scatter, *refs):
    field_refs = refs[:fields]
    out_refs = refs[fields : 2 * fields]
    scratch, rows = refs[-2:]
    step = rows.shape[0] // POINTS
    used = out_refs[0].shape[0]
    width = scratch.shape[1]
    for out_ref in out_refs:
        out_ref[...] = jnp.zeros(out_ref.shape, F32)
    for unit in range(len(starts)):
        table = order_table(step, offsets[unit], scratch)
        for field_ref, out_ref in zip(field_refs, out_refs):
            for point in range(POINTS):
                rows[pl.ds(point * step, step), :] = field_ref[pl.ds(point * 64 + unit * step, step), :]
            high, low = halves(jnp.transpose(rows[...])[:used])
            both = jnp.concatenate([high, low], axis=0)
            out = dot(both, table, ((1,), (0,)))
            window = pl.ds(starts[unit], width)
            out_ref[:, window] = out_ref[:, window] + (out[:used] + out[used:])
    if has_scatter:
        scatter_ref = refs[2 * fields]
        place = lax.broadcasted_iota(jnp.int32, (SIDE, NODES), 0)
        at = 6 * jnp.bitwise_and(place, 7) + lax.shift_right_logical(place, 3)
        node = lax.broadcasted_iota(jnp.int32, (SIDE, NODES), 1)
        targets = (at, at * SIDE + SIDE - 1, at + (SIDE - 1) * SIDE, at * SIDE)
        for side, target in enumerate(targets):
            scatter_ref[side * SIDE : (side + 1) * SIDE, :] = jnp.where(
                node == target, 1.0, 0.0
            ).astype(BF16)


def conjugate_coefficients(gram, energy):
    zero = jnp.zeros_like(energy)

    def image(vec):
        out = [zero] * 5
        for j in range(4):
            if vec[j] is None:
                continue
            out[j] = out[j] + CENTRE * vec[j]
            out[j + 1] = out[j + 1] + (SPREAD if j == 0 else 0.5 * SPREAD) * vec[j]
            if j > 0:
                out[j - 1] = out[j - 1] + 0.5 * SPREAD * vec[j]
        return out

    def inner(left, right):
        total = zero
        for i in range(4):
            for j in range(4):
                if left[i] is not None and right[j] is not None:
                    total = total + left[i] * right[j] * gram[i][j]
        return total

    moments = [[None] * 4 for _ in range(4)]
    for j in range(3):
        column = image([jnp.ones_like(energy) if i == j else None for i in range(4)])
        for i in range(4):
            total = zero
            for m in range(max(j - 1, 0), j + 2):
                total = total + column[m] * gram[i][m]
            moments[i][j] = total
    for i in range(3):
        moments[i][3] = moments[3][i]
    moments[3][3] = energy

    def pad(vec, size):
        return [vec[i] if i < size else None for i in range(4)]

    residual = [jnp.ones_like(energy), zero, zero, zero, zero]
    direction = list(residual)
    solution = [zero] * 4
    norm_now = gram[0][0]
    for step in range(ITERS):
        trimmed = pad(direction, step + 1)
        bend = zero
        for i in range(step + 1):
            for j in range(step + 1):
                bend = bend + direction[i] * direction[j] * moments[i][j]
        alpha = norm_now / bend
        moved = image(trimmed)
        for i in range(step + 1):
            solution[i] = solution[i] + alpha * direction[i]
        for i in range(step + 2):
            residual[i] = residual[i] - alpha * moved[i]
        if step < ITERS - 1:
            kept = pad(residual, step + 2)
            norm_next = inner(kept, kept)
            ratio = norm_next / norm_now
            direction = [residual[i] + ratio * direction[i] for i in range(5)]
            norm_now = norm_next
    return solution, residual


def last_kernel(slots, ids_ref, partner_ref, side_ref, flip_ref, *refs):
    gath_refs = refs[:slots]
    turned = refs[slots : slots + 5]
    scatter_ref, sol_out, res_out, lines, sides, sol_ref, res_ref, sems = refs[slots + 5 :]
    modes = sol_ref.shape[1]
    used = 3 * modes
    where = pl.ds(line_rows(modes), SUM_ROWS)
    if slots == 1:
        parts = [gath_refs[0][part, where, :] for part in range(gath_refs[0].shape[0])]
    else:
        parts = [ref[where, :] for ref in gath_refs]
    sums = functools.reduce(lambda left, right: left + right, parts)
    collect_sides(gath_refs, ids_ref[0], partner_ref, side_ref, sides, modes)
    g00, g01, g11, g12, g22, g23, g33, energy = [
        jnp.broadcast_to(sums[place : place + 1, :], (8, LANES)) for place in range(8)
    ]
    g02 = 2.0 * g11 - g00
    g03 = 2.0 * g12 - g01
    g13 = (g22 - g00) + g11
    gram = [
        [g00, g01, g02, g03],
        [g01, g11, g12, g13],
        [g02, g12, g22, g23],
        [g03, g13, g23, g33],
    ]
    solution, residual = conjugate_coefficients(gram, energy)
    on_a3 = residual[4] * TWICE
    on_k3 = residual[3] - on_a3 * CENTRE
    on_k2 = residual[2] - residual[4]
    factors = list(solution) + [residual[0], residual[1], on_k2, on_k3, on_a3]
    columns = jnp.transpose(
        jnp.concatenate([value[:1] for value in factors] + [jnp.zeros((LANES - 9, LANES), F32)], axis=0)
    )
    incoming = incoming_lines(sides, 0, partner_ref, flip_ref)
    for side in range(4):
        for i in range(6):
            lines[pl.ds(side * SIDE + i * 8, 8), :] = incoming[side][i] * on_a3
    high, low = halves(jnp.transpose(lines[...])[:used])
    added = dot(jnp.concatenate([high, low], axis=0), scatter_ref[...], ((1,), (0,)))
    copies = []
    for comp in range(3):
        for first in range(0, modes, 8):
            at = comp * modes + first
            rows = [ref[at : at + 8, :] for ref in turned]
            scale = [columns[at : at + 8, place : place + 1] for place in range(9)]
            sol_ref[comp, first : first + 8, :] = (scale[0] * rows[0] + scale[1] * rows[1]) + (
                scale[2] * rows[2] + scale[3] * rows[3]
            )
            res_ref[comp, first : first + 8, :] = (
                (scale[4] * rows[0] + scale[5] * rows[1])
                + (scale[6] * rows[2] + scale[7] * rows[3])
                + (scale[8] * rows[4] + (added[at : at + 8] + added[used + at : used + at + 8]))
            )
        for place, (buffer, out) in enumerate(((sol_ref, sol_out), (res_ref, res_out))):
            copies.append(
                pltpu.make_async_copy(buffer.at[comp], out.at[comp], sems.at[2 * comp + place])
            )
            copies[-1].start()
    for copy in copies:
        copy.wait()


def call(kernel, name, out_shapes, args, scratch, scalars=0, keep=True, aliases=None, outside=False):
    smem = pl.BlockSpec(memory_space=pltpu.SMEM)
    vmem = pl.BlockSpec(memory_space=pltpu.VMEM)
    shapes = [shape if isinstance(shape, jax.ShapeDtypeStruct) else jax.ShapeDtypeStruct(shape, F32) for shape in out_shapes]
    return pl.pallas_call(
        kernel,
        name=name,
        out_shape=[pltpu.VMEM(one.shape, one.dtype) if keep else one for one in shapes],
        in_specs=[smem] * scalars + [pl.BlockSpec(memory_space=pltpu.HBM) if outside else vmem] * (len(args) - scalars),
        out_specs=[vmem if keep else pl.BlockSpec(memory_space=pltpu.HBM)] * len(out_shapes),
        scratch_shapes=[pltpu.VMEM(one, F32) if isinstance(one, tuple) else one for one in scratch],
        input_output_aliases=aliases or {},
        compiler_params=pltpu.CompilerParams(vmem_limit_bytes=VMEM_LIMIT),
    )(*args[:scalars], *[held(arg, pltpu.HBM if outside else pltpu.VMEM) for arg in args[scalars:]])


def held(arg, space):
    return arg if isinstance(arg, np.ndarray) else pltpu.with_memory_space_constraint(arg, space)


def swap_blocks(blocks, dynamic):
    if not dynamic:
        stacked = lax.all_to_all(jnp.stack(blocks), "four", split_axis=0, concat_axis=0, tiled=True)
        return [stacked[place] for place in range(len(blocks))]
    size = len(blocks)
    swapped = list(blocks)
    for place in range(size - 1, 0, -1):
        swapped[place] = lax.ppermute(blocks[place], "four", [(i, i ^ offset_of(place, size)) for i in range(size)])
    return swapped


def share_lines(lines, beside=()):
    parts = lax.axis_size("dom")
    if parts != 8:
        return [lax.all_gather(lines, "dom", axis=0, tiled=False)], list(beside)
    slots = [lines] + [None] * (parts - 1)
    for slot in range(2, parts, 2):
        slots[slot] = lax.ppermute(lines, "dom", [(i, i ^ slot) for i in range(parts)])
        if beside and slot == parts - 2:
            slots[slot], *beside = lax.optimization_barrier((slots[slot], *beside))
    for slot in range(0, parts, 2):
        slots[slot + 1] = lax.ppermute(slots[slot], "dom", [(i, i ^ 1) for i in range(parts)])
    return slots, list(beside)


def shards(velocity, partner, partner_side, flipped):
    modes = velocity.shape[1]
    count = lax.axis_size("four")
    step, chunks = chunk_sizes(count)
    rows = POINTS * step
    sent_rows = 3 * rows // 4 if is_packed(modes) else rows
    dynamic = step == BLOCKS
    (inv_high, inv_low), (back_high, back_low) = transform_tables(count)
    starts, offsets = unit_windows(count)
    table = (rows, 3 * LANES)
    ids = jnp.stack([lax.axis_index("dom"), lax.axis_index("four")]).astype(jnp.int32)
    field = (NODES, LANES)
    blocks = [(sent_rows, LANES)] * count
    lined = line_rows(modes)

    spread = []
    held_velocity = velocity
    for chunk in range(chunks):
        load = chunk == 0
        sent = call(
            functools.partial(
                pack_kernel, step, count, dynamic, load, starts[chunk::chunks], offsets[chunk::chunks]
            ),
            "pack",
            blocks + [velocity.shape] * load,
            (ids, held_velocity),
            [table] + [pltpu.SemaphoreType.DMA((3,))] * load,
            scalars=1,
            outside=load,
        )
        if load:
            *sent, held_velocity = sent
        spread.append(swap_blocks(sent, dynamic))
    local = []
    for chunk in range(chunks):
        sent = call(
            functools.partial(product_kernel, modes, step, count, dynamic),
            "products",
            blocks,
            (ids, *spread[chunk], inv_high, inv_low, back_high, back_low),
            [(count, rows, LANES), (rows, count * LANES), (rows, 3 * LANES), (rows, 6 * LANES), (3, rows, LANES)],
            scalars=1,
        )
        local += swap_blocks(sent, dynamic)

    base, lines = call(
        functools.partial(first_kernel, modes, step, count, chunks, dynamic),
        "first",
        [field, (2 * lined, LANES)],
        (ids, partner, *local),
        [field],
        scalars=2,
    )
    tables = (ids, partner, partner_side, flipped)
    gathered, _ = share_lines(lines)
    slots = len(gathered)
    k0, k1, base, lines, sums = call(
        functools.partial(second_kernel, modes, slots),
        "second",
        [field, field, field, (2 * lined, LANES), (8, LANES)],
        (*tables, *gathered, lines, base),
        [field, (4, 2 * SIDE, LANES)],
        scalars=4,
        aliases={4 + slots + 1: 0},
    )
    flat = (3 * modes, NODES)
    turned = call(
        functools.partial(turn_kernel, starts, offsets, 2, True),
        "turn",
        [flat, flat, jax.ShapeDtypeStruct((4 * SIDE, NODES), BF16)],
        (k0, k1),
        [table, (rows, LANES)],
    )
    gathered, (t0, t1, scatter) = share_lines(lines, turned)
    k2, k3, a3, lines = call(
        functools.partial(third_kernel, modes, slots),
        "third",
        [field, field, field, (lined + SUM_ROWS, LANES)],
        (*tables, *gathered, lines, k1, sums, base),
        [field, (4, 2 * SIDE, LANES)],
        scalars=4,
        aliases={4 + slots + 3: 0},
    )
    turned = call(
        functools.partial(turn_kernel, starts, offsets, 3, False),
        "turn",
        [flat, flat, flat],
        (k2, k3, a3),
        [table, (rows, LANES)],
    )
    gathered, (t2, t3, ta) = share_lines(lines, turned)
    outs = call(
        functools.partial(last_kernel, slots),
        "last",
        [velocity.shape, velocity.shape],
        (*tables, *gathered, t0, t1, t2, t3, ta, scatter),
        [
            (4 * SIDE, LANES),
            (4, SIDE, LANES),
            velocity.shape,
            velocity.shape,
            pltpu.SemaphoreType.DMA((6,)),
        ],
        scalars=4,
        keep=False,
    )
    return tuple(outs)


def solution(mesh):
    return jax.shard_map(
        shards,
        mesh=mesh,
        in_specs=(P(None, "four", "dom"), P("dom", None), P("dom", None), P("dom", None)),
        out_specs=(P(None, "four", "dom"), P(None, "four", "dom")),
        check_vma=False,
    )
```

```python
import functools
import math

import jax
import jax.numpy as jnp
import numpy as np
from jax import lax
from jax.experimental import pallas as pl
from jax.experimental.pallas import tpu as pltpu
from jax.sharding import PartitionSpec as P

ITERS = 4
REACTION = 2.0
WAVE_STEP = 0.0625
LANES = 128
POINTS = 36
BLOCKS = 8
SIDE = 48
SENT = 40
NODES = 2304
CENTRE = 9.0
SPREAD = 9.0
TWICE = 2.0 / SPREAD
SUM_ROWS = 8
VMEM_LIMIT = 32 * 1024 * 1024
F32 = jnp.float32
BF16 = jnp.bfloat16


def gll_tables():
    inner_near = math.sqrt(1.0 / 3.0 - 2.0 * math.sqrt(7.0) / 21.0)
    inner_far = math.sqrt(1.0 / 3.0 + 2.0 * math.sqrt(7.0) / 21.0)
    points = np.array([-1.0, -inner_far, -inner_near, inner_near, inner_far, 1.0])
    values = (63.0 * points**5 - 70.0 * points**3 + 15.0 * points) / 8.0
    weights = 2.0 / (30.0 * values * values)
    spacing = points[:, None] - points[None, :]
    same_point = spacing == 0.0
    derivative = np.where(
        same_point, 0.0, values[:, None] / (values[None, :] * np.where(same_point, 1.0, spacing))
    )
    end_fix = np.array([-7.5, 0.0, 0.0, 0.0, 0.0, 7.5])
    derivative = derivative + np.eye(6) * end_fix[None, :]
    stiffness = derivative.T @ (weights[:, None] * derivative)
    return (weights, derivative, stiffness)


WEIGHTS, DERIV, STIFF = gll_tables()
STIFF_HAT = STIFF / WEIGHTS[:, None]


def fourier_tables(planes):
    plane_ids = np.arange(planes)
    mode_ids = np.arange(planes)
    waves = np.where(mode_ids < 2, 0, mode_ids // 2)
    angle = (plane_ids[:, None] * waves[None, :] % planes) * (2.0 * math.pi / planes)
    is_sine = (mode_ids % 2 == 1) & (mode_ids >= 2)
    basis = np.where(is_sine[None, :], np.sin(angle), np.cos(angle))
    alternating = np.where(plane_ids % 2 == 0, 1.0, -1.0)
    basis = np.where(mode_ids[None, :] == 1, alternating[:, None], basis)
    row_scale = np.where(mode_ids < 2, 1.0, 2.0) / planes
    forward = basis.T * row_scale[:, None]
    rates = (np.arange(planes // 2) * WAVE_STEP)[:, None]
    forward_z = np.zeros_like(forward)
    forward_z[0::2] = rates * forward[1::2]
    forward_z[1::2] = -rates * forward[0::2]
    forward_z[0:2] = 0.0
    return (basis, forward, forward_z)


def split_table(table):
    high = np.asarray(table, np.float32).astype(jnp.bfloat16)
    low = (np.asarray(table, np.float64) - high.astype(np.float64)).astype(np.float32)
    return high, low.astype(jnp.bfloat16)


def transform_tables(count):
    planes = LANES
    modes = planes // count
    basis, forward, forward_z = fourier_tables(planes)
    inverse = np.zeros((count * LANES, 3 * planes))
    for block in range(count):
        ids = slice(block * modes, (block + 1) * modes)
        for comp in range(3):
            at = block * LANES + comp * modes
            inverse[at : at + modes, comp * planes : (comp + 1) * planes] = basis[:, ids].T
    back = -np.concatenate([forward.T, forward_z.T], axis=0)
    return split_table(inverse), split_table(back)


def chunk_sizes(count):
    group = BLOCKS * BLOCKS // count
    step = min(group, BLOCKS)
    return step, group // step


def unit_windows(count):
    step, _ = chunk_sizes(count)
    starts = []
    offsets = []
    for index in range(BLOCKS * BLOCKS // step):
        element = index * step
        first = element // BLOCKS * 6 * SIDE
        starts.append(first // LANES * LANES)
        offsets.append(first % LANES + 6 * (element % BLOCKS))
    return starts, offsets


def order_table(step, offset, scratch):
    width = scratch.shape[1]
    lane = lax.broadcasted_iota(jnp.int32, (step, width), 1)
    gap = lane - 6 * lax.broadcasted_iota(jnp.int32, (step, width), 0) - offset
    for point in range(POINTS):
        hit = gap == point // 6 * SIDE + point % 6
        scratch[pl.ds(point * step, step), :] = jnp.where(hit, 1.0, 0.0)
    return scratch[...].astype(BF16)


def halves(value):
    high = value.astype(BF16)
    low = (value - high.astype(F32)).astype(BF16)
    return high, low


def dot(left, right, dims):
    return lax.dot_general(left, right, (dims, ((), ())), preferred_element_type=F32)


def dot3(left, right_high, right_low):
    high, low = halves(left)
    dims = ((1,), (0,))
    return dot(high, right_high, dims) + (dot(low, right_high, dims) + dot(high, right_low, dims))


def start_of(point, ey):
    return pl.multiple_of(point * 64 + ey * 8, 8)


def get(ref, point, ey):
    return ref[pl.ds(start_of(point, ey), 8), :]


def put(ref, point, ey, value):
    ref[pl.ds(start_of(point, ey), 8), :] = value


def ex_ids():
    return lax.broadcasted_iota(jnp.int32, (8, LANES), 0)


def helmholtz_rates(four, modes):
    lane = lax.broadcasted_iota(jnp.int32, (8, LANES), 1)
    mode = four * modes + lax.rem(lane, jnp.int32(modes))
    wave = jnp.where(mode == 0, 0, jnp.where(mode == 1, LANES // 2, lax.div(mode, jnp.int32(2))))
    scaled = wave.astype(F32) * WAVE_STEP
    return REACTION + scaled * scaled


def glued_flags(partner_ref):
    return [jnp.where(partner_ref[0, side] >= 0, 1.0, 0.0).astype(F32) for side in range(4)]


def col_masks(flags):
    ex = ex_ids()
    return jnp.where(ex == 0, flags[3], 1.0), jnp.where(ex == 7, flags[1], 1.0)


def join_cols(first, last, masks):
    ex = ex_ids()
    from_right = jnp.where(ex < 7, pltpu.roll(first, 7, 0), 0.0)
    from_left = jnp.where(ex > 0, pltpu.roll(last, 1, 0), 0.0)
    return (first + from_left) * masks[0], (last + from_right) * masks[1]


def join_rows(ref, flags, pairs=range(7)):
    ex = ex_ids()
    not_first = jnp.where(ex == 0, 0.0, 1.0)
    not_last = jnp.where(ex == 7, 0.0, 1.0)
    for ix in range(6):
        for ey in pairs:
            total = get(ref, 30 + ix, ey) + get(ref, ix, ey + 1)
            put(ref, 30 + ix, ey, total)
            put(ref, ix, ey + 1, total)
        low = get(ref, ix, 0) * flags[0]
        high = get(ref, 30 + ix, 7) * flags[2]
        if ix == 0:
            low, high = low * not_first, high * not_first
        if ix == 5:
            low, high = low * not_last, high * not_last
        put(ref, ix, 0, low)
        put(ref, 30 + ix, 7, high)


def line_product(line, table, mirrored=1.0):
    sums = [line[j] + line[5 - j] for j in range(3)]
    gaps = [line[j] - line[5 - j] for j in range(3)]
    out = [None] * 6
    for i in range(3):
        even = None
        odd = None
        for j in range(3):
            even_term = sums[j] * float(0.5 * (table[i, j] + table[i, 5 - j]))
            odd_term = gaps[j] * float(0.5 * (table[i, j] - table[i, 5 - j]))
            even = even_term if even is None else even + even_term
            odd = odd_term if odd is None else odd + odd_term
        out[i] = even + odd
        out[5 - i] = even - odd if mirrored > 0 else odd - even
    return out


def apply_local(src, dst, rates, flags, terms=(), products=(), energy=False):
    masks = col_masks(flags)

    def body(ey, sums):
        sums = list(sums)
        for ix in range(6):
            line = []
            for iy in range(6):
                point = 6 * iy + ix
                if not terms:
                    line.append(get(src, point, ey))
                    continue
                values = [get(ref, point, ey) for _, ref in terms]
                value = None
                for (factor, _), part in zip(terms, values):
                    part = -part if factor == -1.0 else part * factor
                    value = part if value is None else value + part
                put(src, point, ey, value)
                line.append(value)
                values.append(value)
                ends = (iy in (0, 5)) + (ix in (0, 5))
                for place, (left, right) in enumerate(products):
                    both = values[left] * values[right]
                    sums[place] = sums[place] + (both * (0.5**ends) if ends else both)
            out = line_product(line, STIFF_HAT)
            for iy in range(6):
                put(dst, 6 * iy + ix, ey, out[iy] + rates * line[iy])
        for iy in range(6):
            line = [get(src, 6 * iy + ix, ey) for ix in range(6)]
            out = line_product(line, STIFF_HAT)
            full = [
                (get(dst, 6 * iy + ix, ey) + out[ix]) * float(WEIGHTS[iy] * WEIGHTS[ix])
                for ix in range(6)
            ]
            if energy:
                for ix in range(6):
                    sums[-1] = sums[-1] + full[ix] * line[ix]
            full[0], full[5] = join_cols(full[0], full[5], masks)
            for ix in range(6):
                put(dst, 6 * iy + ix, ey, full[ix])
        return tuple(sums)

    zero = jnp.zeros((8, LANES), F32)
    sums = lax.fori_loop(0, BLOCKS, body, (zero,) * (len(products) + int(energy)), unroll=2)
    join_rows(dst, flags)
    return sums


def side_slice(side, i):
    if side == 0:
        return pl.ds(i * 64, 8)
    if side == 2:
        return pl.ds((30 + i) * 64 + 56, 8)
    if side == 1:
        return pl.ds((6 * i + 5) * 64 + 7, 8, stride=8)
    return pl.ds(6 * i * 64, 8, stride=8)


def read_line(ref, side):
    return [ref[side_slice(side, i), :] for i in range(6)]


def lane_ids():
    return lax.broadcasted_iota(jnp.int32, (8, LANES), 1)


def is_packed(modes):
    return 3 * modes + modes == LANES


def pack_lanes(values, modes):
    if not is_packed(modes):
        return values
    third = len(values) // 4
    inside = lane_ids() < 3 * modes
    return [
        jnp.where(
            inside,
            values[comp * third + at],
            pltpu.roll(values[3 * third + at], (3 - comp) * modes, 1),
        )
        for comp in range(3)
        for at in range(third)
    ]


def unpack_last(pieces, modes):
    block = lax.div(lane_ids(), jnp.int32(modes))
    turned = [pltpu.roll(pieces[comp], (comp + 1) * modes, 1) for comp in range(3)]
    return jnp.where(block == 0, turned[0], jnp.where(block == 1, turned[1], turned[2]))


def unpack_lanes(values, modes):
    if not is_packed(modes):
        return values
    third = len(values) // 3
    return values + [
        unpack_last([values[comp * third + at] for comp in range(3)], modes) for at in range(third)
    ]


def line_rows(modes):
    return 3 * SENT if is_packed(modes) else 4 * SENT


def first_points(last_points):
    return jnp.where(ex_ids() > 0, pltpu.roll(last_points, 1, 0), 0.0)


def write_lines(ref, lines_ref, base, modes):
    values = []
    for side in range(4):
        values += read_line(ref, side)[1:]
    for at, value in enumerate(pack_lanes(values, modes)):
        lines_ref[pl.ds(base + at * 8, 8), :] = value


def load_lines(lines_ref, modes):
    count = line_rows(modes) // 8
    values = unpack_lanes([lines_ref[pl.ds(at * 8, 8), :] for at in range(count)], modes)
    sides = [values[side * 5 : side * 5 + 5] for side in range(4)]
    return [[first_points(side[4])] + side for side in sides]


def add_lines(ref, lines):
    for side in range(4):
        for i in range(6):
            where = side_slice(side, i)
            ref[where, :] = ref[where, :] + lines[side][i]


def add_all(left, right):
    return [[a + b for a, b in zip(one, two)] for one, two in zip(left, right)]


def reverse_rows(value):
    ex = ex_ids()
    value = pltpu.roll(value, 4, 0)
    value = jnp.where((ex & 2) == 0, pltpu.roll(value, 6, 0), pltpu.roll(value, 2, 0))
    return jnp.where((ex & 1) == 0, pltpu.roll(value, 7, 0), pltpu.roll(value, 1, 0))


def collect_sides(gath_refs, own, partner_ref, side_ref, sides, modes):
    sets = sides.shape[1] // SIDE
    step = line_rows(modes)

    def copy_side(side, load):
        there = jnp.maximum(side_ref[0, side], 0)

        def fill(place, values):
            for i, value in enumerate([first_points(values[4])] + values):
                sides[side, pl.ds(place * SIDE + i * 8, 8), :] = value

        def plain():
            for place in range(sets):
                first = place * step + there * SENT
                fill(place, [load(pl.multiple_of(first + i * 8, 8)) for i in range(5)])

        if not is_packed(modes):
            plain()
            return
        pl.when(there < 3)(plain)

        @pl.when(there == 3)
        def _():
            for place in range(sets):
                first = place * step
                values = []
                for i in range(5):
                    pieces = [load(first + comp * SENT + i * 8) for comp in range(3)]
                    values.append(unpack_last(pieces, modes))
                fill(place, values)

    def body(side, carry):
        part = partner_ref[0, side]
        if len(gath_refs) == 1:
            source = jnp.maximum(part, 0)
            copy_side(side, lambda at: gath_refs[0][source, pl.ds(at, 8), :])
            return carry
        for slot, ref in enumerate(gath_refs):
            here = jnp.logical_and(part >= 0, jnp.bitwise_xor(part, own) == slot)

            @pl.when(here)
            def _(ref=ref):
                copy_side(side, lambda at: ref[pl.ds(at, 8), :])

        return carry

    lax.fori_loop(0, 4, body, 0)


def incoming_lines(sides, place, partner_ref, flip_ref):
    lines = []
    for side in range(4):
        glued = partner_ref[0, side] >= 0
        turned = flip_ref[0, side] == 1
        line = []
        for i in range(6):
            at = pl.multiple_of(place * SIDE + jnp.where(turned, 5 - i, i) * 8, 8)
            value = sides[side, pl.ds(at, 8), :]
            value = jnp.where(turned, reverse_rows(value), value)
            line.append(jnp.where(glued, value, 0.0))
        lines.append(line)
    return lines


def own_reaction(own_lines, rates, flags, scale):
    ex = ex_ids()
    edge = float(WEIGHTS[0])
    corner = float(STIFF[0, 0])
    lines = []
    for side in range(4):
        line = own_lines[side]
        along = line_product(line, STIFF_HAT)
        out = [
            (along[i] * edge + line[i] * (corner + rates * edge)) * float(WEIGHTS[i])
            for i in range(6)
        ]
        first = out[0] + pltpu.roll(out[5], 1, 0)
        last = out[5] + pltpu.roll(out[0], 7, 0)
        out[0] = jnp.where(ex > 0, first, 0.0)
        out[5] = jnp.where(ex < 7, last, 0.0)
        lines.append([value * (flags[side] * scale) for value in out])
    return lines


def pick(index, values):
    if isinstance(index, int):
        return values[index]
    chosen = jnp.int32(values[0])
    for place in range(1, len(values)):
        chosen = jnp.where(index == place, jnp.int32(values[place]), chosen)
    return chosen


def offset_of(place, size):
    return (0, 3, 1, 2)[place] if size == 4 else place


def block_of(place, four, size):
    return place if isinstance(four, int) else jnp.bitwise_xor(four, offset_of(place, size))


def pack_kernel(step, count, dynamic, chunk, chunks, starts, offsets, ids_ref, source_ref, *refs):
    send_refs = refs[:count]
    load = chunk == 0
    scratch = refs[-2] if load else refs[-1]
    width = scratch.shape[1]
    held_ref = refs[count] if load else source_ref
    modes = held_ref.shape[2]
    four = ids_ref[1] if dynamic else 0
    copies = []
    if load:
        for slot in range(chunks * count):
            start = pick(block_of(slot % count, four, count), starts[slot // count :: chunks])
            start = start if isinstance(start, int) else pl.multiple_of(start, LANES)
            window = source_ref.at[:, :, pl.ds(start, width)]
            copies.append(pltpu.make_async_copy(window, held_ref.at[slot], refs[-1].at[slot]))
            copies[-1].start()
    for place in range(count):
        index = block_of(place, four, count)
        table = order_table(step, pick(index, offsets[chunk::chunks]), scratch)
        if load:
            copies[place].wait()
        rows = [held_ref[chunk * count + place, comp] for comp in range(3)]
        pad = jnp.zeros((LANES - 3 * modes, width), F32)
        high, low = halves(jnp.concatenate(rows + [pad], axis=0))
        both = jnp.concatenate([high, low], axis=0)
        out = dot(table, both, ((1,), (1,)))
        out = out[:, :LANES] + out[:, LANES:]
        if not is_packed(modes):
            send_refs[place][...] = out
            continue
        values = [out[point * step : (point + 1) * step] for point in range(POINTS)]
        for at, value in enumerate(pack_lanes(values, modes)):
            send_refs[place][pl.ds(at * step, step), :] = value
    for copy in copies[count:]:
        copy.wait()


def product_kernel(modes, step, count, dynamic, role, ids_ref, *refs):
    recv_refs = refs[:count]
    inv_high, inv_low, back_high, back_low = refs[count : count + 4]
    refs = refs[count + 4 :]
    if role == 1:
        carry_ref, refs = refs[0], refs[1:]
    send_refs, refs = refs[:count], refs[count:]
    if role == 0:
        carry_ref, refs = refs[0], refs[1:]
    full, lined, phys, prod, spec = refs
    four = ids_ref[1] if dynamic else 0
    packed = is_packed(modes)
    for place in range(count):
        index = block_of(place, four, count)
        if packed:
            ready = 3 * POINTS // 4
            values = [recv_refs[place][pl.ds(at * step, step), :] for at in range(ready)]
            for at, value in enumerate(unpack_lanes(values, modes)):
                full[place, pl.ds(at * step, step), :] = value
        else:
            full[place] = recv_refs[place][...]
        first = index * LANES
        first = first if isinstance(first, int) else pl.multiple_of(first, LANES)
        lined[:, pl.ds(first, LANES)] = full[place]
    phys[...] = dot3(lined[...], inv_high[...], inv_low[...])
    width = 2 * LANES

    def field(point, comp):
        return phys[pl.ds(point * step, step), comp * LANES : (comp + 1) * LANES]

    for comp in range(3):
        wide = pl.ds(comp * width, LANES)
        for iy in range(6):
            line = []
            for ix in range(6):
                point = 6 * iy + ix
                value = field(point, comp)
                line.append(value * field(point, 0))
                prod[pl.ds(point * step, step), pl.ds(comp * width + LANES, LANES)] = (
                    value * field(point, 2)
                )
            out = line_product(line, DERIV, -1.0)
            for ix in range(6):
                prod[pl.ds((6 * iy + ix) * step, step), wide] = out[ix]
        for ix in range(6):
            line = [field(6 * iy + ix, comp) * field(6 * iy + ix, 1) for iy in range(6)]
            out = line_product(line, DERIV, -1.0)
            for iy in range(6):
                at = pl.ds((6 * iy + ix) * step, step)
                prod[at, wide] = prod[at, wide] + out[iy]
        spec[comp] = dot3(prod[:, comp * width : (comp + 1) * width], back_high[...], back_low[...])

    lane_block = lax.div(lax.broadcasted_iota(jnp.int32, (step, LANES), 1), jnp.int32(modes))
    masks = []
    shifts = []
    for place in range(count):
        index = block_of(place, four, count)
        masks.append([lane_block == lax.rem(index + comp, count) for comp in range(2)])
        shifts.append(lax.rem(LANES - index * modes, LANES))
    kept = []
    for point in range(POINTS):
        at = pl.ds(point * step, step)
        mass = float(WEIGHTS[point // 6] * WEIGHTS[point % 6])
        turned = [spec[0, at, :]]
        turned += [pltpu.roll(spec[comp, at, :], comp * modes, 1) for comp in (1, 2)]
        for place in range(count):
            mask = masks[place]
            mixed = jnp.where(mask[0], turned[0], jnp.where(mask[1], turned[1], turned[2]))
            nonlinear = pltpu.roll(mixed, shifts[place], 1)
            full[place, at, :] = mass * (REACTION * full[place, at, :] + nonlinear)
    ex = None if role is None else ex_ids()
    for place in range(count):
        values = [full[place, pl.ds(point * step, step), :] for point in range(POINTS)]
        if role is not None:
            left = jnp.zeros((8, LANES), F32)
            sent = []
            for iy in range(6):
                line = values[6 * iy : 6 * iy + 6]
                line[5] = line[5] + jnp.where(ex < 7, pltpu.roll(line[0], 7, 0), 0.0)
                if role == 0 and iy == 5:
                    for ix in range(6):
                        carry_ref[place, pl.ds(ix * 8, 8), :] = line[ix]
                    continue
                if role == 1 and iy == 0:
                    line = [line[ix] + carry_ref[place, pl.ds(ix * 8, 8), :] for ix in range(6)]
                left = jnp.where(ex == iy, pltpu.roll(line[0], iy, 0) if iy else line[0], left)
                sent += line[1:]
            values = sent + [left]
            values += [left] * (-len(values) % 4)
        for at, value in enumerate(pack_lanes(values, modes)):
            send_refs[place][pl.ds(at * step, step), :] = value


def spread_rows(values, masks):
    ex = ex_ids()
    rows = (len(values) - 1) // 5
    left = values[5 * rows]
    points = []
    for iy in range(rows):
        line = values[5 * iy : 5 * iy + 5]
        start = pltpu.roll(left, 8 - iy, 0) if iy else left
        first = jnp.where(ex == 0, start, pltpu.roll(line[4], 1, 0))
        points += [first * masks[0]] + line[:4] + [line[4] * masks[1]]
    return points


def first_kernel(modes, step, count, chunks, dynamic, lean, ids_ref, partner_ref, *refs):
    recv_refs = refs[: count * chunks]
    base_ref, lines_ref, work = refs[count * chunks :]
    four = ids_ref[1] if dynamic else 0
    rates = helmholtz_rates(ids_ref[1], modes)
    flags = glued_flags(partner_ref)
    masks = col_masks(flags)
    for place in range(count):
        block = block_of(place, four, count)
        shares = []
        for chunk in range(chunks):
            ref = recv_refs[chunk * count + place]
            ready = ref.shape[0] // step
            shares.append(
                unpack_lanes([ref[pl.ds(at * step, step), :] for at in range(ready)], modes)
            )
        if lean:
            odd = spread_rows(shares[1][:31], masks)
            shares = [spread_rows(shares[0][:26], masks) + odd[:6], odd]
        for chunk in range(chunks):
            first = (block * chunks + chunk) * step
            for point in range(POINTS):
                at = point * 64 + first
                at = at if isinstance(at, int) else pl.multiple_of(at, step)
                base_ref[pl.ds(at, step), :] = shares[chunk][point]
    if not lean:
        for ey in range(BLOCKS):
            for iy in range(6):
                first, last = join_cols(
                    get(base_ref, 6 * iy, ey), get(base_ref, 6 * iy + 5, ey), masks
                )
                put(base_ref, 6 * iy, ey, first)
                put(base_ref, 6 * iy + 5, ey, last)
    join_rows(base_ref, flags, range(1, 7, 2) if lean else range(7))
    apply_local(base_ref, work, rates, flags)
    write_lines(base_ref, lines_ref, 0, modes)
    write_lines(work, lines_ref, line_rows(modes), modes)


def sum_rows(sums):
    return [jnp.sum(value, axis=0, keepdims=True) for value in sums]


def second_kernel(modes, slots, ids_ref, partner_ref, side_ref, flip_ref, *refs):
    gath_refs = refs[:slots]
    lines_ref, _, k0_ref, k1_ref, k2_ref, next_ref, sums_ref, work, sides = refs[slots:]
    rates = helmholtz_rates(ids_ref[1], modes)
    flags = glued_flags(partner_ref)
    collect_sides(gath_refs, ids_ref[0], partner_ref, side_ref, sides, modes)
    back = own_reaction(load_lines(lines_ref, modes), rates, flags, 1.0)
    add_lines(k0_ref, incoming_lines(sides, 0, partner_ref, flip_ref))
    apply_local(k0_ref, work, rates, flags)
    add_lines(work, add_all(incoming_lines(sides, 1, partner_ref, flip_ref), back))
    sums = apply_local(
        k1_ref, work, rates, flags,
        terms=[(1.0 / SPREAD, work), (-CENTRE / SPREAD, k0_ref)],
        products=[(1, 1), (1, -1), (-1, -1)],
    )
    write_lines(work, next_ref, 0, modes)
    apply_local(
        k2_ref, work, rates, flags,
        terms=[(TWICE, work), (-CENTRE * TWICE, k1_ref), (-1.0, k0_ref)],
    )
    write_lines(work, next_ref, line_rows(modes), modes)
    sums_ref[...] = jnp.concatenate(sum_rows(sums) + [jnp.zeros((5, LANES), F32)], axis=0)


def third_kernel(modes, slots, ids_ref, partner_ref, side_ref, flip_ref, *refs):
    gath_refs = refs[:slots]
    lines_ref, k1_ref, sums_ref, _ = refs[slots : slots + 4]
    k2_ref, k3_ref, a3_ref, next_ref, work, sides = refs[slots + 4 :]
    rates = helmholtz_rates(ids_ref[1], modes)
    flags = glued_flags(partner_ref)
    collect_sides(gath_refs, ids_ref[0], partner_ref, side_ref, sides, modes)
    back = own_reaction(load_lines(lines_ref, modes), rates, flags, TWICE)
    incoming = incoming_lines(sides, 0, partner_ref, flip_ref)
    add_lines(k2_ref, [[value * TWICE for value in line] for line in incoming])
    apply_local(k2_ref, work, rates, flags)
    add_lines(work, add_all(incoming_lines(sides, 1, partner_ref, flip_ref), back))
    sums = apply_local(
        k3_ref, a3_ref, rates, flags,
        terms=[(TWICE, work), (-CENTRE * TWICE, k2_ref), (-1.0, k1_ref)],
        products=[(2, 1), (1, 1), (1, -1), (-1, -1)],
        energy=True,
    )
    write_lines(a3_ref, next_ref, 0, modes)
    next_ref[pl.ds(line_rows(modes), SUM_ROWS), :] = jnp.concatenate(
        [sums_ref[:3, :]] + sum_rows(sums), axis=0
    )


def turn_kernel(starts, offsets, fields, has_scatter, *refs):
    field_refs = refs[:fields]
    out_refs = refs[fields : 2 * fields]
    scratch, rows = refs[-2:]
    step = rows.shape[0] // POINTS
    used = out_refs[0].shape[0]
    width = scratch.shape[1]
    for out_ref in out_refs:
        out_ref[...] = jnp.zeros(out_ref.shape, F32)
    for unit in range(len(starts)):
        table = order_table(step, offsets[unit], scratch)
        for field_ref, out_ref in zip(field_refs, out_refs):
            for point in range(POINTS):
                rows[pl.ds(point * step, step), :] = field_ref[pl.ds(point * 64 + unit * step, step), :]
            high, low = halves(jnp.transpose(rows[...])[:used])
            both = jnp.concatenate([high, low], axis=0)
            out = dot(both, table, ((1,), (0,)))
            window = pl.ds(starts[unit], width)
            out_ref[:, window] = out_ref[:, window] + (out[:used] + out[used:])
    if has_scatter:
        scatter_ref = refs[2 * fields]
        place = lax.broadcasted_iota(jnp.int32, (SIDE, NODES), 0)
        at = 6 * jnp.bitwise_and(place, 7) + lax.shift_right_logical(place, 3)
        node = lax.broadcasted_iota(jnp.int32, (SIDE, NODES), 1)
        targets = (at, at * SIDE + SIDE - 1, at + (SIDE - 1) * SIDE, at * SIDE)
        for side, target in enumerate(targets):
            scatter_ref[side * SIDE : (side + 1) * SIDE, :] = jnp.where(
                node == target, 1.0, 0.0
            ).astype(BF16)


def conjugate_coefficients(gram, energy):
    zero = jnp.zeros_like(energy)

    def image(vec):
        out = [zero] * 5
        for j in range(4):
            if vec[j] is None:
                continue
            out[j] = out[j] + CENTRE * vec[j]
            out[j + 1] = out[j + 1] + (SPREAD if j == 0 else 0.5 * SPREAD) * vec[j]
            if j > 0:
                out[j - 1] = out[j - 1] + 0.5 * SPREAD * vec[j]
        return out

    def inner(left, right):
        total = zero
        for i in range(4):
            for j in range(4):
                if left[i] is not None and right[j] is not None:
                    total = total + left[i] * right[j] * gram[i][j]
        return total

    moments = [[None] * 4 for _ in range(4)]
    for j in range(3):
        column = image([jnp.ones_like(energy) if i == j else None for i in range(4)])
        for i in range(4):
            total = zero
            for m in range(max(j - 1, 0), j + 2):
                total = total + column[m] * gram[i][m]
            moments[i][j] = total
    for i in range(3):
        moments[i][3] = moments[3][i]
    moments[3][3] = energy

    def pad(vec, size):
        return [vec[i] if i < size else None for i in range(4)]

    residual = [jnp.ones_like(energy), zero, zero, zero, zero]
    direction = list(residual)
    solution = [zero] * 4
    norm_now = gram[0][0]
    for step in range(ITERS):
        trimmed = pad(direction, step + 1)
        bend = zero
        for i in range(step + 1):
            for j in range(step + 1):
                bend = bend + direction[i] * direction[j] * moments[i][j]
        alpha = norm_now / bend
        moved = image(trimmed)
        for i in range(step + 1):
            solution[i] = solution[i] + alpha * direction[i]
        for i in range(step + 2):
            residual[i] = residual[i] - alpha * moved[i]
        if step < ITERS - 1:
            kept = pad(residual, step + 2)
            norm_next = inner(kept, kept)
            ratio = norm_next / norm_now
            direction = [residual[i] + ratio * direction[i] for i in range(5)]
            norm_now = norm_next
    return solution, residual


def last_kernel(slots, ids_ref, partner_ref, side_ref, flip_ref, *refs):
    gath_refs = refs[:slots]
    turned = refs[slots : slots + 5]
    scatter_ref, sol_out, res_out, lines, sides, sol_ref, res_ref, sems = refs[slots + 5 :]
    modes = sol_ref.shape[1]
    used = 3 * modes
    where = pl.ds(line_rows(modes), SUM_ROWS)
    if slots == 1:
        parts = [gath_refs[0][part, where, :] for part in range(gath_refs[0].shape[0])]
    else:
        parts = [ref[where, :] for ref in gath_refs]
    sums = functools.reduce(lambda left, right: left + right, parts)
    collect_sides(gath_refs, ids_ref[0], partner_ref, side_ref, sides, modes)
    g00, g01, g11, g12, g22, g23, g33, energy = [
        jnp.broadcast_to(sums[place : place + 1, :], (8, LANES)) for place in range(8)
    ]
    g02 = 2.0 * g11 - g00
    g03 = 2.0 * g12 - g01
    g13 = (g22 - g00) + g11
    gram = [
        [g00, g01, g02, g03],
        [g01, g11, g12, g13],
        [g02, g12, g22, g23],
        [g03, g13, g23, g33],
    ]
    solution, residual = conjugate_coefficients(gram, energy)
    on_a3 = residual[4] * TWICE
    on_k3 = residual[3] - on_a3 * CENTRE
    on_k2 = residual[2] - residual[4]
    factors = list(solution) + [residual[0], residual[1], on_k2, on_k3, on_a3]
    columns = jnp.transpose(
        jnp.concatenate([value[:1] for value in factors] + [jnp.zeros((LANES - 9, LANES), F32)], axis=0)
    )
    incoming = incoming_lines(sides, 0, partner_ref, flip_ref)
    for side in range(4):
        for i in range(6):
            lines[pl.ds(side * SIDE + i * 8, 8), :] = incoming[side][i] * on_a3
    high, low = halves(jnp.transpose(lines[...])[:used])
    added = dot(jnp.concatenate([high, low], axis=0), scatter_ref[...], ((1,), (0,)))
    copies = []
    for comp in range(3):
        for first in range(0, modes, 8):
            at = comp * modes + first
            rows = [ref[at : at + 8, :] for ref in turned]
            scale = [columns[at : at + 8, place : place + 1] for place in range(9)]
            sol_ref[comp, first : first + 8, :] = (scale[0] * rows[0] + scale[1] * rows[1]) + (
                scale[2] * rows[2] + scale[3] * rows[3]
            )
            res_ref[comp, first : first + 8, :] = (
                (scale[4] * rows[0] + scale[5] * rows[1])
                + (scale[6] * rows[2] + scale[7] * rows[3])
                + (scale[8] * rows[4] + (added[at : at + 8] + added[used + at : used + at + 8]))
            )
        for place, (buffer, out) in enumerate(((sol_ref, sol_out), (res_ref, res_out))):
            copies.append(
                pltpu.make_async_copy(buffer.at[comp], out.at[comp], sems.at[2 * comp + place])
            )
            copies[-1].start()
    for copy in copies:
        copy.wait()


def call(kernel, name, out_shapes, args, scratch, scalars=0, keep=True, aliases=None, outside=False):
    smem = pl.BlockSpec(memory_space=pltpu.SMEM)
    vmem = pl.BlockSpec(memory_space=pltpu.VMEM)
    shapes = [shape if isinstance(shape, jax.ShapeDtypeStruct) else jax.ShapeDtypeStruct(shape, F32) for shape in out_shapes]
    return pl.pallas_call(
        kernel,
        name=name,
        out_shape=[pltpu.VMEM(one.shape, one.dtype) if keep else one for one in shapes],
        in_specs=[smem] * scalars + [pl.BlockSpec(memory_space=pltpu.HBM) if outside else vmem] * (len(args) - scalars),
        out_specs=[vmem if keep else pl.BlockSpec(memory_space=pltpu.HBM)] * len(out_shapes),
        scratch_shapes=[pltpu.VMEM(one, F32) if isinstance(one, tuple) else one for one in scratch],
        input_output_aliases=aliases or {},
        compiler_params=pltpu.CompilerParams(vmem_limit_bytes=VMEM_LIMIT),
    )(*args[:scalars], *[held(arg, pltpu.HBM if outside else pltpu.VMEM) for arg in args[scalars:]])


def held(arg, space):
    return arg if isinstance(arg, np.ndarray) else pltpu.with_memory_space_constraint(arg, space)


def swap_blocks(blocks, dynamic):
    if not dynamic:
        stacked = lax.all_to_all(jnp.stack(blocks), "four", split_axis=0, concat_axis=0, tiled=True)
        return [stacked[place] for place in range(len(blocks))]
    size = len(blocks)
    swapped = list(blocks)
    for place in range(size - 1, 0, -1):
        swapped[place] = lax.ppermute(blocks[place], "four", [(i, i ^ offset_of(place, size)) for i in range(size)])
    return swapped


def share_lines(lines, beside=()):
    parts = lax.axis_size("dom")
    if parts != 8:
        return [lax.all_gather(lines, "dom", axis=0, tiled=False)], list(beside)
    slots = [lines] + [None] * (parts - 1)
    for slot in range(2, parts, 2):
        slots[slot] = lax.ppermute(lines, "dom", [(i, i ^ slot) for i in range(parts)])
        if beside and slot == parts - 2:
            slots[slot], *beside = lax.optimization_barrier((slots[slot], *beside))
    for slot in range(0, parts, 2):
        slots[slot + 1] = lax.ppermute(slots[slot], "dom", [(i, i ^ 1) for i in range(parts)])
    return slots, list(beside)


def shards(velocity, partner, partner_side, flipped):
    modes = velocity.shape[1]
    count = lax.axis_size("four")
    step, chunks = chunk_sizes(count)
    rows = POINTS * step
    sent_rows = 3 * rows // 4 if is_packed(modes) else rows
    dynamic = step == BLOCKS
    (inv_high, inv_low), (back_high, back_low) = transform_tables(count)
    starts, offsets = unit_windows(count)
    table = (rows, 3 * LANES)
    ids = jnp.stack([lax.axis_index("dom"), lax.axis_index("four")]).astype(jnp.int32)
    field = (NODES, LANES)
    blocks = [(sent_rows, LANES)] * count
    lined = line_rows(modes)

    lean = dynamic and chunks == 2 and is_packed(modes)
    spread = []
    source = velocity
    for chunk in range(chunks):
        load = chunk == 0
        sent = call(
            functools.partial(pack_kernel, step, count, dynamic, chunk, chunks, starts, offsets),
            "pack",
            blocks + [(chunks * count, 3, modes, 3 * LANES)] * load,
            (ids, source),
            [table] + [pltpu.SemaphoreType.DMA((chunks * count,))] * load,
            scalars=1,
            outside=load,
        )
        if load:
            *sent, source = sent
        spread.append(swap_blocks(sent, dynamic))
    local = []
    carry = []
    for chunk in range(chunks):
        role = chunk if lean else None
        out = [((21, 24)[chunk] * step, LANES)] * count if lean else blocks
        sent = call(
            functools.partial(product_kernel, modes, step, count, dynamic, role),
            "products",
            out + [(count, SIDE, LANES)] * (role == 0),
            (ids, *spread[chunk], inv_high, inv_low, back_high, back_low, *carry),
            [
                (count, rows, LANES),
                (rows, count * LANES),
                (rows, 3 * LANES),
                (rows, 6 * LANES),
                (3, rows, LANES),
            ],
            scalars=1,
        )
        if role == 0:
            *sent, held_row = sent
            carry = [held_row]
        local += swap_blocks(sent, dynamic)

    base, lines = call(
        functools.partial(first_kernel, modes, step, count, chunks, dynamic, lean),
        "first",
        [field, (2 * lined, LANES)],
        (ids, partner, *local),
        [field],
        scalars=2,
    )
    tables = (ids, partner, partner_side, flipped)
    gathered, _ = share_lines(lines)
    slots = len(gathered)
    k0, k1, base, lines, sums = call(
        functools.partial(second_kernel, modes, slots),
        "second",
        [field, field, field, (2 * lined, LANES), (8, LANES)],
        (*tables, *gathered, lines, base),
        [field, (4, 2 * SIDE, LANES)],
        scalars=4,
        aliases={4 + slots + 1: 0},
    )
    flat = (3 * modes, NODES)
    turned = call(
        functools.partial(turn_kernel, starts, offsets, 2, True),
        "turn",
        [flat, flat, jax.ShapeDtypeStruct((4 * SIDE, NODES), BF16)],
        (k0, k1),
        [table, (rows, LANES)],
    )
    gathered, (t0, t1, scatter) = share_lines(lines, turned)
    k2, k3, a3, lines = call(
        functools.partial(third_kernel, modes, slots),
        "third",
        [field, field, field, (lined + SUM_ROWS, LANES)],
        (*tables, *gathered, lines, k1, sums, base),
        [field, (4, 2 * SIDE, LANES)],
        scalars=4,
        aliases={4 + slots + 3: 0},
    )
    turned = call(
        functools.partial(turn_kernel, starts, offsets, 3, False),
        "turn",
        [flat, flat, flat],
        (k2, k3, a3),
        [table, (rows, LANES)],
    )
    gathered, (t2, t3, ta) = share_lines(lines, turned)
    outs = call(
        functools.partial(last_kernel, slots),
        "last",
        [velocity.shape, velocity.shape],
        (*tables, *gathered, t0, t1, t2, t3, ta, scatter),
        [
            (4 * SIDE, LANES),
            (4, SIDE, LANES),
            velocity.shape,
            velocity.shape,
            pltpu.SemaphoreType.DMA((6,)),
        ],
        scalars=4,
        keep=False,
    )
    return tuple(outs)


def solution(mesh):
    return jax.shard_map(
        shards,
        mesh=mesh,
        in_specs=(P(None, "four", "dom"), P("dom", None), P("dom", None), P("dom", None)),
        out_specs=(P(None, "four", "dom"), P(None, "four", "dom")),
        check_vma=False,
    )
```

```python
import functools
import math

import jax
import jax.numpy as jnp
import numpy as np
from jax import lax
from jax.experimental import pallas as pl
from jax.experimental.pallas import tpu as pltpu
from jax.sharding import PartitionSpec as P

ITERS = 4
REACTION = 2.0
WAVE_STEP = 0.0625
LANES = 128
POINTS = 36
BLOCKS = 8
SIDE = 48
SENT = 40
NODES = 2304
CENTRE = 9.0
SPREAD = 9.0
TWICE = 2.0 / SPREAD
SUM_ROWS = 8
VMEM_LIMIT = 32 * 1024 * 1024
F32 = jnp.float32
BF16 = jnp.bfloat16


def gll_tables():
    inner_near = math.sqrt(1.0 / 3.0 - 2.0 * math.sqrt(7.0) / 21.0)
    inner_far = math.sqrt(1.0 / 3.0 + 2.0 * math.sqrt(7.0) / 21.0)
    points = np.array([-1.0, -inner_far, -inner_near, inner_near, inner_far, 1.0])
    values = (63.0 * points**5 - 70.0 * points**3 + 15.0 * points) / 8.0
    weights = 2.0 / (30.0 * values * values)
    spacing = points[:, None] - points[None, :]
    same_point = spacing == 0.0
    derivative = np.where(
        same_point, 0.0, values[:, None] / (values[None, :] * np.where(same_point, 1.0, spacing))
    )
    end_fix = np.array([-7.5, 0.0, 0.0, 0.0, 0.0, 7.5])
    derivative = derivative + np.eye(6) * end_fix[None, :]
    stiffness = derivative.T @ (weights[:, None] * derivative)
    return (weights, derivative, stiffness)


WEIGHTS, DERIV, STIFF = gll_tables()
STIFF_HAT = STIFF / WEIGHTS[:, None]


def fourier_tables(planes):
    plane_ids = np.arange(planes)
    mode_ids = np.arange(planes)
    waves = np.where(mode_ids < 2, 0, mode_ids // 2)
    angle = (plane_ids[:, None] * waves[None, :] % planes) * (2.0 * math.pi / planes)
    is_sine = (mode_ids % 2 == 1) & (mode_ids >= 2)
    basis = np.where(is_sine[None, :], np.sin(angle), np.cos(angle))
    alternating = np.where(plane_ids % 2 == 0, 1.0, -1.0)
    basis = np.where(mode_ids[None, :] == 1, alternating[:, None], basis)
    row_scale = np.where(mode_ids < 2, 1.0, 2.0) / planes
    forward = basis.T * row_scale[:, None]
    rates = (np.arange(planes // 2) * WAVE_STEP)[:, None]
    forward_z = np.zeros_like(forward)
    forward_z[0::2] = rates * forward[1::2]
    forward_z[1::2] = -rates * forward[0::2]
    forward_z[0:2] = 0.0
    return (basis, forward, forward_z)


def split_table(table):
    high = np.asarray(table, np.float32).astype(jnp.bfloat16)
    low = (np.asarray(table, np.float64) - high.astype(np.float64)).astype(np.float32)
    return high, low.astype(jnp.bfloat16)


def transform_tables(count):
    planes = LANES
    modes = planes // count
    basis, forward, forward_z = fourier_tables(planes)
    inverse = np.zeros((count * LANES, 3 * planes))
    for block in range(count):
        ids = slice(block * modes, (block + 1) * modes)
        for comp in range(3):
            at = block * LANES + comp * modes
            inverse[at : at + modes, comp * planes : (comp + 1) * planes] = basis[:, ids].T
    back = -np.concatenate([forward.T, forward_z.T], axis=0)
    return split_table(inverse), split_table(back)


def chunk_sizes(count):
    group = BLOCKS * BLOCKS // count
    step = min(group, BLOCKS)
    return step, group // step


def unit_windows(count):
    step, _ = chunk_sizes(count)
    starts = []
    offsets = []
    for index in range(BLOCKS * BLOCKS // step):
        element = index * step
        first = element // BLOCKS * 6 * SIDE
        starts.append(first // LANES * LANES)
        offsets.append(first % LANES + 6 * (element % BLOCKS))
    return starts, offsets


def order_table(step, offset, scratch):
    width = scratch.shape[1]
    lane = lax.broadcasted_iota(jnp.int32, (step, width), 1)
    gap = lane - 6 * lax.broadcasted_iota(jnp.int32, (step, width), 0) - offset
    for point in range(POINTS):
        hit = gap == point // 6 * SIDE + point % 6
        scratch[pl.ds(point * step, step), :] = jnp.where(hit, 1.0, 0.0)
    return scratch[...].astype(BF16)


def halves(value):
    high = value.astype(BF16)
    low = (value - high.astype(F32)).astype(BF16)
    return high, low


def dot(left, right, dims):
    return lax.dot_general(left, right, (dims, ((), ())), preferred_element_type=F32)


def dot3(left, right_high, right_low):
    high, low = halves(left)
    dims = ((1,), (0,))
    return dot(high, right_high, dims) + (dot(low, right_high, dims) + dot(high, right_low, dims))


def start_of(point, ey):
    return pl.multiple_of(point * 64 + ey * 8, 8)


def get(ref, point, ey):
    return ref[pl.ds(start_of(point, ey), 8), :]


def put(ref, point, ey, value):
    ref[pl.ds(start_of(point, ey), 8), :] = value


def ex_ids():
    return lax.broadcasted_iota(jnp.int32, (8, LANES), 0)


def helmholtz_rates(four, modes):
    lane = lax.broadcasted_iota(jnp.int32, (8, LANES), 1)
    mode = four * modes + lax.rem(lane, jnp.int32(modes))
    wave = jnp.where(mode == 0, 0, jnp.where(mode == 1, LANES // 2, lax.div(mode, jnp.int32(2))))
    scaled = wave.astype(F32) * WAVE_STEP
    return REACTION + scaled * scaled


def glued_flags(partner_ref):
    return [jnp.where(partner_ref[0, side] >= 0, 1.0, 0.0).astype(F32) for side in range(4)]


def col_masks(flags):
    ex = ex_ids()
    return jnp.where(ex == 0, flags[3], 1.0), jnp.where(ex == 7, flags[1], 1.0)


def join_cols(first, last, masks):
    ex = ex_ids()
    from_right = jnp.where(ex < 7, pltpu.roll(first, 7, 0), 0.0)
    from_left = jnp.where(ex > 0, pltpu.roll(last, 1, 0), 0.0)
    return (first + from_left) * masks[0], (last + from_right) * masks[1]


def join_rows(ref, flags, pairs=range(7)):
    ex = ex_ids()
    not_first = jnp.where(ex == 0, 0.0, 1.0)
    not_last = jnp.where(ex == 7, 0.0, 1.0)
    for ix in range(6):
        for ey in pairs:
            total = get(ref, 30 + ix, ey) + get(ref, ix, ey + 1)
            put(ref, 30 + ix, ey, total)
            put(ref, ix, ey + 1, total)
        low = get(ref, ix, 0) * flags[0]
        high = get(ref, 30 + ix, 7) * flags[2]
        if ix == 0:
            low, high = low * not_first, high * not_first
        if ix == 5:
            low, high = low * not_last, high * not_last
        put(ref, ix, 0, low)
        put(ref, 30 + ix, 7, high)


def line_product(line, table, mirrored=1.0):
    sums = [line[j] + line[5 - j] for j in range(3)]
    gaps = [line[j] - line[5 - j] for j in range(3)]
    out = [None] * 6
    for i in range(3):
        even = None
        odd = None
        for j in range(3):
            even_term = sums[j] * float(0.5 * (table[i, j] + table[i, 5 - j]))
            odd_term = gaps[j] * float(0.5 * (table[i, j] - table[i, 5 - j]))
            even = even_term if even is None else even + even_term
            odd = odd_term if odd is None else odd + odd_term
        out[i] = even + odd
        out[5 - i] = even - odd if mirrored > 0 else odd - even
    return out


def apply_local(src, dst, rates, flags, terms=(), products=(), energy=False):
    masks = col_masks(flags)

    def body(ey, sums):
        sums = list(sums)
        for ix in range(6):
            line = []
            for iy in range(6):
                point = 6 * iy + ix
                if not terms:
                    line.append(get(src, point, ey))
                    continue
                values = [get(ref, point, ey) for _, ref in terms]
                value = None
                for (factor, _), part in zip(terms, values):
                    part = -part if factor == -1.0 else part * factor
                    value = part if value is None else value + part
                put(src, point, ey, value)
                line.append(value)
                values.append(value)
                ends = (iy in (0, 5)) + (ix in (0, 5))
                for place, (left, right) in enumerate(products):
                    both = values[left] * values[right]
                    sums[place] = sums[place] + (both * (0.5**ends) if ends else both)
            out = line_product(line, STIFF_HAT)
            for iy in range(6):
                put(dst, 6 * iy + ix, ey, out[iy] + rates * line[iy])
        for iy in range(6):
            line = [get(src, 6 * iy + ix, ey) for ix in range(6)]
            out = line_product(line, STIFF_HAT)
            full = [
                (get(dst, 6 * iy + ix, ey) + out[ix]) * float(WEIGHTS[iy] * WEIGHTS[ix])
                for ix in range(6)
            ]
            if energy:
                for ix in range(6):
                    sums[-1] = sums[-1] + full[ix] * line[ix]
            full[0], full[5] = join_cols(full[0], full[5], masks)
            for ix in range(6):
                put(dst, 6 * iy + ix, ey, full[ix])
        return tuple(sums)

    zero = jnp.zeros((8, LANES), F32)
    sums = lax.fori_loop(0, BLOCKS, body, (zero,) * (len(products) + int(energy)), unroll=2)
    join_rows(dst, flags)
    return sums


def side_slice(side, i):
    if side == 0:
        return pl.ds(i * 64, 8)
    if side == 2:
        return pl.ds((30 + i) * 64 + 56, 8)
    if side == 1:
        return pl.ds((6 * i + 5) * 64 + 7, 8, stride=8)
    return pl.ds(6 * i * 64, 8, stride=8)


def read_line(ref, side):
    return [ref[side_slice(side, i), :] for i in range(6)]


def lane_ids():
    return lax.broadcasted_iota(jnp.int32, (8, LANES), 1)


def is_packed(modes):
    return 3 * modes + modes == LANES


def pack_lanes(values, modes):
    if not is_packed(modes):
        return values
    third = len(values) // 4
    inside = lane_ids() < 3 * modes
    return [
        jnp.where(
            inside,
            values[comp * third + at],
            pltpu.roll(values[3 * third + at], (3 - comp) * modes, 1),
        )
        for comp in range(3)
        for at in range(third)
    ]


def unpack_last(pieces, modes):
    block = lax.div(lane_ids(), jnp.int32(modes))
    turned = [pltpu.roll(pieces[comp], (comp + 1) * modes, 1) for comp in range(3)]
    return jnp.where(block == 0, turned[0], jnp.where(block == 1, turned[1], turned[2]))


def unpack_lanes(values, modes):
    if not is_packed(modes):
        return values
    third = len(values) // 3
    return values + [
        unpack_last([values[comp * third + at] for comp in range(3)], modes) for at in range(third)
    ]


def line_rows(modes):
    return 3 * SENT if is_packed(modes) else 4 * SENT


def first_points(last_points):
    return jnp.where(ex_ids() > 0, pltpu.roll(last_points, 1, 0), 0.0)


def write_lines(ref, lines_ref, base, modes):
    values = []
    for side in range(4):
        values += read_line(ref, side)[1:]
    for at, value in enumerate(pack_lanes(values, modes)):
        lines_ref[pl.ds(base + at * 8, 8), :] = value


def load_lines(lines_ref, modes):
    count = line_rows(modes) // 8
    values = unpack_lanes([lines_ref[pl.ds(at * 8, 8), :] for at in range(count)], modes)
    sides = [values[side * 5 : side * 5 + 5] for side in range(4)]
    return [[first_points(side[4])] + side for side in sides]


def add_lines(ref, lines):
    for side in range(4):
        for i in range(6):
            where = side_slice(side, i)
            ref[where, :] = ref[where, :] + lines[side][i]


def add_all(left, right):
    return [[a + b for a, b in zip(one, two)] for one, two in zip(left, right)]


def reverse_rows(value):
    ex = ex_ids()
    value = pltpu.roll(value, 4, 0)
    value = jnp.where((ex & 2) == 0, pltpu.roll(value, 6, 0), pltpu.roll(value, 2, 0))
    return jnp.where((ex & 1) == 0, pltpu.roll(value, 7, 0), pltpu.roll(value, 1, 0))


def collect_sides(gath_refs, own, partner_ref, side_ref, sides, modes):
    sets = sides.shape[1] // SIDE
    step = line_rows(modes)

    def copy_side(side, load):
        there = jnp.maximum(side_ref[0, side], 0)

        def fill(place, values):
            for i, value in enumerate([first_points(values[4])] + values):
                sides[side, pl.ds(place * SIDE + i * 8, 8), :] = value

        def plain():
            for place in range(sets):
                first = place * step + there * SENT
                fill(place, [load(pl.multiple_of(first + i * 8, 8)) for i in range(5)])

        if not is_packed(modes):
            plain()
            return
        pl.when(there < 3)(plain)

        @pl.when(there == 3)
        def _():
            for place in range(sets):
                first = place * step
                values = []
                for i in range(5):
                    pieces = [load(first + comp * SENT + i * 8) for comp in range(3)]
                    values.append(unpack_last(pieces, modes))
                fill(place, values)

    def body(side, carry):
        part = partner_ref[0, side]
        if len(gath_refs) == 1:
            source = jnp.maximum(part, 0)
            copy_side(side, lambda at: gath_refs[0][source, pl.ds(at, 8), :])
            return carry
        for slot, ref in enumerate(gath_refs):
            here = jnp.logical_and(part >= 0, jnp.bitwise_xor(part, own) == slot)

            @pl.when(here)
            def _(ref=ref):
                copy_side(side, lambda at: ref[pl.ds(at, 8), :])

        return carry

    lax.fori_loop(0, 4, body, 0)


def incoming_lines(sides, place, partner_ref, flip_ref):
    lines = []
    for side in range(4):
        glued = partner_ref[0, side] >= 0
        turned = flip_ref[0, side] == 1
        line = []
        for i in range(6):
            at = pl.multiple_of(place * SIDE + jnp.where(turned, 5 - i, i) * 8, 8)
            value = sides[side, pl.ds(at, 8), :]
            value = jnp.where(turned, reverse_rows(value), value)
            line.append(jnp.where(glued, value, 0.0))
        lines.append(line)
    return lines


def own_reaction(own_lines, rates, flags, scale):
    ex = ex_ids()
    edge = float(WEIGHTS[0])
    corner = float(STIFF[0, 0])
    lines = []
    for side in range(4):
        line = own_lines[side]
        along = line_product(line, STIFF_HAT)
        out = [
            (along[i] * edge + line[i] * (corner + rates * edge)) * float(WEIGHTS[i])
            for i in range(6)
        ]
        first = out[0] + pltpu.roll(out[5], 1, 0)
        last = out[5] + pltpu.roll(out[0], 7, 0)
        out[0] = jnp.where(ex > 0, first, 0.0)
        out[5] = jnp.where(ex < 7, last, 0.0)
        lines.append([value * (flags[side] * scale) for value in out])
    return lines


def pick(index, values):
    if isinstance(index, int):
        return values[index]
    chosen = jnp.int32(values[0])
    for place in range(1, len(values)):
        chosen = jnp.where(index == place, jnp.int32(values[place]), chosen)
    return chosen


def offset_of(place, size):
    return (0, 3, 1, 2)[place] if size == 4 else place


def block_of(place, four, size):
    return place if isinstance(four, int) else jnp.bitwise_xor(four, offset_of(place, size))


def pack_kernel(step, count, dynamic, chunk, chunks, starts, offsets, ids_ref, source_ref, *refs):
    send_refs = refs[:count]
    load = chunk == 0
    scratch = refs[-2] if load else refs[-1]
    width = scratch.shape[1]
    held_ref = refs[count] if load else source_ref
    modes = held_ref.shape[1]
    four = ids_ref[1] if dynamic else 0
    copies = []
    if load:
        for slot in range(3 * modes // 8):
            at = slot // (modes // 8), pl.ds(slot % (modes // 8) * 8, 8)
            copies.append(
                pltpu.make_async_copy(source_ref.at[at], held_ref.at[at], refs[-1].at[slot])
            )
            copies[-1].start()
    for place in range(count):
        index = block_of(place, four, count)
        table = order_table(step, pick(index, offsets[chunk::chunks]), scratch)
        if place == 0:
            for copy in copies:
                copy.wait()
        start = pick(index, starts[chunk::chunks])
        start = start if isinstance(start, int) else pl.multiple_of(start, LANES)
        rows = [held_ref[comp, :, pl.ds(start, width)] for comp in range(3)]
        pad = jnp.zeros((LANES - 3 * modes, width), F32)
        high, low = halves(jnp.concatenate(rows + [pad], axis=0))
        both = jnp.concatenate([high, low], axis=0)
        out = dot(table, both, ((1,), (1,)))
        out = out[:, :LANES] + out[:, LANES:]
        if not is_packed(modes):
            send_refs[place][...] = out
            continue
        values = [out[point * step : (point + 1) * step] for point in range(POINTS)]
        for at, value in enumerate(pack_lanes(values, modes)):
            send_refs[place][pl.ds(at * step, step), :] = value


def product_kernel(modes, step, count, dynamic, role, ids_ref, *refs):
    recv_refs = refs[:count]
    inv_high, inv_low, back_high, back_low = refs[count : count + 4]
    refs = refs[count + 4 :]
    if role == 1:
        carry_ref, refs = refs[0], refs[1:]
    send_refs, refs = refs[:count], refs[count:]
    if role == 0:
        carry_ref, refs = refs[0], refs[1:]
    full, lined, phys, prod, spec = refs
    four = ids_ref[1] if dynamic else 0
    packed = is_packed(modes)
    for place in range(count):
        index = block_of(place, four, count)
        if packed:
            ready = 3 * POINTS // 4
            values = [recv_refs[place][pl.ds(at * step, step), :] for at in range(ready)]
            for at, value in enumerate(unpack_lanes(values, modes)):
                full[place, pl.ds(at * step, step), :] = value
        else:
            full[place] = recv_refs[place][...]
        first = index * LANES
        first = first if isinstance(first, int) else pl.multiple_of(first, LANES)
        lined[:, pl.ds(first, LANES)] = full[place]
    phys[...] = dot3(lined[...], inv_high[...], inv_low[...])
    width = 2 * LANES

    def field(point, comp):
        return phys[pl.ds(point * step, step), comp * LANES : (comp + 1) * LANES]

    for comp in range(3):
        wide = pl.ds(comp * width, LANES)
        for iy in range(6):
            line = []
            for ix in range(6):
                point = 6 * iy + ix
                value = field(point, comp)
                line.append(value * field(point, 0))
                prod[pl.ds(point * step, step), pl.ds(comp * width + LANES, LANES)] = (
                    value * field(point, 2)
                )
            out = line_product(line, DERIV, -1.0)
            for ix in range(6):
                prod[pl.ds((6 * iy + ix) * step, step), wide] = out[ix]
        for ix in range(6):
            line = [field(6 * iy + ix, comp) * field(6 * iy + ix, 1) for iy in range(6)]
            out = line_product(line, DERIV, -1.0)
            for iy in range(6):
                at = pl.ds((6 * iy + ix) * step, step)
                prod[at, wide] = prod[at, wide] + out[iy]
        spec[comp] = dot3(prod[:, comp * width : (comp + 1) * width], back_high[...], back_low[...])

    lane_block = lax.div(lax.broadcasted_iota(jnp.int32, (step, LANES), 1), jnp.int32(modes))
    masks = []
    shifts = []
    for place in range(count):
        index = block_of(place, four, count)
        masks.append([lane_block == lax.rem(index + comp, count) for comp in range(2)])
        shifts.append(lax.rem(LANES - index * modes, LANES))
    kept = []
    for point in range(POINTS):
        at = pl.ds(point * step, step)
        mass = float(WEIGHTS[point // 6] * WEIGHTS[point % 6])
        turned = [spec[0, at, :]]
        turned += [pltpu.roll(spec[comp, at, :], comp * modes, 1) for comp in (1, 2)]
        for place in range(count):
            mask = masks[place]
            mixed = jnp.where(mask[0], turned[0], jnp.where(mask[1], turned[1], turned[2]))
            nonlinear = pltpu.roll(mixed, shifts[place], 1)
            full[place, at, :] = mass * (REACTION * full[place, at, :] + nonlinear)
    ex = None if role is None else ex_ids()
    for place in range(count):
        values = [full[place, pl.ds(point * step, step), :] for point in range(POINTS)]
        if role is not None:
            left = jnp.zeros((8, LANES), F32)
            sent = []
            for iy in range(6):
                line = values[6 * iy : 6 * iy + 6]
                line[5] = line[5] + jnp.where(ex < 7, pltpu.roll(line[0], 7, 0), 0.0)
                if role == 0 and iy == 5:
                    for ix in range(6):
                        carry_ref[place, pl.ds(ix * 8, 8), :] = line[ix]
                    continue
                if role == 1 and iy == 0:
                    line = [line[ix] + carry_ref[place, pl.ds(ix * 8, 8), :] for ix in range(6)]
                left = jnp.where(ex == iy, pltpu.roll(line[0], iy, 0) if iy else line[0], left)
                sent += line[1:]
            values = sent + [left]
            values += [left] * (-len(values) % 4)
        for at, value in enumerate(pack_lanes(values, modes)):
            send_refs[place][pl.ds(at * step, step), :] = value


def spread_rows(values, masks):
    ex = ex_ids()
    rows = (len(values) - 1) // 5
    left = values[5 * rows]
    points = []
    for iy in range(rows):
        line = values[5 * iy : 5 * iy + 5]
        start = pltpu.roll(left, 8 - iy, 0) if iy else left
        first = jnp.where(ex == 0, start, pltpu.roll(line[4], 1, 0))
        points += [first * masks[0]] + line[:4] + [line[4] * masks[1]]
    return points


def first_kernel(modes, step, count, chunks, dynamic, lean, ids_ref, partner_ref, *refs):
    recv_refs = refs[: count * chunks]
    base_ref, lines_ref, work = refs[count * chunks :]
    four = ids_ref[1] if dynamic else 0
    rates = helmholtz_rates(ids_ref[1], modes)
    flags = glued_flags(partner_ref)
    masks = col_masks(flags)
    for place in range(count):
        block = block_of(place, four, count)
        shares = []
        for chunk in range(chunks):
            ref = recv_refs[chunk * count + place]
            ready = ref.shape[0] // step
            shares.append(
                unpack_lanes([ref[pl.ds(at * step, step), :] for at in range(ready)], modes)
            )
        if lean:
            odd = spread_rows(shares[1][:31], masks)
            shares = [spread_rows(shares[0][:26], masks) + odd[:6], odd]
        for chunk in range(chunks):
            first = (block * chunks + chunk) * step
            for point in range(POINTS):
                at = point * 64 + first
                at = at if isinstance(at, int) else pl.multiple_of(at, step)
                base_ref[pl.ds(at, step), :] = shares[chunk][point]
    if not lean:
        for ey in range(BLOCKS):
            for iy in range(6):
                first, last = join_cols(
                    get(base_ref, 6 * iy, ey), get(base_ref, 6 * iy + 5, ey), masks
                )
                put(base_ref, 6 * iy, ey, first)
                put(base_ref, 6 * iy + 5, ey, last)
    join_rows(base_ref, flags, range(1, 7, 2) if lean else range(7))
    apply_local(base_ref, work, rates, flags)
    write_lines(base_ref, lines_ref, 0, modes)
    write_lines(work, lines_ref, line_rows(modes), modes)


def sum_rows(sums):
    return [jnp.sum(value, axis=0, keepdims=True) for value in sums]


def second_kernel(modes, slots, ids_ref, partner_ref, side_ref, flip_ref, *refs):
    gath_refs = refs[:slots]
    lines_ref, _, k0_ref, k1_ref, k2_ref, next_ref, sums_ref, work, sides = refs[slots:]
    rates = helmholtz_rates(ids_ref[1], modes)
    flags = glued_flags(partner_ref)
    collect_sides(gath_refs, ids_ref[0], partner_ref, side_ref, sides, modes)
    back = own_reaction(load_lines(lines_ref, modes), rates, flags, 1.0)
    add_lines(k0_ref, incoming_lines(sides, 0, partner_ref, flip_ref))
    apply_local(k0_ref, work, rates, flags)
    add_lines(work, add_all(incoming_lines(sides, 1, partner_ref, flip_ref), back))
    sums = apply_local(
        k1_ref, work, rates, flags,
        terms=[(1.0 / SPREAD, work), (-CENTRE / SPREAD, k0_ref)],
        products=[(1, 1), (1, -1), (-1, -1)],
    )
    write_lines(work, next_ref, 0, modes)
    apply_local(
        k2_ref, work, rates, flags,
        terms=[(TWICE, work), (-CENTRE * TWICE, k1_ref), (-1.0, k0_ref)],
    )
    write_lines(work, next_ref, line_rows(modes), modes)
    sums_ref[...] = jnp.concatenate(sum_rows(sums) + [jnp.zeros((5, LANES), F32)], axis=0)


def third_kernel(modes, slots, ids_ref, partner_ref, side_ref, flip_ref, *refs):
    gath_refs = refs[:slots]
    lines_ref, k1_ref, sums_ref, _ = refs[slots : slots + 4]
    k2_ref, k3_ref, a3_ref, next_ref, work, sides = refs[slots + 4 :]
    rates = helmholtz_rates(ids_ref[1], modes)
    flags = glued_flags(partner_ref)
    collect_sides(gath_refs, ids_ref[0], partner_ref, side_ref, sides, modes)
    back = own_reaction(load_lines(lines_ref, modes), rates, flags, TWICE)
    incoming = incoming_lines(sides, 0, partner_ref, flip_ref)
    add_lines(k2_ref, [[value * TWICE for value in line] for line in incoming])
    apply_local(k2_ref, work, rates, flags)
    add_lines(work, add_all(incoming_lines(sides, 1, partner_ref, flip_ref), back))
    sums = apply_local(
        k3_ref, a3_ref, rates, flags,
        terms=[(TWICE, work), (-CENTRE * TWICE, k2_ref), (-1.0, k1_ref)],
        products=[(2, 1), (1, 1), (1, -1), (-1, -1)],
        energy=True,
    )
    write_lines(a3_ref, next_ref, 0, modes)
    next_ref[pl.ds(line_rows(modes), SUM_ROWS), :] = jnp.concatenate(
        [sums_ref[:3, :]] + sum_rows(sums), axis=0
    )


def turn_kernel(starts, offsets, fields, has_scatter, *refs):
    field_refs = refs[:fields]
    out_refs = refs[fields : 2 * fields]
    scratch, rows = refs[-2:]
    step = rows.shape[0] // POINTS
    used = out_refs[0].shape[0]
    width = scratch.shape[1]
    for out_ref in out_refs:
        out_ref[...] = jnp.zeros(out_ref.shape, F32)
    for unit in range(len(starts)):
        table = order_table(step, offsets[unit], scratch)
        for field_ref, out_ref in zip(field_refs, out_refs):
            for point in range(POINTS):
                rows[pl.ds(point * step, step), :] = field_ref[pl.ds(point * 64 + unit * step, step), :]
            high, low = halves(jnp.transpose(rows[...])[:used])
            both = jnp.concatenate([high, low], axis=0)
            out = dot(both, table, ((1,), (0,)))
            window = pl.ds(starts[unit], width)
            out_ref[:, window] = out_ref[:, window] + (out[:used] + out[used:])
    if has_scatter:
        scatter_ref = refs[2 * fields]
        place = lax.broadcasted_iota(jnp.int32, (SIDE, NODES), 0)
        at = 6 * jnp.bitwise_and(place, 7) + lax.shift_right_logical(place, 3)
        node = lax.broadcasted_iota(jnp.int32, (SIDE, NODES), 1)
        targets = (at, at * SIDE + SIDE - 1, at + (SIDE - 1) * SIDE, at * SIDE)
        for side, target in enumerate(targets):
            scatter_ref[side * SIDE : (side + 1) * SIDE, :] = jnp.where(
                node == target, 1.0, 0.0
            ).astype(BF16)


def conjugate_coefficients(gram, energy):
    zero = jnp.zeros_like(energy)

    def image(vec):
        out = [zero] * 5
        for j in range(4):
            if vec[j] is None:
                continue
            out[j] = out[j] + CENTRE * vec[j]
            out[j + 1] = out[j + 1] + (SPREAD if j == 0 else 0.5 * SPREAD) * vec[j]
            if j > 0:
                out[j - 1] = out[j - 1] + 0.5 * SPREAD * vec[j]
        return out

    def inner(left, right):
        total = zero
        for i in range(4):
            for j in range(4):
                if left[i] is not None and right[j] is not None:
                    total = total + left[i] * right[j] * gram[i][j]
        return total

    moments = [[None] * 4 for _ in range(4)]
    for j in range(3):
        column = image([jnp.ones_like(energy) if i == j else None for i in range(4)])
        for i in range(4):
            total = zero
            for m in range(max(j - 1, 0), j + 2):
                total = total + column[m] * gram[i][m]
            moments[i][j] = total
    for i in range(3):
        moments[i][3] = moments[3][i]
    moments[3][3] = energy

    def pad(vec, size):
        return [vec[i] if i < size else None for i in range(4)]

    residual = [jnp.ones_like(energy), zero, zero, zero, zero]
    direction = list(residual)
    solution = [zero] * 4
    norm_now = gram[0][0]
    for step in range(ITERS):
        trimmed = pad(direction, step + 1)
        bend = zero
        for i in range(step + 1):
            for j in range(step + 1):
                bend = bend + direction[i] * direction[j] * moments[i][j]
        alpha = norm_now / bend
        moved = image(trimmed)
        for i in range(step + 1):
            solution[i] = solution[i] + alpha * direction[i]
        for i in range(step + 2):
            residual[i] = residual[i] - alpha * moved[i]
        if step < ITERS - 1:
            kept = pad(residual, step + 2)
            norm_next = inner(kept, kept)
            ratio = norm_next / norm_now
            direction = [residual[i] + ratio * direction[i] for i in range(5)]
            norm_now = norm_next
    return solution, residual


def last_kernel(slots, ids_ref, partner_ref, side_ref, flip_ref, *refs):
    gath_refs = refs[:slots]
    turned = refs[slots : slots + 5]
    scatter_ref, sol_out, res_out, lines, sides, sol_ref, res_ref, sems = refs[slots + 5 :]
    modes = sol_ref.shape[1]
    used = 3 * modes
    where = pl.ds(line_rows(modes), SUM_ROWS)
    if slots == 1:
        parts = [gath_refs[0][part, where, :] for part in range(gath_refs[0].shape[0])]
    else:
        parts = [ref[where, :] for ref in gath_refs]
    sums = functools.reduce(lambda left, right: left + right, parts)
    collect_sides(gath_refs, ids_ref[0], partner_ref, side_ref, sides, modes)
    g00, g01, g11, g12, g22, g23, g33, energy = [
        jnp.broadcast_to(sums[place : place + 1, :], (8, LANES)) for place in range(8)
    ]
    g02 = 2.0 * g11 - g00
    g03 = 2.0 * g12 - g01
    g13 = (g22 - g00) + g11
    gram = [
        [g00, g01, g02, g03],
        [g01, g11, g12, g13],
        [g02, g12, g22, g23],
        [g03, g13, g23, g33],
    ]
    solution, residual = conjugate_coefficients(gram, energy)
    on_a3 = residual[4] * TWICE
    on_k3 = residual[3] - on_a3 * CENTRE
    on_k2 = residual[2] - residual[4]
    factors = list(solution) + [residual[0], residual[1], on_k2, on_k3, on_a3]
    columns = jnp.transpose(
        jnp.concatenate([value[:1] for value in factors] + [jnp.zeros((LANES - 9, LANES), F32)], axis=0)
    )
    incoming = incoming_lines(sides, 0, partner_ref, flip_ref)
    for side in range(4):
        for i in range(6):
            lines[pl.ds(side * SIDE + i * 8, 8), :] = incoming[side][i] * on_a3
    high, low = halves(jnp.transpose(lines[...])[:used])
    added = dot(jnp.concatenate([high, low], axis=0), scatter_ref[...], ((1,), (0,)))
    copies = []
    for comp in range(3):
        for first in range(0, modes, 8):
            at = comp * modes + first
            rows = [ref[at : at + 8, :] for ref in turned]
            scale = [columns[at : at + 8, place : place + 1] for place in range(9)]
            sol_ref[comp, first : first + 8, :] = (scale[0] * rows[0] + scale[1] * rows[1]) + (
                scale[2] * rows[2] + scale[3] * rows[3]
            )
            res_ref[comp, first : first + 8, :] = (
                (scale[4] * rows[0] + scale[5] * rows[1])
                + (scale[6] * rows[2] + scale[7] * rows[3])
                + (scale[8] * rows[4] + (added[at : at + 8] + added[used + at : used + at + 8]))
            )
        for place, (buffer, out) in enumerate(((sol_ref, sol_out), (res_ref, res_out))):
            copies.append(
                pltpu.make_async_copy(buffer.at[comp], out.at[comp], sems.at[2 * comp + place])
            )
            copies[-1].start()
    for copy in copies:
        copy.wait()


def call(kernel, name, out_shapes, args, scratch, scalars=0, keep=True, aliases=None, outside=False):
    smem = pl.BlockSpec(memory_space=pltpu.SMEM)
    vmem = pl.BlockSpec(memory_space=pltpu.VMEM)
    shapes = [shape if isinstance(shape, jax.ShapeDtypeStruct) else jax.ShapeDtypeStruct(shape, F32) for shape in out_shapes]
    return pl.pallas_call(
        kernel,
        name=name,
        out_shape=[pltpu.VMEM(one.shape, one.dtype) if keep else one for one in shapes],
        in_specs=[smem] * scalars + [pl.BlockSpec(memory_space=pltpu.HBM) if outside else vmem] * (len(args) - scalars),
        out_specs=[vmem if keep else pl.BlockSpec(memory_space=pltpu.HBM)] * len(out_shapes),
        scratch_shapes=[pltpu.VMEM(one, F32) if isinstance(one, tuple) else one for one in scratch],
        input_output_aliases=aliases or {},
        compiler_params=pltpu.CompilerParams(vmem_limit_bytes=VMEM_LIMIT),
    )(*args[:scalars], *[held(arg, pltpu.HBM if outside else pltpu.VMEM) for arg in args[scalars:]])


def held(arg, space):
    return arg if isinstance(arg, np.ndarray) else pltpu.with_memory_space_constraint(arg, space)


def swap_blocks(blocks, dynamic):
    if not dynamic:
        stacked = lax.all_to_all(jnp.stack(blocks), "four", split_axis=0, concat_axis=0, tiled=True)
        return [stacked[place] for place in range(len(blocks))]
    size = len(blocks)
    swapped = list(blocks)
    for place in range(size - 1, 0, -1):
        swapped[place] = lax.ppermute(blocks[place], "four", [(i, i ^ offset_of(place, size)) for i in range(size)])
    return swapped


def share_lines(lines, beside=()):
    parts = lax.axis_size("dom")
    if parts != 8:
        return [lax.all_gather(lines, "dom", axis=0, tiled=False)], list(beside)
    slots = [lines] + [None] * (parts - 1)
    for slot in range(2, parts, 2):
        slots[slot] = lax.ppermute(lines, "dom", [(i, i ^ slot) for i in range(parts)])
        if beside and slot == parts - 2:
            slots[slot], *beside = lax.optimization_barrier((slots[slot], *beside))
    for slot in range(0, parts, 2):
        slots[slot + 1] = lax.ppermute(slots[slot], "dom", [(i, i ^ 1) for i in range(parts)])
    return slots, list(beside)


def shards(velocity, partner, partner_side, flipped):
    modes = velocity.shape[1]
    count = lax.axis_size("four")
    step, chunks = chunk_sizes(count)
    rows = POINTS * step
    sent_rows = 3 * rows // 4 if is_packed(modes) else rows
    dynamic = step == BLOCKS
    (inv_high, inv_low), (back_high, back_low) = transform_tables(count)
    starts, offsets = unit_windows(count)
    table = (rows, 3 * LANES)
    ids = jnp.stack([lax.axis_index("dom"), lax.axis_index("four")]).astype(jnp.int32)
    field = (NODES, LANES)
    blocks = [(sent_rows, LANES)] * count
    lined = line_rows(modes)

    lean = dynamic and chunks == 2 and is_packed(modes)
    spread = []
    source = velocity
    for chunk in range(chunks):
        load = chunk == 0
        sent = call(
            functools.partial(pack_kernel, step, count, dynamic, chunk, chunks, starts, offsets),
            "pack",
            blocks + [velocity.shape] * load,
            (ids, source),
            [table] + [pltpu.SemaphoreType.DMA((3 * modes // 8,))] * load,
            scalars=1,
            outside=load,
        )
        if load:
            *sent, source = sent
        spread.append(swap_blocks(sent, dynamic))
    local = []
    carry = []
    for chunk in range(chunks):
        role = chunk if lean else None
        out = [((21, 24)[chunk] * step, LANES)] * count if lean else blocks
        sent = call(
            functools.partial(product_kernel, modes, step, count, dynamic, role),
            "products",
            out + [(count, SIDE, LANES)] * (role == 0),
            (ids, *spread[chunk], inv_high, inv_low, back_high, back_low, *carry),
            [
                (count, rows, LANES),
                (rows, count * LANES),
                (rows, 3 * LANES),
                (rows, 6 * LANES),
                (3, rows, LANES),
            ],
            scalars=1,
        )
        if role == 0:
            *sent, held_row = sent
            carry = [held_row]
        if role == 1:
            sent, local = lax.optimization_barrier((sent, local))
        local += swap_blocks(sent, dynamic)

    base, lines = call(
        functools.partial(first_kernel, modes, step, count, chunks, dynamic, lean),
        "first",
        [field, (2 * lined, LANES)],
        (ids, partner, *local),
        [field],
        scalars=2,
    )
    tables = (ids, partner, partner_side, flipped)
    gathered, _ = share_lines(lines)
    slots = len(gathered)
    k0, k1, base, lines, sums = call(
        functools.partial(second_kernel, modes, slots),
        "second",
        [field, field, field, (2 * lined, LANES), (8, LANES)],
        (*tables, *gathered, lines, base),
        [field, (4, 2 * SIDE, LANES)],
        scalars=4,
        aliases={4 + slots + 1: 0},
    )
    flat = (3 * modes, NODES)
    turned = call(
        functools.partial(turn_kernel, starts, offsets, 2, True),
        "turn",
        [flat, flat, jax.ShapeDtypeStruct((4 * SIDE, NODES), BF16)],
        (k0, k1),
        [table, (rows, LANES)],
    )
    gathered, (t0, t1, scatter) = share_lines(lines, turned)
    k2, k3, a3, lines = call(
        functools.partial(third_kernel, modes, slots),
        "third",
        [field, field, field, (lined + SUM_ROWS, LANES)],
        (*tables, *gathered, lines, k1, sums, base),
        [field, (4, 2 * SIDE, LANES)],
        scalars=4,
        aliases={4 + slots + 3: 0},
    )
    turned = call(
        functools.partial(turn_kernel, starts, offsets, 3, False),
        "turn",
        [flat, flat, flat],
        (k2, k3, a3),
        [table, (rows, LANES)],
    )
    gathered, (t2, t3, ta) = share_lines(lines, turned)
    outs = call(
        functools.partial(last_kernel, slots),
        "last",
        [velocity.shape, velocity.shape],
        (*tables, *gathered, t0, t1, t2, t3, ta, scatter),
        [
            (4 * SIDE, LANES),
            (4, SIDE, LANES),
            velocity.shape,
            velocity.shape,
            pltpu.SemaphoreType.DMA((6,)),
        ],
        scalars=4,
        keep=False,
    )
    return tuple(outs)


def solution(mesh):
    return jax.shard_map(
        shards,
        mesh=mesh,
        in_specs=(P(None, "four", "dom"), P("dom", None), P("dom", None), P("dom", None)),
        out_specs=(P(None, "four", "dom"), P(None, "four", "dom")),
        check_vma=False,
    )
```

```python
import functools
import math

import jax
import jax.numpy as jnp
import numpy as np
from jax import lax
from jax.experimental import pallas as pl
from jax.experimental.pallas import tpu as pltpu
from jax.sharding import PartitionSpec as P

ITERS = 4
REACTION = 2.0
WAVE_STEP = 0.0625
LANES = 128
POINTS = 36
BLOCKS = 8
SIDE = 48
SENT = 40
NODES = 2304
CENTRE = 9.0
SPREAD = 9.0
TWICE = 2.0 / SPREAD
SUM_ROWS = 8
VMEM_LIMIT = 32 * 1024 * 1024
F32 = jnp.float32
BF16 = jnp.bfloat16


def gll_tables():
    inner_near = math.sqrt(1.0 / 3.0 - 2.0 * math.sqrt(7.0) / 21.0)
    inner_far = math.sqrt(1.0 / 3.0 + 2.0 * math.sqrt(7.0) / 21.0)
    points = np.array([-1.0, -inner_far, -inner_near, inner_near, inner_far, 1.0])
    values = (63.0 * points**5 - 70.0 * points**3 + 15.0 * points) / 8.0
    weights = 2.0 / (30.0 * values * values)
    spacing = points[:, None] - points[None, :]
    same_point = spacing == 0.0
    derivative = np.where(
        same_point, 0.0, values[:, None] / (values[None, :] * np.where(same_point, 1.0, spacing))
    )
    end_fix = np.array([-7.5, 0.0, 0.0, 0.0, 0.0, 7.5])
    derivative = derivative + np.eye(6) * end_fix[None, :]
    stiffness = derivative.T @ (weights[:, None] * derivative)
    return (weights, derivative, stiffness)


WEIGHTS, DERIV, STIFF = gll_tables()
STIFF_HAT = STIFF / WEIGHTS[:, None]


def fourier_tables(planes):
    plane_ids = np.arange(planes)
    mode_ids = np.arange(planes)
    waves = np.where(mode_ids < 2, 0, mode_ids // 2)
    angle = (plane_ids[:, None] * waves[None, :] % planes) * (2.0 * math.pi / planes)
    is_sine = (mode_ids % 2 == 1) & (mode_ids >= 2)
    basis = np.where(is_sine[None, :], np.sin(angle), np.cos(angle))
    alternating = np.where(plane_ids % 2 == 0, 1.0, -1.0)
    basis = np.where(mode_ids[None, :] == 1, alternating[:, None], basis)
    row_scale = np.where(mode_ids < 2, 1.0, 2.0) / planes
    forward = basis.T * row_scale[:, None]
    rates = (np.arange(planes // 2) * WAVE_STEP)[:, None]
    forward_z = np.zeros_like(forward)
    forward_z[0::2] = rates * forward[1::2]
    forward_z[1::2] = -rates * forward[0::2]
    forward_z[0:2] = 0.0
    return (basis, forward, forward_z)


def split_table(table):
    high = np.asarray(table, np.float32).astype(jnp.bfloat16)
    low = (np.asarray(table, np.float64) - high.astype(np.float64)).astype(np.float32)
    return high, low.astype(jnp.bfloat16)


def transform_tables(count):
    planes = LANES
    modes = planes // count
    basis, forward, forward_z = fourier_tables(planes)
    inverse = np.zeros((count * LANES, 3 * planes))
    for block in range(count):
        ids = slice(block * modes, (block + 1) * modes)
        for comp in range(3):
            at = block * LANES + comp * modes
            inverse[at : at + modes, comp * planes : (comp + 1) * planes] = basis[:, ids].T
    back = -np.concatenate([forward.T, forward_z.T], axis=0)
    return split_table(inverse), split_table(back)


def chunk_sizes(count):
    group = BLOCKS * BLOCKS // count
    step = min(group, BLOCKS)
    return step, group // step


def unit_windows(count):
    step, _ = chunk_sizes(count)
    starts = []
    offsets = []
    for index in range(BLOCKS * BLOCKS // step):
        element = index * step
        first = element // BLOCKS * 6 * SIDE
        starts.append(first // LANES * LANES)
        offsets.append(first % LANES + 6 * (element % BLOCKS))
    return starts, offsets


def order_table(step, offset, scratch):
    width = scratch.shape[1]
    lane = lax.broadcasted_iota(jnp.int32, (step, width), 1)
    gap = lane - 6 * lax.broadcasted_iota(jnp.int32, (step, width), 0) - offset
    for point in range(POINTS):
        hit = gap == point // 6 * SIDE + point % 6
        scratch[pl.ds(point * step, step), :] = jnp.where(hit, 1.0, 0.0)
    return scratch[...].astype(BF16)


def halves(value):
    high = value.astype(BF16)
    low = (value - high.astype(F32)).astype(BF16)
    return high, low


def dot(left, right, dims):
    return lax.dot_general(left, right, (dims, ((), ())), preferred_element_type=F32)


def dot3(left, right_high, right_low):
    high, low = halves(left)
    dims = ((1,), (0,))
    return dot(high, right_high, dims) + (dot(low, right_high, dims) + dot(high, right_low, dims))


def start_of(point, ey):
    return pl.multiple_of(point * 64 + ey * 8, 8)


def get(ref, point, ey):
    return ref[pl.ds(start_of(point, ey), 8), :]


def put(ref, point, ey, value):
    ref[pl.ds(start_of(point, ey), 8), :] = value


def ex_ids():
    return lax.broadcasted_iota(jnp.int32, (8, LANES), 0)


def helmholtz_rates(four, modes):
    lane = lax.broadcasted_iota(jnp.int32, (8, LANES), 1)
    mode = four * modes + lax.rem(lane, jnp.int32(modes))
    wave = jnp.where(mode == 0, 0, jnp.where(mode == 1, LANES // 2, lax.div(mode, jnp.int32(2))))
    scaled = wave.astype(F32) * WAVE_STEP
    return REACTION + scaled * scaled


def glued_flags(partner_ref):
    return [jnp.where(partner_ref[0, side] >= 0, 1.0, 0.0).astype(F32) for side in range(4)]


def col_masks(flags):
    ex = ex_ids()
    return jnp.where(ex == 0, flags[3], 1.0), jnp.where(ex == 7, flags[1], 1.0)


def join_cols(first, last, masks):
    ex = ex_ids()
    from_right = jnp.where(ex < 7, pltpu.roll(first, 7, 0), 0.0)
    from_left = jnp.where(ex > 0, pltpu.roll(last, 1, 0), 0.0)
    return (first + from_left) * masks[0], (last + from_right) * masks[1]


def join_rows(ref, flags, pairs=range(7)):
    ex = ex_ids()
    not_first = jnp.where(ex == 0, 0.0, 1.0)
    not_last = jnp.where(ex == 7, 0.0, 1.0)
    for ix in range(6):
        for ey in pairs:
            total = get(ref, 30 + ix, ey) + get(ref, ix, ey + 1)
            put(ref, 30 + ix, ey, total)
            put(ref, ix, ey + 1, total)
        low = get(ref, ix, 0) * flags[0]
        high = get(ref, 30 + ix, 7) * flags[2]
        if ix == 0:
            low, high = low * not_first, high * not_first
        if ix == 5:
            low, high = low * not_last, high * not_last
        put(ref, ix, 0, low)
        put(ref, 30 + ix, 7, high)


def line_product(line, table, mirrored=1.0):
    sums = [line[j] + line[5 - j] for j in range(3)]
    gaps = [line[j] - line[5 - j] for j in range(3)]
    out = [None] * 6
    for i in range(3):
        even = None
        odd = None
        for j in range(3):
            even_term = sums[j] * float(0.5 * (table[i, j] + table[i, 5 - j]))
            odd_term = gaps[j] * float(0.5 * (table[i, j] - table[i, 5 - j]))
            even = even_term if even is None else even + even_term
            odd = odd_term if odd is None else odd + odd_term
        out[i] = even + odd
        out[5 - i] = even - odd if mirrored > 0 else odd - even
    return out


def apply_local(src, dst, rates, flags, terms=(), products=(), energy=False):
    masks = col_masks(flags)

    def body(ey, sums):
        sums = list(sums)
        for ix in range(6):
            line = []
            for iy in range(6):
                point = 6 * iy + ix
                if not terms:
                    line.append(get(src, point, ey))
                    continue
                values = [get(ref, point, ey) for _, ref in terms]
                value = None
                for (factor, _), part in zip(terms, values):
                    part = -part if factor == -1.0 else part * factor
                    value = part if value is None else value + part
                put(src, point, ey, value)
                line.append(value)
                values.append(value)
                ends = (iy in (0, 5)) + (ix in (0, 5))
                for place, (left, right) in enumerate(products):
                    both = values[left] * values[right]
                    sums[place] = sums[place] + (both * (0.5**ends) if ends else both)
            out = line_product(line, STIFF_HAT)
            for iy in range(6):
                put(dst, 6 * iy + ix, ey, out[iy] + rates * line[iy])
        for iy in range(6):
            line = [get(src, 6 * iy + ix, ey) for ix in range(6)]
            out = line_product(line, STIFF_HAT)
            full = [
                (get(dst, 6 * iy + ix, ey) + out[ix]) * float(WEIGHTS[iy] * WEIGHTS[ix])
                for ix in range(6)
            ]
            if energy:
                for ix in range(6):
                    sums[-1] = sums[-1] + full[ix] * line[ix]
            full[0], full[5] = join_cols(full[0], full[5], masks)
            for ix in range(6):
                put(dst, 6 * iy + ix, ey, full[ix])
        return tuple(sums)

    zero = jnp.zeros((8, LANES), F32)
    sums = lax.fori_loop(0, BLOCKS, body, (zero,) * (len(products) + int(energy)), unroll=2)
    join_rows(dst, flags)
    return sums


def side_slice(side, i):
    if side == 0:
        return pl.ds(i * 64, 8)
    if side == 2:
        return pl.ds((30 + i) * 64 + 56, 8)
    if side == 1:
        return pl.ds((6 * i + 5) * 64 + 7, 8, stride=8)
    return pl.ds(6 * i * 64, 8, stride=8)


def read_line(ref, side):
    return [ref[side_slice(side, i), :] for i in range(6)]


def lane_ids():
    return lax.broadcasted_iota(jnp.int32, (8, LANES), 1)


def is_packed(modes):
    return 3 * modes + modes == LANES


def pack_lanes(values, modes):
    if not is_packed(modes):
        return values
    third = len(values) // 4
    inside = lane_ids() < 3 * modes
    return [
        jnp.where(
            inside,
            values[comp * third + at],
            pltpu.roll(values[3 * third + at], (3 - comp) * modes, 1),
        )
        for comp in range(3)
        for at in range(third)
    ]


def unpack_last(pieces, modes):
    block = lax.div(lane_ids(), jnp.int32(modes))
    turned = [pltpu.roll(pieces[comp], (comp + 1) * modes, 1) for comp in range(3)]
    return jnp.where(block == 0, turned[0], jnp.where(block == 1, turned[1], turned[2]))


def unpack_lanes(values, modes):
    if not is_packed(modes):
        return values
    third = len(values) // 3
    return values + [
        unpack_last([values[comp * third + at] for comp in range(3)], modes) for at in range(third)
    ]


def line_rows(modes):
    return 3 * SENT if is_packed(modes) else 4 * SENT


def first_points(last_points):
    return jnp.where(ex_ids() > 0, pltpu.roll(last_points, 1, 0), 0.0)


def write_lines(ref, lines_ref, base, modes):
    values = []
    for side in range(4):
        values += read_line(ref, side)[1:]
    for at, value in enumerate(pack_lanes(values, modes)):
        lines_ref[pl.ds(base + at * 8, 8), :] = value


def load_lines(lines_ref, modes):
    count = line_rows(modes) // 8
    values = unpack_lanes([lines_ref[pl.ds(at * 8, 8), :] for at in range(count)], modes)
    sides = [values[side * 5 : side * 5 + 5] for side in range(4)]
    return [[first_points(side[4])] + side for side in sides]


def add_lines(ref, lines):
    for side in range(4):
        for i in range(6):
            where = side_slice(side, i)
            ref[where, :] = ref[where, :] + lines[side][i]


def add_all(left, right):
    return [[a + b for a, b in zip(one, two)] for one, two in zip(left, right)]


def reverse_rows(value):
    ex = ex_ids()
    value = pltpu.roll(value, 4, 0)
    value = jnp.where((ex & 2) == 0, pltpu.roll(value, 6, 0), pltpu.roll(value, 2, 0))
    return jnp.where((ex & 1) == 0, pltpu.roll(value, 7, 0), pltpu.roll(value, 1, 0))


def collect_sides(gath_refs, own, partner_ref, side_ref, sides, modes):
    sets = sides.shape[1] // SIDE
    step = line_rows(modes)

    def copy_side(side, load):
        there = jnp.maximum(side_ref[0, side], 0)

        def fill(place, values):
            for i, value in enumerate([first_points(values[4])] + values):
                sides[side, pl.ds(place * SIDE + i * 8, 8), :] = value

        def plain():
            for place in range(sets):
                first = place * step + there * SENT
                fill(place, [load(pl.multiple_of(first + i * 8, 8)) for i in range(5)])

        if not is_packed(modes):
            plain()
            return
        pl.when(there < 3)(plain)

        @pl.when(there == 3)
        def _():
            for place in range(sets):
                first = place * step
                values = []
                for i in range(5):
                    pieces = [load(first + comp * SENT + i * 8) for comp in range(3)]
                    values.append(unpack_last(pieces, modes))
                fill(place, values)

    def body(side, carry):
        part = partner_ref[0, side]
        if len(gath_refs) == 1:
            source = jnp.maximum(part, 0)
            copy_side(side, lambda at: gath_refs[0][source, pl.ds(at, 8), :])
            return carry
        for slot, ref in enumerate(gath_refs):
            here = jnp.logical_and(part >= 0, jnp.bitwise_xor(part, own) == slot)

            @pl.when(here)
            def _(ref=ref):
                copy_side(side, lambda at: ref[pl.ds(at, 8), :])

        return carry

    lax.fori_loop(0, 4, body, 0)


def incoming_lines(sides, place, partner_ref, flip_ref):
    lines = []
    for side in range(4):
        glued = partner_ref[0, side] >= 0
        turned = flip_ref[0, side] == 1
        line = []
        for i in range(6):
            at = pl.multiple_of(place * SIDE + jnp.where(turned, 5 - i, i) * 8, 8)
            value = sides[side, pl.ds(at, 8), :]
            value = jnp.where(turned, reverse_rows(value), value)
            line.append(jnp.where(glued, value, 0.0))
        lines.append(line)
    return lines


def own_reaction(own_lines, rates, flags, scale):
    ex = ex_ids()
    edge = float(WEIGHTS[0])
    corner = float(STIFF[0, 0])
    lines = []
    for side in range(4):
        line = own_lines[side]
        along = line_product(line, STIFF_HAT)
        out = [
            (along[i] * edge + line[i] * (corner + rates * edge)) * float(WEIGHTS[i])
            for i in range(6)
        ]
        first = out[0] + pltpu.roll(out[5], 1, 0)
        last = out[5] + pltpu.roll(out[0], 7, 0)
        out[0] = jnp.where(ex > 0, first, 0.0)
        out[5] = jnp.where(ex < 7, last, 0.0)
        lines.append([value * (flags[side] * scale) for value in out])
    return lines


def pick(index, values):
    if isinstance(index, int):
        return values[index]
    chosen = jnp.int32(values[0])
    for place in range(1, len(values)):
        chosen = jnp.where(index == place, jnp.int32(values[place]), chosen)
    return chosen


def offset_of(place, size):
    return (0, 3, 1, 2)[place] if size == 4 else place


def block_of(place, four, size):
    return place if isinstance(four, int) else jnp.bitwise_xor(four, offset_of(place, size))


def pack_kernel(step, count, dynamic, chunk, chunks, starts, offsets, ids_ref, source_ref, *refs):
    send_refs = refs[:count]
    load = chunk == 0
    scratch = refs[-2] if load else refs[-1]
    width = scratch.shape[1]
    held_ref = refs[count] if load else source_ref
    modes = held_ref.shape[1]
    four = ids_ref[1] if dynamic else 0
    copies = []
    if load:
        for comp in range(3):
            copies.append(
                pltpu.make_async_copy(source_ref.at[comp], held_ref.at[comp], refs[-1].at[comp])
            )
            copies[-1].start()
    for place in range(count):
        index = block_of(place, four, count)
        table = order_table(step, pick(index, offsets[chunk::chunks]), scratch)
        if place == 0:
            for copy in copies:
                copy.wait()
        start = pick(index, starts[chunk::chunks])
        start = start if isinstance(start, int) else pl.multiple_of(start, LANES)
        rows = [held_ref[comp, :, pl.ds(start, width)] for comp in range(3)]
        pad = jnp.zeros((LANES - 3 * modes, width), F32)
        high, low = halves(jnp.concatenate(rows + [pad], axis=0))
        both = jnp.concatenate([high, low], axis=0)
        out = dot(table, both, ((1,), (1,)))
        out = out[:, :LANES] + out[:, LANES:]
        if not is_packed(modes):
            send_refs[place][...] = out
            continue
        values = [out[point * step : (point + 1) * step] for point in range(POINTS)]
        for at, value in enumerate(pack_lanes(values, modes)):
            send_refs[place][pl.ds(at * step, step), :] = value


def product_kernel(modes, step, count, dynamic, role, ids_ref, *refs):
    recv_refs = refs[:count]
    inv_high, inv_low, back_high, back_low = refs[count : count + 4]
    refs = refs[count + 4 :]
    if role == 1:
        carry_ref, refs = refs[0], refs[1:]
    send_refs, refs = refs[:count], refs[count:]
    if role == 0:
        carry_ref, refs = refs[0], refs[1:]
    full, lined, phys, prod, spec = refs
    four = ids_ref[1] if dynamic else 0
    packed = is_packed(modes)
    for place in range(count):
        index = block_of(place, four, count)
        if packed:
            ready = 3 * POINTS // 4
            values = [recv_refs[place][pl.ds(at * step, step), :] for at in range(ready)]
            for at, value in enumerate(unpack_lanes(values, modes)):
                full[place, pl.ds(at * step, step), :] = value
        else:
            full[place] = recv_refs[place][...]
        first = index * LANES
        first = first if isinstance(first, int) else pl.multiple_of(first, LANES)
        lined[:, pl.ds(first, LANES)] = full[place]
    phys[...] = dot3(lined[...], inv_high[...], inv_low[...])
    width = 2 * LANES

    def field(point, comp):
        return phys[pl.ds(point * step, step), comp * LANES : (comp + 1) * LANES]

    for comp in range(3):
        wide = pl.ds(comp * width, LANES)
        for iy in range(6):
            line = []
            for ix in range(6):
                point = 6 * iy + ix
                value = field(point, comp)
                line.append(value * field(point, 0))
                prod[pl.ds(point * step, step), pl.ds(comp * width + LANES, LANES)] = (
                    value * field(point, 2)
                )
            out = line_product(line, DERIV, -1.0)
            for ix in range(6):
                prod[pl.ds((6 * iy + ix) * step, step), wide] = out[ix]
        for ix in range(6):
            line = [field(6 * iy + ix, comp) * field(6 * iy + ix, 1) for iy in range(6)]
            out = line_product(line, DERIV, -1.0)
            for iy in range(6):
                at = pl.ds((6 * iy + ix) * step, step)
                prod[at, wide] = prod[at, wide] + out[iy]
        spec[comp] = dot3(prod[:, comp * width : (comp + 1) * width], back_high[...], back_low[...])

    lane_block = lax.div(lax.broadcasted_iota(jnp.int32, (step, LANES), 1), jnp.int32(modes))
    masks = []
    shifts = []
    for place in range(count):
        index = block_of(place, four, count)
        masks.append([lane_block == lax.rem(index + comp, count) for comp in range(2)])
        shifts.append(lax.rem(LANES - index * modes, LANES))
    kept = []
    for point in range(POINTS):
        at = pl.ds(point * step, step)
        mass = float(WEIGHTS[point // 6] * WEIGHTS[point % 6])
        turned = [spec[0, at, :]]
        turned += [pltpu.roll(spec[comp, at, :], comp * modes, 1) for comp in (1, 2)]
        for place in range(count):
            mask = masks[place]
            mixed = jnp.where(mask[0], turned[0], jnp.where(mask[1], turned[1], turned[2]))
            nonlinear = pltpu.roll(mixed, shifts[place], 1)
            full[place, at, :] = mass * (REACTION * full[place, at, :] + nonlinear)
    ex = None if role is None else ex_ids()
    for place in range(count):
        values = [full[place, pl.ds(point * step, step), :] for point in range(POINTS)]
        if role is not None:
            left = jnp.zeros((8, LANES), F32)
            sent = []
            for iy in range(6):
                line = values[6 * iy : 6 * iy + 6]
                line[5] = line[5] + jnp.where(ex < 7, pltpu.roll(line[0], 7, 0), 0.0)
                if role == 0 and iy == 5:
                    for ix in range(6):
                        carry_ref[place, pl.ds(ix * 8, 8), :] = line[ix]
                    continue
                if role == 1 and iy == 0:
                    line = [line[ix] + carry_ref[place, pl.ds(ix * 8, 8), :] for ix in range(6)]
                left = jnp.where(ex == iy, pltpu.roll(line[0], iy, 0) if iy else line[0], left)
                sent += line[1:]
            values = sent + [left]
            values += [left] * (32 - len(values))
        for at, value in enumerate(pack_lanes(values, modes)):
            send_refs[place][pl.ds(at * step, step), :] = value


def spread_rows(values, masks):
    ex = ex_ids()
    rows = (len(values) - 1) // 5
    left = values[5 * rows]
    points = []
    for iy in range(rows):
        line = values[5 * iy : 5 * iy + 5]
        start = pltpu.roll(left, 8 - iy, 0) if iy else left
        first = jnp.where(ex == 0, start, pltpu.roll(line[4], 1, 0))
        points += [first * masks[0]] + line[:4] + [line[4] * masks[1]]
    return points


def first_kernel(modes, step, count, chunks, dynamic, lean, ids_ref, partner_ref, *refs):
    recv_refs = refs[: count * chunks]
    base_ref, lines_ref, work = refs[count * chunks :]
    four = ids_ref[1] if dynamic else 0
    rates = helmholtz_rates(ids_ref[1], modes)
    flags = glued_flags(partner_ref)
    masks = col_masks(flags)
    for place in range(count):
        block = block_of(place, four, count)
        shares = []
        for chunk in range(chunks):
            ref = recv_refs[chunk * count + place]
            ready = ref.shape[0] // step
            shares.append(
                unpack_lanes([ref[pl.ds(at * step, step), :] for at in range(ready)], modes)
            )
        if lean:
            odd = spread_rows(shares[1][:31], masks)
            shares = [spread_rows(shares[0][:26], masks) + odd[:6], odd]
        for chunk in range(chunks):
            first = (block * chunks + chunk) * step
            for point in range(POINTS):
                at = point * 64 + first
                at = at if isinstance(at, int) else pl.multiple_of(at, step)
                base_ref[pl.ds(at, step), :] = shares[chunk][point]
    if not lean:
        for ey in range(BLOCKS):
            for iy in range(6):
                first, last = join_cols(
                    get(base_ref, 6 * iy, ey), get(base_ref, 6 * iy + 5, ey), masks
                )
                put(base_ref, 6 * iy, ey, first)
                put(base_ref, 6 * iy + 5, ey, last)
    join_rows(base_ref, flags, range(1, 7, 2) if lean else range(7))
    apply_local(base_ref, work, rates, flags)
    write_lines(base_ref, lines_ref, 0, modes)
    write_lines(work, lines_ref, line_rows(modes), modes)


def sum_rows(sums):
    return [jnp.sum(value, axis=0, keepdims=True) for value in sums]


def second_kernel(modes, slots, ids_ref, partner_ref, side_ref, flip_ref, *refs):
    gath_refs = refs[:slots]
    lines_ref, _, k0_ref, k1_ref, k2_ref, next_ref, sums_ref, work, sides = refs[slots:]
    rates = helmholtz_rates(ids_ref[1], modes)
    flags = glued_flags(partner_ref)
    collect_sides(gath_refs, ids_ref[0], partner_ref, side_ref, sides, modes)
    back = own_reaction(load_lines(lines_ref, modes), rates, flags, 1.0)
    add_lines(k0_ref, incoming_lines(sides, 0, partner_ref, flip_ref))
    apply_local(k0_ref, work, rates, flags)
    add_lines(work, add_all(incoming_lines(sides, 1, partner_ref, flip_ref), back))
    sums = apply_local(
        k1_ref, work, rates, flags,
        terms=[(1.0 / SPREAD, work), (-CENTRE / SPREAD, k0_ref)],
        products=[(1, 1), (1, -1), (-1, -1)],
    )
    write_lines(work, next_ref, 0, modes)
    apply_local(
        k2_ref, work, rates, flags,
        terms=[(TWICE, work), (-CENTRE * TWICE, k1_ref), (-1.0, k0_ref)],
    )
    write_lines(work, next_ref, line_rows(modes), modes)
    sums_ref[...] = jnp.concatenate(sum_rows(sums) + [jnp.zeros((5, LANES), F32)], axis=0)


def third_kernel(modes, slots, ids_ref, partner_ref, side_ref, flip_ref, *refs):
    gath_refs = refs[:slots]
    lines_ref, k1_ref, sums_ref, _ = refs[slots : slots + 4]
    k2_ref, k3_ref, a3_ref, next_ref, work, sides = refs[slots + 4 :]
    rates = helmholtz_rates(ids_ref[1], modes)
    flags = glued_flags(partner_ref)
    collect_sides(gath_refs, ids_ref[0], partner_ref, side_ref, sides, modes)
    back = own_reaction(load_lines(lines_ref, modes), rates, flags, TWICE)
    incoming = incoming_lines(sides, 0, partner_ref, flip_ref)
    add_lines(k2_ref, [[value * TWICE for value in line] for line in incoming])
    apply_local(k2_ref, work, rates, flags)
    add_lines(work, add_all(incoming_lines(sides, 1, partner_ref, flip_ref), back))
    sums = apply_local(
        k3_ref, a3_ref, rates, flags,
        terms=[(TWICE, work), (-CENTRE * TWICE, k2_ref), (-1.0, k1_ref)],
        products=[(2, 1), (1, 1), (1, -1), (-1, -1)],
        energy=True,
    )
    write_lines(a3_ref, next_ref, 0, modes)
    next_ref[pl.ds(line_rows(modes), SUM_ROWS), :] = jnp.concatenate(
        [sums_ref[:3, :]] + sum_rows(sums), axis=0
    )


def turn_kernel(starts, offsets, fields, has_scatter, *refs):
    field_refs = refs[:fields]
    out_refs = refs[fields : 2 * fields]
    scratch, rows = refs[-2:]
    step = rows.shape[0] // POINTS
    used = out_refs[0].shape[0]
    width = scratch.shape[1]
    for out_ref in out_refs:
        out_ref[...] = jnp.zeros(out_ref.shape, F32)
    for unit in range(len(starts)):
        table = order_table(step, offsets[unit], scratch)
        for field_ref, out_ref in zip(field_refs, out_refs):
            for point in range(POINTS):
                rows[pl.ds(point * step, step), :] = field_ref[pl.ds(point * 64 + unit * step, step), :]
            high, low = halves(jnp.transpose(rows[...])[:used])
            both = jnp.concatenate([high, low], axis=0)
            out = dot(both, table, ((1,), (0,)))
            window = pl.ds(starts[unit], width)
            out_ref[:, window] = out_ref[:, window] + (out[:used] + out[used:])
    if has_scatter:
        scatter_ref = refs[2 * fields]
        place = lax.broadcasted_iota(jnp.int32, (SIDE, NODES), 0)
        at = 6 * jnp.bitwise_and(place, 7) + lax.shift_right_logical(place, 3)
        node = lax.broadcasted_iota(jnp.int32, (SIDE, NODES), 1)
        targets = (at, at * SIDE + SIDE - 1, at + (SIDE - 1) * SIDE, at * SIDE)
        for side, target in enumerate(targets):
            scatter_ref[side * SIDE : (side + 1) * SIDE, :] = jnp.where(
                node == target, 1.0, 0.0
            ).astype(BF16)


def conjugate_coefficients(gram, energy):
    zero = jnp.zeros_like(energy)

    def image(vec):
        out = [zero] * 5
        for j in range(4):
            if vec[j] is None:
                continue
            out[j] = out[j] + CENTRE * vec[j]
            out[j + 1] = out[j + 1] + (SPREAD if j == 0 else 0.5 * SPREAD) * vec[j]
            if j > 0:
                out[j - 1] = out[j - 1] + 0.5 * SPREAD * vec[j]
        return out

    def inner(left, right):
        total = zero
        for i in range(4):
            for j in range(4):
                if left[i] is not None and right[j] is not None:
                    total = total + left[i] * right[j] * gram[i][j]
        return total

    moments = [[None] * 4 for _ in range(4)]
    for j in range(3):
        column = image([jnp.ones_like(energy) if i == j else None for i in range(4)])
        for i in range(4):
            total = zero
            for m in range(max(j - 1, 0), j + 2):
                total = total + column[m] * gram[i][m]
            moments[i][j] = total
    for i in range(3):
        moments[i][3] = moments[3][i]
    moments[3][3] = energy

    def pad(vec, size):
        return [vec[i] if i < size else None for i in range(4)]

    residual = [jnp.ones_like(energy), zero, zero, zero, zero]
    direction = list(residual)
    solution = [zero] * 4
    norm_now = gram[0][0]
    for step in range(ITERS):
        trimmed = pad(direction, step + 1)
        bend = zero
        for i in range(step + 1):
            for j in range(step + 1):
                bend = bend + direction[i] * direction[j] * moments[i][j]
        alpha = norm_now / bend
        moved = image(trimmed)
        for i in range(step + 1):
            solution[i] = solution[i] + alpha * direction[i]
        for i in range(step + 2):
            residual[i] = residual[i] - alpha * moved[i]
        if step < ITERS - 1:
            kept = pad(residual, step + 2)
            norm_next = inner(kept, kept)
            ratio = norm_next / norm_now
            direction = [residual[i] + ratio * direction[i] for i in range(5)]
            norm_now = norm_next
    return solution, residual


def last_kernel(slots, ids_ref, partner_ref, side_ref, flip_ref, *refs):
    gath_refs = refs[:slots]
    turned = refs[slots : slots + 5]
    scatter_ref, sol_out, res_out, lines, sides, sol_ref, res_ref, sems = refs[slots + 5 :]
    modes = sol_ref.shape[1]
    used = 3 * modes
    where = pl.ds(line_rows(modes), SUM_ROWS)
    if slots == 1:
        parts = [gath_refs[0][part, where, :] for part in range(gath_refs[0].shape[0])]
    else:
        parts = [ref[where, :] for ref in gath_refs]
    sums = functools.reduce(lambda left, right: left + right, parts)
    collect_sides(gath_refs, ids_ref[0], partner_ref, side_ref, sides, modes)
    g00, g01, g11, g12, g22, g23, g33, energy = [
        jnp.broadcast_to(sums[place : place + 1, :], (8, LANES)) for place in range(8)
    ]
    g02 = 2.0 * g11 - g00
    g03 = 2.0 * g12 - g01
    g13 = (g22 - g00) + g11
    gram = [
        [g00, g01, g02, g03],
        [g01, g11, g12, g13],
        [g02, g12, g22, g23],
        [g03, g13, g23, g33],
    ]
    solution, residual = conjugate_coefficients(gram, energy)
    on_a3 = residual[4] * TWICE
    on_k3 = residual[3] - on_a3 * CENTRE
    on_k2 = residual[2] - residual[4]
    factors = list(solution) + [residual[0], residual[1], on_k2, on_k3, on_a3]
    columns = jnp.transpose(
        jnp.concatenate([value[:1] for value in factors] + [jnp.zeros((LANES - 9, LANES), F32)], axis=0)
    )
    incoming = incoming_lines(sides, 0, partner_ref, flip_ref)
    for side in range(4):
        for i in range(6):
            lines[pl.ds(side * SIDE + i * 8, 8), :] = incoming[side][i] * on_a3
    high, low = halves(jnp.transpose(lines[...])[:used])
    added = dot(jnp.concatenate([high, low], axis=0), scatter_ref[...], ((1,), (0,)))
    copies = []
    for comp in range(3):
        for first in range(0, modes, 8):
            at = comp * modes + first
            rows = [ref[at : at + 8, :] for ref in turned]
            scale = [columns[at : at + 8, place : place + 1] for place in range(9)]
            sol_ref[comp, first : first + 8, :] = (scale[0] * rows[0] + scale[1] * rows[1]) + (
                scale[2] * rows[2] + scale[3] * rows[3]
            )
            res_ref[comp, first : first + 8, :] = (
                (scale[4] * rows[0] + scale[5] * rows[1])
                + (scale[6] * rows[2] + scale[7] * rows[3])
                + (scale[8] * rows[4] + (added[at : at + 8] + added[used + at : used + at + 8]))
            )
        for place, (buffer, out) in enumerate(((sol_ref, sol_out), (res_ref, res_out))):
            copies.append(
                pltpu.make_async_copy(buffer.at[comp], out.at[comp], sems.at[2 * comp + place])
            )
            copies[-1].start()
    for copy in copies:
        copy.wait()


def call(kernel, name, out_shapes, args, scratch, scalars=0, keep=True, aliases=None, outside=False):
    smem = pl.BlockSpec(memory_space=pltpu.SMEM)
    vmem = pl.BlockSpec(memory_space=pltpu.VMEM)
    shapes = [shape if isinstance(shape, jax.ShapeDtypeStruct) else jax.ShapeDtypeStruct(shape, F32) for shape in out_shapes]
    return pl.pallas_call(
        kernel,
        name=name,
        out_shape=[pltpu.VMEM(one.shape, one.dtype) if keep else one for one in shapes],
        in_specs=[smem] * scalars + [pl.BlockSpec(memory_space=pltpu.HBM) if outside else vmem] * (len(args) - scalars),
        out_specs=[vmem if keep else pl.BlockSpec(memory_space=pltpu.HBM)] * len(out_shapes),
        scratch_shapes=[pltpu.VMEM(one, F32) if isinstance(one, tuple) else one for one in scratch],
        input_output_aliases=aliases or {},
        compiler_params=pltpu.CompilerParams(vmem_limit_bytes=VMEM_LIMIT),
    )(*args[:scalars], *[held(arg, pltpu.HBM if outside else pltpu.VMEM) for arg in args[scalars:]])


def held(arg, space):
    return arg if isinstance(arg, np.ndarray) else pltpu.with_memory_space_constraint(arg, space)


def swap_blocks(blocks, dynamic):
    if not dynamic:
        stacked = lax.all_to_all(jnp.stack(blocks), "four", split_axis=0, concat_axis=0, tiled=True)
        return [stacked[place] for place in range(len(blocks))]
    size = len(blocks)
    swapped = list(blocks)
    for place in range(size - 1, 0, -1):
        swapped[place] = lax.ppermute(blocks[place], "four", [(i, i ^ offset_of(place, size)) for i in range(size)])
    return swapped


def share_lines(lines, beside=()):
    parts = lax.axis_size("dom")
    if parts != 8:
        return [lax.all_gather(lines, "dom", axis=0, tiled=False)], list(beside)
    slots = [lines] + [None] * (parts - 1)
    for slot in range(2, parts, 2):
        slots[slot] = lax.ppermute(lines, "dom", [(i, i ^ slot) for i in range(parts)])
        if beside and slot == parts - 2:
            slots[slot], *beside = lax.optimization_barrier((slots[slot], *beside))
    for slot in range(0, parts, 2):
        slots[slot + 1] = lax.ppermute(slots[slot], "dom", [(i, i ^ 1) for i in range(parts)])
    return slots, list(beside)


def shards(velocity, partner, partner_side, flipped):
    modes = velocity.shape[1]
    count = lax.axis_size("four")
    step, chunks = chunk_sizes(count)
    rows = POINTS * step
    sent_rows = 3 * rows // 4 if is_packed(modes) else rows
    dynamic = step == BLOCKS
    (inv_high, inv_low), (back_high, back_low) = transform_tables(count)
    starts, offsets = unit_windows(count)
    table = (rows, 3 * LANES)
    ids = jnp.stack([lax.axis_index("dom"), lax.axis_index("four")]).astype(jnp.int32)
    field = (NODES, LANES)
    blocks = [(sent_rows, LANES)] * count
    lined = line_rows(modes)

    lean = dynamic and chunks == 2 and is_packed(modes)
    spread = []
    source = velocity
    for chunk in range(chunks):
        load = chunk == 0
        sent = call(
            functools.partial(pack_kernel, step, count, dynamic, chunk, chunks, starts, offsets),
            "pack",
            blocks + [velocity.shape] * load,
            (ids, source),
            [table] + [pltpu.SemaphoreType.DMA((3,))] * load,
            scalars=1,
            outside=load,
        )
        if load:
            *sent, source = sent
        spread.append(swap_blocks(sent, dynamic))
    local = []
    carry = []
    for chunk in range(chunks):
        role = chunk if lean else None
        out = [(24 * step, LANES)] * count if lean else blocks
        sent = call(
            functools.partial(product_kernel, modes, step, count, dynamic, role),
            "products",
            out + [(count, SIDE, LANES)] * (role == 0),
            (ids, *spread[chunk], inv_high, inv_low, back_high, back_low, *carry),
            [
                (count, rows, LANES),
                (rows, count * LANES),
                (rows, 3 * LANES),
                (rows, 6 * LANES),
                (3, rows, LANES),
            ],
            scalars=1,
        )
        if role == 0:
            *sent, held_row = sent
            carry = [held_row]
        local += swap_blocks(sent, dynamic)

    base, lines = call(
        functools.partial(first_kernel, modes, step, count, chunks, dynamic, lean),
        "first",
        [field, (2 * lined, LANES)],
        (ids, partner, *local),
        [field],
        scalars=2,
    )
    tables = (ids, partner, partner_side, flipped)
    gathered, _ = share_lines(lines)
    slots = len(gathered)
    k0, k1, base, lines, sums = call(
        functools.partial(second_kernel, modes, slots),
        "second",
        [field, field, field, (2 * lined, LANES), (8, LANES)],
        (*tables, *gathered, lines, base),
        [field, (4, 2 * SIDE, LANES)],
        scalars=4,
        aliases={4 + slots + 1: 0},
    )
    flat = (3 * modes, NODES)
    turned = call(
        functools.partial(turn_kernel, starts, offsets, 2, True),
        "turn",
        [flat, flat, jax.ShapeDtypeStruct((4 * SIDE, NODES), BF16)],
        (k0, k1),
        [table, (rows, LANES)],
    )
    gathered, (t0, t1, scatter) = share_lines(lines, turned)
    k2, k3, a3, lines = call(
        functools.partial(third_kernel, modes, slots),
        "third",
        [field, field, field, (lined + SUM_ROWS, LANES)],
        (*tables, *gathered, lines, k1, sums, base),
        [field, (4, 2 * SIDE, LANES)],
        scalars=4,
        aliases={4 + slots + 3: 0},
    )
    turned = call(
        functools.partial(turn_kernel, starts, offsets, 3, False),
        "turn",
        [flat, flat, flat],
        (k2, k3, a3),
        [table, (rows, LANES)],
    )
    gathered, (t2, t3, ta) = share_lines(lines, turned)
    outs = call(
        functools.partial(last_kernel, slots),
        "last",
        [velocity.shape, velocity.shape],
        (*tables, *gathered, t0, t1, t2, t3, ta, scatter),
        [
            (4 * SIDE, LANES),
            (4, SIDE, LANES),
            velocity.shape,
            velocity.shape,
            pltpu.SemaphoreType.DMA((6,)),
        ],
        scalars=4,
        keep=False,
    )
    return tuple(outs)


def solution(mesh):
    return jax.shard_map(
        shards,
        mesh=mesh,
        in_specs=(P(None, "four", "dom"), P("dom", None), P("dom", None), P("dom", None)),
        out_specs=(P(None, "four", "dom"), P(None, "four", "dom")),
        check_vma=False,
    )
```

```python
import functools
import math

import jax
import jax.numpy as jnp
import numpy as np
from jax import lax
from jax.experimental import pallas as pl
from jax.experimental.pallas import tpu as pltpu
from jax.sharding import PartitionSpec as P

ITERS = 4
REACTION = 2.0
WAVE_STEP = 0.0625
LANES = 128
POINTS = 36
BLOCKS = 8
SIDE = 48
SENT = 40
NODES = 2304
CENTRE = 9.0
SPREAD = 9.0
TWICE = 2.0 / SPREAD
SUM_ROWS = 8
VMEM_LIMIT = 32 * 1024 * 1024
F32 = jnp.float32
BF16 = jnp.bfloat16


def gll_tables():
    inner_near = math.sqrt(1.0 / 3.0 - 2.0 * math.sqrt(7.0) / 21.0)
    inner_far = math.sqrt(1.0 / 3.0 + 2.0 * math.sqrt(7.0) / 21.0)
    points = np.array([-1.0, -inner_far, -inner_near, inner_near, inner_far, 1.0])
    values = (63.0 * points**5 - 70.0 * points**3 + 15.0 * points) / 8.0
    weights = 2.0 / (30.0 * values * values)
    spacing = points[:, None] - points[None, :]
    same_point = spacing == 0.0
    derivative = np.where(
        same_point, 0.0, values[:, None] / (values[None, :] * np.where(same_point, 1.0, spacing))
    )
    end_fix = np.array([-7.5, 0.0, 0.0, 0.0, 0.0, 7.5])
    derivative = derivative + np.eye(6) * end_fix[None, :]
    stiffness = derivative.T @ (weights[:, None] * derivative)
    return (weights, derivative, stiffness)


WEIGHTS, DERIV, STIFF = gll_tables()
STIFF_HAT = STIFF / WEIGHTS[:, None]


def fourier_tables(planes):
    plane_ids = np.arange(planes)
    mode_ids = np.arange(planes)
    waves = np.where(mode_ids < 2, 0, mode_ids // 2)
    angle = (plane_ids[:, None] * waves[None, :] % planes) * (2.0 * math.pi / planes)
    is_sine = (mode_ids % 2 == 1) & (mode_ids >= 2)
    basis = np.where(is_sine[None, :], np.sin(angle), np.cos(angle))
    alternating = np.where(plane_ids % 2 == 0, 1.0, -1.0)
    basis = np.where(mode_ids[None, :] == 1, alternating[:, None], basis)
    row_scale = np.where(mode_ids < 2, 1.0, 2.0) / planes
    forward = basis.T * row_scale[:, None]
    rates = (np.arange(planes // 2) * WAVE_STEP)[:, None]
    forward_z = np.zeros_like(forward)
    forward_z[0::2] = rates * forward[1::2]
    forward_z[1::2] = -rates * forward[0::2]
    forward_z[0:2] = 0.0
    return (basis, forward, forward_z)


def split_table(table):
    high = np.asarray(table, np.float32).astype(jnp.bfloat16)
    low = (np.asarray(table, np.float64) - high.astype(np.float64)).astype(np.float32)
    return np.concatenate([high, low.astype(jnp.bfloat16)], axis=1)


def transform_tables(count):
    planes = LANES
    modes = planes // count
    basis, forward, forward_z = fourier_tables(planes)
    inverse = np.zeros((count * LANES, 3 * planes))
    for block in range(count):
        ids = slice(block * modes, (block + 1) * modes)
        for comp in range(3):
            at = block * LANES + comp * modes
            inverse[at : at + modes, comp * planes : (comp + 1) * planes] = basis[:, ids].T
    back = -np.concatenate([forward.T, forward_z.T], axis=0)
    return split_table(inverse), split_table(back)


def chunk_sizes(count):
    group = BLOCKS * BLOCKS // count
    step = min(group, BLOCKS)
    return step, group // step


def unit_windows(count):
    step, _ = chunk_sizes(count)
    starts = []
    offsets = []
    for index in range(BLOCKS * BLOCKS // step):
        element = index * step
        first = element // BLOCKS * 6 * SIDE
        starts.append(first // LANES * LANES)
        offsets.append(first % LANES + 6 * (element % BLOCKS))
    return starts, offsets


def order_table(step, offset, scratch):
    width = scratch.shape[1]
    lane = lax.broadcasted_iota(jnp.int32, (step, width), 1)
    gap = lane - 6 * lax.broadcasted_iota(jnp.int32, (step, width), 0) - offset
    for point in range(POINTS):
        hit = gap == point // 6 * SIDE + point % 6
        scratch[pl.ds(point * step, step), :] = jnp.where(hit, 1.0, 0.0)
    return scratch[...].astype(BF16)


def halves(value):
    high = value.astype(BF16)
    low = (value - high.astype(F32)).astype(BF16)
    return high, low


def dot(left, right, dims):
    return lax.dot_general(left, right, (dims, ((), ())), preferred_element_type=F32)


def dot3(left, right):
    high, low = halves(left)
    dims = ((1,), (0,))
    width = right.shape[1] // 2
    both = dot(high, right, dims)
    return both[:, :width] + (both[:, width:] + dot(low, right[:, :width], dims))


def start_of(point, ey):
    return pl.multiple_of(point * 64 + ey * 8, 8)


def get(ref, point, ey):
    return ref[pl.ds(start_of(point, ey), 8), :]


def put(ref, point, ey, value):
    ref[pl.ds(start_of(point, ey), 8), :] = value


def ex_ids():
    return lax.broadcasted_iota(jnp.int32, (8, LANES), 0)


def helmholtz_rates(four, modes):
    lane = lax.broadcasted_iota(jnp.int32, (8, LANES), 1)
    mode = four * modes + lax.rem(lane, jnp.int32(modes))
    wave = jnp.where(mode == 0, 0, jnp.where(mode == 1, LANES // 2, lax.div(mode, jnp.int32(2))))
    scaled = wave.astype(F32) * WAVE_STEP
    return REACTION + scaled * scaled


def glued_flags(partner_ref):
    return [jnp.where(partner_ref[0, side] >= 0, 1.0, 0.0).astype(F32) for side in range(4)]


def col_masks(flags):
    ex = ex_ids()
    return jnp.where(ex == 0, flags[3], 1.0), jnp.where(ex == 7, flags[1], 1.0)


def join_cols(first, last, masks):
    ex = ex_ids()
    from_right = jnp.where(ex < 7, pltpu.roll(first, 7, 0), 0.0)
    from_left = jnp.where(ex > 0, pltpu.roll(last, 1, 0), 0.0)
    return (first + from_left) * masks[0], (last + from_right) * masks[1]


def join_rows(ref, flags, pairs=range(7)):
    ex = ex_ids()
    not_first = jnp.where(ex == 0, 0.0, 1.0)
    not_last = jnp.where(ex == 7, 0.0, 1.0)
    for ix in range(6):
        for ey in pairs:
            total = get(ref, 30 + ix, ey) + get(ref, ix, ey + 1)
            put(ref, 30 + ix, ey, total)
            put(ref, ix, ey + 1, total)
        low = get(ref, ix, 0) * flags[0]
        high = get(ref, 30 + ix, 7) * flags[2]
        if ix == 0:
            low, high = low * not_first, high * not_first
        if ix == 5:
            low, high = low * not_last, high * not_last
        put(ref, ix, 0, low)
        put(ref, 30 + ix, 7, high)


def line_product(line, table, mirrored=1.0):
    sums = [line[j] + line[5 - j] for j in range(3)]
    gaps = [line[j] - line[5 - j] for j in range(3)]
    out = [None] * 6
    for i in range(3):
        even = None
        odd = None
        for j in range(3):
            even_term = sums[j] * float(0.5 * (table[i, j] + table[i, 5 - j]))
            odd_term = gaps[j] * float(0.5 * (table[i, j] - table[i, 5 - j]))
            even = even_term if even is None else even + even_term
            odd = odd_term if odd is None else odd + odd_term
        out[i] = even + odd
        out[5 - i] = even - odd if mirrored > 0 else odd - even
    return out


def apply_local(src, dst, rates, flags, terms=(), products=(), energy=False):
    masks = col_masks(flags)

    def body(ey, sums):
        sums = list(sums)
        for ix in range(6):
            line = []
            for iy in range(6):
                point = 6 * iy + ix
                if not terms:
                    line.append(get(src, point, ey))
                    continue
                values = [get(ref, point, ey) for _, ref in terms]
                value = None
                for (factor, _), part in zip(terms, values):
                    part = -part if factor == -1.0 else part * factor
                    value = part if value is None else value + part
                put(src, point, ey, value)
                line.append(value)
                values.append(value)
                ends = (iy in (0, 5)) + (ix in (0, 5))
                for place, (left, right) in enumerate(products):
                    both = values[left] * values[right]
                    sums[place] = sums[place] + (both * (0.5**ends) if ends else both)
            out = line_product(line, STIFF_HAT)
            for iy in range(6):
                put(dst, 6 * iy + ix, ey, out[iy] + rates * line[iy])
        for iy in range(6):
            line = [get(src, 6 * iy + ix, ey) for ix in range(6)]
            out = line_product(line, STIFF_HAT)
            full = [
                (get(dst, 6 * iy + ix, ey) + out[ix]) * float(WEIGHTS[iy] * WEIGHTS[ix])
                for ix in range(6)
            ]
            if energy:
                for ix in range(6):
                    sums[-1] = sums[-1] + full[ix] * line[ix]
            full[0], full[5] = join_cols(full[0], full[5], masks)
            for ix in range(6):
                put(dst, 6 * iy + ix, ey, full[ix])
        return tuple(sums)

    zero = jnp.zeros((8, LANES), F32)
    sums = lax.fori_loop(0, BLOCKS, body, (zero,) * (len(products) + int(energy)), unroll=2)
    join_rows(dst, flags)
    return sums


def side_slice(side, i):
    if side == 0:
        return pl.ds(i * 64, 8)
    if side == 2:
        return pl.ds((30 + i) * 64 + 56, 8)
    if side == 1:
        return pl.ds((6 * i + 5) * 64 + 7, 8, stride=8)
    return pl.ds(6 * i * 64, 8, stride=8)


def read_line(ref, side):
    return [ref[side_slice(side, i), :] for i in range(6)]


def lane_ids():
    return lax.broadcasted_iota(jnp.int32, (8, LANES), 1)


def is_packed(modes):
    return 3 * modes + modes == LANES


def pack_lanes(values, modes):
    if not is_packed(modes):
        return values
    third = len(values) // 4
    inside = lane_ids() < 3 * modes
    return [
        jnp.where(
            inside,
            values[comp * third + at],
            pltpu.roll(values[3 * third + at], (3 - comp) * modes, 1),
        )
        for comp in range(3)
        for at in range(third)
    ]


def unpack_last(pieces, modes):
    block = lax.div(lane_ids(), jnp.int32(modes))
    turned = [pltpu.roll(pieces[comp], (comp + 1) * modes, 1) for comp in range(3)]
    return jnp.where(block == 0, turned[0], jnp.where(block == 1, turned[1], turned[2]))


def unpack_lanes(values, modes):
    if not is_packed(modes):
        return values
    third = len(values) // 3
    return values + [
        unpack_last([values[comp * third + at] for comp in range(3)], modes) for at in range(third)
    ]


def line_rows(modes):
    return 3 * SENT if is_packed(modes) else 4 * SENT


def first_points(last_points):
    return jnp.where(ex_ids() > 0, pltpu.roll(last_points, 1, 0), 0.0)


def write_lines(ref, lines_ref, base, modes):
    values = []
    for side in range(4):
        values += read_line(ref, side)[1:]
    for at, value in enumerate(pack_lanes(values, modes)):
        lines_ref[pl.ds(base + at * 8, 8), :] = value


def load_lines(lines_ref, modes):
    count = line_rows(modes) // 8
    values = unpack_lanes([lines_ref[pl.ds(at * 8, 8), :] for at in range(count)], modes)
    sides = [values[side * 5 : side * 5 + 5] for side in range(4)]
    return [[first_points(side[4])] + side for side in sides]


def add_lines(ref, lines):
    for side in range(4):
        for i in range(6):
            where = side_slice(side, i)
            ref[where, :] = ref[where, :] + lines[side][i]


def add_all(left, right):
    return [[a + b for a, b in zip(one, two)] for one, two in zip(left, right)]


def reverse_rows(value):
    ex = ex_ids()
    value = pltpu.roll(value, 4, 0)
    value = jnp.where((ex & 2) == 0, pltpu.roll(value, 6, 0), pltpu.roll(value, 2, 0))
    return jnp.where((ex & 1) == 0, pltpu.roll(value, 7, 0), pltpu.roll(value, 1, 0))


def collect_sides(gath_refs, own, partner_ref, side_ref, sides, modes):
    sets = sides.shape[1] // SIDE
    step = line_rows(modes)

    def copy_side(side, load):
        there = jnp.maximum(side_ref[0, side], 0)

        def fill(place, values):
            for i, value in enumerate([first_points(values[4])] + values):
                sides[side, pl.ds(place * SIDE + i * 8, 8), :] = value

        def plain():
            for place in range(sets):
                first = place * step + there * SENT
                fill(place, [load(pl.multiple_of(first + i * 8, 8)) for i in range(5)])

        if not is_packed(modes):
            plain()
            return
        pl.when(there < 3)(plain)

        @pl.when(there == 3)
        def _():
            for place in range(sets):
                first = place * step
                values = []
                for i in range(5):
                    pieces = [load(first + comp * SENT + i * 8) for comp in range(3)]
                    values.append(unpack_last(pieces, modes))
                fill(place, values)

    def body(side, carry):
        part = partner_ref[0, side]
        if len(gath_refs) == 1:
            source = jnp.maximum(part, 0)
            copy_side(side, lambda at: gath_refs[0][source, pl.ds(at, 8), :])
            return carry
        for slot, ref in enumerate(gath_refs):
            here = jnp.logical_and(part >= 0, jnp.bitwise_xor(part, own) == slot)

            @pl.when(here)
            def _(ref=ref):
                copy_side(side, lambda at: ref[pl.ds(at, 8), :])

        return carry

    lax.fori_loop(0, 4, body, 0)


def incoming_lines(sides, place, partner_ref, flip_ref):
    lines = []
    for side in range(4):
        glued = partner_ref[0, side] >= 0
        turned = flip_ref[0, side] == 1
        line = []
        for i in range(6):
            at = pl.multiple_of(place * SIDE + jnp.where(turned, 5 - i, i) * 8, 8)
            value = sides[side, pl.ds(at, 8), :]
            value = jnp.where(turned, reverse_rows(value), value)
            line.append(jnp.where(glued, value, 0.0))
        lines.append(line)
    return lines


def own_reaction(own_lines, rates, flags, scale):
    ex = ex_ids()
    edge = float(WEIGHTS[0])
    corner = float(STIFF[0, 0])
    lines = []
    for side in range(4):
        line = own_lines[side]
        along = line_product(line, STIFF_HAT)
        out = [
            (along[i] * edge + line[i] * (corner + rates * edge)) * float(WEIGHTS[i])
            for i in range(6)
        ]
        first = out[0] + pltpu.roll(out[5], 1, 0)
        last = out[5] + pltpu.roll(out[0], 7, 0)
        out[0] = jnp.where(ex > 0, first, 0.0)
        out[5] = jnp.where(ex < 7, last, 0.0)
        lines.append([value * (flags[side] * scale) for value in out])
    return lines


def pick(index, values):
    if isinstance(index, int):
        return values[index]
    chosen = jnp.int32(values[0])
    for place in range(1, len(values)):
        chosen = jnp.where(index == place, jnp.int32(values[place]), chosen)
    return chosen


def offset_of(place, size):
    return (0, 3, 1, 2)[place] if size == 4 else place


def block_of(place, four, size):
    return place if isinstance(four, int) else jnp.bitwise_xor(four, offset_of(place, size))


def pack_kernel(step, count, dynamic, chunk, chunks, starts, offsets, ids_ref, source_ref, *refs):
    send_refs = refs[:count]
    load = chunk == 0
    scratch = refs[-2] if load else refs[-1]
    width = scratch.shape[1]
    held_ref = refs[count] if load else source_ref
    modes = held_ref.shape[1]
    four = ids_ref[1] if dynamic else 0
    copies = []
    if load:
        for comp in range(3):
            copies.append(
                pltpu.make_async_copy(source_ref.at[comp], held_ref.at[comp], refs[-1].at[comp])
            )
            copies[-1].start()
    for place in range(count):
        index = block_of(place, four, count)
        table = order_table(step, pick(index, offsets[chunk::chunks]), scratch)
        if place == 0:
            for copy in copies:
                copy.wait()
        start = pick(index, starts[chunk::chunks])
        start = start if isinstance(start, int) else pl.multiple_of(start, LANES)
        rows = [held_ref[comp, :, pl.ds(start, width)] for comp in range(3)]
        pad = jnp.zeros((LANES - 3 * modes, width), F32)
        high, low = halves(jnp.concatenate(rows + [pad], axis=0))
        both = jnp.concatenate([high, low], axis=0)
        out = dot(table, both, ((1,), (1,)))
        out = out[:, :LANES] + out[:, LANES:]
        if not is_packed(modes):
            send_refs[place][...] = out
            continue
        values = [out[point * step : (point + 1) * step] for point in range(POINTS)]
        for at, value in enumerate(pack_lanes(values, modes)):
            send_refs[place][pl.ds(at * step, step), :] = value


def product_kernel(modes, step, count, dynamic, role, ids_ref, *refs):
    recv_refs = refs[:count]
    inverse_ref, back_ref = refs[count : count + 2]
    refs = refs[count + 2 :]
    if role == 1:
        carry_ref, refs = refs[0], refs[1:]
    send_refs, refs = refs[:count], refs[count:]
    if role == 0:
        carry_ref, refs = refs[0], refs[1:]
    full, lined, phys, prod, spec = refs
    four = ids_ref[1] if dynamic else 0
    packed = is_packed(modes)
    for place in range(count):
        index = block_of(place, four, count)
        if packed:
            ready = 3 * POINTS // 4
            values = [recv_refs[place][pl.ds(at * step, step), :] for at in range(ready)]
            for at, value in enumerate(unpack_lanes(values, modes)):
                full[place, pl.ds(at * step, step), :] = value
        else:
            full[place] = recv_refs[place][...]
        first = index * LANES
        first = first if isinstance(first, int) else pl.multiple_of(first, LANES)
        lined[:, pl.ds(first, LANES)] = full[place]
    phys[...] = dot3(lined[...], inverse_ref[...])
    width = 2 * LANES

    def field(point, comp):
        return phys[pl.ds(point * step, step), comp * LANES : (comp + 1) * LANES]

    for comp in range(3):
        wide = pl.ds(comp * width, LANES)
        for iy in range(6):
            line = []
            for ix in range(6):
                point = 6 * iy + ix
                value = field(point, comp)
                line.append(value * field(point, 0))
                prod[pl.ds(point * step, step), pl.ds(comp * width + LANES, LANES)] = (
                    value * field(point, 2)
                )
            out = line_product(line, DERIV, -1.0)
            for ix in range(6):
                prod[pl.ds((6 * iy + ix) * step, step), wide] = out[ix]
        for ix in range(6):
            line = [field(6 * iy + ix, comp) * field(6 * iy + ix, 1) for iy in range(6)]
            out = line_product(line, DERIV, -1.0)
            for iy in range(6):
                at = pl.ds((6 * iy + ix) * step, step)
                prod[at, wide] = prod[at, wide] + out[iy]
        spec[comp] = dot3(prod[:, comp * width : (comp + 1) * width], back_ref[...])

    lane_block = lax.div(lax.broadcasted_iota(jnp.int32, (step, LANES), 1), jnp.int32(modes))
    masks = []
    shifts = []
    for place in range(count):
        index = block_of(place, four, count)
        masks.append([lane_block == lax.rem(index + comp, count) for comp in range(2)])
        shifts.append(lax.rem(LANES - index * modes, LANES))
    kept = []
    for point in range(POINTS):
        at = pl.ds(point * step, step)
        mass = float(WEIGHTS[point // 6] * WEIGHTS[point % 6])
        turned = [spec[0, at, :]]
        turned += [pltpu.roll(spec[comp, at, :], comp * modes, 1) for comp in (1, 2)]
        for place in range(count):
            mask = masks[place]
            mixed = jnp.where(mask[0], turned[0], jnp.where(mask[1], turned[1], turned[2]))
            nonlinear = pltpu.roll(mixed, shifts[place], 1)
            full[place, at, :] = mass * (REACTION * full[place, at, :] + nonlinear)
    ex = None if role is None else ex_ids()
    for place in range(count):
        values = [full[place, pl.ds(point * step, step), :] for point in range(POINTS)]
        if role is not None:
            left = jnp.zeros((8, LANES), F32)
            sent = []
            for iy in range(6):
                line = values[6 * iy : 6 * iy + 6]
                line[5] = line[5] + jnp.where(ex < 7, pltpu.roll(line[0], 7, 0), 0.0)
                if role == 0 and iy == 5:
                    for ix in range(6):
                        carry_ref[place, pl.ds(ix * 8, 8), :] = line[ix]
                    continue
                if role == 1 and iy == 0:
                    line = [line[ix] + carry_ref[place, pl.ds(ix * 8, 8), :] for ix in range(6)]
                left = jnp.where(ex == iy, pltpu.roll(line[0], iy, 0) if iy else line[0], left)
                sent += line[1:]
            values = sent + [left]
            values += [left] * (32 - len(values))
        for at, value in enumerate(pack_lanes(values, modes)):
            send_refs[place][pl.ds(at * step, step), :] = value


def spread_rows(values, masks):
    ex = ex_ids()
    rows = (len(values) - 1) // 5
    left = values[5 * rows]
    points = []
    for iy in range(rows):
        line = values[5 * iy : 5 * iy + 5]
        start = pltpu.roll(left, 8 - iy, 0) if iy else left
        first = jnp.where(ex == 0, start, pltpu.roll(line[4], 1, 0))
        points += [first * masks[0]] + line[:4] + [line[4] * masks[1]]
    return points


def first_kernel(modes, step, count, chunks, dynamic, lean, ids_ref, partner_ref, *refs):
    recv_refs = refs[: count * chunks]
    base_ref, lines_ref, work = refs[count * chunks :]
    four = ids_ref[1] if dynamic else 0
    rates = helmholtz_rates(ids_ref[1], modes)
    flags = glued_flags(partner_ref)
    masks = col_masks(flags)
    for place in range(count):
        block = block_of(place, four, count)
        shares = []
        for chunk in range(chunks):
            ref = recv_refs[chunk * count + place]
            ready = ref.shape[0] // step
            shares.append(
                unpack_lanes([ref[pl.ds(at * step, step), :] for at in range(ready)], modes)
            )
        if lean:
            odd = spread_rows(shares[1][:31], masks)
            shares = [spread_rows(shares[0][:26], masks) + odd[:6], odd]
        for chunk in range(chunks):
            first = (block * chunks + chunk) * step
            for point in range(POINTS):
                at = point * 64 + first
                at = at if isinstance(at, int) else pl.multiple_of(at, step)
                base_ref[pl.ds(at, step), :] = shares[chunk][point]
    if not lean:
        for ey in range(BLOCKS):
            for iy in range(6):
                first, last = join_cols(
                    get(base_ref, 6 * iy, ey), get(base_ref, 6 * iy + 5, ey), masks
                )
                put(base_ref, 6 * iy, ey, first)
                put(base_ref, 6 * iy + 5, ey, last)
    join_rows(base_ref, flags, range(1, 7, 2) if lean else range(7))
    apply_local(base_ref, work, rates, flags)
    write_lines(base_ref, lines_ref, 0, modes)
    write_lines(work, lines_ref, line_rows(modes), modes)


def sum_rows(sums):
    return [jnp.sum(value, axis=0, keepdims=True) for value in sums]


def second_kernel(modes, slots, ids_ref, partner_ref, side_ref, flip_ref, *refs):
    gath_refs = refs[:slots]
    lines_ref, _, k0_ref, k1_ref, k2_ref, next_ref, sums_ref, work, sides = refs[slots:]
    rates = helmholtz_rates(ids_ref[1], modes)
    flags = glued_flags(partner_ref)
    collect_sides(gath_refs, ids_ref[0], partner_ref, side_ref, sides, modes)
    back = own_reaction(load_lines(lines_ref, modes), rates, flags, 1.0)
    add_lines(k0_ref, incoming_lines(sides, 0, partner_ref, flip_ref))
    apply_local(k0_ref, work, rates, flags)
    add_lines(work, add_all(incoming_lines(sides, 1, partner_ref, flip_ref), back))
    sums = apply_local(
        k1_ref, work, rates, flags,
        terms=[(1.0 / SPREAD, work), (-CENTRE / SPREAD, k0_ref)],
        products=[(1, 1), (1, -1), (-1, -1)],
    )
    write_lines(work, next_ref, 0, modes)
    apply_local(
        k2_ref, work, rates, flags,
        terms=[(TWICE, work), (-CENTRE * TWICE, k1_ref), (-1.0, k0_ref)],
    )
    write_lines(work, next_ref, line_rows(modes), modes)
    sums_ref[...] = jnp.concatenate(sum_rows(sums) + [jnp.zeros((5, LANES), F32)], axis=0)


def third_kernel(modes, slots, ids_ref, partner_ref, side_ref, flip_ref, *refs):
    gath_refs = refs[:slots]
    lines_ref, k1_ref, sums_ref, _ = refs[slots : slots + 4]
    k2_ref, k3_ref, a3_ref, next_ref, work, sides = refs[slots + 4 :]
    rates = helmholtz_rates(ids_ref[1], modes)
    flags = glued_flags(partner_ref)
    collect_sides(gath_refs, ids_ref[0], partner_ref, side_ref, sides, modes)
    back = own_reaction(load_lines(lines_ref, modes), rates, flags, TWICE)
    incoming = incoming_lines(sides, 0, partner_ref, flip_ref)
    add_lines(k2_ref, [[value * TWICE for value in line] for line in incoming])
    apply_local(k2_ref, work, rates, flags)
    add_lines(work, add_all(incoming_lines(sides, 1, partner_ref, flip_ref), back))
    sums = apply_local(
        k3_ref, a3_ref, rates, flags,
        terms=[(TWICE, work), (-CENTRE * TWICE, k2_ref), (-1.0, k1_ref)],
        products=[(2, 1), (1, 1), (1, -1), (-1, -1)],
        energy=True,
    )
    write_lines(a3_ref, next_ref, 0, modes)
    next_ref[pl.ds(line_rows(modes), SUM_ROWS), :] = jnp.concatenate(
        [sums_ref[:3, :]] + sum_rows(sums), axis=0
    )


def turn_kernel(starts, offsets, fields, has_scatter, *refs):
    field_refs = refs[:fields]
    out_refs = refs[fields : 2 * fields]
    scratch, rows = refs[-2:]
    step = rows.shape[0] // POINTS
    used = out_refs[0].shape[0]
    width = scratch.shape[1]
    for out_ref in out_refs:
        out_ref[...] = jnp.zeros(out_ref.shape, F32)
    for unit in range(len(starts)):
        table = order_table(step, offsets[unit], scratch)
        for field_ref, out_ref in zip(field_refs, out_refs):
            for point in range(POINTS):
                rows[pl.ds(point * step, step), :] = field_ref[pl.ds(point * 64 + unit * step, step), :]
            high, low = halves(jnp.transpose(rows[...])[:used])
            both = jnp.concatenate([high, low], axis=0)
            out = dot(both, table, ((1,), (0,)))
            window = pl.ds(starts[unit], width)
            out_ref[:, window] = out_ref[:, window] + (out[:used] + out[used:])
    if has_scatter:
        scatter_ref = refs[2 * fields]
        place = lax.broadcasted_iota(jnp.int32, (SIDE, NODES), 0)
        at = 6 * jnp.bitwise_and(place, 7) + lax.shift_right_logical(place, 3)
        node = lax.broadcasted_iota(jnp.int32, (SIDE, NODES), 1)
        targets = (at, at * SIDE + SIDE - 1, at + (SIDE - 1) * SIDE, at * SIDE)
        for side, target in enumerate(targets):
            scatter_ref[side * SIDE : (side + 1) * SIDE, :] = jnp.where(
                node == target, 1.0, 0.0
            ).astype(BF16)


def conjugate_coefficients(gram, energy):
    zero = jnp.zeros_like(energy)

    def image(vec):
        out = [zero] * 5
        for j in range(4):
            if vec[j] is None:
                continue
            out[j] = out[j] + CENTRE * vec[j]
            out[j + 1] = out[j + 1] + (SPREAD if j == 0 else 0.5 * SPREAD) * vec[j]
            if j > 0:
                out[j - 1] = out[j - 1] + 0.5 * SPREAD * vec[j]
        return out

    def inner(left, right):
        total = zero
        for i in range(4):
            for j in range(4):
                if left[i] is not None and right[j] is not None:
                    total = total + left[i] * right[j] * gram[i][j]
        return total

    moments = [[None] * 4 for _ in range(4)]
    for j in range(3):
        column = image([jnp.ones_like(energy) if i == j else None for i in range(4)])
        for i in range(4):
            total = zero
            for m in range(max(j - 1, 0), j + 2):
                total = total + column[m] * gram[i][m]
            moments[i][j] = total
    for i in range(3):
        moments[i][3] = moments[3][i]
    moments[3][3] = energy

    def pad(vec, size):
        return [vec[i] if i < size else None for i in range(4)]

    residual = [jnp.ones_like(energy), zero, zero, zero, zero]
    direction = list(residual)
    solution = [zero] * 4
    norm_now = gram[0][0]
    for step in range(ITERS):
        trimmed = pad(direction, step + 1)
        bend = zero
        for i in range(step + 1):
            for j in range(step + 1):
                bend = bend + direction[i] * direction[j] * moments[i][j]
        alpha = norm_now / bend
        moved = image(trimmed)
        for i in range(step + 1):
            solution[i] = solution[i] + alpha * direction[i]
        for i in range(step + 2):
            residual[i] = residual[i] - alpha * moved[i]
        if step < ITERS - 1:
            kept = pad(residual, step + 2)
            norm_next = inner(kept, kept)
            ratio = norm_next / norm_now
            direction = [residual[i] + ratio * direction[i] for i in range(5)]
            norm_now = norm_next
    return solution, residual


def last_kernel(slots, ids_ref, partner_ref, side_ref, flip_ref, *refs):
    gath_refs = refs[:slots]
    turned = refs[slots : slots + 5]
    scatter_ref, sol_out, res_out, lines, sides, sol_ref, res_ref, sems = refs[slots + 5 :]
    modes = sol_ref.shape[1]
    used = 3 * modes
    where = pl.ds(line_rows(modes), SUM_ROWS)
    if slots == 1:
        parts = [gath_refs[0][part, where, :] for part in range(gath_refs[0].shape[0])]
    else:
        parts = [ref[where, :] for ref in gath_refs]
    sums = functools.reduce(lambda left, right: left + right, parts)
    g00, g01, g11, g12, g22, g23, g33, energy = [
        jnp.broadcast_to(sums[place : place + 1, :], (8, LANES)) for place in range(8)
    ]
    g02 = 2.0 * g11 - g00
    g03 = 2.0 * g12 - g01
    g13 = (g22 - g00) + g11
    gram = [
        [g00, g01, g02, g03],
        [g01, g11, g12, g13],
        [g02, g12, g22, g23],
        [g03, g13, g23, g33],
    ]
    solution, residual = conjugate_coefficients(gram, energy)
    on_a3 = residual[4] * TWICE
    on_k3 = residual[3] - on_a3 * CENTRE
    on_k2 = residual[2] - residual[4]
    factors = list(solution) + [residual[0], residual[1], on_k2, on_k3, on_a3]
    columns = jnp.transpose(
        jnp.concatenate([value[:1] for value in factors] + [jnp.zeros((LANES - 9, LANES), F32)], axis=0)
    )
    copies = []

    def send(comp, place, buffer, out):
        copies.append(pltpu.make_async_copy(buffer.at[comp], out.at[comp], sems.at[2 * comp + place]))
        copies[-1].start()

    def scaled(at, first):
        rows = [ref[at : at + 8, :] for ref in turned[: 5 if first else 4]]
        terms = [columns[at : at + 8, first + k : first + k + 1] * row for k, row in enumerate(rows)]
        return functools.reduce(lambda left, right: left + right, terms)

    for comp in range(3):
        for first in range(0, modes, 8):
            sol_ref[comp, first : first + 8, :] = scaled(comp * modes + first, 0)
        send(comp, 0, sol_ref, sol_out)
    collect_sides(gath_refs, ids_ref[0], partner_ref, side_ref, sides, modes)
    incoming = incoming_lines(sides, 0, partner_ref, flip_ref)
    for side in range(4):
        for i in range(6):
            lines[pl.ds(side * SIDE + i * 8, 8), :] = incoming[side][i] * on_a3
    high, low = halves(jnp.transpose(lines[...])[:used])
    added = dot(jnp.concatenate([high, low], axis=0), scatter_ref[...], ((1,), (0,)))
    for comp in range(3):
        for first in range(0, modes, 8):
            at = comp * modes + first
            res_ref[comp, first : first + 8, :] = scaled(at, 4) + (
                added[at : at + 8] + added[used + at : used + at + 8]
            )
        send(comp, 1, res_ref, res_out)
    for copy in copies:
        copy.wait()


def call(kernel, name, out_shapes, args, scratch, scalars=0, keep=True, aliases=None, outside=False):
    smem = pl.BlockSpec(memory_space=pltpu.SMEM)
    vmem = pl.BlockSpec(memory_space=pltpu.VMEM)
    shapes = [shape if isinstance(shape, jax.ShapeDtypeStruct) else jax.ShapeDtypeStruct(shape, F32) for shape in out_shapes]
    return pl.pallas_call(
        kernel,
        name=name,
        out_shape=[pltpu.VMEM(one.shape, one.dtype) if keep else one for one in shapes],
        in_specs=[smem] * scalars + [pl.BlockSpec(memory_space=pltpu.HBM) if outside else vmem] * (len(args) - scalars),
        out_specs=[vmem if keep else pl.BlockSpec(memory_space=pltpu.HBM)] * len(out_shapes),
        scratch_shapes=[pltpu.VMEM(one, F32) if isinstance(one, tuple) else one for one in scratch],
        input_output_aliases=aliases or {},
        compiler_params=pltpu.CompilerParams(vmem_limit_bytes=VMEM_LIMIT),
    )(*args[:scalars], *[held(arg, pltpu.HBM if outside else pltpu.VMEM) for arg in args[scalars:]])


def held(arg, space):
    return arg if isinstance(arg, np.ndarray) else pltpu.with_memory_space_constraint(arg, space)


def swap_blocks(blocks, dynamic):
    if not dynamic:
        stacked = lax.all_to_all(jnp.stack(blocks), "four", split_axis=0, concat_axis=0, tiled=True)
        return [stacked[place] for place in range(len(blocks))]
    size = len(blocks)
    swapped = list(blocks)
    for place in range(size - 1, 0, -1):
        swapped[place] = lax.ppermute(blocks[place], "four", [(i, i ^ offset_of(place, size)) for i in range(size)])
    return swapped


def share_lines(lines, beside=()):
    parts = lax.axis_size("dom")
    if parts != 8:
        return [lax.all_gather(lines, "dom", axis=0, tiled=False)], list(beside)
    slots = [lines] + [None] * (parts - 1)
    for slot in range(2, parts, 2):
        slots[slot] = lax.ppermute(lines, "dom", [(i, i ^ slot) for i in range(parts)])
        if beside and slot == parts - 2:
            slots[slot], *beside = lax.optimization_barrier((slots[slot], *beside))
    for slot in range(0, parts, 2):
        slots[slot + 1] = lax.ppermute(slots[slot], "dom", [(i, i ^ 1) for i in range(parts)])
    return slots, list(beside)


def shards(velocity, partner, partner_side, flipped):
    modes = velocity.shape[1]
    count = lax.axis_size("four")
    step, chunks = chunk_sizes(count)
    rows = POINTS * step
    sent_rows = 3 * rows // 4 if is_packed(modes) else rows
    dynamic = step == BLOCKS
    inverse, back = transform_tables(count)
    starts, offsets = unit_windows(count)
    table = (rows, 3 * LANES)
    ids = jnp.stack([lax.axis_index("dom"), lax.axis_index("four")]).astype(jnp.int32)
    field = (NODES, LANES)
    blocks = [(sent_rows, LANES)] * count
    lined = line_rows(modes)

    lean = dynamic and chunks == 2 and is_packed(modes)
    spread = []
    source = velocity
    for chunk in range(chunks):
        load = chunk == 0
        sent = call(
            functools.partial(pack_kernel, step, count, dynamic, chunk, chunks, starts, offsets),
            "pack",
            blocks + [velocity.shape] * load,
            (ids, source),
            [table] + [pltpu.SemaphoreType.DMA((3,))] * load,
            scalars=1,
            outside=load,
        )
        if load:
            *sent, source = sent
        spread.append(swap_blocks(sent, dynamic))
    local = []
    carry = []
    for chunk in range(chunks):
        role = chunk if lean else None
        out = [(24 * step, LANES)] * count if lean else blocks
        sent = call(
            functools.partial(product_kernel, modes, step, count, dynamic, role),
            "products",
            out + [(count, SIDE, LANES)] * (role == 0),
            (ids, *spread[chunk], inverse, back, *carry),
            [
                (count, rows, LANES),
                (rows, count * LANES),
                (rows, 3 * LANES),
                (rows, 6 * LANES),
                (3, rows, LANES),
            ],
            scalars=1,
        )
        if role == 0:
            *sent, held_row = sent
            carry = [held_row]
        local += swap_blocks(sent, dynamic)

    base, lines = call(
        functools.partial(first_kernel, modes, step, count, chunks, dynamic, lean),
        "first",
        [field, (2 * lined, LANES)],
        (ids, partner, *local),
        [field],
        scalars=2,
    )
    tables = (ids, partner, partner_side, flipped)
    gathered, _ = share_lines(lines)
    slots = len(gathered)
    k0, k1, base, lines, sums = call(
        functools.partial(second_kernel, modes, slots),
        "second",
        [field, field, field, (2 * lined, LANES), (8, LANES)],
        (*tables, *gathered, lines, base),
        [field, (4, 2 * SIDE, LANES)],
        scalars=4,
        aliases={4 + slots + 1: 0},
    )
    flat = (3 * modes, NODES)
    turned = call(
        functools.partial(turn_kernel, starts, offsets, 2, True),
        "turn",
        [flat, flat, jax.ShapeDtypeStruct((4 * SIDE, NODES), BF16)],
        (k0, k1),
        [table, (rows, LANES)],
    )
    gathered, (t0, t1, scatter) = share_lines(lines, turned)
    k2, k3, a3, lines = call(
        functools.partial(third_kernel, modes, slots),
        "third",
        [field, field, field, (lined + SUM_ROWS, LANES)],
        (*tables, *gathered, lines, k1, sums, base),
        [field, (4, 2 * SIDE, LANES)],
        scalars=4,
        aliases={4 + slots + 3: 0},
    )
    turned = call(
        functools.partial(turn_kernel, starts, offsets, 3, False),
        "turn",
        [flat, flat, flat],
        (k2, k3, a3),
        [table, (rows, LANES)],
    )
    gathered, (t2, t3, ta) = share_lines(lines, turned)
    outs = call(
        functools.partial(last_kernel, slots),
        "last",
        [velocity.shape, velocity.shape],
        (*tables, *gathered, t0, t1, t2, t3, ta, scatter),
        [
            (4 * SIDE, LANES),
            (4, SIDE, LANES),
            velocity.shape,
            velocity.shape,
            pltpu.SemaphoreType.DMA((6,)),
        ],
        scalars=4,
        keep=False,
    )
    return tuple(outs)


def solution(mesh):
    return jax.shard_map(
        shards,
        mesh=mesh,
        in_specs=(P(None, "four", "dom"), P("dom", None), P("dom", None), P("dom", None)),
        out_specs=(P(None, "four", "dom"), P(None, "four", "dom")),
        check_vma=False,
    )
```

```python
import functools
import math

import jax
import jax.numpy as jnp
import numpy as np
from jax import lax
from jax.experimental import pallas as pl
from jax.experimental.pallas import tpu as pltpu
from jax.sharding import PartitionSpec as P

ITERS = 4
REACTION = 2.0
WAVE_STEP = 0.0625
LANES = 128
POINTS = 36
BLOCKS = 8
SIDE = 48
SENT = 40
NODES = 2304
CENTRE = 9.0
SPREAD = 9.0
TWICE = 2.0 / SPREAD
SUM_ROWS = 8
VMEM_LIMIT = 32 * 1024 * 1024
F32 = jnp.float32
BF16 = jnp.bfloat16


def gll_tables():
    inner_near = math.sqrt(1.0 / 3.0 - 2.0 * math.sqrt(7.0) / 21.0)
    inner_far = math.sqrt(1.0 / 3.0 + 2.0 * math.sqrt(7.0) / 21.0)
    points = np.array([-1.0, -inner_far, -inner_near, inner_near, inner_far, 1.0])
    values = (63.0 * points**5 - 70.0 * points**3 + 15.0 * points) / 8.0
    weights = 2.0 / (30.0 * values * values)
    spacing = points[:, None] - points[None, :]
    same_point = spacing == 0.0
    derivative = np.where(
        same_point, 0.0, values[:, None] / (values[None, :] * np.where(same_point, 1.0, spacing))
    )
    end_fix = np.array([-7.5, 0.0, 0.0, 0.0, 0.0, 7.5])
    derivative = derivative + np.eye(6) * end_fix[None, :]
    stiffness = derivative.T @ (weights[:, None] * derivative)
    return (weights, derivative, stiffness)


WEIGHTS, DERIV, STIFF = gll_tables()
STIFF_HAT = STIFF / WEIGHTS[:, None]


def fourier_tables(planes):
    plane_ids = np.arange(planes)
    mode_ids = np.arange(planes)
    waves = np.where(mode_ids < 2, 0, mode_ids // 2)
    angle = (plane_ids[:, None] * waves[None, :] % planes) * (2.0 * math.pi / planes)
    is_sine = (mode_ids % 2 == 1) & (mode_ids >= 2)
    basis = np.where(is_sine[None, :], np.sin(angle), np.cos(angle))
    alternating = np.where(plane_ids % 2 == 0, 1.0, -1.0)
    basis = np.where(mode_ids[None, :] == 1, alternating[:, None], basis)
    row_scale = np.where(mode_ids < 2, 1.0, 2.0) / planes
    forward = basis.T * row_scale[:, None]
    rates = (np.arange(planes // 2) * WAVE_STEP)[:, None]
    forward_z = np.zeros_like(forward)
    forward_z[0::2] = rates * forward[1::2]
    forward_z[1::2] = -rates * forward[0::2]
    forward_z[0:2] = 0.0
    return (basis, forward, forward_z)


def split_table(table):
    high = np.asarray(table, np.float32).astype(jnp.bfloat16)
    low = (np.asarray(table, np.float64) - high.astype(np.float64)).astype(np.float32)
    return np.concatenate([high, low.astype(jnp.bfloat16)], axis=1)


def transform_tables(count):
    planes = LANES
    modes = planes // count
    basis, forward, forward_z = fourier_tables(planes)
    inverse = np.zeros((count * LANES, 3 * planes))
    for block in range(count):
        ids = slice(block * modes, (block + 1) * modes)
        for comp in range(3):
            at = block * LANES + comp * modes
            inverse[at : at + modes, comp * planes : (comp + 1) * planes] = basis[:, ids].T
    back = -np.concatenate([forward.T, forward_z.T], axis=0)
    return split_table(inverse), split_table(back)


def chunk_sizes(count):
    group = BLOCKS * BLOCKS // count
    step = min(group, BLOCKS)
    return step, group // step


def unit_windows(count):
    step, _ = chunk_sizes(count)
    starts = []
    offsets = []
    for index in range(BLOCKS * BLOCKS // step):
        element = index * step
        first = element // BLOCKS * 6 * SIDE
        starts.append(first // LANES * LANES)
        offsets.append(first % LANES + 6 * (element % BLOCKS))
    return starts, offsets


def order_table(step, offset, scratch):
    width = scratch.shape[1]
    lane = lax.broadcasted_iota(jnp.int32, (step, width), 1)
    gap = lane - 6 * lax.broadcasted_iota(jnp.int32, (step, width), 0) - offset
    for point in range(POINTS):
        hit = gap == point // 6 * SIDE + point % 6
        scratch[pl.ds(point * step, step), :] = jnp.where(hit, 1.0, 0.0)
    return scratch[...].astype(BF16)


def halves(value):
    high = value.astype(BF16)
    low = (value - high.astype(F32)).astype(BF16)
    return high, low


def dot(left, right, dims):
    return lax.dot_general(left, right, (dims, ((), ())), preferred_element_type=F32)


def dot3(left, right):
    high, low = halves(left)
    dims = ((1,), (0,))
    width = right.shape[1] // 2
    both = dot(high, right, dims)
    return both[:, :width] + (both[:, width:] + dot(low, right[:, :width], dims))


def start_of(point, ey):
    return pl.multiple_of(point * 64 + ey * 8, 8)


def get(ref, point, ey):
    return ref[pl.ds(start_of(point, ey), 8), :]


def put(ref, point, ey, value):
    ref[pl.ds(start_of(point, ey), 8), :] = value


def ex_ids():
    return lax.broadcasted_iota(jnp.int32, (8, LANES), 0)


def helmholtz_rates(four, modes):
    lane = lax.broadcasted_iota(jnp.int32, (8, LANES), 1)
    mode = four * modes + lax.rem(lane, jnp.int32(modes))
    wave = jnp.where(mode == 0, 0, jnp.where(mode == 1, LANES // 2, lax.div(mode, jnp.int32(2))))
    scaled = wave.astype(F32) * WAVE_STEP
    return REACTION + scaled * scaled


def glued_flags(partner_ref):
    return [jnp.where(partner_ref[0, side] >= 0, 1.0, 0.0).astype(F32) for side in range(4)]


def col_masks(flags):
    ex = ex_ids()
    return jnp.where(ex == 0, flags[3], 1.0), jnp.where(ex == 7, flags[1], 1.0)


def join_cols(first, last, masks):
    ex = ex_ids()
    from_right = jnp.where(ex < 7, pltpu.roll(first, 7, 0), 0.0)
    from_left = jnp.where(ex > 0, pltpu.roll(last, 1, 0), 0.0)
    return (first + from_left) * masks[0], (last + from_right) * masks[1]


def join_rows(ref, flags, pairs=range(7)):
    ex = ex_ids()
    not_first = jnp.where(ex == 0, 0.0, 1.0)
    not_last = jnp.where(ex == 7, 0.0, 1.0)
    for ix in range(6):
        for ey in pairs:
            total = get(ref, 30 + ix, ey) + get(ref, ix, ey + 1)
            put(ref, 30 + ix, ey, total)
            put(ref, ix, ey + 1, total)
        low = get(ref, ix, 0) * flags[0]
        high = get(ref, 30 + ix, 7) * flags[2]
        if ix == 0:
            low, high = low * not_first, high * not_first
        if ix == 5:
            low, high = low * not_last, high * not_last
        put(ref, ix, 0, low)
        put(ref, 30 + ix, 7, high)


def line_product(line, table, mirrored=1.0):
    sums = [line[j] + line[5 - j] for j in range(3)]
    gaps = [line[j] - line[5 - j] for j in range(3)]
    out = [None] * 6
    for i in range(3):
        even = None
        odd = None
        for j in range(3):
            even_term = sums[j] * float(0.5 * (table[i, j] + table[i, 5 - j]))
            odd_term = gaps[j] * float(0.5 * (table[i, j] - table[i, 5 - j]))
            even = even_term if even is None else even + even_term
            odd = odd_term if odd is None else odd + odd_term
        out[i] = even + odd
        out[5 - i] = even - odd if mirrored > 0 else odd - even
    return out


def apply_local(src, dst, rates, flags, terms=(), products=(), energy=False):
    masks = col_masks(flags)

    def body(ey, sums):
        sums = list(sums)
        for ix in range(6):
            line = []
            for iy in range(6):
                point = 6 * iy + ix
                if not terms:
                    line.append(get(src, point, ey))
                    continue
                values = [get(ref, point, ey) for _, ref in terms]
                value = None
                for (factor, _), part in zip(terms, values):
                    part = -part if factor == -1.0 else part * factor
                    value = part if value is None else value + part
                put(src, point, ey, value)
                line.append(value)
                values.append(value)
                ends = (iy in (0, 5)) + (ix in (0, 5))
                for place, (left, right) in enumerate(products):
                    both = values[left] * values[right]
                    sums[place] = sums[place] + (both * (0.5**ends) if ends else both)
            out = line_product(line, STIFF_HAT)
            for iy in range(6):
                put(dst, 6 * iy + ix, ey, out[iy] + rates * line[iy])
        for iy in range(6):
            line = [get(src, 6 * iy + ix, ey) for ix in range(6)]
            out = line_product(line, STIFF_HAT)
            full = [
                (get(dst, 6 * iy + ix, ey) + out[ix]) * float(WEIGHTS[iy] * WEIGHTS[ix])
                for ix in range(6)
            ]
            if energy:
                for ix in range(6):
                    sums[-1] = sums[-1] + full[ix] * line[ix]
            full[0], full[5] = join_cols(full[0], full[5], masks)
            for ix in range(6):
                put(dst, 6 * iy + ix, ey, full[ix])
        return tuple(sums)

    zero = jnp.zeros((8, LANES), F32)
    sums = lax.fori_loop(0, BLOCKS, body, (zero,) * (len(products) + int(energy)), unroll=2)
    join_rows(dst, flags)
    return sums


def side_slice(side, i):
    if side == 0:
        return pl.ds(i * 64, 8)
    if side == 2:
        return pl.ds((30 + i) * 64 + 56, 8)
    if side == 1:
        return pl.ds((6 * i + 5) * 64 + 7, 8, stride=8)
    return pl.ds(6 * i * 64, 8, stride=8)


def read_line(ref, side):
    return [ref[side_slice(side, i), :] for i in range(6)]


def lane_ids():
    return lax.broadcasted_iota(jnp.int32, (8, LANES), 1)


def is_packed(modes):
    return 3 * modes + modes == LANES


def pack_lanes(values, modes):
    if not is_packed(modes):
        return values
    third = len(values) // 4
    inside = lane_ids() < 3 * modes
    return [
        jnp.where(
            inside,
            values[comp * third + at],
            pltpu.roll(values[3 * third + at], (3 - comp) * modes, 1),
        )
        for comp in range(3)
        for at in range(third)
    ]


def unpack_last(pieces, modes):
    block = lax.div(lane_ids(), jnp.int32(modes))
    turned = [pltpu.roll(pieces[comp], (comp + 1) * modes, 1) for comp in range(3)]
    return jnp.where(block == 0, turned[0], jnp.where(block == 1, turned[1], turned[2]))


def unpack_lanes(values, modes):
    if not is_packed(modes):
        return values
    third = len(values) // 3
    return values + [
        unpack_last([values[comp * third + at] for comp in range(3)], modes) for at in range(third)
    ]


def line_rows(modes):
    return 3 * SENT if is_packed(modes) else 4 * SENT


def first_points(last_points):
    return jnp.where(ex_ids() > 0, pltpu.roll(last_points, 1, 0), 0.0)


def write_lines(ref, lines_ref, base, modes):
    values = []
    for side in range(4):
        values += read_line(ref, side)[1:]
    for at, value in enumerate(pack_lanes(values, modes)):
        lines_ref[pl.ds(base + at * 8, 8), :] = value


def load_lines(lines_ref, modes):
    count = line_rows(modes) // 8
    values = unpack_lanes([lines_ref[pl.ds(at * 8, 8), :] for at in range(count)], modes)
    sides = [values[side * 5 : side * 5 + 5] for side in range(4)]
    return [[first_points(side[4])] + side for side in sides]


def add_lines(ref, lines):
    for side in range(4):
        for i in range(6):
            where = side_slice(side, i)
            ref[where, :] = ref[where, :] + lines[side][i]


def add_all(left, right):
    return [[a + b for a, b in zip(one, two)] for one, two in zip(left, right)]


def reverse_rows(value):
    ex = ex_ids()
    value = pltpu.roll(value, 4, 0)
    value = jnp.where((ex & 2) == 0, pltpu.roll(value, 6, 0), pltpu.roll(value, 2, 0))
    return jnp.where((ex & 1) == 0, pltpu.roll(value, 7, 0), pltpu.roll(value, 1, 0))


def collect_sides(gath_refs, own, partner_ref, side_ref, sides, modes):
    sets = sides.shape[1] // SIDE
    step = line_rows(modes)

    def copy_side(side, load):
        there = jnp.maximum(side_ref[0, side], 0)

        def fill(place, values):
            for i, value in enumerate([first_points(values[4])] + values):
                sides[side, pl.ds(place * SIDE + i * 8, 8), :] = value

        def plain():
            for place in range(sets):
                first = place * step + there * SENT
                fill(place, [load(pl.multiple_of(first + i * 8, 8)) for i in range(5)])

        if not is_packed(modes):
            plain()
            return
        pl.when(there < 3)(plain)

        @pl.when(there == 3)
        def _():
            for place in range(sets):
                first = place * step
                values = []
                for i in range(5):
                    pieces = [load(first + comp * SENT + i * 8) for comp in range(3)]
                    values.append(unpack_last(pieces, modes))
                fill(place, values)

    def body(side, carry):
        part = partner_ref[0, side]
        if len(gath_refs) == 1:
            source = jnp.maximum(part, 0)
            copy_side(side, lambda at: gath_refs[0][source, pl.ds(at, 8), :])
            return carry
        for slot, ref in enumerate(gath_refs):
            here = jnp.logical_and(part >= 0, jnp.bitwise_xor(part, own) == slot)

            @pl.when(here)
            def _(ref=ref):
                copy_side(side, lambda at: ref[pl.ds(at, 8), :])

        return carry

    lax.fori_loop(0, 4, body, 0)


def incoming_lines(sides, place, partner_ref, flip_ref):
    lines = []
    for side in range(4):
        glued = partner_ref[0, side] >= 0
        turned = flip_ref[0, side] == 1
        line = []
        for i in range(6):
            at = pl.multiple_of(place * SIDE + jnp.where(turned, 5 - i, i) * 8, 8)
            value = sides[side, pl.ds(at, 8), :]
            value = jnp.where(turned, reverse_rows(value), value)
            line.append(jnp.where(glued, value, 0.0))
        lines.append(line)
    return lines


def own_reaction(own_lines, rates, flags, scale):
    ex = ex_ids()
    edge = float(WEIGHTS[0])
    corner = float(STIFF[0, 0])
    lines = []
    for side in range(4):
        line = own_lines[side]
        along = line_product(line, STIFF_HAT)
        out = [
            (along[i] * edge + line[i] * (corner + rates * edge)) * float(WEIGHTS[i])
            for i in range(6)
        ]
        first = out[0] + pltpu.roll(out[5], 1, 0)
        last = out[5] + pltpu.roll(out[0], 7, 0)
        out[0] = jnp.where(ex > 0, first, 0.0)
        out[5] = jnp.where(ex < 7, last, 0.0)
        lines.append([value * (flags[side] * scale) for value in out])
    return lines


def pick(index, values):
    if isinstance(index, int):
        return values[index]
    chosen = jnp.int32(values[0])
    for place in range(1, len(values)):
        chosen = jnp.where(index == place, jnp.int32(values[place]), chosen)
    return chosen


def offset_of(place, size):
    return (0, 3, 1, 2)[place] if size == 4 else place


def block_of(place, four, size):
    return place if isinstance(four, int) else jnp.bitwise_xor(four, offset_of(place, size))


def pack_kernel(step, count, dynamic, chunk, chunks, starts, offsets, ids_ref, source_ref, *refs):
    send_refs = refs[:count]
    load = chunk == 0
    scratch = refs[-2] if load else refs[-1]
    width = scratch.shape[1]
    held_ref = refs[count] if load else source_ref
    modes = held_ref.shape[1]
    four = ids_ref[1] if dynamic else 0
    copies = []
    if load:
        for comp in range(3):
            copies.append(
                pltpu.make_async_copy(source_ref.at[comp], held_ref.at[comp], refs[-1].at[comp])
            )
            copies[-1].start()
    for place in range(count):
        index = block_of(place, four, count)
        table = order_table(step, pick(index, offsets[chunk::chunks]), scratch)
        if place == 0:
            for copy in copies:
                copy.wait()
        start = pick(index, starts[chunk::chunks])
        start = start if isinstance(start, int) else pl.multiple_of(start, LANES)
        rows = [held_ref[comp, :, pl.ds(start, width)] for comp in range(3)]
        pad = jnp.zeros((LANES - 3 * modes, width), F32)
        high, low = halves(jnp.concatenate(rows + [pad], axis=0))
        both = jnp.concatenate([high, low], axis=0)
        out = dot(table, both, ((1,), (1,)))
        out = out[:, :LANES] + out[:, LANES:]
        if not is_packed(modes):
            send_refs[place][...] = out
            continue
        values = [out[point * step : (point + 1) * step] for point in range(POINTS)]
        for at, value in enumerate(pack_lanes(values, modes)):
            send_refs[place][pl.ds(at * step, step), :] = value


def product_kernel(modes, step, count, dynamic, role, ids_ref, *refs):
    recv_refs = refs[:count]
    inverse_ref, back_ref = refs[count : count + 2]
    refs = refs[count + 2 :]
    if role == 1:
        carry_ref, refs = refs[0], refs[1:]
    send_refs, refs = refs[:count], refs[count:]
    if role == 0:
        carry_ref, refs = refs[0], refs[1:]
    full, lined, phys, prod, spec = refs
    four = ids_ref[1] if dynamic else 0
    packed = is_packed(modes)
    for place in range(count):
        index = block_of(place, four, count)
        if packed:
            ready = 3 * POINTS // 4
            values = [recv_refs[place][pl.ds(at * step, step), :] for at in range(ready)]
            for at, value in enumerate(unpack_lanes(values, modes)):
                full[place, pl.ds(at * step, step), :] = value
        else:
            full[place] = recv_refs[place][...]
        first = index * LANES
        first = first if isinstance(first, int) else pl.multiple_of(first, LANES)
        lined[:, pl.ds(first, LANES)] = full[place]
    phys[...] = dot3(lined[...], inverse_ref[...])
    width = 2 * LANES

    def field(point, comp):
        return phys[pl.ds(point * step, step), comp * LANES : (comp + 1) * LANES]

    for comp in range(3):
        wide = pl.ds(comp * width, LANES)
        for iy in range(6):
            line = []
            for ix in range(6):
                point = 6 * iy + ix
                value = field(point, comp)
                line.append(value * field(point, 0))
                prod[pl.ds(point * step, step), pl.ds(comp * width + LANES, LANES)] = (
                    value * field(point, 2)
                )
            out = line_product(line, DERIV, -1.0)
            for ix in range(6):
                prod[pl.ds((6 * iy + ix) * step, step), wide] = out[ix]
        for ix in range(6):
            line = [field(6 * iy + ix, comp) * field(6 * iy + ix, 1) for iy in range(6)]
            out = line_product(line, DERIV, -1.0)
            for iy in range(6):
                at = pl.ds((6 * iy + ix) * step, step)
                prod[at, wide] = prod[at, wide] + out[iy]
        spec[comp] = dot3(prod[:, comp * width : (comp + 1) * width], back_ref[...])

    lane_block = lax.div(lax.broadcasted_iota(jnp.int32, (step, LANES), 1), jnp.int32(modes))
    masks = []
    shifts = []
    for place in range(count):
        index = block_of(place, four, count)
        masks.append([lane_block == lax.rem(index + comp, count) for comp in range(2)])
        shifts.append(lax.rem(LANES - index * modes, LANES))
    kept = []
    for point in range(POINTS):
        at = pl.ds(point * step, step)
        mass = float(WEIGHTS[point // 6] * WEIGHTS[point % 6])
        turned = [spec[0, at, :]]
        turned += [pltpu.roll(spec[comp, at, :], comp * modes, 1) for comp in (1, 2)]
        for place in range(count):
            mask = masks[place]
            mixed = jnp.where(mask[0], turned[0], jnp.where(mask[1], turned[1], turned[2]))
            nonlinear = pltpu.roll(mixed, shifts[place], 1)
            full[place, at, :] = mass * (REACTION * full[place, at, :] + nonlinear)
    ex = None if role is None else ex_ids()
    for place in range(count):
        values = [full[place, pl.ds(point * step, step), :] for point in range(POINTS)]
        if role is not None:
            left = jnp.zeros((8, LANES), F32)
            sent = []
            for iy in range(6):
                line = values[6 * iy : 6 * iy + 6]
                line[5] = line[5] + jnp.where(ex < 7, pltpu.roll(line[0], 7, 0), 0.0)
                if role == 0 and iy == 5:
                    for ix in range(6):
                        carry_ref[place, pl.ds(ix * 8, 8), :] = line[ix]
                    continue
                if role == 1 and iy == 0:
                    line = [line[ix] + carry_ref[place, pl.ds(ix * 8, 8), :] for ix in range(6)]
                left = jnp.where(ex == iy, pltpu.roll(line[0], iy, 0) if iy else line[0], left)
                sent += line[1:]
            values = sent + [left]
            values += [left] * (32 - len(values))
        for at, value in enumerate(pack_lanes(values, modes)):
            send_refs[place][pl.ds(at * step, step), :] = value


def spread_rows(values, masks):
    ex = ex_ids()
    rows = (len(values) - 1) // 5
    left = values[5 * rows]
    points = []
    for iy in range(rows):
        line = values[5 * iy : 5 * iy + 5]
        start = pltpu.roll(left, 8 - iy, 0) if iy else left
        first = jnp.where(ex == 0, start, pltpu.roll(line[4], 1, 0))
        points += [first * masks[0]] + line[:4] + [line[4] * masks[1]]
    return points


def first_kernel(modes, step, count, chunks, dynamic, lean, ids_ref, partner_ref, *refs):
    recv_refs = refs[: count * chunks]
    base_ref, lines_ref, work = refs[count * chunks :]
    four = ids_ref[1] if dynamic else 0
    rates = helmholtz_rates(ids_ref[1], modes)
    flags = glued_flags(partner_ref)
    masks = col_masks(flags)
    for place in range(count):
        block = block_of(place, four, count)
        shares = []
        for chunk in range(chunks):
            ref = recv_refs[chunk * count + place]
            ready = ref.shape[0] // step
            shares.append(
                unpack_lanes([ref[pl.ds(at * step, step), :] for at in range(ready)], modes)
            )
        if lean:
            odd = spread_rows(shares[1][:31], masks)
            shares = [spread_rows(shares[0][:26], masks) + odd[:6], odd]
        for chunk in range(chunks):
            first = (block * chunks + chunk) * step
            for point in range(POINTS):
                at = point * 64 + first
                at = at if isinstance(at, int) else pl.multiple_of(at, step)
                base_ref[pl.ds(at, step), :] = shares[chunk][point]
    if not lean:
        for ey in range(BLOCKS):
            for iy in range(6):
                first, last = join_cols(
                    get(base_ref, 6 * iy, ey), get(base_ref, 6 * iy + 5, ey), masks
                )
                put(base_ref, 6 * iy, ey, first)
                put(base_ref, 6 * iy + 5, ey, last)
    join_rows(base_ref, flags, range(1, 7, 2) if lean else range(7))
    apply_local(base_ref, work, rates, flags)
    write_lines(base_ref, lines_ref, 0, modes)
    write_lines(work, lines_ref, line_rows(modes), modes)


def sum_rows(sums):
    return [jnp.sum(value, axis=0, keepdims=True) for value in sums]


def second_kernel(modes, slots, ids_ref, partner_ref, side_ref, flip_ref, *refs):
    gath_refs = refs[:slots]
    lines_ref, _, k0_ref, k1_ref, k2_ref, next_ref, sums_ref, work, sides = refs[slots:]
    rates = helmholtz_rates(ids_ref[1], modes)
    flags = glued_flags(partner_ref)
    collect_sides(gath_refs, ids_ref[0], partner_ref, side_ref, sides, modes)
    back = own_reaction(load_lines(lines_ref, modes), rates, flags, 1.0)
    add_lines(k0_ref, incoming_lines(sides, 0, partner_ref, flip_ref))
    apply_local(k0_ref, work, rates, flags)
    add_lines(work, add_all(incoming_lines(sides, 1, partner_ref, flip_ref), back))
    sums = apply_local(
        k1_ref, work, rates, flags,
        terms=[(1.0 / SPREAD, work), (-CENTRE / SPREAD, k0_ref)],
        products=[(1, 1), (1, -1), (-1, -1)],
    )
    write_lines(work, next_ref, 0, modes)
    apply_local(
        k2_ref, work, rates, flags,
        terms=[(TWICE, work), (-CENTRE * TWICE, k1_ref), (-1.0, k0_ref)],
    )
    write_lines(work, next_ref, line_rows(modes), modes)
    sums_ref[...] = jnp.concatenate(sum_rows(sums) + [jnp.zeros((5, LANES), F32)], axis=0)


def third_kernel(modes, slots, ids_ref, partner_ref, side_ref, flip_ref, *refs):
    gath_refs = refs[:slots]
    lines_ref, k1_ref, sums_ref, _ = refs[slots : slots + 4]
    k2_ref, k3_ref, a3_ref, next_ref, work, sides = refs[slots + 4 :]
    rates = helmholtz_rates(ids_ref[1], modes)
    flags = glued_flags(partner_ref)
    collect_sides(gath_refs, ids_ref[0], partner_ref, side_ref, sides, modes)
    back = own_reaction(load_lines(lines_ref, modes), rates, flags, TWICE)
    incoming = incoming_lines(sides, 0, partner_ref, flip_ref)
    add_lines(k2_ref, [[value * TWICE for value in line] for line in incoming])
    apply_local(k2_ref, work, rates, flags)
    add_lines(work, add_all(incoming_lines(sides, 1, partner_ref, flip_ref), back))
    sums = apply_local(
        k3_ref, a3_ref, rates, flags,
        terms=[(TWICE, work), (-CENTRE * TWICE, k2_ref), (-1.0, k1_ref)],
        products=[(2, 1), (1, 1), (1, -1), (-1, -1)],
        energy=True,
    )
    write_lines(a3_ref, next_ref, 0, modes)
    next_ref[pl.ds(line_rows(modes), SUM_ROWS), :] = jnp.concatenate(
        [sums_ref[:3, :]] + sum_rows(sums), axis=0
    )


def turn_kernel(starts, offsets, fields, has_scatter, *refs):
    field_refs = refs[:fields]
    out_refs = refs[fields : 2 * fields]
    scratch, rows = refs[-2:]
    step = rows.shape[0] // POINTS
    used = out_refs[0].shape[0]
    width = scratch.shape[1]
    for out_ref in out_refs:
        out_ref[...] = jnp.zeros(out_ref.shape, F32)
    for unit in range(len(starts)):
        table = order_table(step, offsets[unit], scratch)
        for field_ref, out_ref in zip(field_refs, out_refs):
            for point in range(POINTS):
                rows[pl.ds(point * step, step), :] = field_ref[pl.ds(point * 64 + unit * step, step), :]
            high, low = halves(jnp.transpose(rows[...])[:used])
            both = jnp.concatenate([high, low], axis=0)
            out = dot(both, table, ((1,), (0,)))
            window = pl.ds(starts[unit], width)
            out_ref[:, window] = out_ref[:, window] + (out[:used] + out[used:])
    if has_scatter:
        scatter_ref = refs[2 * fields]
        place = lax.broadcasted_iota(jnp.int32, (SIDE, NODES), 0)
        at = 6 * jnp.bitwise_and(place, 7) + lax.shift_right_logical(place, 3)
        node = lax.broadcasted_iota(jnp.int32, (SIDE, NODES), 1)
        targets = (at, at * SIDE + SIDE - 1, at + (SIDE - 1) * SIDE, at * SIDE)
        for side, target in enumerate(targets):
            scatter_ref[side * SIDE : (side + 1) * SIDE, :] = jnp.where(
                node == target, 1.0, 0.0
            ).astype(BF16)


def conjugate_coefficients(gram, energy):
    zero = jnp.zeros_like(energy)

    def image(vec):
        out = [zero] * 5
        for j in range(4):
            if vec[j] is None:
                continue
            out[j] = out[j] + CENTRE * vec[j]
            out[j + 1] = out[j + 1] + (SPREAD if j == 0 else 0.5 * SPREAD) * vec[j]
            if j > 0:
                out[j - 1] = out[j - 1] + 0.5 * SPREAD * vec[j]
        return out

    def inner(left, right):
        total = zero
        for i in range(4):
            for j in range(4):
                if left[i] is not None and right[j] is not None:
                    total = total + left[i] * right[j] * gram[i][j]
        return total

    moments = [[None] * 4 for _ in range(4)]
    for j in range(3):
        column = image([jnp.ones_like(energy) if i == j else None for i in range(4)])
        for i in range(4):
            total = zero
            for m in range(max(j - 1, 0), j + 2):
                total = total + column[m] * gram[i][m]
            moments[i][j] = total
    for i in range(3):
        moments[i][3] = moments[3][i]
    moments[3][3] = energy

    def pad(vec, size):
        return [vec[i] if i < size else None for i in range(4)]

    residual = [jnp.ones_like(energy), zero, zero, zero, zero]
    direction = list(residual)
    solution = [zero] * 4
    norm_now = gram[0][0]
    for step in range(ITERS):
        trimmed = pad(direction, step + 1)
        bend = zero
        for i in range(step + 1):
            for j in range(step + 1):
                bend = bend + direction[i] * direction[j] * moments[i][j]
        alpha = norm_now / bend
        moved = image(trimmed)
        for i in range(step + 1):
            solution[i] = solution[i] + alpha * direction[i]
        for i in range(step + 2):
            residual[i] = residual[i] - alpha * moved[i]
        if step < ITERS - 1:
            kept = pad(residual, step + 2)
            norm_next = inner(kept, kept)
            ratio = norm_next / norm_now
            direction = [residual[i] + ratio * direction[i] for i in range(5)]
            norm_now = norm_next
    return solution, residual


def last_kernel(slots, ids_ref, partner_ref, side_ref, flip_ref, *refs):
    gath_refs = refs[:slots]
    turned = refs[slots : slots + 5]
    scatter_ref, sol_out, res_out, lines, sides, sol_ref, res_ref, sems = refs[slots + 5 :]
    modes = sol_ref.shape[1]
    used = 3 * modes
    where = pl.ds(line_rows(modes), SUM_ROWS)
    if slots == 1:
        parts = [gath_refs[0][part, where, :] for part in range(gath_refs[0].shape[0])]
    else:
        parts = [ref[where, :] for ref in gath_refs]
    sums = functools.reduce(lambda left, right: left + right, parts)
    g00, g01, g11, g12, g22, g23, g33, energy = [
        jnp.broadcast_to(sums[place : place + 1, :], (8, LANES)) for place in range(8)
    ]
    g02 = 2.0 * g11 - g00
    g03 = 2.0 * g12 - g01
    g13 = (g22 - g00) + g11
    gram = [
        [g00, g01, g02, g03],
        [g01, g11, g12, g13],
        [g02, g12, g22, g23],
        [g03, g13, g23, g33],
    ]
    solution, residual = conjugate_coefficients(gram, energy)
    on_a3 = residual[4] * TWICE
    on_k3 = residual[3] - on_a3 * CENTRE
    on_k2 = residual[2] - residual[4]
    factors = list(solution) + [residual[0], residual[1], on_k2, on_k3, on_a3]
    columns = jnp.transpose(
        jnp.concatenate([value[:1] for value in factors] + [jnp.zeros((LANES - 9, LANES), F32)], axis=0)
    )
    copies = []

    def send(comp, place, buffer, out):
        copies.append(pltpu.make_async_copy(buffer.at[comp], out.at[comp], sems.at[2 * comp + place]))
        copies[-1].start()

    def scaled(at, first):
        rows = [ref[at : at + 8, :] for ref in turned[: 5 if first else 4]]
        terms = [columns[at : at + 8, first + k : first + k + 1] * row for k, row in enumerate(rows)]
        return functools.reduce(lambda left, right: left + right, terms)

    for comp in range(3):
        for first in range(0, modes, 8):
            sol_ref[comp, first : first + 8, :] = scaled(comp * modes + first, 0)
        send(comp, 0, sol_ref, sol_out)
    collect_sides(gath_refs, ids_ref[0], partner_ref, side_ref, sides, modes)
    incoming = incoming_lines(sides, 0, partner_ref, flip_ref)
    for side in range(4):
        for i in range(6):
            lines[pl.ds(side * SIDE + i * 8, 8), :] = incoming[side][i] * on_a3
    high, low = halves(jnp.transpose(lines[...])[:used])
    added = dot(jnp.concatenate([high, low], axis=0), scatter_ref[...], ((1,), (0,)))
    for comp in range(3):
        for first in range(0, modes, 8):
            at = comp * modes + first
            res_ref[comp, first : first + 8, :] = scaled(at, 4) + (
                added[at : at + 8] + added[used + at : used + at + 8]
            )
        send(comp, 1, res_ref, res_out)
    for copy in copies:
        copy.wait()


def call(kernel, name, out_shapes, args, scratch, scalars=0, keep=True, aliases=None, outside=False):
    smem = pl.BlockSpec(memory_space=pltpu.SMEM)
    vmem = pl.BlockSpec(memory_space=pltpu.VMEM)
    shapes = [shape if isinstance(shape, jax.ShapeDtypeStruct) else jax.ShapeDtypeStruct(shape, F32) for shape in out_shapes]
    return pl.pallas_call(
        kernel,
        name=name,
        out_shape=[pltpu.VMEM(one.shape, one.dtype) if keep else one for one in shapes],
        in_specs=[smem] * scalars + [pl.BlockSpec(memory_space=pltpu.HBM) if outside else vmem] * (len(args) - scalars),
        out_specs=[vmem if keep else pl.BlockSpec(memory_space=pltpu.HBM)] * len(out_shapes),
        scratch_shapes=[pltpu.VMEM(one, F32) if isinstance(one, tuple) else one for one in scratch],
        input_output_aliases=aliases or {},
        compiler_params=pltpu.CompilerParams(vmem_limit_bytes=VMEM_LIMIT),
    )(*args[:scalars], *[held(arg, pltpu.HBM if outside else pltpu.VMEM) for arg in args[scalars:]])


def held(arg, space):
    return arg if isinstance(arg, np.ndarray) else pltpu.with_memory_space_constraint(arg, space)


def swap_blocks(blocks, dynamic):
    if not dynamic:
        stacked = lax.all_to_all(jnp.stack(blocks), "four", split_axis=0, concat_axis=0, tiled=True)
        return [stacked[place] for place in range(len(blocks))]
    size = len(blocks)
    swapped = list(blocks)
    for place in range(size - 1, 0, -1):
        swapped[place] = lax.ppermute(blocks[place], "four", [(i, i ^ offset_of(place, size)) for i in range(size)])
    return swapped


def share_lines(lines, beside=()):
    parts = lax.axis_size("dom")
    if parts != 8:
        return [lax.all_gather(lines, "dom", axis=0, tiled=False)], list(beside)
    slots = [lines] + [None] * (parts - 1)
    for slot in range(2, parts, 2):
        slots[slot] = lax.ppermute(lines, "dom", [(i, i ^ slot) for i in range(parts)])
        if beside and slot == parts // 2:
            slots[slot], *beside = lax.optimization_barrier((slots[slot], *beside))
    for slot in range(0, parts, 2):
        slots[slot + 1] = lax.ppermute(slots[slot], "dom", [(i, i ^ 1) for i in range(parts)])
    return slots, list(beside)


def shards(velocity, partner, partner_side, flipped):
    modes = velocity.shape[1]
    count = lax.axis_size("four")
    step, chunks = chunk_sizes(count)
    rows = POINTS * step
    sent_rows = 3 * rows // 4 if is_packed(modes) else rows
    dynamic = step == BLOCKS
    inverse, back = transform_tables(count)
    starts, offsets = unit_windows(count)
    table = (rows, 3 * LANES)
    ids = jnp.stack([lax.axis_index("dom"), lax.axis_index("four")]).astype(jnp.int32)
    field = (NODES, LANES)
    blocks = [(sent_rows, LANES)] * count
    lined = line_rows(modes)

    lean = dynamic and chunks == 2 and is_packed(modes)
    spread = []
    source = velocity
    for chunk in range(chunks):
        load = chunk == 0
        sent = call(
            functools.partial(pack_kernel, step, count, dynamic, chunk, chunks, starts, offsets),
            "pack",
            blocks + [velocity.shape] * load,
            (ids, source),
            [table] + [pltpu.SemaphoreType.DMA((3,))] * load,
            scalars=1,
            outside=load,
        )
        if load:
            *sent, source = sent
        spread.append(swap_blocks(sent, dynamic))
    local = []
    carry = []
    for chunk in range(chunks):
        role = chunk if lean else None
        out = [(24 * step, LANES)] * count if lean else blocks
        sent = call(
            functools.partial(product_kernel, modes, step, count, dynamic, role),
            "products",
            out + [(count, SIDE, LANES)] * (role == 0),
            (ids, *spread[chunk], inverse, back, *carry),
            [
                (count, rows, LANES),
                (rows, count * LANES),
                (rows, 3 * LANES),
                (rows, 6 * LANES),
                (3, rows, LANES),
            ],
            scalars=1,
        )
        if role == 0:
            *sent, held_row = sent
            carry = [held_row]
        local += swap_blocks(sent, dynamic)

    base, lines = call(
        functools.partial(first_kernel, modes, step, count, chunks, dynamic, lean),
        "first",
        [field, (2 * lined, LANES)],
        (ids, partner, *local),
        [field],
        scalars=2,
    )
    tables = (ids, partner, partner_side, flipped)
    gathered, _ = share_lines(lines)
    slots = len(gathered)
    k0, k1, base, lines, sums = call(
        functools.partial(second_kernel, modes, slots),
        "second",
        [field, field, field, (2 * lined, LANES), (8, LANES)],
        (*tables, *gathered, lines, base),
        [field, (4, 2 * SIDE, LANES)],
        scalars=4,
        aliases={4 + slots + 1: 0},
    )
    flat = (3 * modes, NODES)
    turned = call(
        functools.partial(turn_kernel, starts, offsets, 2, True),
        "turn",
        [flat, flat, jax.ShapeDtypeStruct((4 * SIDE, NODES), BF16)],
        (k0, k1),
        [table, (rows, LANES)],
    )
    gathered, (t0, t1, scatter) = share_lines(lines, turned)
    k2, k3, a3, lines = call(
        functools.partial(third_kernel, modes, slots),
        "third",
        [field, field, field, (lined + SUM_ROWS, LANES)],
        (*tables, *gathered, lines, k1, sums, base),
        [field, (4, 2 * SIDE, LANES)],
        scalars=4,
        aliases={4 + slots + 3: 0},
    )
    turned = call(
        functools.partial(turn_kernel, starts, offsets, 3, False),
        "turn",
        [flat, flat, flat],
        (k2, k3, a3),
        [table, (rows, LANES)],
    )
    gathered, (t2, t3, ta) = share_lines(lines, turned)
    outs = call(
        functools.partial(last_kernel, slots),
        "last",
        [velocity.shape, velocity.shape],
        (*tables, *gathered, t0, t1, t2, t3, ta, scatter),
        [
            (4 * SIDE, LANES),
            (4, SIDE, LANES),
            velocity.shape,
            velocity.shape,
            pltpu.SemaphoreType.DMA((6,)),
        ],
        scalars=4,
        keep=False,
    )
    return tuple(outs)


def solution(mesh):
    return jax.shard_map(
        shards,
        mesh=mesh,
        in_specs=(P(None, "four", "dom"), P("dom", None), P("dom", None), P("dom", None)),
        out_specs=(P(None, "four", "dom"), P(None, "four", "dom")),
        check_vma=False,
    )
```

```python
import functools
import math

import jax
import jax.numpy as jnp
import numpy as np
from jax import lax
from jax.experimental import pallas as pl
from jax.experimental.pallas import tpu as pltpu
from jax.sharding import PartitionSpec as P

ITERS = 4
REACTION = 2.0
WAVE_STEP = 0.0625
LANES = 128
POINTS = 36
BLOCKS = 8
SIDE = 48
SENT = 40
NODES = 2304
CENTRE = 9.0
SPREAD = 9.0
TWICE = 2.0 / SPREAD
SUM_ROWS = 8
VMEM_LIMIT = 32 * 1024 * 1024
F32 = jnp.float32
BF16 = jnp.bfloat16


def gll_tables():
    inner_near = math.sqrt(1.0 / 3.0 - 2.0 * math.sqrt(7.0) / 21.0)
    inner_far = math.sqrt(1.0 / 3.0 + 2.0 * math.sqrt(7.0) / 21.0)
    points = np.array([-1.0, -inner_far, -inner_near, inner_near, inner_far, 1.0])
    values = (63.0 * points**5 - 70.0 * points**3 + 15.0 * points) / 8.0
    weights = 2.0 / (30.0 * values * values)
    spacing = points[:, None] - points[None, :]
    same_point = spacing == 0.0
    derivative = np.where(
        same_point, 0.0, values[:, None] / (values[None, :] * np.where(same_point, 1.0, spacing))
    )
    end_fix = np.array([-7.5, 0.0, 0.0, 0.0, 0.0, 7.5])
    derivative = derivative + np.eye(6) * end_fix[None, :]
    stiffness = derivative.T @ (weights[:, None] * derivative)
    return (weights, derivative, stiffness)


WEIGHTS, DERIV, STIFF = gll_tables()
STIFF_HAT = STIFF / WEIGHTS[:, None]


def fourier_tables(planes):
    plane_ids = np.arange(planes)
    mode_ids = np.arange(planes)
    waves = np.where(mode_ids < 2, 0, mode_ids // 2)
    angle = (plane_ids[:, None] * waves[None, :] % planes) * (2.0 * math.pi / planes)
    is_sine = (mode_ids % 2 == 1) & (mode_ids >= 2)
    basis = np.where(is_sine[None, :], np.sin(angle), np.cos(angle))
    alternating = np.where(plane_ids % 2 == 0, 1.0, -1.0)
    basis = np.where(mode_ids[None, :] == 1, alternating[:, None], basis)
    row_scale = np.where(mode_ids < 2, 1.0, 2.0) / planes
    forward = basis.T * row_scale[:, None]
    rates = (np.arange(planes // 2) * WAVE_STEP)[:, None]
    forward_z = np.zeros_like(forward)
    forward_z[0::2] = rates * forward[1::2]
    forward_z[1::2] = -rates * forward[0::2]
    forward_z[0:2] = 0.0
    return (basis, forward, forward_z)


def split_table(table):
    high = np.asarray(table, np.float32).astype(jnp.bfloat16)
    low = (np.asarray(table, np.float64) - high.astype(np.float64)).astype(np.float32)
    return np.concatenate([high, low.astype(jnp.bfloat16)], axis=1)


def transform_tables(count):
    planes = LANES
    modes = planes // count
    basis, forward, forward_z = fourier_tables(planes)
    inverse = np.zeros((count * LANES, 3 * planes))
    for block in range(count):
        ids = slice(block * modes, (block + 1) * modes)
        for comp in range(3):
            at = block * LANES + comp * modes
            inverse[at : at + modes, comp * planes : (comp + 1) * planes] = basis[:, ids].T
    back = -np.concatenate([forward.T, forward_z.T], axis=0)
    return split_table(inverse), split_table(back)


def chunk_sizes(count):
    group = BLOCKS * BLOCKS // count
    step = min(group, BLOCKS)
    return step, group // step


def unit_windows(count):
    step, _ = chunk_sizes(count)
    starts = []
    offsets = []
    for index in range(BLOCKS * BLOCKS // step):
        element = index * step
        first = element // BLOCKS * 6 * SIDE
        starts.append(first // LANES * LANES)
        offsets.append(first % LANES + 6 * (element % BLOCKS))
    return starts, offsets


def order_table(step, offset, scratch):
    width = scratch.shape[1]
    lane = lax.broadcasted_iota(jnp.int32, (step, width), 1)
    gap = lane - 6 * lax.broadcasted_iota(jnp.int32, (step, width), 0) - offset
    for point in range(POINTS):
        hit = gap == point // 6 * SIDE + point % 6
        scratch[pl.ds(point * step, step), :] = jnp.where(hit, 1.0, 0.0)
    return scratch[...].astype(BF16)


def halves(value):
    high = value.astype(BF16)
    low = (value - high.astype(F32)).astype(BF16)
    return high, low


def dot(left, right, dims):
    return lax.dot_general(left, right, (dims, ((), ())), preferred_element_type=F32)


def dot3(left, right):
    high, low = halves(left)
    dims = ((1,), (0,))
    width = right.shape[1] // 2
    both = dot(high, right, dims)
    return both[:, :width] + (both[:, width:] + dot(low, right[:, :width], dims))


def start_of(point, ey):
    return pl.multiple_of(point * 64 + ey * 8, 8)


def get(ref, point, ey):
    return ref[pl.ds(start_of(point, ey), 8), :]


def put(ref, point, ey, value):
    ref[pl.ds(start_of(point, ey), 8), :] = value


def ex_ids():
    return lax.broadcasted_iota(jnp.int32, (8, LANES), 0)


def helmholtz_rates(four, modes):
    lane = lax.broadcasted_iota(jnp.int32, (8, LANES), 1)
    mode = four * modes + lax.rem(lane, jnp.int32(modes))
    wave = jnp.where(mode == 0, 0, jnp.where(mode == 1, LANES // 2, lax.div(mode, jnp.int32(2))))
    scaled = wave.astype(F32) * WAVE_STEP
    return REACTION + scaled * scaled


def glued_flags(partner_ref):
    return [jnp.where(partner_ref[0, side] >= 0, 1.0, 0.0).astype(F32) for side in range(4)]


def col_masks(flags):
    ex = ex_ids()
    return jnp.where(ex == 0, flags[3], 1.0), jnp.where(ex == 7, flags[1], 1.0)


def join_cols(first, last, masks):
    ex = ex_ids()
    from_right = jnp.where(ex < 7, pltpu.roll(first, 7, 0), 0.0)
    from_left = jnp.where(ex > 0, pltpu.roll(last, 1, 0), 0.0)
    return (first + from_left) * masks[0], (last + from_right) * masks[1]


def join_rows(ref, flags, pairs=range(7)):
    ex = ex_ids()
    not_first = jnp.where(ex == 0, 0.0, 1.0)
    not_last = jnp.where(ex == 7, 0.0, 1.0)
    for ix in range(6):
        for ey in pairs:
            total = get(ref, 30 + ix, ey) + get(ref, ix, ey + 1)
            put(ref, 30 + ix, ey, total)
            put(ref, ix, ey + 1, total)
        low = get(ref, ix, 0) * flags[0]
        high = get(ref, 30 + ix, 7) * flags[2]
        if ix == 0:
            low, high = low * not_first, high * not_first
        if ix == 5:
            low, high = low * not_last, high * not_last
        put(ref, ix, 0, low)
        put(ref, 30 + ix, 7, high)


def line_product(line, table, mirrored=1.0):
    sums = [line[j] + line[5 - j] for j in range(3)]
    gaps = [line[j] - line[5 - j] for j in range(3)]
    out = [None] * 6
    for i in range(3):
        even = None
        odd = None
        for j in range(3):
            even_term = sums[j] * float(0.5 * (table[i, j] + table[i, 5 - j]))
            odd_term = gaps[j] * float(0.5 * (table[i, j] - table[i, 5 - j]))
            even = even_term if even is None else even + even_term
            odd = odd_term if odd is None else odd + odd_term
        out[i] = even + odd
        out[5 - i] = even - odd if mirrored > 0 else odd - even
    return out


def apply_local(src, dst, rates, flags, terms=(), products=(), energy=False):
    masks = col_masks(flags)

    def body(ey, sums):
        sums = list(sums)
        for ix in range(6):
            line = []
            for iy in range(6):
                point = 6 * iy + ix
                if not terms:
                    line.append(get(src, point, ey))
                    continue
                values = [get(ref, point, ey) for _, ref in terms]
                value = None
                for (factor, _), part in zip(terms, values):
                    part = -part if factor == -1.0 else part * factor
                    value = part if value is None else value + part
                put(src, point, ey, value)
                line.append(value)
                values.append(value)
                ends = (iy in (0, 5)) + (ix in (0, 5))
                for place, (left, right) in enumerate(products):
                    both = values[left] * values[right]
                    sums[place] = sums[place] + (both * (0.5**ends) if ends else both)
            out = line_product(line, STIFF_HAT)
            for iy in range(6):
                put(dst, 6 * iy + ix, ey, out[iy] + rates * line[iy])
        for iy in range(6):
            line = [get(src, 6 * iy + ix, ey) for ix in range(6)]
            out = line_product(line, STIFF_HAT)
            full = [
                (get(dst, 6 * iy + ix, ey) + out[ix]) * float(WEIGHTS[iy] * WEIGHTS[ix])
                for ix in range(6)
            ]
            if energy:
                for ix in range(6):
                    sums[-1] = sums[-1] + full[ix] * line[ix]
            full[0], full[5] = join_cols(full[0], full[5], masks)
            for ix in range(6):
                put(dst, 6 * iy + ix, ey, full[ix])
        return tuple(sums)

    zero = jnp.zeros((8, LANES), F32)
    sums = lax.fori_loop(0, BLOCKS, body, (zero,) * (len(products) + int(energy)), unroll=2)
    join_rows(dst, flags)
    return sums


def side_slice(side, i):
    if side == 0:
        return pl.ds(i * 64, 8)
    if side == 2:
        return pl.ds((30 + i) * 64 + 56, 8)
    if side == 1:
        return pl.ds((6 * i + 5) * 64 + 7, 8, stride=8)
    return pl.ds(6 * i * 64, 8, stride=8)


def read_line(ref, side):
    return [ref[side_slice(side, i), :] for i in range(6)]


def lane_ids():
    return lax.broadcasted_iota(jnp.int32, (8, LANES), 1)


def is_packed(modes):
    return 3 * modes + modes == LANES


def pack_lanes(values, modes):
    if not is_packed(modes):
        return values
    third = len(values) // 4
    inside = lane_ids() < 3 * modes
    return [
        jnp.where(
            inside,
            values[comp * third + at],
            pltpu.roll(values[3 * third + at], (3 - comp) * modes, 1),
        )
        for comp in range(3)
        for at in range(third)
    ]


def unpack_last(pieces, modes):
    block = lax.div(lane_ids(), jnp.int32(modes))
    turned = [pltpu.roll(pieces[comp], (comp + 1) * modes, 1) for comp in range(3)]
    return jnp.where(block == 0, turned[0], jnp.where(block == 1, turned[1], turned[2]))


def unpack_lanes(values, modes):
    if not is_packed(modes):
        return values
    third = len(values) // 3
    return values + [
        unpack_last([values[comp * third + at] for comp in range(3)], modes) for at in range(third)
    ]


def line_rows(modes):
    return 3 * SENT if is_packed(modes) else 4 * SENT


def first_points(last_points):
    return jnp.where(ex_ids() > 0, pltpu.roll(last_points, 1, 0), 0.0)


def write_lines(ref, lines_ref, base, modes):
    values = []
    for side in range(4):
        values += read_line(ref, side)[1:]
    for at, value in enumerate(pack_lanes(values, modes)):
        lines_ref[pl.ds(base + at * 8, 8), :] = value


def load_lines(lines_ref, modes):
    count = line_rows(modes) // 8
    values = unpack_lanes([lines_ref[pl.ds(at * 8, 8), :] for at in range(count)], modes)
    sides = [values[side * 5 : side * 5 + 5] for side in range(4)]
    return [[first_points(side[4])] + side for side in sides]


def add_lines(ref, lines):
    for side in range(4):
        for i in range(6):
            where = side_slice(side, i)
            ref[where, :] = ref[where, :] + lines[side][i]


def add_all(left, right):
    return [[a + b for a, b in zip(one, two)] for one, two in zip(left, right)]


def reverse_rows(value):
    ex = ex_ids()
    value = pltpu.roll(value, 4, 0)
    value = jnp.where((ex & 2) == 0, pltpu.roll(value, 6, 0), pltpu.roll(value, 2, 0))
    return jnp.where((ex & 1) == 0, pltpu.roll(value, 7, 0), pltpu.roll(value, 1, 0))


def collect_sides(gath_refs, own, partner_ref, side_ref, sides, modes):
    sets = sides.shape[1] // SIDE
    step = line_rows(modes)

    def copy_side(side, load):
        there = jnp.maximum(side_ref[0, side], 0)

        def fill(place, values):
            for i, value in enumerate([first_points(values[4])] + values):
                sides[side, pl.ds(place * SIDE + i * 8, 8), :] = value

        def plain():
            for place in range(sets):
                first = place * step + there * SENT
                fill(place, [load(pl.multiple_of(first + i * 8, 8)) for i in range(5)])

        if not is_packed(modes):
            plain()
            return
        pl.when(there < 3)(plain)

        @pl.when(there == 3)
        def _():
            for place in range(sets):
                first = place * step
                values = []
                for i in range(5):
                    pieces = [load(first + comp * SENT + i * 8) for comp in range(3)]
                    values.append(unpack_last(pieces, modes))
                fill(place, values)

    def body(side, carry):
        part = partner_ref[0, side]
        if len(gath_refs) == 1:
            source = jnp.maximum(part, 0)
            copy_side(side, lambda at: gath_refs[0][source, pl.ds(at, 8), :])
            return carry
        for slot, ref in enumerate(gath_refs):
            here = jnp.logical_and(part >= 0, jnp.bitwise_xor(part, own) == slot)

            @pl.when(here)
            def _(ref=ref):
                copy_side(side, lambda at: ref[pl.ds(at, 8), :])

        return carry

    lax.fori_loop(0, 4, body, 0)


def incoming_lines(sides, place, partner_ref, flip_ref):
    lines = []
    for side in range(4):
        glued = partner_ref[0, side] >= 0
        turned = flip_ref[0, side] == 1
        line = []
        for i in range(6):
            at = pl.multiple_of(place * SIDE + jnp.where(turned, 5 - i, i) * 8, 8)
            value = sides[side, pl.ds(at, 8), :]
            value = jnp.where(turned, reverse_rows(value), value)
            line.append(jnp.where(glued, value, 0.0))
        lines.append(line)
    return lines


def own_reaction(own_lines, rates, flags, scale):
    ex = ex_ids()
    edge = float(WEIGHTS[0])
    corner = float(STIFF[0, 0])
    lines = []
    for side in range(4):
        line = own_lines[side]
        along = line_product(line, STIFF_HAT)
        out = [
            (along[i] * edge + line[i] * (corner + rates * edge)) * float(WEIGHTS[i])
            for i in range(6)
        ]
        first = out[0] + pltpu.roll(out[5], 1, 0)
        last = out[5] + pltpu.roll(out[0], 7, 0)
        out[0] = jnp.where(ex > 0, first, 0.0)
        out[5] = jnp.where(ex < 7, last, 0.0)
        lines.append([value * (flags[side] * scale) for value in out])
    return lines


def pick(index, values):
    if isinstance(index, int):
        return values[index]
    chosen = jnp.int32(values[0])
    for place in range(1, len(values)):
        chosen = jnp.where(index == place, jnp.int32(values[place]), chosen)
    return chosen


def offset_of(place, size):
    return (0, 3, 1, 2)[place] if size == 4 else place


def block_of(place, four, size):
    return place if isinstance(four, int) else jnp.bitwise_xor(four, offset_of(place, size))


def pack_kernel(step, count, dynamic, chunk, chunks, starts, offsets, ids_ref, source_ref, *refs):
    send_refs = refs[:count]
    load = chunk == 0
    scratch = refs[-2] if load else refs[-1]
    width = scratch.shape[1]
    held_ref = refs[count] if load else source_ref
    modes = held_ref.shape[1]
    four = ids_ref[1] if dynamic else 0
    copies = []
    if load:
        for comp in range(3):
            copies.append(
                pltpu.make_async_copy(source_ref.at[comp], held_ref.at[comp], refs[-1].at[comp])
            )
            copies[-1].start()
    for place in range(count):
        index = block_of(place, four, count)
        table = order_table(step, pick(index, offsets[chunk::chunks]), scratch)
        if place == 0:
            for copy in copies:
                copy.wait()
        start = pick(index, starts[chunk::chunks])
        start = start if isinstance(start, int) else pl.multiple_of(start, LANES)
        rows = [held_ref[comp, :, pl.ds(start, width)] for comp in range(3)]
        pad = jnp.zeros((LANES - 3 * modes, width), F32)
        high, low = halves(jnp.concatenate(rows + [pad], axis=0))
        both = jnp.concatenate([high, low], axis=0)
        out = dot(table, both, ((1,), (1,)))
        out = out[:, :LANES] + out[:, LANES:]
        if not is_packed(modes):
            send_refs[place][...] = out
            continue
        values = [out[point * step : (point + 1) * step] for point in range(POINTS)]
        for at, value in enumerate(pack_lanes(values, modes)):
            send_refs[place][pl.ds(at * step, step), :] = value


def product_kernel(modes, step, count, dynamic, role, ids_ref, *refs):
    recv_refs = refs[:count]
    inverse_ref, back_ref = refs[count : count + 2]
    refs = refs[count + 2 :]
    if role == 1:
        carry_ref, refs = refs[0], refs[1:]
    send_refs, refs = refs[:count], refs[count:]
    if role == 0:
        carry_ref, refs = refs[0], refs[1:]
    full, lined, phys, prod, spec = refs
    four = ids_ref[1] if dynamic else 0
    packed = is_packed(modes)
    for place in range(count):
        index = block_of(place, four, count)
        if packed:
            ready = 3 * POINTS // 4
            values = [recv_refs[place][pl.ds(at * step, step), :] for at in range(ready)]
            for at, value in enumerate(unpack_lanes(values, modes)):
                full[place, pl.ds(at * step, step), :] = value
        else:
            full[place] = recv_refs[place][...]
        first = index * LANES
        first = first if isinstance(first, int) else pl.multiple_of(first, LANES)
        lined[:, pl.ds(first, LANES)] = full[place]
    phys[...] = dot3(lined[...], inverse_ref[...])
    width = 2 * LANES

    def field(point, comp):
        return phys[pl.ds(point * step, step), comp * LANES : (comp + 1) * LANES]

    for comp in range(3):
        wide = pl.ds(comp * width, LANES)
        for iy in range(6):
            line = []
            for ix in range(6):
                point = 6 * iy + ix
                value = field(point, comp)
                line.append(value * field(point, 0))
                prod[pl.ds(point * step, step), pl.ds(comp * width + LANES, LANES)] = (
                    value * field(point, 2)
                )
            out = line_product(line, DERIV, -1.0)
            for ix in range(6):
                prod[pl.ds((6 * iy + ix) * step, step), wide] = out[ix]
        for ix in range(6):
            line = [field(6 * iy + ix, comp) * field(6 * iy + ix, 1) for iy in range(6)]
            out = line_product(line, DERIV, -1.0)
            for iy in range(6):
                at = pl.ds((6 * iy + ix) * step, step)
                prod[at, wide] = prod[at, wide] + out[iy]
        spec[comp] = dot3(prod[:, comp * width : (comp + 1) * width], back_ref[...])

    lane_block = lax.div(lax.broadcasted_iota(jnp.int32, (step, LANES), 1), jnp.int32(modes))
    masks = []
    shifts = []
    for place in range(count):
        index = block_of(place, four, count)
        masks.append([lane_block == lax.rem(index + comp, count) for comp in range(2)])
        shifts.append(lax.rem(LANES - index * modes, LANES))
    kept = []
    for point in range(POINTS):
        at = pl.ds(point * step, step)
        mass = float(WEIGHTS[point // 6] * WEIGHTS[point % 6])
        turned = [spec[0, at, :]]
        turned += [pltpu.roll(spec[comp, at, :], comp * modes, 1) for comp in (1, 2)]
        for place in range(count):
            mask = masks[place]
            mixed = jnp.where(mask[0], turned[0], jnp.where(mask[1], turned[1], turned[2]))
            nonlinear = pltpu.roll(mixed, shifts[place], 1)
            full[place, at, :] = mass * (REACTION * full[place, at, :] + nonlinear)
    ex = None if role is None else ex_ids()
    for place in range(count):
        values = [full[place, pl.ds(point * step, step), :] for point in range(POINTS)]
        if role is not None:
            left = jnp.zeros((8, LANES), F32)
            sent = []
            for iy in range(6):
                line = values[6 * iy : 6 * iy + 6]
                line[5] = line[5] + jnp.where(ex < 7, pltpu.roll(line[0], 7, 0), 0.0)
                if role == 0 and iy == 5:
                    for ix in range(6):
                        carry_ref[place, pl.ds(ix * 8, 8), :] = line[ix]
                    continue
                if role == 1 and iy == 0:
                    line = [line[ix] + carry_ref[place, pl.ds(ix * 8, 8), :] for ix in range(6)]
                left = jnp.where(ex == iy, pltpu.roll(line[0], iy, 0) if iy else line[0], left)
                sent += line[1:]
            values = sent + [left]
            values += [left] * (32 - len(values))
        for at, value in enumerate(pack_lanes(values, modes)):
            send_refs[place][pl.ds(at * step, step), :] = value


def spread_rows(values, masks):
    ex = ex_ids()
    rows = (len(values) - 1) // 5
    left = values[5 * rows]
    points = []
    for iy in range(rows):
        line = values[5 * iy : 5 * iy + 5]
        start = pltpu.roll(left, 8 - iy, 0) if iy else left
        first = jnp.where(ex == 0, start, pltpu.roll(line[4], 1, 0))
        points += [first * masks[0]] + line[:4] + [line[4] * masks[1]]
    return points


def first_kernel(modes, step, count, chunks, dynamic, lean, ids_ref, partner_ref, *refs):
    recv_refs = refs[: count * chunks]
    base_ref, lines_ref, work = refs[count * chunks :]
    four = ids_ref[1] if dynamic else 0
    rates = helmholtz_rates(ids_ref[1], modes)
    flags = glued_flags(partner_ref)
    masks = col_masks(flags)
    for place in range(count):
        block = block_of(place, four, count)
        shares = []
        for chunk in range(chunks):
            ref = recv_refs[chunk * count + place]
            ready = ref.shape[0] // step
            shares.append(
                unpack_lanes([ref[pl.ds(at * step, step), :] for at in range(ready)], modes)
            )
        if lean:
            odd = spread_rows(shares[1][:31], masks)
            shares = [spread_rows(shares[0][:26], masks) + odd[:6], odd]
        for chunk in range(chunks):
            first = (block * chunks + chunk) * step
            for point in range(POINTS):
                at = point * 64 + first
                at = at if isinstance(at, int) else pl.multiple_of(at, step)
                base_ref[pl.ds(at, step), :] = shares[chunk][point]
    if not lean:
        for ey in range(BLOCKS):
            for iy in range(6):
                first, last = join_cols(
                    get(base_ref, 6 * iy, ey), get(base_ref, 6 * iy + 5, ey), masks
                )
                put(base_ref, 6 * iy, ey, first)
                put(base_ref, 6 * iy + 5, ey, last)
    join_rows(base_ref, flags, range(1, 7, 2) if lean else range(7))
    apply_local(base_ref, work, rates, flags)
    write_lines(base_ref, lines_ref, 0, modes)
    write_lines(work, lines_ref, line_rows(modes), modes)


def sum_rows(sums):
    return [jnp.sum(value, axis=0, keepdims=True) for value in sums]


def second_kernel(modes, slots, ids_ref, partner_ref, side_ref, flip_ref, *refs):
    gath_refs = refs[:slots]
    lines_ref, _, k0_ref, k1_ref, k2_ref, next_ref, sums_ref, work, sides = refs[slots:]
    rates = helmholtz_rates(ids_ref[1], modes)
    flags = glued_flags(partner_ref)
    collect_sides(gath_refs, ids_ref[0], partner_ref, side_ref, sides, modes)
    back = own_reaction(load_lines(lines_ref, modes), rates, flags, 1.0)
    add_lines(k0_ref, incoming_lines(sides, 0, partner_ref, flip_ref))
    apply_local(k0_ref, work, rates, flags)
    add_lines(work, add_all(incoming_lines(sides, 1, partner_ref, flip_ref), back))
    sums = apply_local(
        k1_ref, work, rates, flags,
        terms=[(1.0 / SPREAD, work), (-CENTRE / SPREAD, k0_ref)],
        products=[(1, 1), (1, -1), (-1, -1)],
    )
    write_lines(work, next_ref, 0, modes)
    apply_local(
        k2_ref, work, rates, flags,
        terms=[(TWICE, work), (-CENTRE * TWICE, k1_ref), (-1.0, k0_ref)],
    )
    write_lines(work, next_ref, line_rows(modes), modes)
    sums_ref[...] = jnp.concatenate(sum_rows(sums) + [jnp.zeros((5, LANES), F32)], axis=0)


def third_kernel(modes, slots, ids_ref, partner_ref, side_ref, flip_ref, *refs):
    gath_refs = refs[:slots]
    lines_ref, k1_ref, sums_ref, _ = refs[slots : slots + 4]
    k2_ref, k3_ref, a3_ref, next_ref, work, sides = refs[slots + 4 :]
    rates = helmholtz_rates(ids_ref[1], modes)
    flags = glued_flags(partner_ref)
    collect_sides(gath_refs, ids_ref[0], partner_ref, side_ref, sides, modes)
    back = own_reaction(load_lines(lines_ref, modes), rates, flags, TWICE)
    incoming = incoming_lines(sides, 0, partner_ref, flip_ref)
    add_lines(k2_ref, [[value * TWICE for value in line] for line in incoming])
    apply_local(k2_ref, work, rates, flags)
    add_lines(work, add_all(incoming_lines(sides, 1, partner_ref, flip_ref), back))
    sums = apply_local(
        k3_ref, a3_ref, rates, flags,
        terms=[(TWICE, work), (-CENTRE * TWICE, k2_ref), (-1.0, k1_ref)],
        products=[(2, 1), (1, 1), (1, -1), (-1, -1)],
        energy=True,
    )
    write_lines(a3_ref, next_ref, 0, modes)
    next_ref[pl.ds(line_rows(modes), SUM_ROWS), :] = jnp.concatenate(
        [sums_ref[:3, :]] + sum_rows(sums), axis=0
    )


def turn_kernel(starts, offsets, fields, has_scatter, *refs):
    field_refs = refs[:fields]
    out_refs = refs[fields : 2 * fields]
    scratch, rows = refs[-2:]
    step = rows.shape[0] // POINTS
    used = out_refs[0].shape[0]
    width = scratch.shape[1]
    for out_ref in out_refs:
        out_ref[...] = jnp.zeros(out_ref.shape, F32)
    for unit in range(len(starts)):
        table = order_table(step, offsets[unit], scratch)
        for field_ref, out_ref in zip(field_refs, out_refs):
            for point in range(POINTS):
                rows[pl.ds(point * step, step), :] = field_ref[pl.ds(point * 64 + unit * step, step), :]
            high, low = halves(jnp.transpose(rows[...])[:used])
            both = jnp.concatenate([high, low], axis=0)
            out = dot(both, table, ((1,), (0,)))
            window = pl.ds(starts[unit], width)
            out_ref[:, window] = out_ref[:, window] + (out[:used] + out[used:])
    if has_scatter:
        scatter_ref = refs[2 * fields]
        place = lax.broadcasted_iota(jnp.int32, (SIDE, NODES), 0)
        at = 6 * jnp.bitwise_and(place, 7) + lax.shift_right_logical(place, 3)
        node = lax.broadcasted_iota(jnp.int32, (SIDE, NODES), 1)
        targets = (at, at * SIDE + SIDE - 1, at + (SIDE - 1) * SIDE, at * SIDE)
        for side, target in enumerate(targets):
            scatter_ref[side * SIDE : (side + 1) * SIDE, :] = jnp.where(
                node == target, 1.0, 0.0
            ).astype(BF16)


def conjugate_coefficients(gram, energy):
    zero = jnp.zeros_like(energy)

    def image(vec):
        out = [zero] * 5
        for j in range(4):
            if vec[j] is None:
                continue
            out[j] = out[j] + CENTRE * vec[j]
            out[j + 1] = out[j + 1] + (SPREAD if j == 0 else 0.5 * SPREAD) * vec[j]
            if j > 0:
                out[j - 1] = out[j - 1] + 0.5 * SPREAD * vec[j]
        return out

    def inner(left, right):
        total = zero
        for i in range(4):
            for j in range(4):
                if left[i] is not None and right[j] is not None:
                    total = total + left[i] * right[j] * gram[i][j]
        return total

    moments = [[None] * 4 for _ in range(4)]
    for j in range(3):
        column = image([jnp.ones_like(energy) if i == j else None for i in range(4)])
        for i in range(4):
            total = zero
            for m in range(max(j - 1, 0), j + 2):
                total = total + column[m] * gram[i][m]
            moments[i][j] = total
    for i in range(3):
        moments[i][3] = moments[3][i]
    moments[3][3] = energy

    def pad(vec, size):
        return [vec[i] if i < size else None for i in range(4)]

    residual = [jnp.ones_like(energy), zero, zero, zero, zero]
    direction = list(residual)
    solution = [zero] * 4
    norm_now = gram[0][0]
    for step in range(ITERS):
        trimmed = pad(direction, step + 1)
        bend = zero
        for i in range(step + 1):
            for j in range(step + 1):
                bend = bend + direction[i] * direction[j] * moments[i][j]
        alpha = norm_now / bend
        moved = image(trimmed)
        for i in range(step + 1):
            solution[i] = solution[i] + alpha * direction[i]
        for i in range(step + 2):
            residual[i] = residual[i] - alpha * moved[i]
        if step < ITERS - 1:
            kept = pad(residual, step + 2)
            norm_next = inner(kept, kept)
            ratio = norm_next / norm_now
            direction = [residual[i] + ratio * direction[i] for i in range(5)]
            norm_now = norm_next
    return solution, residual


def last_kernel(slots, ids_ref, partner_ref, side_ref, flip_ref, *refs):
    gath_refs = refs[:slots]
    turned = refs[slots : slots + 5]
    scatter_ref, sol_out, res_out, lines, sides, sol_ref, res_ref, sems = refs[slots + 5 :]
    modes = sol_ref.shape[1]
    used = 3 * modes
    where = pl.ds(line_rows(modes), SUM_ROWS)
    if slots == 1:
        parts = [gath_refs[0][part, where, :] for part in range(gath_refs[0].shape[0])]
    else:
        parts = [ref[where, :] for ref in gath_refs]
    sums = functools.reduce(lambda left, right: left + right, parts)
    g00, g01, g11, g12, g22, g23, g33, energy = [
        jnp.broadcast_to(sums[place : place + 1, :], (8, LANES)) for place in range(8)
    ]
    g02 = 2.0 * g11 - g00
    g03 = 2.0 * g12 - g01
    g13 = (g22 - g00) + g11
    gram = [
        [g00, g01, g02, g03],
        [g01, g11, g12, g13],
        [g02, g12, g22, g23],
        [g03, g13, g23, g33],
    ]
    solution, residual = conjugate_coefficients(gram, energy)
    on_a3 = residual[4] * TWICE
    on_k3 = residual[3] - on_a3 * CENTRE
    on_k2 = residual[2] - residual[4]
    factors = list(solution) + [residual[0], residual[1], on_k2, on_k3, on_a3]
    columns = jnp.transpose(
        jnp.concatenate([value[:1] for value in factors] + [jnp.zeros((LANES - 9, LANES), F32)], axis=0)
    )
    copies = []

    def send(comp, place, buffer, out):
        copies.append(pltpu.make_async_copy(buffer.at[comp], out.at[comp], sems.at[2 * comp + place]))
        copies[-1].start()

    def scaled(at, first):
        rows = [ref[at : at + 8, :] for ref in turned[: 5 if first else 4]]
        terms = [columns[at : at + 8, first + k : first + k + 1] * row for k, row in enumerate(rows)]
        return functools.reduce(lambda left, right: left + right, terms)

    for comp in range(3):
        for first in range(0, modes, 8):
            sol_ref[comp, first : first + 8, :] = scaled(comp * modes + first, 0)
        send(comp, 0, sol_ref, sol_out)
    collect_sides(gath_refs, ids_ref[0], partner_ref, side_ref, sides, modes)
    incoming = incoming_lines(sides, 0, partner_ref, flip_ref)
    for side in range(4):
        for i in range(6):
            lines[pl.ds(side * SIDE + i * 8, 8), :] = incoming[side][i] * on_a3
    high, low = halves(jnp.transpose(lines[...])[:used])
    added = dot(jnp.concatenate([high, low], axis=0), scatter_ref[...], ((1,), (0,)))
    for comp in range(3):
        for first in range(0, modes, 8):
            at = comp * modes + first
            res_ref[comp, first : first + 8, :] = scaled(at, 4) + (
                added[at : at + 8] + added[used + at : used + at + 8]
            )
        send(comp, 1, res_ref, res_out)
    for copy in copies:
        copy.wait()


def call(kernel, name, out_shapes, args, scratch, scalars=0, keep=True, aliases=None, outside=False):
    smem = pl.BlockSpec(memory_space=pltpu.SMEM)
    vmem = pl.BlockSpec(memory_space=pltpu.VMEM)
    shapes = [shape if isinstance(shape, jax.ShapeDtypeStruct) else jax.ShapeDtypeStruct(shape, F32) for shape in out_shapes]
    return pl.pallas_call(
        kernel,
        name=name,
        out_shape=[pltpu.VMEM(one.shape, one.dtype) if keep else one for one in shapes],
        in_specs=[smem] * scalars + [pl.BlockSpec(memory_space=pltpu.HBM) if outside else vmem] * (len(args) - scalars),
        out_specs=[vmem if keep else pl.BlockSpec(memory_space=pltpu.HBM)] * len(out_shapes),
        scratch_shapes=[pltpu.VMEM(one, F32) if isinstance(one, tuple) else one for one in scratch],
        input_output_aliases=aliases or {},
        compiler_params=pltpu.CompilerParams(vmem_limit_bytes=VMEM_LIMIT),
    )(*args[:scalars], *[held(arg, pltpu.HBM if outside else pltpu.VMEM) for arg in args[scalars:]])


def held(arg, space):
    return arg if isinstance(arg, np.ndarray) else pltpu.with_memory_space_constraint(arg, space)


def swap_blocks(blocks, dynamic):
    if not dynamic:
        stacked = lax.all_to_all(jnp.stack(blocks), "four", split_axis=0, concat_axis=0, tiled=True)
        return [stacked[place] for place in range(len(blocks))]
    size = len(blocks)
    swapped = list(blocks)
    for place in range(size - 1, 0, -1):
        swapped[place] = lax.ppermute(blocks[place], "four", [(i, i ^ offset_of(place, size)) for i in range(size)])
    return swapped


def share_lines(lines, beside=()):
    parts = lax.axis_size("dom")
    if parts != 8:
        return [lax.all_gather(lines, "dom", axis=0, tiled=False)], list(beside)
    slots = [lines] + [None] * (parts - 1)
    for slot in range(2, parts, 2):
        slots[slot] = lax.ppermute(lines, "dom", [(i, i ^ slot) for i in range(parts)])
        if beside and slot == parts // 2:
            slots[slot], *beside = lax.optimization_barrier((slots[slot], *beside))
    for slot in range(0, parts, 2):
        slots[slot + 1] = lax.ppermute(slots[slot], "dom", [(i, i ^ 1) for i in range(parts)])
    return slots, list(beside)


def shards(velocity, partner, partner_side, flipped):
    modes = velocity.shape[1]
    count = lax.axis_size("four")
    step, chunks = chunk_sizes(count)
    rows = POINTS * step
    sent_rows = 3 * rows // 4 if is_packed(modes) else rows
    dynamic = step == BLOCKS
    inverse, back = transform_tables(count)
    starts, offsets = unit_windows(count)
    table = (rows, 3 * LANES)
    ids = jnp.stack([lax.axis_index("dom"), lax.axis_index("four")]).astype(jnp.int32)
    field = (NODES, LANES)
    blocks = [(sent_rows, LANES)] * count
    lined = line_rows(modes)

    lean = dynamic and chunks == 2 and is_packed(modes)
    spread = []
    source = velocity
    for chunk in range(chunks):
        load = chunk == 0
        sent = call(
            functools.partial(pack_kernel, step, count, dynamic, chunk, chunks, starts, offsets),
            "pack",
            blocks + [velocity.shape] * load,
            (ids, source),
            [table] + [pltpu.SemaphoreType.DMA((3,))] * load,
            scalars=1,
            outside=load,
        )
        if load:
            *sent, source = sent
        spread.append(swap_blocks(sent, dynamic))
    local = []
    carry = []
    for chunk in range(chunks):
        role = chunk if lean else None
        out = [(24 * step, LANES)] * count if lean else blocks
        sent = call(
            functools.partial(product_kernel, modes, step, count, dynamic, role),
            "products",
            out + [(count, SIDE, LANES)] * (role == 0),
            (ids, *spread[chunk], inverse, back, *carry),
            [
                (count, rows, LANES),
                (rows, count * LANES),
                (rows, 3 * LANES),
                (rows, 6 * LANES),
                (3, rows, LANES),
            ],
            scalars=1,
        )
        if role == 0:
            *sent, held_row = sent
            carry = [held_row]
        local += swap_blocks(sent, dynamic)

    base, lines = call(
        functools.partial(first_kernel, modes, step, count, chunks, dynamic, lean),
        "first",
        [field, (2 * lined, LANES)],
        (ids, partner, *local),
        [field],
        scalars=2,
    )
    tables = (ids, partner, partner_side, flipped)
    gathered, (base,) = share_lines(lines, (base,))
    slots = len(gathered)
    k0, k1, base, lines, sums = call(
        functools.partial(second_kernel, modes, slots),
        "second",
        [field, field, field, (2 * lined, LANES), (8, LANES)],
        (*tables, *gathered, lines, base),
        [field, (4, 2 * SIDE, LANES)],
        scalars=4,
        aliases={4 + slots + 1: 0},
    )
    flat = (3 * modes, NODES)
    turned = call(
        functools.partial(turn_kernel, starts, offsets, 2, True),
        "turn",
        [flat, flat, jax.ShapeDtypeStruct((4 * SIDE, NODES), BF16)],
        (k0, k1),
        [table, (rows, LANES)],
    )
    gathered, (t0, t1, scatter) = share_lines(lines, turned)
    k2, k3, a3, lines = call(
        functools.partial(third_kernel, modes, slots),
        "third",
        [field, field, field, (lined + SUM_ROWS, LANES)],
        (*tables, *gathered, lines, k1, sums, base),
        [field, (4, 2 * SIDE, LANES)],
        scalars=4,
        aliases={4 + slots + 3: 0},
    )
    turned = call(
        functools.partial(turn_kernel, starts, offsets, 3, False),
        "turn",
        [flat, flat, flat],
        (k2, k3, a3),
        [table, (rows, LANES)],
    )
    gathered, (t2, t3, ta) = share_lines(lines, turned)
    outs = call(
        functools.partial(last_kernel, slots),
        "last",
        [velocity.shape, velocity.shape],
        (*tables, *gathered, t0, t1, t2, t3, ta, scatter),
        [
            (4 * SIDE, LANES),
            (4, SIDE, LANES),
            velocity.shape,
            velocity.shape,
            pltpu.SemaphoreType.DMA((6,)),
        ],
        scalars=4,
        keep=False,
    )
    return tuple(outs)


def solution(mesh):
    return jax.shard_map(
        shards,
        mesh=mesh,
        in_specs=(P(None, "four", "dom"), P("dom", None), P("dom", None), P("dom", None)),
        out_specs=(P(None, "four", "dom"), P(None, "four", "dom")),
        check_vma=False,
    )
```
